32 devices in a mesh: seq: 16 (over z, x, core), batch: 2 (over y).
Axes of the slice: x: 2, y: 2, z: 4, core: 2. Of those that a mesh axis runs over, the one named last changes fastest.
Arguments:
- inputs: bfloat16 [2, 4096, 768], P('batch', 'seq'), may hold values from -6 to 6
- lengths: int32 [2], P('batch'), may hold values from 1024 to 4096, as said below
- cotangent: bfloat16 [2, 4096, 768], P('batch', 'seq'), may hold values from -6 to 6
- triple_weight: float32 [768, 2304], P(('seq', 'batch')), may hold values from -0.3125 to 0.3125
- query_bias: float32 [768], P(('seq', 'batch')), may hold values from -3 to 3
- value_bias: float32 [768], P(('seq', 'batch')), may hold values from -3 to 3
- output_weight: float32 [768, 768], P(('seq', 'batch')), may hold values from -1.75 to 1.75
- output_bias: float32 [768], P(('seq', 'batch')), may hold values from -3 to 3
- first_gain: float32 [768], P(('seq', 'batch')), may hold values from 0.5 to 1.5
- first_shift: float32 [768], P(('seq', 'batch')), may hold values from -3 to 3
- expand_weight: float32 [768, 3072], P(('seq', 'batch')), may hold values from -0.21875 to 0.21875
- expand_bias: float32 [3072], P(('seq', 'batch')), may hold values from -3 to 3
- shrink_weight: float32 [3072, 768], P(('seq', 'batch')), may hold values from -0.109375 to 0.109375
- shrink_bias: float32 [768], P(('seq', 'batch')), may hold values from -3 to 3
- second_gain: float32 [768], P(('seq', 'batch')), may hold values from 0.5 to 1.5
- second_shift: float32 [768], P(('seq', 'batch')), may hold values from -3 to 3
Outputs:
- output: bfloat16 [2, 4096, 768], P('batch', 'seq')
- input_grad: bfloat16 [2, 4096, 768], P('batch', 'seq')
- grad_triple_weight: float32 [768, 2304], P(('seq', 'batch'))
- grad_query_bias: float32 [768], P(('seq', 'batch'))
- grad_value_bias: float32 [768], P(('seq', 'batch'))
- grad_output_weight: float32 [768, 768], P(('seq', 'batch'))
- grad_output_bias: float32 [768], P(('seq', 'batch'))
- grad_first_gain: float32 [768], P(('seq', 'batch'))
- grad_first_shift: float32 [768], P(('seq', 'batch'))
- grad_expand_weight: float32 [768, 3072], P(('seq', 'batch'))
- grad_expand_bias: float32 [3072], P(('seq', 'batch'))
- grad_shrink_weight: float32 [3072, 768], P(('seq', 'batch'))
- grad_shrink_bias: float32 [768], P(('seq', 'batch'))
- grad_second_gain: float32 [768], P(('seq', 'batch'))
- grad_second_shift: float32 [768], P(('seq', 'batch'))
The draws below stay inside these ranges and needn't reach their ends.
Inputs may be any that keep to these rules, and one draw needn't show every extreme that they name: The first lengths slots of a sequence hold its tokens, the others are padding; in every draw some sequence fills all 4096 slots.
All inputs are finite; a program needn't handle non-finite values.
Results may differ from the reference program's by a relative error of at most 0.019.
The reference program's roundings to bfloat16 on the way count: a program that leaves them out, or rounds other values in their place, can miss the bound.
Values may be sent and summed in bfloat16 or wider, within the bound.
No kernel may reach another device: no remote copies, remote signals or barrier semaphores. Data moves between devices by JAX's collectives and lax.ppermute only.
A program may use at most 192 MiB of HBM per device.

```python
import math
import jax
import jax.numpy as jnp
from jax import lax

D = 768
HEADS = 12
HEAD_DIM = 64
FF = 3072
LEN = 4096
SEQS = 2


def draw_lengths(key, part):
    first_draw = jax.random.randint(jax.random.fold_in(key, 11), (SEQS,), LEN // 4, LEN + 1)
    second_draw = jax.random.randint(jax.random.fold_in(key, 12), (SEQS,), LEN // 4, LEN + 1)
    drawn = jnp.maximum(first_draw, second_draw)
    chosen = jax.random.randint(jax.random.fold_in(key, 13), (), 0, SEQS)
    return jnp.where(jnp.arange(SEQS) == chosen, LEN, drawn).astype(jnp.int32)


def block_scale(own_key, extent, cuts, smallest, top_value):
    loudness = 1.0
    for position, shards_of in cuts:
        steps = jax.random.uniform(jax.random.fold_in(jax.random.fold_in(own_key, 6), position), (shards_of,), jnp.float32, smallest / len(cuts), top_value / len(cuts))
        loudness = loudness * jnp.repeat(jnp.exp(steps), extent[position] // shards_of).reshape((-1,) + (1,) * (len(extent) - 1 - position))
    return loudness


def bell_draw(own_key, extent, scale, reach, pieces=(), kind=jnp.bfloat16):
    values = scale * jax.random.normal(own_key, extent, jnp.float32)
    if pieces:
        values = values * block_scale(own_key, extent, pieces, -0.22, 0.18)
    return jnp.clip(values, -reach, reach).astype(kind)


def setup_inputs(seed: int = 0) -> dict:
    streams_of = jax.random.split(jax.random.key(seed), 17)
    return {
        "inputs": bell_draw(streams_of[0], (SEQS, LEN, D), 1.0, 6.0, ((0, 2), (1, 16))),
        "lengths": draw_lengths(jax.random.fold_in(streams_of[16], 71), 0),
        "cotangent": bell_draw(streams_of[2], (SEQS, LEN, D), 1.0, 6.0, ((0, 2), (1, 16))),
        "triple_weight": bell_draw(streams_of[3], (D, 3 * D), (D // 2) ** -0.5, 0.3125, ((0, 32),), jnp.float32),
        "query_bias": bell_draw(streams_of[4], (D,), 0.5, 3.0, ((0, 32),), jnp.float32),
        "value_bias": bell_draw(streams_of[5], (D,), 0.5, 3.0, ((0, 32),), jnp.float32),
        "output_weight": bell_draw(streams_of[6], (D, D), (D // 64) ** -0.5, 1.75, ((0, 32),), jnp.float32),
        "output_bias": bell_draw(streams_of[7], (D,), 0.5, 3.0, ((0, 32),), jnp.float32),
        "first_gain": jnp.clip(1.0 + 0.1 * jax.random.normal(streams_of[8], (D,), jnp.float32), 0.5, 1.5),
        "first_shift": bell_draw(streams_of[9], (D,), 0.5, 3.0, ((0, 32),), jnp.float32),
        "expand_weight": bell_draw(streams_of[10], (D, FF), D ** -0.5, 0.21875, ((0, 32),), jnp.float32),
        "expand_bias": bell_draw(streams_of[11], (FF,), 0.5, 3.0, ((0, 32),), jnp.float32),
        "shrink_weight": bell_draw(streams_of[12], (FF, D), FF ** -0.5, 0.109375, ((0, 32),), jnp.float32),
        "shrink_bias": bell_draw(streams_of[13], (D,), 0.5, 3.0, ((0, 32),), jnp.float32),
        "second_gain": jnp.clip(1.0 + 0.1 * jax.random.normal(streams_of[14], (D,), jnp.float32), 0.5, 1.5),
        "second_shift": bell_draw(streams_of[15], (D,), 0.5, 3.0, ((0, 32),), jnp.float32),
    }


@jax.custom_vjp
def low(v):
    return lax.optimization_barrier(v.astype(jnp.bfloat16)).astype(jnp.float32)

@jax.custom_vjp
def low_back(v):
    return v

def low_keep(v):
    return (low(v), None)

def low_pass(kept, grad):
    return (grad,)

def back_keep(v):
    return (v, None)

def back_low(kept, grad):
    return (low(grad),)
low.defvjp(low_keep, low_pass)
low_back.defvjp(back_keep, back_low)
highest = lax.Precision.HIGHEST
masked_score = -1e+30
norm_eps = 1e-12

def layer_norm(row_block, norm_gain, norm_shift):
    center = row_block - lax.optimization_barrier(jnp.mean(row_block, axis=-1, keepdims=True))
    spread = lax.optimization_barrier(jnp.mean(center * center, axis=-1, keepdims=True))
    return center * lax.rsqrt(spread + norm_eps) * norm_gain + norm_shift

def one_sequence(tokens, length, weights):
    triple_weight, query_bias, value_bias, output_weight, output_bias, first_gain, first_shift, expand_weight, expand_bias, shrink_weight, shrink_bias, second_gain, second_shift = weights
    row_total = tokens.shape[0]
    model_width = tokens.shape[1]
    joint_rows = jnp.dot(tokens, low(triple_weight), precision=highest)
    queries = low_back(low(joint_rows[:, :model_width] + low(query_bias)))
    key_rows = low_back(low(joint_rows[:, model_width:2 * model_width]))
    value_rows = low_back(low(joint_rows[:, 2 * model_width:] + low(value_bias)))
    query_heads = queries.reshape(row_total, HEADS, HEAD_DIM)
    key_heads = key_rows.reshape(row_total, HEADS, HEAD_DIM)
    value_heads = value_rows.reshape(row_total, HEADS, HEAD_DIM)
    valid_keys = jnp.arange(row_total) < length
    block_rows = math.gcd(row_total, 512)
    score_scale = HEAD_DIM ** (-0.5)

    def attend(query_block):
        scores = jnp.einsum('rhd,khd->hrk', query_block, key_heads, precision=highest) * score_scale
        scores = low_back(scores)
        scores = jnp.where(valid_keys[None, None, :], scores, masked_score)
        prob_block = low(jax.nn.softmax(scores, axis=-1))
        mixed_rows = jnp.einsum('hrk,khd->rhd', prob_block, value_heads, precision=highest)
        return mixed_rows.reshape(query_block.shape[0], model_width)
    attended = lax.map(jax.checkpoint(attend), query_heads.reshape(row_total // block_rows, block_rows, HEADS, HEAD_DIM))
    attended = low_back(low(attended.reshape(row_total, model_width)))
    branch = low_back(jnp.dot(attended, low(output_weight), precision=highest) + low(output_bias))
    hidden = layer_norm(tokens + branch, low(first_gain), low(first_shift))
    expanded = low_back(jnp.dot(low(hidden), low(expand_weight), precision=highest) + low(expand_bias))
    active = jax.nn.gelu(expanded, approximate=False)
    shrunk = low_back(jnp.dot(low(active), low(shrink_weight), precision=highest) + low(shrink_bias))
    return layer_norm(hidden + shrunk, low(second_gain), low(second_shift))

def reference(inputs, lengths, cotangent, triple_weight, query_bias, value_bias, output_weight, output_bias, first_gain, first_shift, expand_weight, expand_bias, shrink_weight, shrink_bias, second_gain, second_shift):
    weights = (triple_weight, query_bias, value_bias, output_weight, output_bias, first_gain, first_shift, expand_weight, expand_bias, shrink_weight, shrink_bias, second_gain, second_shift)
    tokens = inputs.astype(jnp.float32)

    def forward(tokens_all, weights_all):

        def one_member(members):
            return one_sequence(members[0], members[1], weights_all)
        return lax.map(one_member, (tokens_all, lengths))
    results, pullback = jax.vjp(forward, tokens, weights)
    positions = jnp.arange(LEN, dtype=jnp.int32)
    row_weight = (positions[None, :] < lengths[:, None]).astype(jnp.float32)
    seed_grad = cotangent.astype(jnp.float32) * row_weight[:, :, None]
    token_grad, weight_grads = pullback(seed_grad)
    grad_triple, grad_query, grad_value, grad_output, grad_obias, grad_gain1, grad_shift1, grad_expand, grad_ebias, grad_shrink, grad_sbias, grad_gain2, grad_shift2 = weight_grads
    return (results.astype(jnp.bfloat16), token_grad.astype(jnp.bfloat16), grad_triple, grad_query, grad_value, grad_output, grad_obias, grad_gain1, grad_shift1, grad_expand, grad_ebias, grad_shrink, grad_sbias, grad_gain2, grad_shift2)
```

```python
from functools import partial

import jax
import jax.numpy as jnp
from jax import lax
from jax.experimental import pallas as pl
from jax.experimental.pallas import tpu as pltpu
from jax.sharding import Mesh, PartitionSpec as P

HEADS = 12
HEAD_DIM = 64
GROUPS = 4
OWN_HEADS = HEADS // GROUPS
OWN_WIDTH = OWN_HEADS * HEAD_DIM
LANES = 128

bf16 = jnp.bfloat16
f32 = jnp.float32
masked_score = -1e30
norm_eps = 1e-12
log2_e = 1.4426950408889634
CONTRACT_LAST = (((1,), (1,)), ((), ()))
VMEM_BYTES = 60 * 1024 * 1024
AXES = ("q", "x", "c", "b")


def layer_norm(row_block, norm_gain, norm_shift):
    center = row_block - jnp.mean(row_block, axis=-1, keepdims=True)
    spread = jnp.mean(center * center, axis=-1, keepdims=True)
    return center * lax.rsqrt(spread + norm_eps) * norm_gain + norm_shift


def split_three(value):
    high = value.astype(bf16).astype(f32)
    rest = value - high
    mid = rest.astype(bf16).astype(f32)
    low = (rest - mid).astype(bf16).astype(f32)
    return high, mid, low


def forward_kernel(first, last, block_q, block_k, *refs):
    refs = list(refs)
    where_ref = refs.pop(0)
    pieces = [refs.pop(0) for _ in range(4)]
    wk_ref, wv_ref, vb_ref = [refs.pop(0) for _ in range(3)]
    if first:
        wq_ref, qb_ref = [refs.pop(0) for _ in range(2)]
    else:
        qx_ref, peak_in, sum_in = [refs.pop(0) for _ in range(3)]
    kx_ref, vx_ref = [refs.pop(0) for _ in range(2)]
    if first:
        qx_ref, qp_ref = [refs.pop(0) for _ in range(2)]
    if last:
        att_ref, attx_ref, qx2_ref = [refs.pop(0) for _ in range(3)]
    else:
        peak_out, sum_out = [refs.pop(0) for _ in range(2)]
    (vt_ref,) = refs
    piece_rows = pieces[0].shape[0]
    rows_in = 4 * piece_rows
    lane = lax.broadcasted_iota(jnp.int32, (piece_rows, LANES), 1)
    row = lax.broadcasted_iota(jnp.int32, (piece_rows, LANES), 0)
    length = where_ref[4]
    three = (lane >= HEAD_DIM) & (lane < HEAD_DIM + 3)
    for p in range(4):
        rows = slice(p * piece_rows, (p + 1) * piece_rows)
        x = pieces[p][...]
        keys = jnp.dot(x, wk_ref[...], preferred_element_type=f32)
        values = jnp.dot(x, wv_ref[...], preferred_element_type=f32) + vb_ref[...]
        bias = jnp.where(where_ref[p] + row < length, 0.0, masked_score)
        key_extra = jnp.where(three, 1.0, jnp.where(lane == HEAD_DIM + 3, bias, 0.0))
        if first:
            queries = jnp.dot(x, wq_ref[...], preferred_element_type=f32) + qb_ref[...]
        for h in range(OWN_HEADS):
            cols = slice(h * LANES, (h + 1) * LANES)
            k = keys[:, cols]
            kx_ref[h, rows, :LANES] = (k + pltpu.roll(k, HEAD_DIM, 1)).astype(bf16)
            kx_ref[h, rows, LANES:] = (k + key_extra).astype(bf16)
            v = values[:, cols]
            vx_ref[h, rows, :] = jnp.where(three, -1.0, v).astype(bf16)
            vt = jnp.where(lane == HEAD_DIM, 1.0, v).T
            vt_ref[h, :, rows] = vt[:80].astype(bf16)
            if first:
                q = queries[:, cols].astype(bf16).astype(f32)
                qp_ref[h, rows, :] = q.astype(bf16)
                high, mid, low = split_three(q * (HEAD_DIM**-0.5 * log2_e))
                qx_ref[h, rows, :LANES] = (high + pltpu.roll(mid, HEAD_DIM, 1)).astype(bf16)
                qx_ref[h, rows, LANES:] = jnp.where(lane == HEAD_DIM + 3, 1.0, low).astype(bf16)
    for h in range(OWN_HEADS):
        for i in range(rows_in // block_q):
            cols = slice(i * block_q, (i + 1) * block_q)
            q = qx_ref[h, cols, :]
            if first:
                peak = jnp.full((1, block_q), masked_score, f32)
                total = jnp.zeros((80, block_q), f32)
            else:
                peak = peak_in[h, :1, cols]
                total = sum_in[h, :, cols]
            for j in range(rows_in // block_k):
                ks = slice(j * block_k, (j + 1) * block_k)
                s = lax.dot_general(kx_ref[h, ks, :], q, CONTRACT_LAST, preferred_element_type=f32)
                new_peak = jnp.maximum(peak, jnp.max(s, axis=0, keepdims=True))
                prob = jnp.exp2(s - new_peak).astype(bf16)
                total = total * jnp.exp2(peak - new_peak) + jnp.dot(
                    vt_ref[h, :, ks], prob, preferred_element_type=f32
                )
                peak = new_peak
            if last:
                denom = total[HEAD_DIM : HEAD_DIM + 1]
                n_high, n_mid, n_low = split_three(-(peak + jnp.log2(denom)))
                tall = jnp.concatenate(
                    [
                        total[:HEAD_DIM] / denom,
                        n_high,
                        n_mid,
                        n_low,
                        jnp.zeros((HEAD_DIM - 3, block_q), f32),
                    ],
                    axis=0,
                )
                attx_ref[h, cols, :] = tall.T
            else:
                peak_out[h, :, cols] = jnp.broadcast_to(peak, (8, block_q))
                sum_out[h, :, cols] = total
    if last:
        lane_all = lax.broadcasted_iota(jnp.int32, (rows_in, LANES), 1)
        heads = [jnp.where(lane_all < HEAD_DIM, attx_ref[h], 0.0) for h in range(OWN_HEADS)]
        att_ref[:, :LANES] = (heads[0] + pltpu.roll(heads[1], HEAD_DIM, 1)).astype(bf16)
        att_ref[:, LANES:] = heads[2][:, :HEAD_DIM].astype(bf16)
        mark = (lane_all >= HEAD_DIM) & (lane_all < HEAD_DIM + 3)
        for h in range(OWN_HEADS):
            qx2_ref[h, :, :LANES] = qx_ref[h, :, :LANES]
            qx2_ref[h, :, LANES:] = jnp.where(
                mark, attx_ref[h], qx_ref[h, :, LANES:].astype(f32)
            ).astype(bf16)


def vmem_specs(n):
    return [pl.BlockSpec(memory_space=pltpu.VMEM) for _ in range(n)]


def attend_chunk(first, last, where, pieces, weights, carry):
    rows = 4 * pieces[0].shape[0]
    wk, wv, vb, wq, qb = weights
    operands = [where, *pieces, wk, wv, vb]
    operands += [wq, qb] if first else list(carry)
    out_shape = [
        jax.ShapeDtypeStruct((OWN_HEADS, rows, 2 * LANES), bf16),
        jax.ShapeDtypeStruct((OWN_HEADS, rows, LANES), bf16),
    ]
    if first:
        out_shape += [
            jax.ShapeDtypeStruct((OWN_HEADS, rows, 2 * LANES), bf16),
            jax.ShapeDtypeStruct((OWN_HEADS, rows, LANES), bf16),
        ]
    if last:
        out_shape += [
            jax.ShapeDtypeStruct((rows, OWN_WIDTH), bf16),
            jax.ShapeDtypeStruct((OWN_HEADS, rows, LANES), f32),
            jax.ShapeDtypeStruct((OWN_HEADS, rows, 2 * LANES), bf16),
        ]
    else:
        out_shape += [
            jax.ShapeDtypeStruct((OWN_HEADS, 8, rows), f32),
            jax.ShapeDtypeStruct((OWN_HEADS, 80, rows), f32),
        ]
    return pl.pallas_call(
        partial(forward_kernel, first, last, min(512, rows), min(1024, rows)),
        out_shape=out_shape,
        in_specs=[pl.BlockSpec(memory_space=pltpu.SMEM)] + vmem_specs(len(operands) - 1),
        out_specs=vmem_specs(len(out_shape)),
        scratch_shapes=[pltpu.VMEM((OWN_HEADS, 80, rows), bf16)],
        compiler_params=pltpu.CompilerParams(vmem_limit_bytes=VMEM_BYTES),
        cost_estimate=pl.CostEstimate(
            flops=int(8e9), transcendentals=OWN_HEADS * rows * rows, bytes_accessed=int(1e7)
        ),
        name="attend_forward",
    )(*operands)


def backward_kernel(first, last, block_q, block_k, *refs):
    refs = list(refs)
    kx_ref, vx_ref, qx_ref, qp_ref, wk_ref, wv_ref = [refs.pop(0) for _ in range(6)]
    if first:
        pieces = [refs.pop(0) for _ in range(4)]
        attx_ref = refs.pop(0)
    else:
        dox_ref, dqt_in = [refs.pop(0) for _ in range(2)]
    if last:
        wq_ref = refs.pop(0)
    dkv_ref, dx_ref = [refs.pop(0) for _ in range(2)]
    if first:
        dox_ref = refs.pop(0)
    if last:
        dq_ref = refs.pop(0)
        dqt_ref = refs.pop()
    else:
        dqt_ref = refs.pop(0)
    (kt_ref,) = refs
    rows_in = kx_ref.shape[1]
    scale = HEAD_DIM**-0.5
    if first:
        piece_rows = pieces[0].shape[0]
        lane = lax.broadcasted_iota(jnp.int32, (piece_rows, LANES), 1)
        for p in range(4):
            rows = slice(p * piece_rows, (p + 1) * piece_rows)
            left = pieces[p][:, :LANES].astype(f32)
            right = pieces[p][:, LANES:].astype(f32)
            right = jnp.concatenate([right, jnp.zeros_like(right)], axis=1)
            for h, wide in enumerate((left, pltpu.roll(left, HEAD_DIM, 1), right)):
                grad = jnp.where(lane < HEAD_DIM, wide, 0.0)
                delta = jnp.sum(grad * attx_ref[h, rows, :], axis=1, keepdims=True)
                d_high, d_mid, d_low = split_three(delta)
                grad = jnp.where(lane == HEAD_DIM, d_high, grad)
                grad = jnp.where(lane == HEAD_DIM + 1, d_mid, grad)
                grad = jnp.where(lane == HEAD_DIM + 2, d_low, grad)
                dox_ref[h, rows, :] = grad.astype(bf16)
        dqt_ref[...] = jnp.zeros_like(dqt_ref)
    else:
        dqt_ref[...] = dqt_in[...]
    for h in range(OWN_HEADS):
        kt_ref[h] = kx_ref[h, :, LANES:].astype(f32).T[:HEAD_DIM].astype(bf16)
    for h in range(OWN_HEADS):
        for j in range(rows_in // block_k):
            ks = slice(j * block_k, (j + 1) * block_k)
            k = kx_ref[h, ks, :]
            v = vx_ref[h, ks, :]
            kt = kt_ref[h, :, ks]
            dk = jnp.zeros((block_k, LANES), f32)
            dv = jnp.zeros((block_k, LANES), f32)
            for i in range(rows_in // block_q):
                qs = slice(i * block_q, (i + 1) * block_q)
                s = lax.dot_general(k, qx_ref[h, qs, :], CONTRACT_LAST, preferred_element_type=f32)
                prob = jnp.exp2(s)
                do = dox_ref[h, qs, :]
                dp = lax.dot_general(v, do, CONTRACT_LAST, preferred_element_type=f32)
                ds = (prob * dp).astype(bf16)
                dv = dv + jnp.dot(prob.astype(bf16), do, preferred_element_type=f32)
                dk = dk + jnp.dot(ds, qp_ref[h, qs, :], preferred_element_type=f32)
                dqt_ref[h, :, qs] += jnp.dot(kt, ds, preferred_element_type=f32)
            dkv_ref[ks, h * LANES : (h + 1) * LANES] = (dk * scale).astype(bf16)
            cols = slice((OWN_HEADS + h) * LANES, (OWN_HEADS + h + 1) * LANES)
            dkv_ref[ks, cols] = dv.astype(bf16)
    wide = OWN_HEADS * LANES
    if last:
        for h in range(OWN_HEADS):
            dqt = dqt_ref[h] * scale
            dqt = jnp.concatenate([dqt, jnp.zeros_like(dqt)], axis=0)
            dq_ref[:, h * LANES : (h + 1) * LANES] = dqt.T.astype(bf16)
    for j in range(rows_in // block_k):
        ks = slice(j * block_k, (j + 1) * block_k)
        dx = lax.dot_general(
            dkv_ref[ks, :wide], wk_ref[...], CONTRACT_LAST, preferred_element_type=f32
        )
        dx = dx + lax.dot_general(
            dkv_ref[ks, wide:], wv_ref[...], CONTRACT_LAST, preferred_element_type=f32
        )
        if last:
            dx = dx + lax.dot_general(
                dq_ref[ks, :], wq_ref[...], CONTRACT_LAST, preferred_element_type=f32
            )
        dx_ref[ks, :] = dx.astype(bf16)


def attend_back_chunk(first, last, chunk, shared, carry):
    kx, vx = chunk
    qx2, qp, wk, wv, wq, grads, attx = shared
    rows, width = kx.shape[1], wk.shape[0]
    operands = [kx, vx, qx2, qp, wk, wv]
    operands += [*grads, attx] if first else list(carry)
    if last:
        operands.append(wq)
    out_shape = [
        jax.ShapeDtypeStruct((rows, 2 * OWN_HEADS * LANES), bf16),
        jax.ShapeDtypeStruct((rows, width), bf16),
    ]
    if first:
        out_shape.append(jax.ShapeDtypeStruct((OWN_HEADS, rows, LANES), bf16))
    scratch = [pltpu.VMEM((OWN_HEADS, HEAD_DIM, rows), bf16)]
    if last:
        out_shape.append(jax.ShapeDtypeStruct((rows, OWN_HEADS * LANES), bf16))
        scratch.append(pltpu.VMEM((OWN_HEADS, HEAD_DIM, rows), f32))
    else:
        out_shape.append(jax.ShapeDtypeStruct((OWN_HEADS, HEAD_DIM, rows), f32))
    return pl.pallas_call(
        partial(backward_kernel, first, last, min(512, rows), min(512, rows)),
        out_shape=out_shape,
        in_specs=vmem_specs(len(operands)),
        out_specs=vmem_specs(len(out_shape)),
        scratch_shapes=scratch,
        compiler_params=pltpu.CompilerParams(vmem_limit_bytes=VMEM_BYTES),
        cost_estimate=pl.CostEstimate(
            flops=int(1.5e10), transcendentals=OWN_HEADS * rows * rows, bytes_accessed=int(1e7)
        ),
        name="attend_backward",
    )(*operands)


def from_shift(value, axis, count, step):
    return lax.ppermute(value, axis, [((i + step) % count, i) for i in range(count)])


def square_swap(value, r):
    if r == 0:
        return value
    if r == 1:
        return lax.ppermute(value, "c", [(0, 1), (1, 0)])
    if r == 2:
        return lax.ppermute(value, "x", [(0, 1), (1, 0)])
    return lax.ppermute(value, ("x", "c"), [(0, 3), (3, 0), (1, 2), (2, 1)])


def pick(stacked, index):
    return lax.dynamic_index_in_dim(stacked, index, 0, keepdims=False)


def pad_heads(matrix):
    lead = matrix.shape[:-1]
    heads = matrix.reshape(*lead, OWN_HEADS, HEAD_DIM)
    pad = [(0, 0)] * len(lead) + [(0, 0), (0, LANES - HEAD_DIM)]
    return jnp.pad(heads, pad).reshape(*lead, OWN_HEADS * LANES)


def per_device(
    n_q,
    n_b,
    inputs,
    lengths,
    cotangent,
    triple_weight,
    query_bias,
    value_bias,
    output_weight,
    output_bias,
    first_gain,
    first_shift,
    expand_weight,
    expand_bias,
    shrink_weight,
    shrink_bias,
    second_gain,
    second_shift,
):
    zi, xi, ci, bi = [lax.axis_index(a) for a in AXES]
    group = 2 * xi + ci
    _, seq_rows, width = inputs.shape
    own_rows = triple_weight.shape[0]
    ff = expand_weight.shape[1]
    own_ff = shrink_weight.shape[0]
    n_dev = 4 * n_q * n_b
    x_own = inputs[0]

    fold = ff // width
    packed = jnp.concatenate(
        [
            output_weight.astype(bf16),
            expand_weight.astype(bf16)
            .reshape(own_rows, fold, width)
            .transpose(1, 0, 2)
            .reshape(fold * own_rows, width),
            shrink_weight.astype(bf16),
        ],
        axis=0,
    )

    thirds = triple_weight.astype(bf16).reshape(own_rows, 3, GROUPS, OWN_WIDTH)
    thirds = thirds.transpose(2, 1, 0, 3).reshape(GROUPS, 3 * own_rows, OWN_WIDTH)
    small = jnp.concatenate(
        [
            query_bias,
            value_bias,
            output_bias,
            first_gain,
            first_shift,
            shrink_bias,
            second_gain,
            second_shift,
            expand_bias,
        ]
    ).astype(bf16)
    small_size = small.shape[0]
    small_rows = -(-small_size // OWN_WIDTH)
    small = jnp.pad(small, (0, small_rows * OWN_WIDTH - small_size)).reshape(small_rows, OWN_WIDTH)
    parts = []
    for r in range(4):
        block = jnp.concatenate([pick(thirds, group ^ r), small], axis=0)
        parts.append(square_swap(block, r))
    square = jnp.stack(parts)
    square = jnp.stack([pick(square, group ^ g) for g in range(4)])
    rows_b = jnp.stack([square] + [from_shift(square, "b", n_b, j) for j in range(1, n_b)])
    rows_q = jnp.stack([rows_b] + [from_shift(rows_b, "q", n_q, j) for j in range(1, n_q)])
    rows_q = jnp.stack([pick(rows_q, (i - zi) % n_q) for i in range(n_q)])
    gathered = jnp.stack(
        [lax.dynamic_index_in_dim(rows_q, (i - bi) % n_b, 1, keepdims=False) for i in range(n_b)],
        axis=1,
    )
    gathered = gathered.transpose(0, 2, 1, 3, 4).reshape(n_dev, -1, OWN_WIDTH)
    joint = gathered[:, : 3 * own_rows].reshape(n_dev, 3, own_rows, OWN_WIDTH)
    joint = joint.transpose(1, 0, 2, 3).reshape(3, width, OWN_WIDTH)
    wq, wk, wv = [pad_heads(joint[i]) for i in range(3)]
    smalls = gathered[:, 3 * own_rows :].reshape(n_dev, -1)[:, :small_size].astype(f32)

    def small_vector(i):
        return smalls[:, i * own_rows : (i + 1) * own_rows].reshape(1, width)

    qbias, vbias, obias, gain1, shift1, sbias, gain2, shift2 = [small_vector(i) for i in range(8)]
    ebias = smalls[:, 8 * own_rows :].reshape(1, ff)
    qb = pad_heads(lax.dynamic_slice_in_dim(qbias, group * OWN_WIDTH, OWN_WIDTH, 1))
    vb = pad_heads(lax.dynamic_slice_in_dim(vbias, group * OWN_WIDTH, OWN_WIDTH, 1))

    chunk_x = []
    for j in range(n_q):
        own = x_own if j == 0 else from_shift(x_own, "q", n_q, j)
        other = square_swap(own, 2)
        chunk_x.append([own, square_swap(own, 1), other, square_swap(other, 1)])

    gathered_ffn = lax.all_gather(packed, AXES, axis=0, tiled=False)

    def where_of(j):
        zj = (zi + j) % n_q
        spots = [(zj * 4 + (group ^ r)) * seq_rows for r in range(4)]
        return jnp.stack(spots + [lengths[0]]).astype(jnp.int32)

    weights = (wk, wv, vb, wq, qb)
    kept = []
    carry = None
    for j in range(n_q):
        first, last = j == 0, j == n_q - 1
        outs = attend_chunk(first, last, where_of(j), chunk_x[j], weights, carry)
        kept.append((outs[0], outs[1]))
        outs = outs[2:]
        if first:
            qx, qp = outs[:2]
            outs = outs[2:]
        carry = (qx, *outs)
    _, att, attx, qx2 = carry

    blocks = jnp.stack(
        [square_swap(att[r * seq_rows : (r + 1) * seq_rows], r) for r in range(4)]
    )
    attended_low = jnp.concatenate([pick(blocks, group ^ g) for g in range(4)], axis=1)

    output_low = gathered_ffn[:, :own_rows].reshape(width, width)
    expand_low = gathered_ffn[:, own_rows : (1 + fold) * own_rows]
    expand_low = (
        expand_low.reshape(n_dev, fold, own_rows, width).transpose(0, 2, 1, 3).reshape(width, ff)
    )
    shrink_low = gathered_ffn[:, (1 + fold) * own_rows :].reshape(ff, width)
    branch = jnp.dot(attended_low, output_low, preferred_element_type=f32) + obias
    resid_first = x_own.astype(f32) + branch
    hidden, first_pull = jax.vjp(layer_norm, resid_first, gain1[0], shift1[0])
    hidden_low = hidden.astype(bf16)
    expanded = jnp.dot(hidden_low, expand_low, preferred_element_type=f32) + ebias
    active, gelu_pull = jax.vjp(partial(jax.nn.gelu, approximate=False), expanded)
    active_low = active.astype(bf16)
    shrunk = jnp.dot(active_low, shrink_low, preferred_element_type=f32) + sbias
    result, second_pull = jax.vjp(layer_norm, hidden + shrunk, gain2[0], shift2[0])
    output = result[None].astype(bf16)
    positions = (zi * 4 + group) * seq_rows + jnp.arange(seq_rows, dtype=jnp.int32)
    row_weight = (positions < lengths[0]).astype(f32)[:, None]
    seed_grad = cotangent[0].astype(f32) * row_weight
    resid_second_grad, grad_gain2, grad_shift2 = second_pull(seed_grad)
    shrunk_grad = resid_second_grad.astype(bf16)
    grad_shrink = jnp.einsum("nf,nd->fd", active_low, shrunk_grad, preferred_element_type=f32)
    grad_sbias = jnp.sum(shrunk_grad.astype(f32), axis=0)
    active_grad = jnp.einsum("nd,fd->nf", shrunk_grad, shrink_low, preferred_element_type=f32)
    (expanded_grad_full,) = gelu_pull(active_grad)
    expanded_grad = expanded_grad_full.astype(bf16)
    grad_expand = jnp.einsum("nd,nf->df", hidden_low, expanded_grad, preferred_element_type=f32)
    grad_ebias = jnp.sum(expanded_grad.astype(f32), axis=0)
    hidden_grad = resid_second_grad + jnp.einsum(
        "nf,df->nd", expanded_grad, expand_low, preferred_element_type=f32
    )
    resid_first_grad, grad_gain1, grad_shift1 = first_pull(hidden_grad)
    branch_grad = resid_first_grad.astype(bf16)
    grad_output = jnp.einsum("na,nd->ad", attended_low, branch_grad, preferred_element_type=f32)
    grad_obias = jnp.sum(branch_grad.astype(f32), axis=0)
    attended_grad = jnp.einsum(
        "nd,ad->na", branch_grad, output_low, preferred_element_type=f32
    ).astype(bf16)

    grad_packed = jnp.concatenate(
        [
            grad_output.astype(bf16).reshape(n_dev, own_rows, width),
            grad_expand.astype(bf16)
            .reshape(n_dev, own_rows, fold, width)
            .transpose(0, 2, 1, 3)
            .reshape(n_dev, fold * own_rows, width),
            grad_shrink.astype(bf16).reshape(n_dev, own_ff, width),
        ],
        axis=1,
    )
    summed = lax.psum_scatter(grad_packed, AXES, scatter_dimension=0, tiled=False).astype(f32)

    grad_groups = attended_grad.reshape(seq_rows, GROUPS, OWN_WIDTH).transpose(1, 0, 2)
    grads = [square_swap(pick(grad_groups, group ^ r), r) for r in range(4)]
    shared = (qx2, qp, wk, wv, wq, grads, attx)
    carry = None
    order = list(range(1, n_q)) + [0]
    dkv, arrived = {}, []
    for step, j in enumerate(order):
        first, last = step == 0, step == n_q - 1
        outs = attend_back_chunk(first, last, kept[j], shared, carry)
        dkv[j], dx = outs[:2]
        if first:
            dox, dqt = outs[2:]
            carry = (dox, dqt)
        elif not last:
            carry = (dox, outs[2])
        else:
            dq = outs[2]
        dx = dx.reshape(2, 2, seq_rows, width)
        dx = dx[:, 0].astype(f32) + square_swap(dx[:, 1], 1).astype(f32)
        dx = dx[0] + square_swap(dx[1].astype(bf16), 2).astype(f32)
        if j:
            dx = from_shift(dx.astype(bf16), "q", n_q, n_q - j).astype(f32)
        arrived.append(dx)
    token_grad = resid_first_grad
    for part in arrived:
        token_grad = token_grad + part
    input_grad = token_grad[None].astype(bf16)

    grad_kv = sum(
        jnp.einsum("nd,nj->dj", jnp.concatenate(chunk_x[j], axis=0), dkv[j], preferred_element_type=f32)
        for j in range(n_q)
    )
    grad_q = jnp.einsum(
        "nd,nj->dj", jnp.concatenate(chunk_x[0], axis=0), dq, preferred_element_type=f32
    )
    grad_joint = jnp.concatenate([grad_q, grad_kv], axis=1).reshape(width, 3, OWN_HEADS, LANES)
    grad_joint = grad_joint[..., :HEAD_DIM].reshape(width, 3 * OWN_WIDTH)
    col_q = jnp.sum(dq.astype(f32), axis=0)
    col_v = sum(jnp.sum(dkv[j][:, OWN_HEADS * LANES :].astype(f32), axis=0) for j in range(n_q))
    bias_grads = jnp.zeros((2, GROUPS, OWN_WIDTH), f32)
    own_bias = jnp.stack([col_q, col_v]).reshape(2, OWN_HEADS, LANES)[..., :HEAD_DIM]
    bias_grads = lax.dynamic_update_slice(
        bias_grads, own_bias.reshape(2, 1, OWN_WIDTH), (0, group, 0)
    ).reshape(2, width)
    vectors = [
        bias_grads[0],
        bias_grads[1],
        grad_obias,
        grad_gain1,
        grad_shift1,
        grad_sbias,
        grad_gain2,
        grad_shift2,
    ]
    small_grads = jnp.concatenate(
        [v.reshape(n_dev, own_rows) for v in vectors] + [grad_ebias.reshape(n_dev, own_ff)], axis=1
    )

    def reduce_axis(value, axis, count, index, dim, dtype):
        part = lax.dynamic_index_in_dim(value, index, dim, keepdims=False).astype(f32)
        for j in range(1, count):
            away = lax.dynamic_index_in_dim(value, (index + j) % count, dim, keepdims=False)
            part = part + from_shift(away.astype(dtype), axis, count, count - j).astype(f32)
        return part

    def reduce_rows(value, dtype):
        value = value.reshape(n_q, 4, n_b, *value.shape[1:])
        value = reduce_axis(value, "b", n_b, bi, 2, dtype)
        value = reduce_axis(value, "q", n_q, zi, 0, dtype)
        return [square_swap(pick(value, group ^ r), r) for r in range(4)]

    joint_parts = reduce_rows(grad_joint.reshape(n_dev, own_rows, 3 * OWN_WIDTH), bf16)
    joint_parts = jnp.stack(joint_parts)
    joint_parts = jnp.stack([pick(joint_parts, group ^ g) for g in range(4)])
    grad_triple = (
        joint_parts.reshape(GROUPS, own_rows, 3, OWN_WIDTH).transpose(1, 2, 0, 3).reshape(own_rows, -1)
    )
    small_sum = sum(reduce_rows(small_grads, f32))

    def small_grad(i):
        return small_sum[i * own_rows : (i + 1) * own_rows]

    grad_expand_own = (
        summed[own_rows : (1 + fold) * own_rows]
        .reshape(fold, own_rows, width)
        .transpose(1, 0, 2)
        .reshape(own_rows, ff)
    )
    return (
        output,
        input_grad,
        grad_triple,
        small_grad(0),
        small_grad(1),
        summed[:own_rows],
        small_grad(2),
        small_grad(3),
        small_grad(4),
        grad_expand_own,
        small_sum[8 * own_rows :],
        summed[(1 + fold) * own_rows :],
        small_grad(5),
        small_grad(6),
        small_grad(7),
    )


def solution(mesh):
    n_seq, n_b = mesh.shape["seq"], mesh.shape["batch"]
    n_q = n_seq // GROUPS
    fine = Mesh(mesh.devices.reshape(n_q, 2, 2, n_b), AXES)
    tokens = P("b", ("q", "x", "c"), None)
    matrix = P(AXES, None)
    vector = P(AXES)
    in_specs = (
        tokens,
        P("b"),
        tokens,
        matrix,
        vector,
        vector,
        matrix,
        vector,
        vector,
        vector,
        matrix,
        vector,
        matrix,
        vector,
        vector,
        vector,
    )
    out_specs = (
        tokens,
        tokens,
        matrix,
        vector,
        vector,
        matrix,
        vector,
        vector,
        vector,
        matrix,
        vector,
        matrix,
        vector,
        vector,
        vector,
    )
    return jax.shard_map(
        partial(per_device, n_q, n_b),
        mesh=fine,
        in_specs=in_specs,
        out_specs=out_specs,
        check_vma=False,
    )
```

```python
from functools import partial
import math

import jax
import jax.numpy as jnp
from jax import lax
from jax.experimental import pallas as pl
from jax.experimental.pallas import tpu as pltpu
from jax.sharding import Mesh, PartitionSpec as P

HEADS = 12
HEAD_DIM = 64
GROUPS = 4
OWN_HEADS = HEADS // GROUPS
OWN_WIDTH = OWN_HEADS * HEAD_DIM
LANES = 128
WIDE = 640
VECTORS = 3 * OWN_WIDTH

bf16 = jnp.bfloat16
f32 = jnp.float32
masked_score = -1e30
norm_eps = 1e-12
log2_e = 1.4426950408889634
CONTRACT_LAST = (((1,), (1,)), ((), ()))
VMEM_BYTES = 60 * 1024 * 1024
AXES = ("q", "x", "c", "b")


def split_three(value):
    high = value.astype(bf16).astype(f32)
    rest = value - high
    mid = rest.astype(bf16).astype(f32)
    low = (rest - mid).astype(bf16).astype(f32)
    return high, mid, low


def low_half(tile, lane, from_high):
    turned = pltpu.roll(tile, HEAD_DIM, 1)
    low = lane < HEAD_DIM
    return jnp.where(low, turned, tile) if from_high else jnp.where(low, tile, turned)


def place_of(kind, h):
    slot = kind * OWN_HEADS + h
    return slot // 2, slot % 2


def forward_kernel(first, last, block_q, block_k, *refs):
    refs = list(refs)
    where_ref = refs.pop(0)
    pieces = [refs.pop(0) for _ in range(4)]
    w_ref, bias_ref = [refs.pop(0) for _ in range(2)]
    if not first:
        qx_ref, peak_in, sum_in = [refs.pop(0) for _ in range(3)]
    kx_ref, vx_ref = [refs.pop(0) for _ in range(2)]
    if first:
        qx_ref, qp_ref = [refs.pop(0) for _ in range(2)]
    if last:
        att_refs = [refs.pop(0) for _ in range(4)]
        attx_ref, qx2_ref = [refs.pop(0) for _ in range(2)]
    else:
        peak_out, sum_out = [refs.pop(0) for _ in range(2)]
    (vt_ref,) = refs
    piece_rows = pieces[0].shape[0]
    rows_in = 4 * piece_rows
    lane = lax.broadcasted_iota(jnp.int32, (piece_rows, LANES), 1)
    row = lax.broadcasted_iota(jnp.int32, (piece_rows, LANES), 0)
    low = lane < HEAD_DIM
    length = where_ref[4]
    three = (lane >= HEAD_DIM) & (lane < HEAD_DIM + 3)
    skip = 0 if first else LANES
    for p in range(4):
        rows = slice(p * piece_rows, (p + 1) * piece_rows)
        joint = jnp.dot(pieces[p][...], w_ref[:, skip:], preferred_element_type=f32)
        joint = joint + bias_ref[:, skip:]
        bias = jnp.where(where_ref[p] + row < length, 0.0, masked_score)
        key_extra = jnp.where(three, 1.0, jnp.where(lane == HEAD_DIM + 3, bias, 0.0))

        def head_of(kind, h):
            tile, high = place_of(kind, h)
            return low_half(joint[:, tile * LANES - skip : (tile + 1) * LANES - skip], lane, high)

        for h in range(OWN_HEADS):
            k = head_of(1, h)
            kx_ref[h, rows, :LANES] = k.astype(bf16)
            kx_ref[h, rows, LANES:] = jnp.where(low, k, key_extra).astype(bf16)
            v = jnp.where(low, head_of(2, h), 0.0)
            vx_ref[h, rows, :] = jnp.where(three, -1.0, v).astype(bf16)
            vt = jnp.where(lane == HEAD_DIM, 1.0, v).T
            vt_ref[h, :, rows] = vt[:80].astype(bf16)
            if first:
                q = head_of(0, h).astype(bf16).astype(f32)
                qp_ref[h, rows, :] = jnp.where(low, q, 0.0).astype(bf16)
                high, mid, rest = split_three(q * (HEAD_DIM**-0.5 * log2_e))
                qx_ref[h, rows, :LANES] = jnp.where(low, high, mid).astype(bf16)
                one = jnp.where(lane == HEAD_DIM + 3, 1.0, 0.0)
                qx_ref[h, rows, LANES:] = jnp.where(low, rest, one).astype(bf16)
    for h in range(OWN_HEADS):
        for i in range(rows_in // block_q):
            cols = slice(i * block_q, (i + 1) * block_q)
            q = qx_ref[h, cols, :]
            if first:
                peak = jnp.full((1, block_q), masked_score, f32)
                total = jnp.zeros((80, block_q), f32)
            else:
                peak = peak_in[h, :1, cols]
                total = sum_in[h, :, cols]
            for j in range(rows_in // block_k):
                ks = slice(j * block_k, (j + 1) * block_k)
                s = lax.dot_general(kx_ref[h, ks, :], q, CONTRACT_LAST, preferred_element_type=f32)
                new_peak = jnp.maximum(peak, jnp.max(s, axis=0, keepdims=True))
                prob = jnp.exp2(s - new_peak).astype(bf16)
                total = total * jnp.exp2(peak - new_peak) + jnp.dot(
                    vt_ref[h, :, ks], prob, preferred_element_type=f32
                )
                peak = new_peak
            if last:
                denom = total[HEAD_DIM : HEAD_DIM + 1]
                n_high, n_mid, n_low = split_three(-(peak + jnp.log2(denom)))
                tall = jnp.concatenate(
                    [
                        total[:HEAD_DIM] / denom,
                        n_high,
                        n_mid,
                        n_low,
                        jnp.zeros((HEAD_DIM - 3, block_q), f32),
                    ],
                    axis=0,
                )
                attx_ref[h, cols, :] = tall.T
            else:
                peak_out[h, :, cols] = jnp.broadcast_to(peak, (8, block_q))
                sum_out[h, :, cols] = total
    if last:
        for p in range(4):
            rows = slice(p * piece_rows, (p + 1) * piece_rows)
            heads = [attx_ref[h, rows, :] for h in range(OWN_HEADS)]
            pair = jnp.where(low, heads[0], pltpu.roll(heads[1], HEAD_DIM, 1))
            att_refs[p][:, :LANES] = pair.astype(bf16)
            att_refs[p][:, LANES:] = heads[2][:, :HEAD_DIM].astype(bf16)
            for h in range(OWN_HEADS):
                qx2_ref[h, rows, :LANES] = qx_ref[h, rows, :LANES]
                old = qx_ref[h, rows, LANES:].astype(f32)
                qx2_ref[h, rows, LANES:] = jnp.where(three, heads[h], old).astype(bf16)


def vmem_specs(n):
    return [pl.BlockSpec(memory_space=pltpu.VMEM) for _ in range(n)]


def attend_chunk(first, last, where, pieces, weights, carry):
    piece_rows = pieces[0].shape[0]
    rows = 4 * piece_rows
    operands = [where, *pieces, *weights]
    operands += [] if first else list(carry)
    wide_keys = jax.ShapeDtypeStruct((OWN_HEADS, rows, 2 * LANES), bf16)
    out_shape = [wide_keys, jax.ShapeDtypeStruct((OWN_HEADS, rows, LANES), bf16)]
    if first:
        out_shape += [wide_keys, jax.ShapeDtypeStruct((OWN_HEADS, rows, LANES), bf16)]
    if last:
        out_shape += [jax.ShapeDtypeStruct((piece_rows, OWN_WIDTH), bf16)] * 4
        out_shape += [jax.ShapeDtypeStruct((OWN_HEADS, rows, LANES), f32), wide_keys]
    else:
        out_shape += [
            jax.ShapeDtypeStruct((OWN_HEADS, 8, rows), f32),
            jax.ShapeDtypeStruct((OWN_HEADS, 80, rows), f32),
        ]
    return pl.pallas_call(
        partial(forward_kernel, first, last, min(512, rows), min(1024, rows)),
        out_shape=out_shape,
        in_specs=[pl.BlockSpec(memory_space=pltpu.SMEM)] + vmem_specs(len(operands) - 1),
        out_specs=vmem_specs(len(out_shape)),
        scratch_shapes=[pltpu.VMEM((OWN_HEADS, 80, rows), bf16)],
        compiler_params=pltpu.CompilerParams(vmem_limit_bytes=VMEM_BYTES),
        cost_estimate=pl.CostEstimate(
            flops=int(8e9), transcendentals=OWN_HEADS * rows * rows, bytes_accessed=int(1e7)
        ),
        name="attend_forward",
    )(*operands)


def backward_kernel(first, last, block_q, block_k, *refs):
    refs = list(refs)
    kx_ref, vx_ref, qx_ref, qp_ref, w_ref = [refs.pop(0) for _ in range(5)]
    pieces = [refs.pop(0) for _ in range(4)]
    if first:
        grads = [refs.pop(0) for _ in range(4)]
        attx_ref = refs.pop(0)
    else:
        dox_ref, dqt_in, dw_in, col_in = [refs.pop(0) for _ in range(4)]
    keep_ref, send_ref = [refs.pop(0) for _ in range(2)]
    if first:
        dox_ref = refs.pop(0)
    if last:
        dw_out, col_out = [refs.pop(0) for _ in range(2)]
        dqt_ref = refs.pop()
    else:
        dqt_ref, dw_out, col_out = [refs.pop(0) for _ in range(3)]
    kt_ref, all_ref = refs
    rows_in = kx_ref.shape[1]
    piece_rows = rows_in // 4
    scale = HEAD_DIM**-0.5
    lane = lax.broadcasted_iota(jnp.int32, (piece_rows, LANES), 1)
    if first:
        for p in range(4):
            rows = slice(p * piece_rows, (p + 1) * piece_rows)
            left = grads[p][:, :LANES].astype(f32)
            right = grads[p][:, LANES:].astype(f32)
            right = jnp.concatenate([right, jnp.zeros_like(right)], axis=1)
            for h, wide in enumerate((left, pltpu.roll(left, HEAD_DIM, 1), right)):
                grad = jnp.where(lane < HEAD_DIM, wide, 0.0)
                delta = jnp.sum(grad * attx_ref[h, rows, :], axis=1, keepdims=True)
                d_high, d_mid, d_low = split_three(delta)
                grad = jnp.where(lane == HEAD_DIM, d_high, grad)
                grad = jnp.where(lane == HEAD_DIM + 1, d_mid, grad)
                grad = jnp.where(lane == HEAD_DIM + 2, d_low, grad)
                dox_ref[h, rows, :] = grad.astype(bf16)
        dqt_ref[...] = jnp.zeros_like(dqt_ref)
    else:
        dqt_ref[...] = dqt_in[...]
    for h in range(OWN_HEADS):
        kt_ref[h] = kx_ref[h, :, LANES:].astype(f32).T[:HEAD_DIM].astype(bf16)
    lane_k = lax.broadcasted_iota(jnp.int32, (block_k, LANES), 1)
    low_k = lane_k < HEAD_DIM
    for j in range(rows_in // block_k):
        ks = slice(j * block_k, (j + 1) * block_k)
        parts = {}
        for h in range(OWN_HEADS):
            k = kx_ref[h, ks, :]
            v = vx_ref[h, ks, :]
            kt = kt_ref[h, :, ks]
            dk = jnp.zeros((block_k, LANES), f32)
            dv = jnp.zeros((block_k, LANES), f32)
            for i in range(rows_in // block_q):
                qs = slice(i * block_q, (i + 1) * block_q)
                s = lax.dot_general(k, qx_ref[h, qs, :], CONTRACT_LAST, preferred_element_type=f32)
                prob = jnp.exp2(s)
                do = dox_ref[h, qs, :]
                dp = lax.dot_general(v, do, CONTRACT_LAST, preferred_element_type=f32)
                ds = (prob * dp).astype(bf16)
                dv = dv + jnp.dot(prob.astype(bf16), do, preferred_element_type=f32)
                dk = dk + jnp.dot(ds, qp_ref[h, qs, :], preferred_element_type=f32)
                dqt_ref[h, :, qs] += jnp.dot(kt, ds, preferred_element_type=f32)
            parts[OWN_HEADS + h] = dk * scale
            parts[2 * OWN_HEADS + h] = dv
        for tile in range(1, WIDE // LANES):
            left, right = parts.get(2 * tile), parts.get(2 * tile + 1)
            left = jnp.zeros((block_k, LANES), f32) if left is None else left
            right = 0.0 if right is None else pltpu.roll(right, HEAD_DIM, 1)
            both = jnp.where(low_k, left, right).astype(bf16)
            all_ref[ks, tile * LANES : (tile + 1) * LANES] = both
    if last:
        tall = jnp.concatenate([dqt_ref[0], dqt_ref[1]], axis=0) * scale
        all_ref[:, :LANES] = tall.T.astype(bf16)
        tall = dqt_ref[2] * scale
        tall = jnp.concatenate([tall, jnp.zeros_like(tall)], axis=0).T
        lane_all = lax.broadcasted_iota(jnp.int32, (rows_in, LANES), 1)
        old = all_ref[:, LANES : 2 * LANES].astype(f32)
        all_ref[:, LANES : 2 * LANES] = jnp.where(lane_all < HEAD_DIM, tall, old).astype(bf16)
    skip = 0 if last else LANES
    d_weight = [None, None]
    for p in range(4):
        rows = slice(p * piece_rows, (p + 1) * piece_rows)
        own = all_ref[rows, skip:]
        dx = lax.dot_general(own, w_ref[:, skip:], CONTRACT_LAST, preferred_element_type=f32)
        out_ref = keep_ref if p % 2 == 0 else send_ref
        out_ref[p // 2] = dx.astype(bf16)
        piece = lax.dot_general(
            pieces[p][...], own, (((0,), (0,)), ((), ())), preferred_element_type=f32
        )
        d_weight[0] = piece if p == 0 else d_weight[0] + piece
        col = jnp.sum(own.astype(f32), axis=0, keepdims=True)
        d_weight[1] = col if p == 0 else d_weight[1] + col
    grad, col = d_weight
    if last:
        dw_out[:, :LANES] = grad[:, :LANES].astype(bf16)
        dw_out[:, LANES:] = (grad[:, LANES:] + dw_in[...]).astype(bf16)
        col_out[:, :LANES] = jnp.broadcast_to(col[:, :LANES], (8, LANES))
        col_out[:, LANES:] = col[:, LANES:] + col_in[...]
    elif first:
        dw_out[...] = grad
        col_out[...] = jnp.broadcast_to(col, col_out.shape)
    else:
        dw_out[...] = grad + dw_in[...]
        col_out[...] = col + col_in[...]


def attend_back_chunk(first, last, chunk, pieces, shared, carry):
    kx, vx = chunk
    qx2, qp, w, grads, attx = shared
    rows, width = kx.shape[1], w.shape[0]
    operands = [kx, vx, qx2, qp, w, *pieces]
    operands += [*grads, attx] if first else list(carry)
    half = jax.ShapeDtypeStruct((2, rows // 4, width), bf16)
    out_shape = [half, half]
    scratch = [
        pltpu.VMEM((OWN_HEADS, HEAD_DIM, rows), bf16),
        pltpu.VMEM((rows, WIDE), bf16),
    ]
    if first:
        out_shape.append(jax.ShapeDtypeStruct((OWN_HEADS, rows, LANES), bf16))
    if last:
        out_shape.append(jax.ShapeDtypeStruct((width, WIDE), bf16))
        out_shape.append(jax.ShapeDtypeStruct((8, WIDE), f32))
        scratch.append(pltpu.VMEM((OWN_HEADS, HEAD_DIM, rows), f32))
    else:
        out_shape.append(jax.ShapeDtypeStruct((OWN_HEADS, HEAD_DIM, rows), f32))
        out_shape.append(jax.ShapeDtypeStruct((width, WIDE - LANES), f32))
        out_shape.append(jax.ShapeDtypeStruct((8, WIDE - LANES), f32))
    return pl.pallas_call(
        partial(backward_kernel, first, last, min(512, rows), min(512, rows)),
        out_shape=out_shape,
        in_specs=vmem_specs(len(operands)),
        out_specs=vmem_specs(len(out_shape)),
        scratch_shapes=scratch,
        compiler_params=pltpu.CompilerParams(vmem_limit_bytes=VMEM_BYTES),
        cost_estimate=pl.CostEstimate(
            flops=int(1.5e10), transcendentals=OWN_HEADS * rows * rows, bytes_accessed=int(1e7)
        ),
        name="attend_backward",
    )(*operands)


def norm_forward(value, gain, shift):
    center = value - jnp.mean(value, axis=-1, keepdims=True)
    spread = jnp.mean(center * center, axis=-1, keepdims=True)
    inverse = lax.rsqrt(spread + norm_eps)
    normal = center * inverse
    return normal * gain + shift, normal, inverse


def norm_backward(grad, gain, normal, inverse):
    inner = grad * gain
    mean = jnp.mean(inner, axis=-1, keepdims=True)
    along = jnp.mean(inner * normal, axis=-1, keepdims=True)
    return inverse * (inner - mean - normal * along)


CONTRACT_FIRST = (((0,), (0,)), ((), ()))


def ffn_kernel(layout, *refs):
    n_q, n_b, own_rows, fold, aligned = layout
    refs = list(refs)
    where_ref = refs.pop(0)
    att_refs = [refs.pop(0) for _ in range(4)]
    x_ref, cot_ref, vec_ref, eb_ref, packed = [refs.pop(0) for _ in range(5)]
    out_ref, resid_ref = [refs.pop(0) for _ in range(2)]
    da_refs = [refs.pop(0) for _ in range(4)]
    vec_out = refs.pop(0)
    targets = [refs.pop(0) for _ in range(4 if aligned else 2)]
    wo, w1, w2, go, g1, g2, act, slope, in_sem, out_sem = refs
    group, zi, xi, ci, bi, start, length = [where_ref[i] for i in range(7)]
    rows, width = x_ref.shape

    def lanes(i):
        return slice(i * width, (i + 1) * width)

    loads = [pltpu.make_async_copy(packed.at[:, lanes(0)], wo, in_sem.at[0])]
    for k in range(fold):
        loads.append(pltpu.make_async_copy(packed.at[:, lanes(1 + k)], w1.at[k], in_sem.at[1 + k]))
    for k in range(fold):
        sem = in_sem.at[1 + fold + k]
        loads.append(pltpu.make_async_copy(packed.at[:, lanes(1 + fold + k)], w2.at[k], sem))
    for load in loads:
        load.start()

    def group_rows(r):
        other = (2 * (xi ^ (r // 2))) + (ci ^ (r % 2))
        return pl.ds(pl.multiple_of(other * OWN_WIDTH, HEAD_DIM), OWN_WIDTH)

    obias, gain1, shift1, sbias, gain2, shift2 = [vec_ref[i : i + 1, :] for i in range(2, 8)]
    loads[0].wait()
    branch = obias + jnp.zeros((rows, width), f32)
    for r in range(4):
        branch += jnp.dot(att_refs[r][...], wo[group_rows(r), :], preferred_element_type=f32)
    hidden, normal1, inverse1 = norm_forward(x_ref[...].astype(f32) + branch, gain1, shift1)
    hidden_low = hidden.astype(bf16)
    shrunk = sbias + hidden
    for k in range(fold):
        loads[1 + k].wait()
        expanded = jnp.dot(hidden_low, w1[k], preferred_element_type=f32) + eb_ref[k : k + 1, :]
        cdf = 0.5 * (1.0 + lax.erf(expanded * (2.0**-0.5)))
        pdf = jnp.exp(-0.5 * expanded * expanded) * ((2.0 * math.pi) ** -0.5)
        act[k] = (expanded * cdf).astype(bf16)
        slope[k] = cdf + expanded * pdf
        loads[1 + fold + k].wait()
        shrunk += jnp.dot(act[k], w2[k], preferred_element_type=f32)
    result, normal2, inverse2 = norm_forward(shrunk, gain2, shift2)
    out_ref[...] = result.astype(bf16)
    row = lax.broadcasted_iota(jnp.int32, (rows, width), 0)
    seed = jnp.where(start + row < length, cot_ref[...].astype(f32), 0.0)
    vec_out[4:5, :] = jnp.sum(seed * normal2, axis=0, keepdims=True)
    vec_out[5:6, :] = jnp.sum(seed, axis=0, keepdims=True)
    resid2 = norm_backward(seed, gain2, normal2, inverse2)
    shrunk_low = resid2.astype(bf16)
    vec_out[3:4, :] = jnp.sum(shrunk_low.astype(f32), axis=0, keepdims=True)
    hidden_grad = resid2
    for k in range(fold):
        active_grad = lax.dot_general(
            shrunk_low, w2[k], CONTRACT_LAST, preferred_element_type=f32
        )
        expanded_low = (active_grad * slope[k]).astype(bf16)
        vec_out[8 + k : 9 + k, :] = jnp.sum(expanded_low.astype(f32), axis=0, keepdims=True)
        hidden_grad += lax.dot_general(
            expanded_low, w1[k], CONTRACT_LAST, preferred_element_type=f32
        )
        g2[k] = lax.dot_general(
            act[k], shrunk_low, CONTRACT_FIRST, preferred_element_type=f32
        ).astype(bf16)
        g1[k] = lax.dot_general(
            hidden_low, expanded_low, CONTRACT_FIRST, preferred_element_type=f32
        ).astype(bf16)
    vec_out[1:2, :] = jnp.sum(hidden_grad * normal1, axis=0, keepdims=True)
    vec_out[2:3, :] = jnp.sum(hidden_grad, axis=0, keepdims=True)
    resid1 = norm_backward(hidden_grad, gain1, normal1, inverse1)
    resid_ref[...] = resid1
    branch_low = resid1.astype(bf16)
    vec_out[0:1, :] = jnp.sum(branch_low.astype(f32), axis=0, keepdims=True)
    vec_out[6:8, :] = jnp.zeros((2, width), f32)
    vec_out[8 + fold :, :] = jnp.zeros((vec_out.shape[0] - 8 - fold, width), f32)
    for r in range(4):
        da_refs[r][...] = lax.dot_general(
            branch_low, wo[group_rows(r), :], CONTRACT_LAST, preferred_element_type=f32
        ).astype(bf16)
        go[group_rows(r), :] = lax.dot_general(
            att_refs[r][...], branch_low, CONTRACT_FIRST, preferred_element_type=f32
        ).astype(bf16)
    block = n_b * own_rows
    for dc in range(2 if aligned else 1):
        to_one, to_two = targets[2 * dc : 2 * dc + 2]
        if not aligned:
            for k, src in enumerate([go] + [g1.at[k] for k in range(fold)]):
                pltpu.make_async_copy(src, to_one.at[:, lanes(k)], out_sem.at[0]).start()
            for k in range(fold):
                pltpu.make_async_copy(g2.at[k], to_two.at[:, lanes(k)], out_sem.at[1]).start()
            continue
        for dx in range(2):
            for jz in range(n_q):
                m = (lax.rem(zi + jz, n_q) * 2 + (xi ^ dx)) * 2 + (ci ^ dc)
                at = pl.ds(pl.multiple_of(m * block, 16), block)
                for k, src in enumerate([go] + [g1.at[k] for k in range(fold)]):
                    dst = to_one.at[dx, jz, :, lanes(k)]
                    pltpu.make_async_copy(src.at[at], dst, out_sem.at[2 * dc]).start()
                for k in range(fold):
                    dst = to_two.at[dx, jz, :, lanes(k)]
                    pltpu.make_async_copy(g2.at[k, at], dst, out_sem.at[2 * dc + 1]).start()
    for i, dst in enumerate(targets):
        pltpu.make_async_copy(dst, dst, out_sem.at[i]).wait()


def ffn_block(layout, where, att, x, cot, vectors, ebias, packed):
    n_q, n_b, own_rows, fold, aligned = layout
    rows, width = x.shape
    ff = fold * width
    operands = [where, *att, x, cot, vectors, ebias, packed]
    in_specs = [pl.BlockSpec(memory_space=pltpu.SMEM)] + vmem_specs(8)
    in_specs += [pl.BlockSpec(memory_space=pl.ANY)]
    out_shape = [
        jax.ShapeDtypeStruct((rows, width), bf16),
        jax.ShapeDtypeStruct((rows, width), f32),
        *[jax.ShapeDtypeStruct((rows, OWN_WIDTH), bf16)] * 4,
        jax.ShapeDtypeStruct((16, width), f32),
    ]
    lead = (2, n_q, n_b * own_rows) if aligned else (width,)
    pair = [jax.ShapeDtypeStruct((*lead, width + ff), bf16), jax.ShapeDtypeStruct((*lead, ff), bf16)]
    targets = pair + pair if aligned else pair
    weight_scratch = [
        pltpu.VMEM((width, width), bf16),
        pltpu.VMEM((fold, width, width), bf16),
        pltpu.VMEM((fold, width, width), bf16),
    ]
    return pl.pallas_call(
        partial(ffn_kernel, layout),
        out_shape=out_shape + targets,
        in_specs=in_specs,
        out_specs=vmem_specs(len(out_shape)) + [pl.BlockSpec(memory_space=pl.ANY)] * len(targets),
        scratch_shapes=weight_scratch
        + weight_scratch
        + [
            pltpu.VMEM((fold, rows, width), bf16),
            pltpu.VMEM((fold, rows, width), f32),
            pltpu.SemaphoreType.DMA((1 + 2 * fold,)),
            pltpu.SemaphoreType.DMA((4,)),
        ],
        compiler_params=pltpu.CompilerParams(vmem_limit_bytes=VMEM_BYTES),
        cost_estimate=pl.CostEstimate(
            flops=int(2e10), transcendentals=2 * rows * ff, bytes_accessed=int(3e7)
        ),
        name="feed_forward",
    )(*operands)


def from_shift(value, axis, count, step):
    return lax.ppermute(value, axis, [((i + step) % count, i) for i in range(count)])


def square_swap(value, r):
    if r == 0:
        return value
    if r == 1:
        return lax.ppermute(value, "c", [(0, 1), (1, 0)])
    if r == 2:
        return lax.ppermute(value, "x", [(0, 1), (1, 0)])
    return lax.ppermute(value, ("x", "c"), [(0, 3), (3, 0), (1, 2), (2, 1)])


def pick(stacked, index, dim=0):
    return lax.dynamic_index_in_dim(stacked, index, dim, keepdims=False)


def after(value, *others):
    return lax.optimization_barrier((value, *others))[0]


def sum_to_owner(keep, send, n_q, n_b, bi):
    total = keep.astype(f32) + square_swap(send, 1).astype(f32)
    total = total.reshape(2, n_q, n_b, -1, keep.shape[-1])
    own = pick(total, bi, 2)
    for j in range(1, n_b):
        away = pick(total, (bi + j) % n_b, 2).astype(bf16)
        own = own + from_shift(away, "b", n_b, n_b - j).astype(f32)
    for axis, count in (("x", 2), ("q", n_q)):
        total = own
        own = total[0]
        for j in range(1, count):
            own = own + from_shift(total[j].astype(bf16), axis, count, count - j).astype(f32)
    return own


def deinterleave(fold):
    size = fold * LANES
    lane = jnp.arange(size)
    return (lane[:, None] // fold + (lane[:, None] % fold) * LANES == lane[None, :]).astype(bf16)


def per_device(
    n_q,
    n_b,
    inputs,
    lengths,
    cotangent,
    triple_weight,
    query_bias,
    value_bias,
    output_weight,
    output_bias,
    first_gain,
    first_shift,
    expand_weight,
    expand_bias,
    shrink_weight,
    shrink_bias,
    second_gain,
    second_shift,
):
    zi, xi, ci, bi = [lax.axis_index(a) for a in AXES]
    group = 2 * xi + ci
    _, seq_rows, width = inputs.shape
    own_rows = triple_weight.shape[0]
    ff = expand_weight.shape[1]
    fold = ff // width
    aligned = n_b * own_rows % 16 == 0
    x_own = inputs[0]

    turn = deinterleave(fold)
    expand_own = expand_weight.astype(bf16).reshape(own_rows, -1, fold * LANES)
    expand_own = jnp.einsum("rbs,st->rbt", expand_own, turn, preferred_element_type=f32)
    expand_own = expand_own.astype(bf16).reshape(own_rows, -1, fold, LANES).transpose(0, 2, 1, 3)
    packed = jnp.concatenate(
        [
            output_weight.astype(bf16),
            expand_own.reshape(own_rows, ff),
            shrink_weight.astype(bf16).reshape(own_rows, ff),
        ],
        axis=1,
    )
    gathered_ffn = lax.all_gather(packed, AXES, axis=0, tiled=True)

    names = [query_bias, value_bias, output_bias, first_gain, first_shift]
    names += [shrink_bias, second_gain, second_shift]
    vectors = jnp.stack(names, axis=1)
    vectors = jnp.concatenate([vectors, expand_bias.reshape(own_rows, fold)], axis=1).astype(bf16)
    n_vec = vectors.shape[1]
    vectors = jnp.pad(vectors, ((0, 0), (0, WIDE - VECTORS - n_vec)))
    thirds = triple_weight.astype(bf16).reshape(own_rows, 3, GROUPS, OWN_WIDTH)

    def columns_of(g):
        mine = [pick(thirds[:, t], g, 1) for t in range(3)]
        return jnp.concatenate(mine + [vectors], axis=1)

    square = jnp.stack([square_swap(columns_of(group ^ r), r) for r in range(4)])
    rows_q = jnp.stack([square] + [from_shift(square, "q", n_q, j) for j in range(1, n_q)])
    rows_b = jnp.stack([rows_q] + [from_shift(rows_q, "b", n_b, j) for j in range(1, n_b)])
    ordered = jnp.stack([pick(rows_b, (i - bi) % n_b) for i in range(n_b)], axis=3)
    ordered = jnp.stack([pick(ordered, group ^ g, 1) for g in range(4)], axis=1)
    ordered = jnp.stack([pick(ordered, (i - zi) % n_q) for i in range(n_q)])
    w_own = ordered.transpose(0, 1, 3, 2, 4).reshape(width, WIDE)
    turned = w_own[:, VECTORS : VECTORS + n_vec].astype(f32)
    turned = turned.T
    ebias = turned[8:]
    turned = turned[:8]
    own_bias = lax.dynamic_slice_in_dim(turned, group * OWN_WIDTH, OWN_WIDTH, 1)
    zero = jnp.zeros((1, OWN_WIDTH), f32)
    bias_row = jnp.concatenate(
        [own_bias[:1], zero, own_bias[1:2], jnp.zeros((1, WIDE - VECTORS), f32)], axis=1
    )

    chunk_x = {}
    tie = []
    for j in [0] + [k for pair in zip(range(1, n_q), range(n_q - 1, 0, -1)) for k in pair]:
        if j in chunk_x:
            continue
        own = x_own if j == 0 else from_shift(after(x_own, *tie), "q", n_q, j)
        tie = [] if j == 0 else [own]
        chunk_x[j] = [own, None, square_swap(own, 2), None]
    for j, piece in chunk_x.items():
        halves = square_swap(jnp.stack([piece[0], piece[2]]), 1)
        piece[1], piece[3] = halves[0], halves[1]
    arrival = list(chunk_x)

    def where_of(j):
        zj = (zi + j) % n_q
        spots = [(zj * 4 + (group ^ r)) * seq_rows for r in range(4)]
        return jnp.stack(spots + [lengths[0]]).astype(jnp.int32)

    weights = (w_own, bias_row)
    kept = {}
    carry = None
    for step, j in enumerate(arrival):
        first, last = step == 0, step == n_q - 1
        outs = attend_chunk(first, last, where_of(j), chunk_x[j], weights, carry)
        kept[j] = (outs[0], outs[1])
        outs = outs[2:]
        if first:
            qx, qp = outs[:2]
            outs = outs[2:]
        carry = (qx, *outs)
    att, attx, qx2 = carry[1:5], carry[5], carry[6]

    att = [square_swap(att[r], r) for r in range(4)]
    start = (zi * 4 + group) * seq_rows
    where = jnp.stack([group, zi, xi, ci, bi, start, lengths[0]]).astype(jnp.int32)
    layout = (n_q, n_b, own_rows, fold, aligned)
    outs = ffn_block(layout, where, att, x_own, cotangent[0], turned, ebias, gathered_ffn)
    output, resid_first_grad = outs[:2]
    att_grads, vec_grads, summands = outs[2:6], outs[6], outs[7:]
    grads = [square_swap(att_grads[r], r) for r in range(4)]

    if aligned:
        one_keep, two_keep, one_send, two_send = summands
        summed_two = sum_to_owner(two_keep, two_send, n_q, n_b, bi)
        summed_one = sum_to_owner(one_keep, one_send, n_q, n_b, bi)
    else:
        summed = lax.psum_scatter(
            jnp.concatenate(summands, axis=1), AXES, scatter_dimension=0, tiled=True
        ).astype(f32)
        summed_one, summed_two = summed[:, : width + ff], summed[:, width + ff :]

    shared = (qx2, qp, w_own, grads, attx)
    carry = None
    token_grad = resid_first_grad
    for step, j in enumerate(reversed(arrival)):
        first, last = step == 0, step == n_q - 1
        outs = attend_back_chunk(first, last, kept[j], chunk_x[j], shared, carry)
        keep, send = outs[:2]
        outs = outs[2:]
        if first:
            dox = outs[0]
            outs = outs[1:]
        carry = (dox, *outs)
        dx = keep.astype(f32) + square_swap(send, 1).astype(f32)
        dx = dx[0] + square_swap(dx[1].astype(bf16), 2).astype(f32)
        if j:
            dx = from_shift(dx.astype(bf16), "q", n_q, n_q - j).astype(f32)
        token_grad = token_grad + dx
    input_grad = token_grad.astype(bf16)
    grad_joint, col = carry[1:]

    own_bias = jnp.stack([col[0, :OWN_WIDTH], col[0, 2 * OWN_WIDTH : 3 * OWN_WIDTH]])
    bias_grads = lax.dynamic_update_slice(
        jnp.zeros((2, width), f32), own_bias, (0, group * OWN_WIDTH)
    )
    tall = jnp.concatenate([bias_grads, vec_grads[:6], vec_grads[8 : 8 + fold]], axis=0).T
    tall_high = tall.astype(bf16)
    tall_low = (tall - tall_high.astype(f32)).astype(bf16)
    room = jnp.zeros((width, WIDE - VECTORS - 2 * n_vec), bf16)
    blocks = jnp.concatenate([grad_joint[:, :VECTORS], tall_high, tall_low, room], axis=1)
    total = blocks.reshape(n_q, 4, n_b, own_rows, WIDE)
    total = jnp.stack([pick(total, (bi + j) % n_b, 2) for j in range(n_b)])
    for axis, count, index in (("b", n_b, bi), ("q", n_q, zi)):
        if axis == "q":
            total = jnp.stack([pick(total, (zi + j) % n_q) for j in range(n_q)])
        own = total[0].astype(f32)
        for j in range(1, count):
            own = own + from_shift(total[j].astype(bf16), axis, count, count - j).astype(f32)
        total = own
    total = total.astype(bf16)
    parts = jnp.stack([square_swap(pick(total, group ^ r), r) for r in range(4)])
    parts = jnp.stack([pick(parts, group ^ g) for g in range(4)])
    grad_triple = parts[:, :, :VECTORS].reshape(GROUPS, own_rows, 3, OWN_WIDTH)
    grad_triple = grad_triple.transpose(1, 2, 0, 3).reshape(own_rows, -1).astype(f32)
    small = jnp.sum(parts[:, :, VECTORS : VECTORS + 2 * n_vec].astype(f32), axis=0)
    small = small[:, :n_vec] + small[:, n_vec:]
    grad_expand = summed_one[:, width:].reshape(own_rows, fold, -1, LANES).transpose(0, 2, 1, 3)
    grad_expand = jnp.einsum(
        "rbs,ts->rbt",
        grad_expand.reshape(own_rows, -1, fold * LANES),
        turn.astype(f32),
        precision=lax.Precision.HIGHEST,
        preferred_element_type=f32,
    ).reshape(own_rows, ff)
    return (
        output[None],
        input_grad[None],
        grad_triple,
        small[:, 0],
        small[:, 1],
        summed_one[:, :width],
        small[:, 2],
        small[:, 3],
        small[:, 4],
        grad_expand,
        small[:, 8:].reshape(-1),
        summed_two.reshape(-1, width),
        small[:, 5],
        small[:, 6],
        small[:, 7],
    )


def solution(mesh):
    n_seq, n_b = mesh.shape["seq"], mesh.shape["batch"]
    n_q = n_seq // GROUPS
    fine = Mesh(mesh.devices.reshape(n_q, 2, 2, n_b), AXES)
    tokens = P("b", ("q", "x", "c"), None)
    matrix = P(AXES, None)
    vector = P(AXES)
    in_specs = (
        tokens,
        P("b"),
        tokens,
        matrix,
        vector,
        vector,
        matrix,
        vector,
        vector,
        vector,
        matrix,
        vector,
        matrix,
        vector,
        vector,
        vector,
    )
    out_specs = (
        tokens,
        tokens,
        matrix,
        vector,
        vector,
        matrix,
        vector,
        vector,
        vector,
        matrix,
        vector,
        matrix,
        vector,
        vector,
        vector,
    )
    return jax.shard_map(
        partial(per_device, n_q, n_b),
        mesh=fine,
        in_specs=in_specs,
        out_specs=out_specs,
        check_vma=False,
    )
```

```python
from functools import partial
import math

import jax
import jax.numpy as jnp
from jax import lax
from jax.experimental import pallas as pl
from jax.experimental.pallas import tpu as pltpu
from jax.sharding import Mesh, PartitionSpec as P

HEADS = 12
HEAD_DIM = 64
GROUPS = 4
OWN_HEADS = HEADS // GROUPS
OWN_WIDTH = OWN_HEADS * HEAD_DIM
LANES = 128
WIDE = 640
VECTORS = 3 * OWN_WIDTH

bf16 = jnp.bfloat16
f32 = jnp.float32
masked_score = -1e30
norm_eps = 1e-12
log2_e = 1.4426950408889634
CONTRACT_LAST = (((1,), (1,)), ((), ()))
VMEM_BYTES = 60 * 1024 * 1024
AXES = ("q", "x", "c", "b")


def split_three(value):
    high = value.astype(bf16).astype(f32)
    rest = value - high
    mid = rest.astype(bf16).astype(f32)
    low = (rest - mid).astype(bf16).astype(f32)
    return high, mid, low


def low_half(tile, lane, from_high):
    turned = pltpu.roll(tile, HEAD_DIM, 1)
    low = lane < HEAD_DIM
    return jnp.where(low, turned, tile) if from_high else jnp.where(low, tile, turned)


def place_of(kind, h):
    slot = kind * OWN_HEADS + h
    return slot // 2, slot % 2


def forward_kernel(first, last, block_q, block_k, *refs):
    refs = list(refs)
    where_ref = refs.pop(0)
    pieces = [refs.pop(0) for _ in range(4)]
    w_ref, bias_ref = [refs.pop(0) for _ in range(2)]
    if not first:
        qx_ref, peak_in, sum_in = [refs.pop(0) for _ in range(3)]
    kx_ref, vx_ref = [refs.pop(0) for _ in range(2)]
    if first:
        qx_ref, qp_ref = [refs.pop(0) for _ in range(2)]
    if last:
        att_refs = [refs.pop(0) for _ in range(4)]
        attx_ref, qx2_ref = [refs.pop(0) for _ in range(2)]
    else:
        peak_out, sum_out = [refs.pop(0) for _ in range(2)]
    (vt_ref,) = refs
    piece_rows = pieces[0].shape[0]
    rows_in = 4 * piece_rows
    lane = lax.broadcasted_iota(jnp.int32, (piece_rows, LANES), 1)
    row = lax.broadcasted_iota(jnp.int32, (piece_rows, LANES), 0)
    low = lane < HEAD_DIM
    length = where_ref[4]
    three = (lane >= HEAD_DIM) & (lane < HEAD_DIM + 3)
    skip = 0 if first else LANES
    for p in range(4):
        rows = slice(p * piece_rows, (p + 1) * piece_rows)
        joint = jnp.dot(pieces[p][...], w_ref[:, skip:], preferred_element_type=f32)
        joint = joint + bias_ref[:, skip:]
        bias = jnp.where(where_ref[p] + row < length, 0.0, masked_score)
        key_extra = jnp.where(three, 1.0, jnp.where(lane == HEAD_DIM + 3, bias, 0.0))

        def head_of(kind, h):
            tile, high = place_of(kind, h)
            return low_half(joint[:, tile * LANES - skip : (tile + 1) * LANES - skip], lane, high)

        for h in range(OWN_HEADS):
            k = head_of(1, h)
            kx_ref[h, rows, :LANES] = k.astype(bf16)
            kx_ref[h, rows, LANES:] = jnp.where(low, k, key_extra).astype(bf16)
            v = jnp.where(low, head_of(2, h), 0.0)
            vx_ref[h, rows, :] = jnp.where(three, -1.0, v).astype(bf16)
            vt = jnp.where(lane == HEAD_DIM, 1.0, v).T
            vt_ref[h, :, rows] = vt[:80].astype(bf16)
            if first:
                q = head_of(0, h).astype(bf16).astype(f32)
                qp_ref[h, rows, :] = jnp.where(low, q, 0.0).astype(bf16)
                high, mid, rest = split_three(q * (HEAD_DIM**-0.5 * log2_e))
                qx_ref[h, rows, :LANES] = jnp.where(low, high, mid).astype(bf16)
                one = jnp.where(lane == HEAD_DIM + 3, 1.0, 0.0)
                qx_ref[h, rows, LANES:] = jnp.where(low, rest, one).astype(bf16)
    for h in range(OWN_HEADS):
        for i in range(rows_in // block_q):
            cols = slice(i * block_q, (i + 1) * block_q)
            q = qx_ref[h, cols, :]
            if first:
                peak = jnp.full((1, block_q), masked_score, f32)
                total = jnp.zeros((80, block_q), f32)
            else:
                peak = peak_in[h, :1, cols]
                total = sum_in[h, :, cols]
            for j in range(rows_in // block_k):
                ks = slice(j * block_k, (j + 1) * block_k)
                s = lax.dot_general(kx_ref[h, ks, :], q, CONTRACT_LAST, preferred_element_type=f32)
                new_peak = jnp.maximum(peak, jnp.max(s, axis=0, keepdims=True))
                prob = jnp.exp2(s - new_peak).astype(bf16)
                total = total * jnp.exp2(peak - new_peak) + jnp.dot(
                    vt_ref[h, :, ks], prob, preferred_element_type=f32
                )
                peak = new_peak
            if last:
                denom = total[HEAD_DIM : HEAD_DIM + 1]
                n_high, n_mid, n_low = split_three(-(peak + jnp.log2(denom)))
                tall = jnp.concatenate(
                    [
                        total[:HEAD_DIM] / denom,
                        n_high,
                        n_mid,
                        n_low,
                        jnp.zeros((HEAD_DIM - 3, block_q), f32),
                    ],
                    axis=0,
                )
                attx_ref[h, cols, :] = tall.T
            else:
                peak_out[h, :, cols] = jnp.broadcast_to(peak, (8, block_q))
                sum_out[h, :, cols] = total
    if last:
        for p in range(4):
            rows = slice(p * piece_rows, (p + 1) * piece_rows)
            heads = [attx_ref[h, rows, :] for h in range(OWN_HEADS)]
            pair = jnp.where(low, heads[0], pltpu.roll(heads[1], HEAD_DIM, 1))
            att_refs[p][:, :LANES] = pair.astype(bf16)
            att_refs[p][:, LANES:] = heads[2][:, :HEAD_DIM].astype(bf16)
            for h in range(OWN_HEADS):
                qx2_ref[h, rows, :LANES] = qx_ref[h, rows, :LANES]
                old = qx_ref[h, rows, LANES:].astype(f32)
                qx2_ref[h, rows, LANES:] = jnp.where(three, heads[h], old).astype(bf16)


def vmem_specs(n):
    return [pl.BlockSpec(memory_space=pltpu.VMEM) for _ in range(n)]


def attend_chunk(first, last, where, pieces, weights, carry):
    piece_rows = pieces[0].shape[0]
    rows = 4 * piece_rows
    operands = [where, *pieces, *weights]
    operands += [] if first else list(carry)
    wide_keys = jax.ShapeDtypeStruct((OWN_HEADS, rows, 2 * LANES), bf16)
    out_shape = [wide_keys, jax.ShapeDtypeStruct((OWN_HEADS, rows, LANES), bf16)]
    if first:
        out_shape += [wide_keys, jax.ShapeDtypeStruct((OWN_HEADS, rows, LANES), bf16)]
    if last:
        out_shape += [jax.ShapeDtypeStruct((piece_rows, OWN_WIDTH), bf16)] * 4
        out_shape += [jax.ShapeDtypeStruct((OWN_HEADS, rows, LANES), f32), wide_keys]
    else:
        out_shape += [
            jax.ShapeDtypeStruct((OWN_HEADS, 8, rows), f32),
            jax.ShapeDtypeStruct((OWN_HEADS, 80, rows), f32),
        ]
    return pl.pallas_call(
        partial(forward_kernel, first, last, min(512, rows), min(1024, rows)),
        out_shape=out_shape,
        in_specs=[pl.BlockSpec(memory_space=pltpu.SMEM)] + vmem_specs(len(operands) - 1),
        out_specs=vmem_specs(len(out_shape)),
        scratch_shapes=[pltpu.VMEM((OWN_HEADS, 80, rows), bf16)],
        compiler_params=pltpu.CompilerParams(vmem_limit_bytes=VMEM_BYTES),
        cost_estimate=pl.CostEstimate(
            flops=int(8e9), transcendentals=OWN_HEADS * rows * rows, bytes_accessed=int(1e7)
        ),
        name="attend_forward",
    )(*operands)


def backward_kernel(first, last, block_q, block_k, *refs):
    refs = list(refs)
    kx_ref, vx_ref, qx_ref, qp_ref, w_ref = [refs.pop(0) for _ in range(5)]
    pieces = [refs.pop(0) for _ in range(4)]
    if first:
        grads = [refs.pop(0) for _ in range(4)]
        attx_ref = refs.pop(0)
    else:
        dox_ref, dqt_in, dw_in, col_in = [refs.pop(0) for _ in range(4)]
    keep_ref, send_ref = [refs.pop(0) for _ in range(2)]
    if first:
        dox_ref = refs.pop(0)
    if last:
        dw_out, col_out = [refs.pop(0) for _ in range(2)]
        dqt_ref = refs.pop()
    else:
        dqt_ref, dw_out, col_out = [refs.pop(0) for _ in range(3)]
    kt_ref, all_ref = refs
    rows_in = kx_ref.shape[1]
    piece_rows = rows_in // 4
    scale = HEAD_DIM**-0.5
    lane = lax.broadcasted_iota(jnp.int32, (piece_rows, LANES), 1)
    if first:
        for p in range(4):
            rows = slice(p * piece_rows, (p + 1) * piece_rows)
            left = grads[p][:, :LANES].astype(f32)
            right = grads[p][:, LANES:].astype(f32)
            right = jnp.concatenate([right, jnp.zeros_like(right)], axis=1)
            for h, wide in enumerate((left, pltpu.roll(left, HEAD_DIM, 1), right)):
                grad = jnp.where(lane < HEAD_DIM, wide, 0.0)
                delta = jnp.sum(grad * attx_ref[h, rows, :], axis=1, keepdims=True)
                d_high, d_mid, d_low = split_three(delta)
                grad = jnp.where(lane == HEAD_DIM, d_high, grad)
                grad = jnp.where(lane == HEAD_DIM + 1, d_mid, grad)
                grad = jnp.where(lane == HEAD_DIM + 2, d_low, grad)
                dox_ref[h, rows, :] = grad.astype(bf16)
        dqt_ref[...] = jnp.zeros_like(dqt_ref)
    else:
        dqt_ref[...] = dqt_in[...]
    for h in range(OWN_HEADS):
        kt_ref[h] = kx_ref[h, :, LANES:].astype(f32).T[:HEAD_DIM].astype(bf16)
    lane_k = lax.broadcasted_iota(jnp.int32, (block_k, LANES), 1)
    low_k = lane_k < HEAD_DIM
    for j in range(rows_in // block_k):
        ks = slice(j * block_k, (j + 1) * block_k)
        parts = {}
        for h in range(OWN_HEADS):
            k = kx_ref[h, ks, :]
            v = vx_ref[h, ks, :]
            kt = kt_ref[h, :, ks]
            dk = jnp.zeros((block_k, LANES), f32)
            dv = jnp.zeros((block_k, LANES), f32)
            for i in range(rows_in // block_q):
                qs = slice(i * block_q, (i + 1) * block_q)
                s = lax.dot_general(k, qx_ref[h, qs, :], CONTRACT_LAST, preferred_element_type=f32)
                prob = jnp.exp2(s)
                do = dox_ref[h, qs, :]
                dp = lax.dot_general(v, do, CONTRACT_LAST, preferred_element_type=f32)
                ds = (prob * dp).astype(bf16)
                dv = dv + jnp.dot(prob.astype(bf16), do, preferred_element_type=f32)
                dk = dk + jnp.dot(ds, qp_ref[h, qs, :], preferred_element_type=f32)
                dqt_ref[h, :, qs] += jnp.dot(kt, ds, preferred_element_type=f32)
            parts[OWN_HEADS + h] = dk * scale
            parts[2 * OWN_HEADS + h] = dv
        for tile in range(1, WIDE // LANES):
            left, right = parts.get(2 * tile), parts.get(2 * tile + 1)
            left = jnp.zeros((block_k, LANES), f32) if left is None else left
            right = 0.0 if right is None else pltpu.roll(right, HEAD_DIM, 1)
            both = jnp.where(low_k, left, right).astype(bf16)
            all_ref[ks, tile * LANES : (tile + 1) * LANES] = both
    if last:
        tall = jnp.concatenate([dqt_ref[0], dqt_ref[1]], axis=0) * scale
        all_ref[:, :LANES] = tall.T.astype(bf16)
        tall = dqt_ref[2] * scale
        tall = jnp.concatenate([tall, jnp.zeros_like(tall)], axis=0).T
        lane_all = lax.broadcasted_iota(jnp.int32, (rows_in, LANES), 1)
        old = all_ref[:, LANES : 2 * LANES].astype(f32)
        all_ref[:, LANES : 2 * LANES] = jnp.where(lane_all < HEAD_DIM, tall, old).astype(bf16)
    skip = 0 if last else LANES
    d_weight = [None, None]
    for p in range(4):
        rows = slice(p * piece_rows, (p + 1) * piece_rows)
        own = all_ref[rows, skip:]
        dx = lax.dot_general(own, w_ref[:, skip:], CONTRACT_LAST, preferred_element_type=f32)
        out_ref = keep_ref if p % 2 == 0 else send_ref
        out_ref[p // 2] = dx.astype(bf16)
        piece = lax.dot_general(
            pieces[p][...], own, (((0,), (0,)), ((), ())), preferred_element_type=f32
        )
        d_weight[0] = piece if p == 0 else d_weight[0] + piece
        col = jnp.sum(own.astype(f32), axis=0, keepdims=True)
        d_weight[1] = col if p == 0 else d_weight[1] + col
    grad, col = d_weight
    if last:
        dw_out[:, :LANES] = grad[:, :LANES].astype(bf16)
        dw_out[:, LANES:] = (grad[:, LANES:] + dw_in[...]).astype(bf16)
        col_out[:, :LANES] = jnp.broadcast_to(col[:, :LANES], (8, LANES))
        col_out[:, LANES:] = col[:, LANES:] + col_in[...]
    elif first:
        dw_out[...] = grad
        col_out[...] = jnp.broadcast_to(col, col_out.shape)
    else:
        dw_out[...] = grad + dw_in[...]
        col_out[...] = col + col_in[...]


def attend_back_chunk(first, last, chunk, pieces, shared, carry):
    kx, vx = chunk
    qx2, qp, w, grads, attx = shared
    rows, width = kx.shape[1], w.shape[0]
    operands = [kx, vx, qx2, qp, w, *pieces]
    operands += [*grads, attx] if first else list(carry)
    half = jax.ShapeDtypeStruct((2, rows // 4, width), bf16)
    out_shape = [half, half]
    scratch = [
        pltpu.VMEM((OWN_HEADS, HEAD_DIM, rows), bf16),
        pltpu.VMEM((rows, WIDE), bf16),
    ]
    if first:
        out_shape.append(jax.ShapeDtypeStruct((OWN_HEADS, rows, LANES), bf16))
    if last:
        out_shape.append(jax.ShapeDtypeStruct((width, WIDE), bf16))
        out_shape.append(jax.ShapeDtypeStruct((8, WIDE), f32))
        scratch.append(pltpu.VMEM((OWN_HEADS, HEAD_DIM, rows), f32))
    else:
        out_shape.append(jax.ShapeDtypeStruct((OWN_HEADS, HEAD_DIM, rows), f32))
        out_shape.append(jax.ShapeDtypeStruct((width, WIDE - LANES), f32))
        out_shape.append(jax.ShapeDtypeStruct((8, WIDE - LANES), f32))
    return pl.pallas_call(
        partial(backward_kernel, first, last, min(512, rows), min(512, rows)),
        out_shape=out_shape,
        in_specs=vmem_specs(len(operands)),
        out_specs=vmem_specs(len(out_shape)),
        scratch_shapes=scratch,
        compiler_params=pltpu.CompilerParams(vmem_limit_bytes=VMEM_BYTES),
        cost_estimate=pl.CostEstimate(
            flops=int(1.5e10), transcendentals=OWN_HEADS * rows * rows, bytes_accessed=int(1e7)
        ),
        name="attend_backward",
    )(*operands)


def norm_forward(value, gain, shift):
    center = value - jnp.mean(value, axis=-1, keepdims=True)
    spread = jnp.mean(center * center, axis=-1, keepdims=True)
    inverse = lax.rsqrt(spread + norm_eps)
    normal = center * inverse
    return normal * gain + shift, normal, inverse


def norm_backward(grad, gain, normal, inverse):
    inner = grad * gain
    mean = jnp.mean(inner, axis=-1, keepdims=True)
    along = jnp.mean(inner * normal, axis=-1, keepdims=True)
    return inverse * (inner - mean - normal * along)


CONTRACT_FIRST = (((0,), (0,)), ((), ()))


def ffn_kernel(layout, *refs):
    n_q, n_b, own_rows, fold, aligned = layout
    refs = list(refs)
    where_ref = refs.pop(0)
    att_refs = [refs.pop(0) for _ in range(4)]
    x_ref, cot_ref, vec_ref, eb_ref, packed = [refs.pop(0) for _ in range(5)]
    out_ref, resid_ref = [refs.pop(0) for _ in range(2)]
    da_refs = [refs.pop(0) for _ in range(4)]
    vec_out = refs.pop(0)
    targets = [refs.pop(0) for _ in range(6 if aligned else 1)]
    wo, w1, w2, go, g1, g2, act, slope, in_sem, out_sem = refs
    group, zi, xi, ci, bi, start, length = [where_ref[i] for i in range(7)]
    rows, width = x_ref.shape

    def lanes(i):
        return slice(i * width, (i + 1) * width)

    loads = [pltpu.make_async_copy(packed.at[:, lanes(0)], wo, in_sem.at[0])]
    for k in range(fold):
        loads.append(pltpu.make_async_copy(packed.at[:, lanes(1 + k)], w1.at[k], in_sem.at[1 + k]))
    for k in range(fold):
        sem = in_sem.at[1 + fold + k]
        loads.append(pltpu.make_async_copy(packed.at[:, lanes(1 + fold + k)], w2.at[k], sem))
    for load in loads:
        load.start()

    def group_rows(r):
        other = (2 * (xi ^ (r // 2))) + (ci ^ (r % 2))
        return pl.ds(pl.multiple_of(other * OWN_WIDTH, HEAD_DIM), OWN_WIDTH)

    obias, gain1, shift1, sbias, gain2, shift2 = [vec_ref[i : i + 1, :] for i in range(2, 8)]
    loads[0].wait()
    branch = obias + jnp.zeros((rows, width), f32)
    for r in range(4):
        branch += jnp.dot(att_refs[r][...], wo[group_rows(r), :], preferred_element_type=f32)
    hidden, normal1, inverse1 = norm_forward(x_ref[...].astype(f32) + branch, gain1, shift1)
    hidden_low = hidden.astype(bf16)
    shrunk = sbias + hidden
    for k in range(fold):
        loads[1 + k].wait()
        expanded = jnp.dot(hidden_low, w1[k], preferred_element_type=f32) + eb_ref[k : k + 1, :]
        cdf = 0.5 * (1.0 + lax.erf(expanded * (2.0**-0.5)))
        pdf = jnp.exp(-0.5 * expanded * expanded) * ((2.0 * math.pi) ** -0.5)
        act[k] = (expanded * cdf).astype(bf16)
        slope[k] = cdf + expanded * pdf
        loads[1 + fold + k].wait()
        shrunk += jnp.dot(act[k], w2[k], preferred_element_type=f32)
    result, normal2, inverse2 = norm_forward(shrunk, gain2, shift2)
    out_ref[...] = result.astype(bf16)
    row = lax.broadcasted_iota(jnp.int32, (rows, width), 0)
    seed = jnp.where(start + row < length, cot_ref[...].astype(f32), 0.0)
    vec_out[4:5, :] = jnp.sum(seed * normal2, axis=0, keepdims=True)
    vec_out[5:6, :] = jnp.sum(seed, axis=0, keepdims=True)
    resid2 = norm_backward(seed, gain2, normal2, inverse2)
    shrunk_low = resid2.astype(bf16)
    vec_out[3:4, :] = jnp.sum(shrunk_low.astype(f32), axis=0, keepdims=True)
    hidden_grad = resid2
    for k in range(fold):
        active_grad = lax.dot_general(
            shrunk_low, w2[k], CONTRACT_LAST, preferred_element_type=f32
        )
        expanded_low = (active_grad * slope[k]).astype(bf16)
        vec_out[8 + k : 9 + k, :] = jnp.sum(expanded_low.astype(f32), axis=0, keepdims=True)
        hidden_grad += lax.dot_general(
            expanded_low, w1[k], CONTRACT_LAST, preferred_element_type=f32
        )
        g2[k] = lax.dot_general(
            act[k], shrunk_low, CONTRACT_FIRST, preferred_element_type=f32
        ).astype(bf16)
        g1[k] = lax.dot_general(
            hidden_low, expanded_low, CONTRACT_FIRST, preferred_element_type=f32
        ).astype(bf16)
    vec_out[1:2, :] = jnp.sum(hidden_grad * normal1, axis=0, keepdims=True)
    vec_out[2:3, :] = jnp.sum(hidden_grad, axis=0, keepdims=True)
    resid1 = norm_backward(hidden_grad, gain1, normal1, inverse1)
    resid_ref[...] = resid1
    branch_low = resid1.astype(bf16)
    vec_out[0:1, :] = jnp.sum(branch_low.astype(f32), axis=0, keepdims=True)
    vec_out[6:8, :] = jnp.zeros((2, width), f32)
    vec_out[8 + fold :, :] = jnp.zeros((vec_out.shape[0] - 8 - fold, width), f32)
    for r in range(4):
        da_refs[r][...] = lax.dot_general(
            branch_low, wo[group_rows(r), :], CONTRACT_LAST, preferred_element_type=f32
        ).astype(bf16)
        go[group_rows(r), :] = lax.dot_general(
            att_refs[r][...], branch_low, CONTRACT_FIRST, preferred_element_type=f32
        ).astype(bf16)
    units = [g2.at[k] for k in range(fold)] + [g1.at[k] for k in range(fold)] + [go]
    if aligned:
        block = n_b * own_rows
        for i, part in enumerate(unit_parts(fold)):
            for dc in range(2):
                target, sem = targets[2 * i + dc], out_sem.at[2 * i + dc]
                for dx in range(2):
                    for jz in range(n_q):
                        m = (lax.rem(zi + jz, n_q) * 2 + (xi ^ dx)) * 2 + (ci ^ dc)
                        at = pl.ds(pl.multiple_of(m * block, 16), block)
                        for place, unit in enumerate(part):
                            dst = target.at[dx, jz, :, lanes(place)]
                            pltpu.make_async_copy(units[unit].at[at], dst, sem).start()
    else:
        for i, unit in enumerate(units):
            pltpu.make_async_copy(unit, targets[0].at[:, lanes(i)], out_sem.at[0]).start()
    for i, dst in enumerate(targets):
        pltpu.make_async_copy(dst, dst, out_sem.at[i]).wait()


def unit_parts(fold):
    count = 1 + 2 * fold
    edges = [count * i // 3 for i in range(4)]
    return [range(edges[i], edges[i + 1]) for i in range(3)]


def ffn_block(layout, where, att, x, cot, vectors, ebias, packed):
    n_q, n_b, own_rows, fold, aligned = layout
    rows, width = x.shape
    ff = fold * width
    operands = [where, *att, x, cot, vectors, ebias, packed]
    in_specs = [pl.BlockSpec(memory_space=pltpu.SMEM)] + vmem_specs(8)
    in_specs += [pl.BlockSpec(memory_space=pl.ANY)]
    out_shape = [
        jax.ShapeDtypeStruct((rows, width), bf16),
        jax.ShapeDtypeStruct((rows, width), f32),
        *[jax.ShapeDtypeStruct((rows, OWN_WIDTH), bf16)] * 4,
        jax.ShapeDtypeStruct((16, width), f32),
    ]
    if aligned:
        lead = (2, n_q, n_b * own_rows)
        sizes = [len(part) * width for part in unit_parts(fold)]
        targets = [jax.ShapeDtypeStruct((*lead, size), bf16) for size in sizes for _ in range(2)]
    else:
        targets = [jax.ShapeDtypeStruct((width, width + 2 * ff), bf16)]
    weight_scratch = [
        pltpu.VMEM((width, width), bf16),
        pltpu.VMEM((fold, width, width), bf16),
        pltpu.VMEM((fold, width, width), bf16),
    ]
    return pl.pallas_call(
        partial(ffn_kernel, layout),
        out_shape=out_shape + targets,
        in_specs=in_specs,
        out_specs=vmem_specs(len(out_shape)) + [pl.BlockSpec(memory_space=pl.ANY)] * len(targets),
        scratch_shapes=weight_scratch
        + weight_scratch
        + [
            pltpu.VMEM((fold, rows, width), bf16),
            pltpu.VMEM((fold, rows, width), f32),
            pltpu.SemaphoreType.DMA((1 + 2 * fold,)),
            pltpu.SemaphoreType.DMA((6,)),
        ],
        compiler_params=pltpu.CompilerParams(vmem_limit_bytes=VMEM_BYTES),
        cost_estimate=pl.CostEstimate(
            flops=int(2e10), transcendentals=2 * rows * ff, bytes_accessed=int(3e7)
        ),
        name="feed_forward",
    )(*operands)


def order_kernel(n_q, n_b, where_ref, blocks_ref, out_ref):
    group, zi, bi = [where_ref[i] for i in range(3)]
    rows = blocks_ref.shape[3]
    for m in range(4 * n_q):
        q, g = m // 4, m % 4
        far, r = lax.rem(q + n_q - zi, n_q), g ^ group
        both = [
            blocks_ref[lax.rem(b + n_b - bi, n_b), far, r].astype(f32) for b in range(n_b)
        ]
        at = slice(m * n_b * rows, (m + 1) * n_b * rows)
        out_ref[at, :] = jnp.concatenate(both, axis=0).astype(bf16)


def order_rows(n_q, n_b, where, blocks):
    rows, lanes = blocks.shape[3:]
    return pl.pallas_call(
        partial(order_kernel, n_q, n_b),
        out_shape=jax.ShapeDtypeStruct((4 * n_q * n_b * rows, lanes), bf16),
        in_specs=[pl.BlockSpec(memory_space=pltpu.SMEM)] + vmem_specs(1),
        out_specs=vmem_specs(1)[0],
        compiler_params=pltpu.CompilerParams(vmem_limit_bytes=VMEM_BYTES),
        name="order_rows",
    )(where, blocks)


def from_shift(value, axis, count, step):
    return lax.ppermute(value, axis, [((i + step) % count, i) for i in range(count)])


def square_swap(value, r):
    if r == 0:
        return value
    if r == 1:
        return lax.ppermute(value, "c", [(0, 1), (1, 0)])
    if r == 2:
        return lax.ppermute(value, "x", [(0, 1), (1, 0)])
    return lax.ppermute(value, ("x", "c"), [(0, 3), (3, 0), (1, 2), (2, 1)])


def pick(stacked, index, dim=0):
    return lax.dynamic_index_in_dim(stacked, index, dim, keepdims=False)


class Chain:
    def __init__(self, state, *steps):
        self.state, self.steps = tuple(state), list(steps)


def run_stage(chains, outs=()):
    for chain in chains:
        chain.state = tuple(chain.steps.pop(0)(*chain.state))
    outs, states = lax.optimization_barrier((tuple(outs), [c.state for c in chains]))
    for chain, state in zip(chains, states):
        chain.state = tuple(state)
    return outs


def away_sum(total, axis, count):
    parts = [total[j].astype(bf16) for j in range(1, count)]
    return [from_shift(part, axis, count, count - j - 1) for j, part in enumerate(parts)]


def weight_sum(keep, send, n_q, n_b, bi):
    def own_b(keep, got, j):
        shape = (2, n_q, n_b, -1, keep.shape[-1])
        both = [pick(v.reshape(shape), (bi + j) % n_b, 2).astype(f32) for v in (keep, got)]
        return both[0] + both[1]

    def over_core(keep, send):
        return keep, square_swap(send, 1)

    def over_b(keep, got):
        away = [own_b(keep, got, j).astype(bf16) for j in range(1, n_b)]
        return keep, got, *[from_shift(v, "b", n_b, n_b - 1 - j) for j, v in enumerate(away)]

    def over_x(keep, got, *more):
        total = own_b(keep, got, 0) + sum(v.astype(f32) for v in more)
        return total[0], *away_sum(total, "x", 2)

    def over_q(own, *more):
        total = own + sum(v.astype(f32) for v in more)
        return total[0], *away_sum(total, "q", n_q)

    return Chain((keep, send), over_core, over_b, over_x, over_q)


def token_sum(keep, send, n_q, j):
    def over_core(keep, send):
        return keep, square_swap(send, 1)

    def over_x(keep, got):
        total = keep.astype(f32) + got.astype(f32)
        return total[0], square_swap(total[1].astype(bf16), 2)

    def over_q(own, got):
        total = own + got.astype(f32)
        return (from_shift(total.astype(bf16), "q", n_q, n_q - j),)

    return Chain((keep, send), over_core, over_x, *([over_q] if j else []))


def chain_sum(chain):
    return sum(v.astype(f32) for v in chain.state)


def deinterleave(fold):
    size = fold * LANES
    lane = jnp.arange(size)
    return (lane[:, None] // fold + (lane[:, None] % fold) * LANES == lane[None, :]).astype(bf16)


def per_device(
    n_q,
    n_b,
    inputs,
    lengths,
    cotangent,
    triple_weight,
    query_bias,
    value_bias,
    output_weight,
    output_bias,
    first_gain,
    first_shift,
    expand_weight,
    expand_bias,
    shrink_weight,
    shrink_bias,
    second_gain,
    second_shift,
):
    zi, xi, ci, bi = [lax.axis_index(a) for a in AXES]
    group = 2 * xi + ci
    _, seq_rows, width = inputs.shape
    own_rows = triple_weight.shape[0]
    ff = expand_weight.shape[1]
    fold = ff // width
    aligned = n_b * own_rows % 16 == 0
    x_own = inputs[0]

    turn = deinterleave(fold)
    expand_own = expand_weight.astype(bf16).reshape(own_rows, -1, fold * LANES)
    expand_own = jnp.einsum("rbs,st->rbt", expand_own, turn, preferred_element_type=f32)
    expand_own = expand_own.astype(bf16).reshape(own_rows, -1, fold, LANES).transpose(0, 2, 1, 3)
    packed = jnp.concatenate(
        [
            output_weight.astype(bf16),
            expand_own.reshape(own_rows, ff),
            shrink_weight.astype(bf16).reshape(own_rows, ff),
        ],
        axis=1,
    )
    gathered_ffn = lax.all_gather(packed, AXES, axis=0, tiled=True)

    names = [query_bias, value_bias, output_bias, first_gain, first_shift]
    names += [shrink_bias, second_gain, second_shift]
    vectors = jnp.stack(names, axis=1)
    vectors = jnp.concatenate([vectors, expand_bias.reshape(own_rows, fold)], axis=1).astype(bf16)
    n_vec = vectors.shape[1]
    vectors = jnp.pad(vectors, ((0, 0), (0, WIDE - VECTORS - n_vec)))
    thirds = triple_weight.astype(bf16).reshape(own_rows, 3, GROUPS, OWN_WIDTH)

    def columns_of(g):
        mine = [pick(thirds[:, t], g, 1) for t in range(3)]
        return jnp.concatenate(mine + [vectors], axis=1)

    def rows_square(*blocks):
        return [square_swap(block, r) for r, block in enumerate(blocks)]

    def rows_q(*blocks):
        square = jnp.stack(blocks)
        return [square] + [from_shift(square, "q", n_q, j) for j in range(1, n_q)]

    def rows_b(*blocks):
        both = jnp.stack(blocks)
        return [both] + [from_shift(both, "b", n_b, j) for j in range(1, n_b)]

    weight_rows = Chain([columns_of(group ^ r) for r in range(4)], rows_square, rows_q, rows_b)

    def token_chunk(j):
        def over_q(own):
            return (from_shift(own, "q", n_q, j),)

        def over_x(own):
            return own, square_swap(own, 2)

        def over_core(own, other):
            halves = square_swap(jnp.stack([own, other]), 1)
            return own, halves[0], other, halves[1]

        return Chain((x_own,), *([over_q] if j else []), over_x, over_core)

    arrival = []
    for j in [k for pair in zip(range(1, n_q), range(n_q - 1, 0, -1)) for k in pair]:
        arrival += [] if j in arrival else [j]
    arrival = [0] + arrival
    chunks = {j: token_chunk(j) for j in arrival}
    line = [chunks[j] for j in arrival]
    for step in range(3):
        ready = [c for i, c in enumerate(line) if i <= step + 1 and c.steps and (i or step < 2)]
        run_stage([weight_rows] + ready)
    chunk_x = {}

    by_distance = jnp.stack(weight_rows.state)
    if aligned:
        spot = jnp.stack([group, zi, bi]).astype(jnp.int32)
        w_own = order_rows(n_q, n_b, spot, by_distance)
    else:
        ordered = jnp.stack([pick(by_distance, (i - bi) % n_b) for i in range(n_b)], axis=3)
        ordered = jnp.stack([pick(ordered, group ^ g, 1) for g in range(4)], axis=1)
        ordered = jnp.stack([pick(ordered, (i - zi) % n_q) for i in range(n_q)])
        w_own = ordered.transpose(0, 1, 3, 2, 4).reshape(width, WIDE)
    turned = w_own[:, VECTORS : VECTORS + n_vec].astype(f32)
    turned = turned.T
    ebias = turned[8:]
    turned = turned[:8]
    own_bias = lax.dynamic_slice_in_dim(turned, group * OWN_WIDTH, OWN_WIDTH, 1)
    zero = jnp.zeros((1, OWN_WIDTH), f32)
    bias_row = jnp.concatenate(
        [own_bias[:1], zero, own_bias[1:2], jnp.zeros((1, WIDE - VECTORS), f32)], axis=1
    )

    def where_of(j):
        zj = (zi + j) % n_q
        spots = [(zj * 4 + (group ^ r)) * seq_rows for r in range(4)]
        return jnp.stack(spots + [lengths[0]]).astype(jnp.int32)

    weights = (w_own, bias_row)
    kept = {}
    carry = None
    for step, j in enumerate(arrival):
        first, last = step == 0, step == n_q - 1
        while chunks[j].steps:
            run_stage([c for c in line[step:] if c.steps])
        chunk_x[j] = chunks[j].state
        outs = attend_chunk(first, last, where_of(j), chunk_x[j], weights, carry)
        outs = run_stage([c for c in line[step + 1 :] if c.steps], outs)
        kept[j] = (outs[0], outs[1])
        outs = outs[2:]
        if first:
            qx, qp = outs[:2]
            outs = outs[2:]
        carry = (qx, *outs)
    att, attx, qx2 = carry[1:5], carry[5], carry[6]

    att = [square_swap(att[r], r) for r in range(4)]
    start = (zi * 4 + group) * seq_rows
    where = jnp.stack([group, zi, xi, ci, bi, start, lengths[0]]).astype(jnp.int32)
    layout = (n_q, n_b, own_rows, fold, aligned)
    outs = ffn_block(layout, where, att, x_own, cotangent[0], turned, ebias, gathered_ffn)
    output, resid_first_grad = outs[:2]
    att_grads, vec_grads, summands = outs[2:6], outs[6], outs[7:]
    square = Chain(att_grads, lambda *parts: [square_swap(v, r) for r, v in enumerate(parts)])

    sums = []
    if aligned:
        for i in range(3):
            sums.append(weight_sum(summands[2 * i], summands[2 * i + 1], n_q, n_b, bi))
    else:
        summed = lax.psum_scatter(summands[0], AXES, scatter_dimension=0, tiled=True).astype(f32)
    run_stage([square] + sums[:1])
    shared = (qx2, qp, w_own, square.state, attx)
    carry = None
    moving = []
    for step, j in enumerate(reversed(arrival)):
        first, last = step == 0, step == n_q - 1
        outs = attend_back_chunk(first, last, kept[j], chunk_x[j], shared, carry)
        begun = [c for c in sums[: step + 2] if c.steps]
        outs = run_stage(begun + [c for c in moving if c.steps], outs)
        keep, send = outs[:2]
        moving.append(token_sum(keep, send, n_q, j))
        outs = outs[2:]
        if first:
            dox = outs[0]
            outs = outs[1:]
        carry = (dox, *outs)
        if not last:
            carry = run_stage(moving[-1:], carry)
    grad_joint, col = carry[1:]

    own_bias = jnp.stack([col[0, :OWN_WIDTH], col[0, 2 * OWN_WIDTH : 3 * OWN_WIDTH]])
    bias_grads = lax.dynamic_update_slice(
        jnp.zeros((2, width), f32), own_bias, (0, group * OWN_WIDTH)
    )
    tall = jnp.concatenate([bias_grads, vec_grads[:6], vec_grads[8 : 8 + fold]], axis=0).T
    tall_high = tall.astype(bf16)
    tall_low = (tall - tall_high.astype(f32)).astype(bf16)
    room = jnp.zeros((width, WIDE - VECTORS - 2 * n_vec), bf16)
    blocks = jnp.concatenate([grad_joint[:, :VECTORS], tall_high, tall_low, room], axis=1)
    total = blocks.reshape(n_q, 4, n_b, own_rows, WIDE)

    def rows_over_b(total):
        parts = [pick(total, (bi + j) % n_b, 2) for j in range(n_b)]
        return parts[0], *away_sum(parts, "b", n_b)

    def rows_over_q(*parts):
        total = sum(v.astype(f32) for v in parts)
        parts = [pick(total, (zi + j) % n_q) for j in range(n_q)]
        return parts[0], *away_sum(parts, "q", n_q)

    def rows_over_square(*parts):
        total = sum(v.astype(f32) for v in parts).astype(bf16)
        return [square_swap(pick(total, group ^ r), r) for r in range(4)]

    rows = Chain((total,), rows_over_b, rows_over_q, rows_over_square)
    while any(c.steps for c in [rows, *sums, *moving]):
        run_stage([c for c in [rows, *sums, *moving] if c.steps])
    token_grad = resid_first_grad
    for chain in moving:
        token_grad = token_grad + chain_sum(chain)
    input_grad = token_grad.astype(bf16)
    if aligned:
        summed = jnp.concatenate([chain_sum(c) for c in sums], axis=1)
    parts = jnp.stack(rows.state)
    parts = jnp.stack([pick(parts, group ^ g) for g in range(4)])
    grad_triple = parts[:, :, :VECTORS].reshape(GROUPS, own_rows, 3, OWN_WIDTH)
    grad_triple = grad_triple.transpose(1, 2, 0, 3).reshape(own_rows, -1).astype(f32)
    small = jnp.sum(parts[:, :, VECTORS : VECTORS + 2 * n_vec].astype(f32), axis=0)
    small = small[:, :n_vec] + small[:, n_vec:]
    grad_expand = summed[:, ff : 2 * ff].reshape(own_rows, fold, -1, LANES).transpose(0, 2, 1, 3)
    grad_expand = jnp.einsum(
        "rbs,ts->rbt",
        grad_expand.reshape(own_rows, -1, fold * LANES),
        turn.astype(f32),
        precision=lax.Precision.HIGHEST,
        preferred_element_type=f32,
    ).reshape(own_rows, ff)
    return (
        output[None],
        input_grad[None],
        grad_triple,
        small[:, 0],
        small[:, 1],
        summed[:, 2 * ff :],
        small[:, 2],
        small[:, 3],
        small[:, 4],
        grad_expand,
        small[:, 8:].reshape(-1),
        summed[:, :ff].reshape(-1, width),
        small[:, 5],
        small[:, 6],
        small[:, 7],
    )


def solution(mesh):
    n_seq, n_b = mesh.shape["seq"], mesh.shape["batch"]
    n_q = n_seq // GROUPS
    fine = Mesh(mesh.devices.reshape(n_q, 2, 2, n_b), AXES)
    tokens = P("b", ("q", "x", "c"), None)
    matrix = P(AXES, None)
    vector = P(AXES)
    in_specs = (
        tokens,
        P("b"),
        tokens,
        matrix,
        vector,
        vector,
        matrix,
        vector,
        vector,
        vector,
        matrix,
        vector,
        matrix,
        vector,
        vector,
        vector,
    )
    out_specs = (
        tokens,
        tokens,
        matrix,
        vector,
        vector,
        matrix,
        vector,
        vector,
        vector,
        matrix,
        vector,
        matrix,
        vector,
        vector,
        vector,
    )
    return jax.shard_map(
        partial(per_device, n_q, n_b),
        mesh=fine,
        in_specs=in_specs,
        out_specs=out_specs,
        check_vma=False,
    )
```

```python
from functools import partial
import math

import jax
import jax.numpy as jnp
from jax import lax
from jax.experimental import pallas as pl
from jax.experimental.pallas import tpu as pltpu
from jax.sharding import Mesh, PartitionSpec as P

HEADS = 12
HEAD_DIM = 64
GROUPS = 4
OWN_HEADS = HEADS // GROUPS
OWN_WIDTH = OWN_HEADS * HEAD_DIM
LANES = 128
WIDE = 640
VECTORS = 3 * OWN_WIDTH

bf16 = jnp.bfloat16
f32 = jnp.float32
masked_score = -1e30
norm_eps = 1e-12
log2_e = 1.4426950408889634
CONTRACT_LAST = (((1,), (1,)), ((), ()))
VMEM_BYTES = 60 * 1024 * 1024
AXES = ("q", "x", "c", "b")


def split_three(value):
    high = value.astype(bf16).astype(f32)
    rest = value - high
    mid = rest.astype(bf16).astype(f32)
    low = (rest - mid).astype(bf16).astype(f32)
    return high, mid, low


def low_half(tile, lane, from_high):
    turned = pltpu.roll(tile, HEAD_DIM, 1)
    low = lane < HEAD_DIM
    return jnp.where(low, turned, tile) if from_high else jnp.where(low, tile, turned)


def place_of(kind, h):
    slot = kind * OWN_HEADS + h
    return slot // 2, slot % 2


def forward_kernel(first, last, block_q, block_k, *refs):
    refs = list(refs)
    where_ref = refs.pop(0)
    pieces = [refs.pop(0) for _ in range(4)]
    w_ref, bias_ref = [refs.pop(0) for _ in range(2)]
    if not first:
        qx_ref, peak_in, sum_in = [refs.pop(0) for _ in range(3)]
    kx_ref, vx_ref = [refs.pop(0) for _ in range(2)]
    if first:
        qx_ref, qp_ref = [refs.pop(0) for _ in range(2)]
    if last:
        att_refs = [refs.pop(0) for _ in range(4)]
        attx_ref, qx2_ref = [refs.pop(0) for _ in range(2)]
    else:
        peak_out, sum_out = [refs.pop(0) for _ in range(2)]
    (vt_ref,) = refs
    piece_rows = pieces[0].shape[0]
    rows_in = 4 * piece_rows
    lane = lax.broadcasted_iota(jnp.int32, (piece_rows, LANES), 1)
    row = lax.broadcasted_iota(jnp.int32, (piece_rows, LANES), 0)
    low = lane < HEAD_DIM
    length = where_ref[4]
    three = (lane >= HEAD_DIM) & (lane < HEAD_DIM + 3)
    skip = 0 if first else LANES
    for p in range(4):
        rows = slice(p * piece_rows, (p + 1) * piece_rows)
        joint = jnp.dot(pieces[p][...], w_ref[:, skip:], preferred_element_type=f32)
        joint = joint + bias_ref[:, skip:]
        bias = jnp.where(where_ref[p] + row < length, 0.0, masked_score)
        key_extra = jnp.where(three, 1.0, jnp.where(lane == HEAD_DIM + 3, bias, 0.0))

        def head_of(kind, h):
            tile, high = place_of(kind, h)
            return low_half(joint[:, tile * LANES - skip : (tile + 1) * LANES - skip], lane, high)

        for h in range(OWN_HEADS):
            k = head_of(1, h)
            kx_ref[h, rows, :LANES] = k.astype(bf16)
            kx_ref[h, rows, LANES:] = jnp.where(low, k, key_extra).astype(bf16)
            v = jnp.where(low, head_of(2, h), 0.0)
            vx_ref[h, rows, :] = jnp.where(three, -1.0, v).astype(bf16)
            vt = jnp.where(lane == HEAD_DIM, 1.0, v).T
            vt_ref[h, :, rows] = vt[:80].astype(bf16)
            if first:
                q = head_of(0, h).astype(bf16).astype(f32)
                qp_ref[h, rows, :] = jnp.where(low, q, 0.0).astype(bf16)
                high, mid, rest = split_three(q * (HEAD_DIM**-0.5 * log2_e))
                qx_ref[h, rows, :LANES] = jnp.where(low, high, mid).astype(bf16)
                one = jnp.where(lane == HEAD_DIM + 3, 1.0, 0.0)
                qx_ref[h, rows, LANES:] = jnp.where(low, rest, one).astype(bf16)
    for h in range(OWN_HEADS):
        for i in range(rows_in // block_q):
            cols = slice(i * block_q, (i + 1) * block_q)
            q = qx_ref[h, cols, :]
            if first:
                peak = jnp.full((1, block_q), masked_score, f32)
                total = jnp.zeros((80, block_q), f32)
            else:
                peak = peak_in[h, :1, cols]
                total = sum_in[h, :, cols]
            for j in range(rows_in // block_k):
                ks = slice(j * block_k, (j + 1) * block_k)
                s = lax.dot_general(kx_ref[h, ks, :], q, CONTRACT_LAST, preferred_element_type=f32)
                new_peak = jnp.maximum(peak, jnp.max(s, axis=0, keepdims=True))
                prob = jnp.exp2(s - new_peak).astype(bf16)
                total = total * jnp.exp2(peak - new_peak) + jnp.dot(
                    vt_ref[h, :, ks], prob, preferred_element_type=f32
                )
                peak = new_peak
            if last:
                denom = total[HEAD_DIM : HEAD_DIM + 1]
                n_high, n_mid, n_low = split_three(-(peak + jnp.log2(denom)))
                tall = jnp.concatenate(
                    [
                        total[:HEAD_DIM] / denom,
                        n_high,
                        n_mid,
                        n_low,
                        jnp.zeros((HEAD_DIM - 3, block_q), f32),
                    ],
                    axis=0,
                )
                attx_ref[h, cols, :] = tall.T
            else:
                peak_out[h, :, cols] = jnp.broadcast_to(peak, (8, block_q))
                sum_out[h, :, cols] = total
    if last:
        for p in range(4):
            rows = slice(p * piece_rows, (p + 1) * piece_rows)
            heads = [attx_ref[h, rows, :] for h in range(OWN_HEADS)]
            pair = jnp.where(low, heads[0], pltpu.roll(heads[1], HEAD_DIM, 1))
            att_refs[p][:, :LANES] = pair.astype(bf16)
            att_refs[p][:, LANES:] = heads[2][:, :HEAD_DIM].astype(bf16)
            for h in range(OWN_HEADS):
                qx2_ref[h, rows, :LANES] = qx_ref[h, rows, :LANES]
                old = qx_ref[h, rows, LANES:].astype(f32)
                qx2_ref[h, rows, LANES:] = jnp.where(three, heads[h], old).astype(bf16)


def vmem_specs(n):
    return [pl.BlockSpec(memory_space=pltpu.VMEM) for _ in range(n)]


def attend_chunk(first, last, where, pieces, weights, carry):
    piece_rows = pieces[0].shape[0]
    rows = 4 * piece_rows
    operands = [where, *pieces, *weights]
    operands += [] if first else list(carry)
    wide_keys = jax.ShapeDtypeStruct((OWN_HEADS, rows, 2 * LANES), bf16)
    out_shape = [wide_keys, jax.ShapeDtypeStruct((OWN_HEADS, rows, LANES), bf16)]
    if first:
        out_shape += [wide_keys, jax.ShapeDtypeStruct((OWN_HEADS, rows, LANES), bf16)]
    if last:
        out_shape += [jax.ShapeDtypeStruct((piece_rows, OWN_WIDTH), bf16)] * 4
        out_shape += [jax.ShapeDtypeStruct((OWN_HEADS, rows, LANES), f32), wide_keys]
    else:
        out_shape += [
            jax.ShapeDtypeStruct((OWN_HEADS, 8, rows), f32),
            jax.ShapeDtypeStruct((OWN_HEADS, 80, rows), f32),
        ]
    return pl.pallas_call(
        partial(forward_kernel, first, last, min(512, rows), min(1024, rows)),
        out_shape=out_shape,
        in_specs=[pl.BlockSpec(memory_space=pltpu.SMEM)] + vmem_specs(len(operands) - 1),
        out_specs=vmem_specs(len(out_shape)),
        scratch_shapes=[pltpu.VMEM((OWN_HEADS, 80, rows), bf16)],
        compiler_params=pltpu.CompilerParams(vmem_limit_bytes=VMEM_BYTES),
        cost_estimate=pl.CostEstimate(
            flops=int(8e9), transcendentals=OWN_HEADS * rows * rows, bytes_accessed=int(1e7)
        ),
        name="attend_forward",
    )(*operands)


def backward_kernel(first, last, block_q, block_k, *refs):
    refs = list(refs)
    kx_ref, vx_ref, qx_ref, qp_ref, w_ref = [refs.pop(0) for _ in range(5)]
    pieces = [refs.pop(0) for _ in range(4)]
    if first:
        grads = [refs.pop(0) for _ in range(4)]
        attx_ref = refs.pop(0)
    else:
        dox_ref, dqt_in, dw_in, col_in = [refs.pop(0) for _ in range(4)]
    keep_ref, send_ref = [refs.pop(0) for _ in range(2)]
    if first:
        dox_ref = refs.pop(0)
    if last:
        dw_out, col_out = [refs.pop(0) for _ in range(2)]
        dqt_ref = refs.pop()
    else:
        dqt_ref, dw_out, col_out = [refs.pop(0) for _ in range(3)]
    kt_ref, all_ref = refs
    rows_in = kx_ref.shape[1]
    piece_rows = rows_in // 4
    scale = HEAD_DIM**-0.5
    lane = lax.broadcasted_iota(jnp.int32, (piece_rows, LANES), 1)
    if first:
        for p in range(4):
            rows = slice(p * piece_rows, (p + 1) * piece_rows)
            left = grads[p][:, :LANES].astype(f32)
            right = grads[p][:, LANES:].astype(f32)
            right = jnp.concatenate([right, jnp.zeros_like(right)], axis=1)
            for h, wide in enumerate((left, pltpu.roll(left, HEAD_DIM, 1), right)):
                grad = jnp.where(lane < HEAD_DIM, wide, 0.0)
                delta = jnp.sum(grad * attx_ref[h, rows, :], axis=1, keepdims=True)
                d_high, d_mid, d_low = split_three(delta)
                grad = jnp.where(lane == HEAD_DIM, d_high, grad)
                grad = jnp.where(lane == HEAD_DIM + 1, d_mid, grad)
                grad = jnp.where(lane == HEAD_DIM + 2, d_low, grad)
                dox_ref[h, rows, :] = grad.astype(bf16)
        dqt_ref[...] = jnp.zeros_like(dqt_ref)
    else:
        dqt_ref[...] = dqt_in[...]
    for h in range(OWN_HEADS):
        kt_ref[h] = kx_ref[h, :, LANES:].astype(f32).T[:HEAD_DIM].astype(bf16)
    lane_k = lax.broadcasted_iota(jnp.int32, (block_k, LANES), 1)
    low_k = lane_k < HEAD_DIM
    for j in range(rows_in // block_k):
        ks = slice(j * block_k, (j + 1) * block_k)
        parts = {}
        for h in range(OWN_HEADS):
            k = kx_ref[h, ks, :]
            v = vx_ref[h, ks, :]
            kt = kt_ref[h, :, ks]
            dk = jnp.zeros((block_k, LANES), f32)
            dv = jnp.zeros((block_k, LANES), f32)
            for i in range(rows_in // block_q):
                qs = slice(i * block_q, (i + 1) * block_q)
                s = lax.dot_general(k, qx_ref[h, qs, :], CONTRACT_LAST, preferred_element_type=f32)
                prob = jnp.exp2(s)
                do = dox_ref[h, qs, :]
                dp = lax.dot_general(v, do, CONTRACT_LAST, preferred_element_type=f32)
                ds = (prob * dp).astype(bf16)
                dv = dv + jnp.dot(prob.astype(bf16), do, preferred_element_type=f32)
                dk = dk + jnp.dot(ds, qp_ref[h, qs, :], preferred_element_type=f32)
                dqt_ref[h, :, qs] += jnp.dot(kt, ds, preferred_element_type=f32)
            parts[OWN_HEADS + h] = dk * scale
            parts[2 * OWN_HEADS + h] = dv
        for tile in range(1, WIDE // LANES):
            left, right = parts.get(2 * tile), parts.get(2 * tile + 1)
            left = jnp.zeros((block_k, LANES), f32) if left is None else left
            right = 0.0 if right is None else pltpu.roll(right, HEAD_DIM, 1)
            both = jnp.where(low_k, left, right).astype(bf16)
            all_ref[ks, tile * LANES : (tile + 1) * LANES] = both
    if last:
        tall = jnp.concatenate([dqt_ref[0], dqt_ref[1]], axis=0) * scale
        all_ref[:, :LANES] = tall.T.astype(bf16)
        tall = dqt_ref[2] * scale
        tall = jnp.concatenate([tall, jnp.zeros_like(tall)], axis=0).T
        lane_all = lax.broadcasted_iota(jnp.int32, (rows_in, LANES), 1)
        old = all_ref[:, LANES : 2 * LANES].astype(f32)
        all_ref[:, LANES : 2 * LANES] = jnp.where(lane_all < HEAD_DIM, tall, old).astype(bf16)
    skip = 0 if last else LANES
    d_weight = [None, None]
    for p in range(4):
        rows = slice(p * piece_rows, (p + 1) * piece_rows)
        own = all_ref[rows, skip:]
        dx = lax.dot_general(own, w_ref[:, skip:], CONTRACT_LAST, preferred_element_type=f32)
        out_ref = keep_ref if p % 2 == 0 else send_ref
        out_ref[p // 2] = dx.astype(bf16)
        piece = lax.dot_general(
            pieces[p][...], own, (((0,), (0,)), ((), ())), preferred_element_type=f32
        )
        d_weight[0] = piece if p == 0 else d_weight[0] + piece
        col = jnp.sum(own.astype(f32), axis=0, keepdims=True)
        d_weight[1] = col if p == 0 else d_weight[1] + col
    grad, col = d_weight
    if last:
        dw_out[:, :LANES] = grad[:, :LANES].astype(bf16)
        dw_out[:, LANES:] = (grad[:, LANES:] + dw_in[...]).astype(bf16)
        col_out[:, :LANES] = jnp.broadcast_to(col[:, :LANES], (8, LANES))
        col_out[:, LANES:] = col[:, LANES:] + col_in[...]
    elif first:
        dw_out[...] = grad
        col_out[...] = jnp.broadcast_to(col, col_out.shape)
    else:
        dw_out[...] = grad + dw_in[...]
        col_out[...] = col + col_in[...]


def attend_back_chunk(first, last, chunk, pieces, shared, carry):
    kx, vx = chunk
    qx2, qp, w, grads, attx = shared
    rows, width = kx.shape[1], w.shape[0]
    operands = [kx, vx, qx2, qp, w, *pieces]
    operands += [*grads, attx] if first else list(carry)
    half = jax.ShapeDtypeStruct((2, rows // 4, width), bf16)
    out_shape = [half, half]
    scratch = [
        pltpu.VMEM((OWN_HEADS, HEAD_DIM, rows), bf16),
        pltpu.VMEM((rows, WIDE), bf16),
    ]
    if first:
        out_shape.append(jax.ShapeDtypeStruct((OWN_HEADS, rows, LANES), bf16))
    if last:
        out_shape.append(jax.ShapeDtypeStruct((width, WIDE), bf16))
        out_shape.append(jax.ShapeDtypeStruct((8, WIDE), f32))
        scratch.append(pltpu.VMEM((OWN_HEADS, HEAD_DIM, rows), f32))
    else:
        out_shape.append(jax.ShapeDtypeStruct((OWN_HEADS, HEAD_DIM, rows), f32))
        out_shape.append(jax.ShapeDtypeStruct((width, WIDE - LANES), f32))
        out_shape.append(jax.ShapeDtypeStruct((8, WIDE - LANES), f32))
    return pl.pallas_call(
        partial(backward_kernel, first, last, min(512, rows), min(512, rows)),
        out_shape=out_shape,
        in_specs=vmem_specs(len(operands)),
        out_specs=vmem_specs(len(out_shape)),
        scratch_shapes=scratch,
        compiler_params=pltpu.CompilerParams(vmem_limit_bytes=VMEM_BYTES),
        cost_estimate=pl.CostEstimate(
            flops=int(1.5e10), transcendentals=OWN_HEADS * rows * rows, bytes_accessed=int(1e7)
        ),
        name="attend_backward",
    )(*operands)


def norm_forward(value, gain, shift):
    center = value - jnp.mean(value, axis=-1, keepdims=True)
    spread = jnp.mean(center * center, axis=-1, keepdims=True)
    inverse = lax.rsqrt(spread + norm_eps)
    normal = center * inverse
    return normal * gain + shift, normal, inverse


def norm_backward(grad, gain, normal, inverse):
    inner = grad * gain
    mean = jnp.mean(inner, axis=-1, keepdims=True)
    along = jnp.mean(inner * normal, axis=-1, keepdims=True)
    return inverse * (inner - mean - normal * along)


CONTRACT_FIRST = (((0,), (0,)), ((), ()))


def ffn_kernel(layout, *refs):
    n_q, n_b, own_rows, fold, aligned = layout
    refs = list(refs)
    where_ref = refs.pop(0)
    att_refs = [refs.pop(0) for _ in range(4)]
    x_ref, cot_ref, vec_ref, eb_ref, packed = [refs.pop(0) for _ in range(5)]
    out_ref, resid_ref = [refs.pop(0) for _ in range(2)]
    da_refs = [refs.pop(0) for _ in range(4)]
    vec_out = refs.pop(0)
    targets = [refs.pop(0) for _ in range(6 if aligned else 1)]
    wo, w1, w2, go, g1, g2, act, slope, in_sem, out_sem = refs
    group, zi, xi, ci, bi, start, length = [where_ref[i] for i in range(7)]
    rows, width = x_ref.shape

    def lanes(i):
        return slice(i * width, (i + 1) * width)

    loads = [pltpu.make_async_copy(packed.at[:, lanes(0)], wo, in_sem.at[0])]
    for k in range(fold):
        loads.append(pltpu.make_async_copy(packed.at[:, lanes(1 + k)], w1.at[k], in_sem.at[1 + k]))
    for k in range(fold):
        sem = in_sem.at[1 + fold + k]
        loads.append(pltpu.make_async_copy(packed.at[:, lanes(1 + fold + k)], w2.at[k], sem))
    for load in loads:
        load.start()

    def group_rows(r):
        other = (2 * (xi ^ (r // 2))) + (ci ^ (r % 2))
        return pl.ds(pl.multiple_of(other * OWN_WIDTH, HEAD_DIM), OWN_WIDTH)

    obias, gain1, shift1, sbias, gain2, shift2 = [vec_ref[i : i + 1, :] for i in range(2, 8)]
    loads[0].wait()
    branch = obias + jnp.zeros((rows, width), f32)
    for r in range(4):
        branch += jnp.dot(att_refs[r][...], wo[group_rows(r), :], preferred_element_type=f32)
    hidden, normal1, inverse1 = norm_forward(x_ref[...].astype(f32) + branch, gain1, shift1)
    hidden_low = hidden.astype(bf16)
    shrunk = sbias + hidden
    for k in range(fold):
        loads[1 + k].wait()
        expanded = jnp.dot(hidden_low, w1[k], preferred_element_type=f32) + eb_ref[k : k + 1, :]
        cdf = 0.5 * (1.0 + lax.erf(expanded * (2.0**-0.5)))
        pdf = jnp.exp(-0.5 * expanded * expanded) * ((2.0 * math.pi) ** -0.5)
        act[k] = (expanded * cdf).astype(bf16)
        slope[k] = cdf + expanded * pdf
        loads[1 + fold + k].wait()
        shrunk += jnp.dot(act[k], w2[k], preferred_element_type=f32)
    result, normal2, inverse2 = norm_forward(shrunk, gain2, shift2)
    out_ref[...] = result.astype(bf16)
    row = lax.broadcasted_iota(jnp.int32, (rows, width), 0)
    seed = jnp.where(start + row < length, cot_ref[...].astype(f32), 0.0)
    vec_out[4:5, :] = jnp.sum(seed * normal2, axis=0, keepdims=True)
    vec_out[5:6, :] = jnp.sum(seed, axis=0, keepdims=True)
    resid2 = norm_backward(seed, gain2, normal2, inverse2)
    shrunk_low = resid2.astype(bf16)
    vec_out[3:4, :] = jnp.sum(shrunk_low.astype(f32), axis=0, keepdims=True)
    hidden_grad = resid2
    for k in range(fold):
        active_grad = lax.dot_general(
            shrunk_low, w2[k], CONTRACT_LAST, preferred_element_type=f32
        )
        expanded_low = (active_grad * slope[k]).astype(bf16)
        vec_out[8 + k : 9 + k, :] = jnp.sum(expanded_low.astype(f32), axis=0, keepdims=True)
        hidden_grad += lax.dot_general(
            expanded_low, w1[k], CONTRACT_LAST, preferred_element_type=f32
        )
        g2[k] = lax.dot_general(
            act[k], shrunk_low, CONTRACT_FIRST, preferred_element_type=f32
        ).astype(bf16)
        g1[k] = lax.dot_general(
            hidden_low, expanded_low, CONTRACT_FIRST, preferred_element_type=f32
        ).astype(bf16)
    vec_out[1:2, :] = jnp.sum(hidden_grad * normal1, axis=0, keepdims=True)
    vec_out[2:3, :] = jnp.sum(hidden_grad, axis=0, keepdims=True)
    resid1 = norm_backward(hidden_grad, gain1, normal1, inverse1)
    resid_ref[...] = resid1
    branch_low = resid1.astype(bf16)
    vec_out[0:1, :] = jnp.sum(branch_low.astype(f32), axis=0, keepdims=True)
    vec_out[6:8, :] = jnp.zeros((2, width), f32)
    vec_out[8 + fold :, :] = jnp.zeros((vec_out.shape[0] - 8 - fold, width), f32)
    for r in range(4):
        da_refs[r][...] = lax.dot_general(
            branch_low, wo[group_rows(r), :], CONTRACT_LAST, preferred_element_type=f32
        ).astype(bf16)
        go[group_rows(r), :] = lax.dot_general(
            att_refs[r][...], branch_low, CONTRACT_FIRST, preferred_element_type=f32
        ).astype(bf16)
    units = [g2.at[k] for k in range(fold)] + [g1.at[k] for k in range(fold)] + [go]
    if aligned:
        block = n_b * own_rows
        for i, part in enumerate(unit_parts(fold)):
            for dc in range(2):
                target, sem = targets[2 * i + dc], out_sem.at[2 * i + dc]
                for dx in range(2):
                    for jz in range(n_q):
                        m = ((zi ^ jz) * 2 + (xi ^ dx)) * 2 + (ci ^ dc)
                        at = pl.ds(pl.multiple_of(m * block, 16), block)
                        for place, unit in enumerate(part):
                            dst = target.at[dx, jz, :, lanes(place)]
                            pltpu.make_async_copy(units[unit].at[at], dst, sem).start()
    else:
        for i, unit in enumerate(units):
            pltpu.make_async_copy(unit, targets[0].at[:, lanes(i)], out_sem.at[0]).start()
    for i, dst in enumerate(targets):
        pltpu.make_async_copy(dst, dst, out_sem.at[i]).wait()


def unit_parts(fold):
    count = 1 + 2 * fold
    edges = [count * i // 3 for i in range(4)]
    return [range(edges[i], edges[i + 1]) for i in range(3)]


def ffn_block(layout, where, att, x, cot, vectors, ebias, packed):
    n_q, n_b, own_rows, fold, aligned = layout
    rows, width = x.shape
    ff = fold * width
    operands = [where, *att, x, cot, vectors, ebias, packed]
    in_specs = [pl.BlockSpec(memory_space=pltpu.SMEM)] + vmem_specs(8)
    in_specs += [pl.BlockSpec(memory_space=pl.ANY)]
    out_shape = [
        jax.ShapeDtypeStruct((rows, width), bf16),
        jax.ShapeDtypeStruct((rows, width), f32),
        *[jax.ShapeDtypeStruct((rows, OWN_WIDTH), bf16)] * 4,
        jax.ShapeDtypeStruct((16, width), f32),
    ]
    if aligned:
        lead = (2, n_q, n_b * own_rows)
        sizes = [len(part) * width for part in unit_parts(fold)]
        targets = [jax.ShapeDtypeStruct((*lead, size), bf16) for size in sizes for _ in range(2)]
    else:
        targets = [jax.ShapeDtypeStruct((width, width + 2 * ff), bf16)]
    weight_scratch = [
        pltpu.VMEM((width, width), bf16),
        pltpu.VMEM((fold, width, width), bf16),
        pltpu.VMEM((fold, width, width), bf16),
    ]
    return pl.pallas_call(
        partial(ffn_kernel, layout),
        out_shape=out_shape + targets,
        in_specs=in_specs,
        out_specs=vmem_specs(len(out_shape)) + [pl.BlockSpec(memory_space=pl.ANY)] * len(targets),
        scratch_shapes=weight_scratch
        + weight_scratch
        + [
            pltpu.VMEM((fold, rows, width), bf16),
            pltpu.VMEM((fold, rows, width), f32),
            pltpu.SemaphoreType.DMA((1 + 2 * fold,)),
            pltpu.SemaphoreType.DMA((6,)),
        ],
        compiler_params=pltpu.CompilerParams(vmem_limit_bytes=VMEM_BYTES),
        cost_estimate=pl.CostEstimate(
            flops=int(2e10), transcendentals=2 * rows * ff, bytes_accessed=int(3e7)
        ),
        name="feed_forward",
    )(*operands)


def order_kernel(n_q, n_b, where_ref, blocks_ref, out_ref):
    group, zi, bi = [where_ref[i] for i in range(3)]
    rows = blocks_ref.shape[3]
    for m in range(4 * n_q):
        q, g = m // 4, m % 4
        far, r = lax.rem(q + n_q - zi, n_q), g ^ group
        both = [
            blocks_ref[lax.rem(b + n_b - bi, n_b), far, r].astype(f32) for b in range(n_b)
        ]
        at = slice(m * n_b * rows, (m + 1) * n_b * rows)
        out_ref[at, :] = jnp.concatenate(both, axis=0).astype(bf16)


def order_rows(n_q, n_b, where, blocks):
    rows, lanes = blocks.shape[3:]
    return pl.pallas_call(
        partial(order_kernel, n_q, n_b),
        out_shape=jax.ShapeDtypeStruct((4 * n_q * n_b * rows, lanes), bf16),
        in_specs=[pl.BlockSpec(memory_space=pltpu.SMEM)] + vmem_specs(1),
        out_specs=vmem_specs(1)[0],
        compiler_params=pltpu.CompilerParams(vmem_limit_bytes=VMEM_BYTES),
        name="order_rows",
    )(where, blocks)


def from_shift(value, axis, count, step):
    return lax.ppermute(value, axis, [((i + step) % count, i) for i in range(count)])


def square_swap(value, r):
    if r == 0:
        return value
    if r == 1:
        return lax.ppermute(value, "c", [(0, 1), (1, 0)])
    if r == 2:
        return lax.ppermute(value, "x", [(0, 1), (1, 0)])
    return lax.ppermute(value, ("x", "c"), [(0, 3), (3, 0), (1, 2), (2, 1)])


def pick(stacked, index, dim=0):
    return lax.dynamic_index_in_dim(stacked, index, dim, keepdims=False)


class Chain:
    def __init__(self, state, *steps):
        self.state, self.steps = tuple(state), list(steps)


def run_stage(chains, outs=()):
    for chain in chains:
        chain.state = tuple(chain.steps.pop(0)(*chain.state))
    outs, states = lax.optimization_barrier((tuple(outs), [c.state for c in chains]))
    for chain, state in zip(chains, states):
        chain.state = tuple(state)
    return outs


def away_sum(total, axis, count):
    parts = [total[j].astype(bf16) for j in range(1, count)]
    return [from_shift(part, axis, count, count - j - 1) for j, part in enumerate(parts)]


def weight_sum(keep, send, n_q, n_b, bi):
    def own_b(keep, got, j):
        shape = (2, n_q, n_b, -1, keep.shape[-1])
        both = [pick(v.reshape(shape), (bi + j) % n_b, 2).astype(f32) for v in (keep, got)]
        return both[0] + both[1]

    def over_core(keep, send):
        return keep, square_swap(send, 1)

    def over_b(keep, got):
        away = [own_b(keep, got, j).astype(bf16) for j in range(1, n_b)]
        return keep, got, *[from_shift(v, "b", n_b, n_b - 1 - j) for j, v in enumerate(away)]

    def over_x(keep, got, *more):
        total = own_b(keep, got, 0) + sum(v.astype(f32) for v in more)
        return total[0], *away_sum(total, "x", 2)

    def halve(half):
        def over_q(own, got):
            total = own + got.astype(f32)
            pairs = [(i, i ^ half) for i in range(n_q)]
            return total[:half], lax.ppermute(total[half:].astype(bf16), "q", pairs)

        return over_q

    halves = [n_q >> (k + 1) for k in range(n_q.bit_length() - 1)]
    return Chain((keep, send), over_core, over_b, over_x, *[halve(half) for half in halves])


def toward(j, n_q):
    return (j - 1, n_q - 1) if 2 * j <= n_q else ((j + 1) % n_q, 1)


def token_sum(keep, send, n_q, j, farther):
    def over_core(keep, send):
        return keep, square_swap(send, 1)

    def over_x(keep, got):
        total = keep.astype(f32) + got.astype(f32)
        return total[0], square_swap(total[1].astype(bf16), 2)

    def over_q(own, got):
        total = own + got.astype(f32) + sum(chain_sum(c) for c in farther)
        return (from_shift(total.astype(bf16), "q", n_q, toward(j, n_q)[1]),)

    return Chain((keep, send), over_core, over_x, *([over_q] if j else []))


def chain_sum(chain):
    return sum(v.astype(f32).reshape(chain.state[0].shape) for v in chain.state)


def deinterleave(fold):
    size = fold * LANES
    lane = jnp.arange(size)
    return (lane[:, None] // fold + (lane[:, None] % fold) * LANES == lane[None, :]).astype(bf16)


def per_device(
    n_q,
    n_b,
    inputs,
    lengths,
    cotangent,
    triple_weight,
    query_bias,
    value_bias,
    output_weight,
    output_bias,
    first_gain,
    first_shift,
    expand_weight,
    expand_bias,
    shrink_weight,
    shrink_bias,
    second_gain,
    second_shift,
):
    zi, xi, ci, bi = [lax.axis_index(a) for a in AXES]
    group = 2 * xi + ci
    _, seq_rows, width = inputs.shape
    own_rows = triple_weight.shape[0]
    ff = expand_weight.shape[1]
    fold = ff // width
    aligned = n_b * own_rows % 16 == 0 and n_q & (n_q - 1) == 0
    x_own = inputs[0]

    turn = deinterleave(fold)
    expand_own = expand_weight.astype(bf16).reshape(own_rows, -1, fold * LANES)
    expand_own = jnp.einsum("rbs,st->rbt", expand_own, turn, preferred_element_type=f32)
    expand_own = expand_own.astype(bf16).reshape(own_rows, -1, fold, LANES).transpose(0, 2, 1, 3)
    packed = jnp.concatenate(
        [
            output_weight.astype(bf16),
            expand_own.reshape(own_rows, ff),
            shrink_weight.astype(bf16).reshape(own_rows, ff),
        ],
        axis=1,
    )
    gathered_ffn = lax.all_gather(packed, AXES, axis=0, tiled=True)

    names = [query_bias, value_bias, output_bias, first_gain, first_shift]
    names += [shrink_bias, second_gain, second_shift]
    vectors = jnp.stack(names, axis=1)
    vectors = jnp.concatenate([vectors, expand_bias.reshape(own_rows, fold)], axis=1).astype(bf16)
    n_vec = vectors.shape[1]
    vectors = jnp.pad(vectors, ((0, 0), (0, WIDE - VECTORS - n_vec)))
    thirds = triple_weight.astype(bf16).reshape(own_rows, 3, GROUPS, OWN_WIDTH)

    def columns_of(g):
        mine = [pick(thirds[:, t], g, 1) for t in range(3)]
        return jnp.concatenate(mine + [vectors], axis=1)

    def rows_square(*blocks):
        return [square_swap(block, r) for r, block in enumerate(blocks)]

    def rows_q(*blocks):
        square = jnp.stack(blocks)
        return [square] + [from_shift(square, "q", n_q, j) for j in range(1, n_q)]

    def rows_b(*blocks):
        both = jnp.stack(blocks)
        return [both] + [from_shift(both, "b", n_b, j) for j in range(1, n_b)]

    weight_rows = Chain([columns_of(group ^ r) for r in range(4)], rows_square, rows_q, rows_b)

    def token_chunk(j):
        def over_q():
            source, step = toward(j, n_q)
            own = chunks[source].state[0] if source else x_own
            return (from_shift(own, "q", n_q, n_q - step),)

        def over_x(own):
            return own, square_swap(own, 2)

        def over_core(own, other):
            halves = square_swap(jnp.stack([own, other]), 1)
            return own, halves[0], other, halves[1]

        return Chain(() if j else (x_own,), *([over_q] if j else []), over_x, over_core)

    arrival = []
    for j in [k for pair in zip(range(1, n_q), range(n_q - 1, 0, -1)) for k in pair]:
        arrival += [] if j in arrival else [j]
    arrival = [0] + arrival
    chunks = {j: token_chunk(j) for j in arrival}
    line = [chunks[j] for j in arrival]

    def moving_at(slot):
        begun = [c for i, c in enumerate(line) if slot >= (i if i > 1 else 0)]
        return [c for c in begun if c.steps]

    for slot in range(3):
        run_stage([weight_rows] + moving_at(slot))
    chunk_x = {}

    by_distance = jnp.stack(weight_rows.state)
    if aligned:
        spot = jnp.stack([group, zi, bi]).astype(jnp.int32)
        w_own = order_rows(n_q, n_b, spot, by_distance)
    else:
        ordered = jnp.stack([pick(by_distance, (i - bi) % n_b) for i in range(n_b)], axis=3)
        ordered = jnp.stack([pick(ordered, group ^ g, 1) for g in range(4)], axis=1)
        ordered = jnp.stack([pick(ordered, (i - zi) % n_q) for i in range(n_q)])
        w_own = ordered.transpose(0, 1, 3, 2, 4).reshape(width, WIDE)
    turned = w_own[:, VECTORS : VECTORS + n_vec].astype(f32)
    turned = turned.T
    ebias = turned[8:]
    turned = turned[:8]
    own_bias = lax.dynamic_slice_in_dim(turned, group * OWN_WIDTH, OWN_WIDTH, 1)
    zero = jnp.zeros((1, OWN_WIDTH), f32)
    bias_row = jnp.concatenate(
        [own_bias[:1], zero, own_bias[1:2], jnp.zeros((1, WIDE - VECTORS), f32)], axis=1
    )

    def where_of(j):
        zj = (zi + j) % n_q
        spots = [(zj * 4 + (group ^ r)) * seq_rows for r in range(4)]
        return jnp.stack(spots + [lengths[0]]).astype(jnp.int32)

    weights = (w_own, bias_row)
    kept = {}
    carry = None
    for step, j in enumerate(arrival):
        first, last = step == 0, step == n_q - 1
        assert not chunks[j].steps
        chunk_x[j] = chunks[j].state
        outs = attend_chunk(first, last, where_of(j), chunk_x[j], weights, carry)
        outs = run_stage(moving_at(3 + step), outs)
        kept[j] = (outs[0], outs[1])
        outs = outs[2:]
        if first:
            qx, qp = outs[:2]
            outs = outs[2:]
        carry = (qx, *outs)
    att, attx, qx2 = carry[1:5], carry[5], carry[6]

    att = [square_swap(att[r], r) for r in range(4)]
    start = (zi * 4 + group) * seq_rows
    where = jnp.stack([group, zi, xi, ci, bi, start, lengths[0]]).astype(jnp.int32)
    layout = (n_q, n_b, own_rows, fold, aligned)
    outs = ffn_block(layout, where, att, x_own, cotangent[0], turned, ebias, gathered_ffn)
    output, resid_first_grad = outs[:2]
    att_grads, vec_grads, summands = outs[2:6], outs[6], outs[7:]
    square = Chain(att_grads, lambda *parts: [square_swap(v, r) for r, v in enumerate(parts)])

    sums = []
    if aligned:
        for i in range(3):
            sums.append(weight_sum(summands[2 * i], summands[2 * i + 1], n_q, n_b, bi))
    else:
        summed = lax.psum_scatter(summands[0], AXES, scatter_dimension=0, tiled=True).astype(f32)
    run_stage([square] + sums[:1])
    shared = (qx2, qp, w_own, square.state, attx)
    carry = None
    moving, moving_to = [], {}
    for step, j in enumerate(reversed(arrival)):
        first, last = step == 0, step == n_q - 1
        outs = attend_back_chunk(first, last, kept[j], chunk_x[j], shared, carry)
        begun = [c for c in sums[: step + 2] if c.steps]
        outs = run_stage(begun + [c for c in moving if c.steps], outs)
        keep, send = outs[:2]
        farther = [c for k, c in moving_to.items() if k and toward(k, n_q)[0] == j and j]
        moving_to[j] = token_sum(keep, send, n_q, j, farther)
        moving.append(moving_to[j])
        outs = outs[2:]
        if first:
            dox = outs[0]
            outs = outs[1:]
        carry = (dox, *outs)
        if not last:
            carry = run_stage(moving[-1:], carry)
    grad_joint, col = carry[1:]

    own_bias = jnp.stack([col[0, :OWN_WIDTH], col[0, 2 * OWN_WIDTH : 3 * OWN_WIDTH]])
    bias_grads = lax.dynamic_update_slice(
        jnp.zeros((2, width), f32), own_bias, (0, group * OWN_WIDTH)
    )
    tall = jnp.concatenate([bias_grads, vec_grads[:6], vec_grads[8 : 8 + fold]], axis=0).T
    tall_high = tall.astype(bf16)
    tall_low = (tall - tall_high.astype(f32)).astype(bf16)
    room = jnp.zeros((width, WIDE - VECTORS - 2 * n_vec), bf16)
    blocks = jnp.concatenate([grad_joint[:, :VECTORS], tall_high, tall_low, room], axis=1)
    total = blocks.reshape(n_q, 4, n_b, own_rows, WIDE)

    def rows_over_b(total):
        parts = [pick(total, (bi + j) % n_b, 2) for j in range(n_b)]
        return parts[0], *away_sum(parts, "b", n_b)

    def rows_over_q(*parts):
        total = sum(v.astype(f32) for v in parts)
        parts = [pick(total, (zi + j) % n_q) for j in range(n_q)]
        return parts[0], *away_sum(parts, "q", n_q)

    def rows_over_square(*parts):
        total = sum(v.astype(f32) for v in parts).astype(bf16)
        return [square_swap(pick(total, group ^ r), r) for r in range(4)]

    rows = Chain((total,), rows_over_b, rows_over_q, rows_over_square)
    while any(c.steps for c in [rows, *sums, *moving]):
        run_stage([c for c in [rows, *sums, *moving] if c.steps])
    token_grad = resid_first_grad
    for j, chain in moving_to.items():
        if j == 0 or toward(j, n_q)[0] == 0:
            token_grad = token_grad + chain_sum(chain)
    input_grad = token_grad.astype(bf16)
    if aligned:
        summed = jnp.concatenate([chain_sum(c)[0] for c in sums], axis=1)
    parts = jnp.stack(rows.state)
    parts = jnp.stack([pick(parts, group ^ g) for g in range(4)])
    grad_triple = parts[:, :, :VECTORS].reshape(GROUPS, own_rows, 3, OWN_WIDTH)
    grad_triple = grad_triple.transpose(1, 2, 0, 3).reshape(own_rows, -1).astype(f32)
    small = jnp.sum(parts[:, :, VECTORS : VECTORS + 2 * n_vec].astype(f32), axis=0)
    small = small[:, :n_vec] + small[:, n_vec:]
    grad_expand = summed[:, ff : 2 * ff].reshape(own_rows, fold, -1, LANES).transpose(0, 2, 1, 3)
    grad_expand = jnp.einsum(
        "rbs,ts->rbt",
        grad_expand.reshape(own_rows, -1, fold * LANES),
        turn.astype(f32),
        precision=lax.Precision.HIGHEST,
        preferred_element_type=f32,
    ).reshape(own_rows, ff)
    return (
        output[None],
        input_grad[None],
        grad_triple,
        small[:, 0],
        small[:, 1],
        summed[:, 2 * ff :],
        small[:, 2],
        small[:, 3],
        small[:, 4],
        grad_expand,
        small[:, 8:].reshape(-1),
        summed[:, :ff].reshape(-1, width),
        small[:, 5],
        small[:, 6],
        small[:, 7],
    )


def solution(mesh):
    n_seq, n_b = mesh.shape["seq"], mesh.shape["batch"]
    n_q = n_seq // GROUPS
    fine = Mesh(mesh.devices.reshape(n_q, 2, 2, n_b), AXES)
    tokens = P("b", ("q", "x", "c"), None)
    matrix = P(AXES, None)
    vector = P(AXES)
    in_specs = (
        tokens,
        P("b"),
        tokens,
        matrix,
        vector,
        vector,
        matrix,
        vector,
        vector,
        vector,
        matrix,
        vector,
        matrix,
        vector,
        vector,
        vector,
    )
    out_specs = (
        tokens,
        tokens,
        matrix,
        vector,
        vector,
        matrix,
        vector,
        vector,
        vector,
        matrix,
        vector,
        matrix,
        vector,
        vector,
        vector,
    )
    return jax.shard_map(
        partial(per_device, n_q, n_b),
        mesh=fine,
        in_specs=in_specs,
        out_specs=out_specs,
        check_vma=False,
    )
```

```python
from functools import partial
import math

import jax
import jax.numpy as jnp
from jax import lax
from jax.experimental import pallas as pl
from jax.experimental.pallas import tpu as pltpu
from jax.sharding import Mesh, PartitionSpec as P

HEADS = 12
HEAD_DIM = 64
GROUPS = 4
OWN_HEADS = HEADS // GROUPS
OWN_WIDTH = OWN_HEADS * HEAD_DIM
LANES = 128
WIDE = 640
VECTORS = 3 * OWN_WIDTH

bf16 = jnp.bfloat16
f32 = jnp.float32
masked_score = -1e30
norm_eps = 1e-12
log2_e = 1.4426950408889634
CONTRACT_LAST = (((1,), (1,)), ((), ()))
MIB = 1024 * 1024
AXES = ("q", "x", "c", "b")


def split_three(value):
    high = value.astype(bf16).astype(f32)
    rest = value - high
    mid = rest.astype(bf16).astype(f32)
    low = (rest - mid).astype(bf16).astype(f32)
    return high, mid, low


def low_half(tile, lane, from_high):
    turned = pltpu.roll(tile, HEAD_DIM, 1)
    low = lane < HEAD_DIM
    return jnp.where(low, turned, tile) if from_high else jnp.where(low, tile, turned)


def place_of(kind, h):
    slot = kind * OWN_HEADS + h
    return slot // 2, slot % 2


def forward_kernel(first, last, block_q, block_k, *refs):
    refs = list(refs)
    where_ref = refs.pop(0)
    pieces = [refs.pop(0) for _ in range(4)]
    w_ref, bias_ref = [refs.pop(0) for _ in range(2)]
    if not first:
        qx_ref, peak_in, sum_in = [refs.pop(0) for _ in range(3)]
    kx_ref, vx_ref = [refs.pop(0) for _ in range(2)]
    if first:
        qx_ref, qp_ref = [refs.pop(0) for _ in range(2)]
    if last:
        att_refs = [refs.pop(0) for _ in range(4)]
        attx_ref, qx2_ref = [refs.pop(0) for _ in range(2)]
    else:
        peak_out, sum_out = [refs.pop(0) for _ in range(2)]
    (vt_ref,) = refs
    piece_rows = pieces[0].shape[0]
    rows_in = 4 * piece_rows
    lane = lax.broadcasted_iota(jnp.int32, (piece_rows, LANES), 1)
    row = lax.broadcasted_iota(jnp.int32, (piece_rows, LANES), 0)
    low = lane < HEAD_DIM
    length = where_ref[4]
    three = (lane >= HEAD_DIM) & (lane < HEAD_DIM + 3)
    skip = 0 if first else LANES
    for p in range(4):
        rows = slice(p * piece_rows, (p + 1) * piece_rows)
        joint = jnp.dot(pieces[p][...], w_ref[:, skip:], preferred_element_type=f32)
        joint = joint + bias_ref[:, skip:]
        bias = jnp.where(where_ref[p] + row < length, 0.0, masked_score)
        key_extra = jnp.where(three, 1.0, jnp.where(lane == HEAD_DIM + 3, bias, 0.0))

        def head_of(kind, h):
            tile, high = place_of(kind, h)
            return low_half(joint[:, tile * LANES - skip : (tile + 1) * LANES - skip], lane, high)

        for h in range(OWN_HEADS):
            k = head_of(1, h)
            kx_ref[h, rows, :LANES] = k.astype(bf16)
            kx_ref[h, rows, LANES:] = jnp.where(low, k, key_extra).astype(bf16)
            v = jnp.where(low, head_of(2, h), 0.0)
            vx_ref[h, rows, :] = jnp.where(three, -1.0, v).astype(bf16)
            vt = jnp.where(lane == HEAD_DIM, 1.0, v).T
            vt_ref[h, :, rows] = vt[:80].astype(bf16)
            if first:
                q = head_of(0, h).astype(bf16).astype(f32)
                qp_ref[h, rows, :] = jnp.where(low, q, 0.0).astype(bf16)
                high, mid, rest = split_three(q * (HEAD_DIM**-0.5 * log2_e))
                qx_ref[h, rows, :LANES] = jnp.where(low, high, mid).astype(bf16)
                one = jnp.where(lane == HEAD_DIM + 3, 1.0, 0.0)
                qx_ref[h, rows, LANES:] = jnp.where(low, rest, one).astype(bf16)
    for h in range(OWN_HEADS):
        for i in range(rows_in // block_q):
            cols = slice(i * block_q, (i + 1) * block_q)
            q = qx_ref[h, cols, :]
            if first:
                peak = jnp.full((1, block_q), masked_score, f32)
                total = jnp.zeros((80, block_q), f32)
            else:
                peak = peak_in[h, :1, cols]
                total = sum_in[h, :, cols]
            for j in range(rows_in // block_k):
                ks = slice(j * block_k, (j + 1) * block_k)
                s = lax.dot_general(kx_ref[h, ks, :], q, CONTRACT_LAST, preferred_element_type=f32)
                new_peak = jnp.maximum(peak, jnp.max(s, axis=0, keepdims=True))
                prob = jnp.exp2(s - new_peak).astype(bf16)
                total = total * jnp.exp2(peak - new_peak) + jnp.dot(
                    vt_ref[h, :, ks], prob, preferred_element_type=f32
                )
                peak = new_peak
            if last:
                denom = total[HEAD_DIM : HEAD_DIM + 1]
                n_high, n_mid, n_low = split_three(-(peak + jnp.log2(denom)))
                tall = jnp.concatenate(
                    [
                        total[:HEAD_DIM] / denom,
                        n_high,
                        n_mid,
                        n_low,
                        jnp.zeros((HEAD_DIM - 3, block_q), f32),
                    ],
                    axis=0,
                )
                attx_ref[h, cols, :] = tall.T
            else:
                peak_out[h, :, cols] = jnp.broadcast_to(peak, (8, block_q))
                sum_out[h, :, cols] = total
    if last:
        for p in range(4):
            rows = slice(p * piece_rows, (p + 1) * piece_rows)
            heads = [attx_ref[h, rows, :] for h in range(OWN_HEADS)]
            pair = jnp.where(low, heads[0], pltpu.roll(heads[1], HEAD_DIM, 1))
            att_refs[p][:, :LANES] = pair.astype(bf16)
            att_refs[p][:, LANES:] = heads[2][:, :HEAD_DIM].astype(bf16)
            for h in range(OWN_HEADS):
                qx2_ref[h, rows, :LANES] = qx_ref[h, rows, :LANES]
                old = qx_ref[h, rows, LANES:].astype(f32)
                qx2_ref[h, rows, LANES:] = jnp.where(three, heads[h], old).astype(bf16)


def vmem_specs(n):
    return [pl.BlockSpec(memory_space=pltpu.VMEM) for _ in range(n)]


def attend_chunk(first, last, where, pieces, weights, carry):
    piece_rows = pieces[0].shape[0]
    rows = 4 * piece_rows
    operands = [where, *pieces, *weights]
    operands += [] if first else list(carry)
    wide_keys = jax.ShapeDtypeStruct((OWN_HEADS, rows, 2 * LANES), bf16)
    out_shape = [wide_keys, jax.ShapeDtypeStruct((OWN_HEADS, rows, LANES), bf16)]
    if first:
        out_shape += [wide_keys, jax.ShapeDtypeStruct((OWN_HEADS, rows, LANES), bf16)]
    if last:
        out_shape += [jax.ShapeDtypeStruct((piece_rows, OWN_WIDTH), bf16)] * 4
        out_shape += [jax.ShapeDtypeStruct((OWN_HEADS, rows, LANES), f32), wide_keys]
    else:
        out_shape += [
            jax.ShapeDtypeStruct((OWN_HEADS, 8, rows), f32),
            jax.ShapeDtypeStruct((OWN_HEADS, 80, rows), f32),
        ]
    return pl.pallas_call(
        partial(forward_kernel, first, last, min(1024, rows), min(1024, rows)),
        out_shape=out_shape,
        in_specs=[pl.BlockSpec(memory_space=pltpu.SMEM)] + vmem_specs(len(operands) - 1),
        out_specs=vmem_specs(len(out_shape)),
        scratch_shapes=[pltpu.VMEM((OWN_HEADS, 80, rows), bf16)],
        compiler_params=pltpu.CompilerParams(vmem_limit_bytes=24 * MIB),
        cost_estimate=pl.CostEstimate(
            flops=int(8e9), transcendentals=OWN_HEADS * rows * rows, bytes_accessed=int(1e7)
        ),
        name="attend_forward",
    )(*operands)


def backward_kernel(first, last, block_q, block_k, *refs):
    refs = list(refs)
    kx_ref, vx_ref, qx_ref, qp_ref, w_ref = [refs.pop(0) for _ in range(5)]
    pieces = [refs.pop(0) for _ in range(4)]
    if first:
        grads = [refs.pop(0) for _ in range(4)]
        attx_ref = refs.pop(0)
    else:
        dox_ref, dqt_in, dw_in, col_in = [refs.pop(0) for _ in range(4)]
    keep_ref, send_ref = [refs.pop(0) for _ in range(2)]
    if first:
        dox_ref = refs.pop(0)
    if last:
        dw_out, col_out = [refs.pop(0) for _ in range(2)]
        dqt_ref = refs.pop()
    else:
        dqt_ref, dw_out, col_out = [refs.pop(0) for _ in range(3)]
    kt_ref, all_ref = refs
    rows_in = kx_ref.shape[1]
    piece_rows = rows_in // 4
    scale = HEAD_DIM**-0.5
    lane = lax.broadcasted_iota(jnp.int32, (piece_rows, LANES), 1)
    if first:
        for p in range(4):
            rows = slice(p * piece_rows, (p + 1) * piece_rows)
            left = grads[p][:, :LANES].astype(f32)
            right = grads[p][:, LANES:].astype(f32)
            right = jnp.concatenate([right, jnp.zeros_like(right)], axis=1)
            for h, wide in enumerate((left, pltpu.roll(left, HEAD_DIM, 1), right)):
                grad = jnp.where(lane < HEAD_DIM, wide, 0.0)
                delta = jnp.sum(grad * attx_ref[h, rows, :], axis=1, keepdims=True)
                d_high, d_mid, d_low = split_three(delta)
                grad = jnp.where(lane == HEAD_DIM, d_high, grad)
                grad = jnp.where(lane == HEAD_DIM + 1, d_mid, grad)
                grad = jnp.where(lane == HEAD_DIM + 2, d_low, grad)
                dox_ref[h, rows, :] = grad.astype(bf16)
        dqt_ref[...] = jnp.zeros_like(dqt_ref)
    else:
        dqt_ref[...] = dqt_in[...]
    for h in range(OWN_HEADS):
        kt_ref[h] = kx_ref[h, :, LANES:].astype(f32).T[:HEAD_DIM].astype(bf16)
    lane_k = lax.broadcasted_iota(jnp.int32, (block_k, LANES), 1)
    low_k = lane_k < HEAD_DIM
    for j in range(rows_in // block_k):
        ks = slice(j * block_k, (j + 1) * block_k)
        parts = {}
        for h in range(OWN_HEADS):
            k = kx_ref[h, ks, :]
            v = vx_ref[h, ks, :]
            kt = kt_ref[h, :, ks]
            dk = jnp.zeros((block_k, LANES), f32)
            dv = jnp.zeros((block_k, LANES), f32)
            for i in range(rows_in // block_q):
                qs = slice(i * block_q, (i + 1) * block_q)
                s = lax.dot_general(k, qx_ref[h, qs, :], CONTRACT_LAST, preferred_element_type=f32)
                prob = jnp.exp2(s)
                do = dox_ref[h, qs, :]
                dp = lax.dot_general(v, do, CONTRACT_LAST, preferred_element_type=f32)
                ds = (prob * dp).astype(bf16)
                dv = dv + jnp.dot(prob.astype(bf16), do, preferred_element_type=f32)
                dk = dk + jnp.dot(ds, qp_ref[h, qs, :], preferred_element_type=f32)
                dqt_ref[h, :, qs] += jnp.dot(kt, ds, preferred_element_type=f32)
            parts[OWN_HEADS + h] = dk * scale
            parts[2 * OWN_HEADS + h] = dv
        for tile in range(1, WIDE // LANES):
            left, right = parts.get(2 * tile), parts.get(2 * tile + 1)
            left = jnp.zeros((block_k, LANES), f32) if left is None else left
            right = 0.0 if right is None else pltpu.roll(right, HEAD_DIM, 1)
            both = jnp.where(low_k, left, right).astype(bf16)
            all_ref[ks, tile * LANES : (tile + 1) * LANES] = both
    if last:
        tall = jnp.concatenate([dqt_ref[0], dqt_ref[1]], axis=0) * scale
        all_ref[:, :LANES] = tall.T.astype(bf16)
        tall = dqt_ref[2] * scale
        tall = jnp.concatenate([tall, jnp.zeros_like(tall)], axis=0).T
        lane_all = lax.broadcasted_iota(jnp.int32, (rows_in, LANES), 1)
        old = all_ref[:, LANES : 2 * LANES].astype(f32)
        all_ref[:, LANES : 2 * LANES] = jnp.where(lane_all < HEAD_DIM, tall, old).astype(bf16)
    skip = 0 if last else LANES
    d_weight = [None, None]
    for p in range(4):
        rows = slice(p * piece_rows, (p + 1) * piece_rows)
        own = all_ref[rows, skip:]
        dx = lax.dot_general(own, w_ref[:, skip:], CONTRACT_LAST, preferred_element_type=f32)
        out_ref = keep_ref if p % 2 == 0 else send_ref
        out_ref[p // 2] = dx.astype(bf16)
        piece = lax.dot_general(
            pieces[p][...], own, (((0,), (0,)), ((), ())), preferred_element_type=f32
        )
        d_weight[0] = piece if p == 0 else d_weight[0] + piece
        col = jnp.sum(own.astype(f32), axis=0, keepdims=True)
        d_weight[1] = col if p == 0 else d_weight[1] + col
    grad, col = d_weight
    if last:
        dw_out[:, :LANES] = grad[:, :LANES].astype(bf16)
        dw_out[:, LANES:] = (grad[:, LANES:] + dw_in[...]).astype(bf16)
        col_out[:, :LANES] = jnp.broadcast_to(col[:, :LANES], (8, LANES))
        col_out[:, LANES:] = col[:, LANES:] + col_in[...]
    elif first:
        dw_out[...] = grad
        col_out[...] = jnp.broadcast_to(col, col_out.shape)
    else:
        dw_out[...] = grad + dw_in[...]
        col_out[...] = col + col_in[...]


def attend_back_chunk(first, last, chunk, pieces, shared, carry):
    kx, vx = chunk
    qx2, qp, w, grads, attx = shared
    rows, width = kx.shape[1], w.shape[0]
    operands = [kx, vx, qx2, qp, w, *pieces]
    operands += [*grads, attx] if first else list(carry)
    half = jax.ShapeDtypeStruct((2, rows // 4, width), bf16)
    out_shape = [half, half]
    scratch = [
        pltpu.VMEM((OWN_HEADS, HEAD_DIM, rows), bf16),
        pltpu.VMEM((rows, WIDE), bf16),
    ]
    if first:
        out_shape.append(jax.ShapeDtypeStruct((OWN_HEADS, rows, LANES), bf16))
    if last:
        out_shape.append(jax.ShapeDtypeStruct((width, WIDE), bf16))
        out_shape.append(jax.ShapeDtypeStruct((8, WIDE), f32))
        scratch.append(pltpu.VMEM((OWN_HEADS, HEAD_DIM, rows), f32))
    else:
        out_shape.append(jax.ShapeDtypeStruct((OWN_HEADS, HEAD_DIM, rows), f32))
        out_shape.append(jax.ShapeDtypeStruct((width, WIDE - LANES), f32))
        out_shape.append(jax.ShapeDtypeStruct((8, WIDE - LANES), f32))
    return pl.pallas_call(
        partial(backward_kernel, first, last, min(256, rows), min(1024, rows)),
        out_shape=out_shape,
        in_specs=vmem_specs(len(operands)),
        out_specs=vmem_specs(len(out_shape)),
        scratch_shapes=scratch,
        compiler_params=pltpu.CompilerParams(vmem_limit_bytes=26 * MIB),
        cost_estimate=pl.CostEstimate(
            flops=int(1.5e10), transcendentals=OWN_HEADS * rows * rows, bytes_accessed=int(1e7)
        ),
        name="attend_backward",
    )(*operands)


def norm_forward(value, gain, shift):
    center = value - jnp.mean(value, axis=-1, keepdims=True)
    spread = jnp.mean(center * center, axis=-1, keepdims=True)
    inverse = lax.rsqrt(spread + norm_eps)
    normal = center * inverse
    return normal * gain + shift, normal, inverse


def norm_backward(grad, gain, normal, inverse):
    inner = grad * gain
    mean = jnp.mean(inner, axis=-1, keepdims=True)
    along = jnp.mean(inner * normal, axis=-1, keepdims=True)
    return inverse * (inner - mean - normal * along)


CONTRACT_FIRST = (((0,), (0,)), ((), ()))


def ffn_kernel(layout, *refs):
    n_q, n_b, own_rows, fold, aligned = layout
    refs = list(refs)
    where_ref = refs.pop(0)
    att_refs = [refs.pop(0) for _ in range(4)]
    x_ref, cot_ref, vec_ref, eb_ref, packed = [refs.pop(0) for _ in range(5)]
    out_ref, resid_ref = [refs.pop(0) for _ in range(2)]
    da_refs = [refs.pop(0) for _ in range(4)]
    vec_out = refs.pop(0)
    targets = [refs.pop(0) for _ in range(6 if aligned else 1)]
    wo, w1, w2, go, g1, g2, act, slope, in_sem, out_sem = refs
    group, zi, xi, ci, bi, start, length = [where_ref[i] for i in range(7)]
    rows, width = x_ref.shape

    def lanes(i):
        return slice(i * width, (i + 1) * width)

    loads = [pltpu.make_async_copy(packed.at[:, lanes(0)], wo, in_sem.at[0])]
    for k in range(fold):
        loads.append(pltpu.make_async_copy(packed.at[:, lanes(1 + k)], w1.at[k], in_sem.at[1 + k]))
    for k in range(fold):
        sem = in_sem.at[1 + fold + k]
        loads.append(pltpu.make_async_copy(packed.at[:, lanes(1 + fold + k)], w2.at[k], sem))
    for load in loads:
        load.start()

    def group_rows(r):
        other = (2 * (xi ^ (r // 2))) + (ci ^ (r % 2))
        return pl.ds(pl.multiple_of(other * OWN_WIDTH, HEAD_DIM), OWN_WIDTH)

    obias, gain1, shift1, sbias, gain2, shift2 = [vec_ref[i : i + 1, :] for i in range(2, 8)]
    loads[0].wait()
    branch = obias + jnp.zeros((rows, width), f32)
    for r in range(4):
        branch += jnp.dot(att_refs[r][...], wo[group_rows(r), :], preferred_element_type=f32)
    hidden, normal1, inverse1 = norm_forward(x_ref[...].astype(f32) + branch, gain1, shift1)
    hidden_low = hidden.astype(bf16)
    shrunk = sbias + hidden
    for k in range(fold):
        loads[1 + k].wait()
        expanded = jnp.dot(hidden_low, w1[k], preferred_element_type=f32) + eb_ref[k : k + 1, :]
        cdf = 0.5 * (1.0 + lax.erf(expanded * (2.0**-0.5)))
        pdf = jnp.exp(-0.5 * expanded * expanded) * ((2.0 * math.pi) ** -0.5)
        act[k] = (expanded * cdf).astype(bf16)
        slope[k] = cdf + expanded * pdf
        loads[1 + fold + k].wait()
        shrunk += jnp.dot(act[k], w2[k], preferred_element_type=f32)
    result, normal2, inverse2 = norm_forward(shrunk, gain2, shift2)
    out_ref[...] = result.astype(bf16)
    row = lax.broadcasted_iota(jnp.int32, (rows, width), 0)
    seed = jnp.where(start + row < length, cot_ref[...].astype(f32), 0.0)
    vec_out[4:5, :] = jnp.sum(seed * normal2, axis=0, keepdims=True)
    vec_out[5:6, :] = jnp.sum(seed, axis=0, keepdims=True)
    resid2 = norm_backward(seed, gain2, normal2, inverse2)
    shrunk_low = resid2.astype(bf16)
    vec_out[3:4, :] = jnp.sum(shrunk_low.astype(f32), axis=0, keepdims=True)
    hidden_grad = resid2
    for k in range(fold):
        active_grad = lax.dot_general(
            shrunk_low, w2[k], CONTRACT_LAST, preferred_element_type=f32
        )
        expanded_low = (active_grad * slope[k]).astype(bf16)
        vec_out[8 + k : 9 + k, :] = jnp.sum(expanded_low.astype(f32), axis=0, keepdims=True)
        hidden_grad += lax.dot_general(
            expanded_low, w1[k], CONTRACT_LAST, preferred_element_type=f32
        )
        g2[k] = lax.dot_general(
            act[k], shrunk_low, CONTRACT_FIRST, preferred_element_type=f32
        ).astype(bf16)
        g1[k] = lax.dot_general(
            hidden_low, expanded_low, CONTRACT_FIRST, preferred_element_type=f32
        ).astype(bf16)
    vec_out[1:2, :] = jnp.sum(hidden_grad * normal1, axis=0, keepdims=True)
    vec_out[2:3, :] = jnp.sum(hidden_grad, axis=0, keepdims=True)
    resid1 = norm_backward(hidden_grad, gain1, normal1, inverse1)
    resid_ref[...] = resid1
    branch_low = resid1.astype(bf16)
    vec_out[0:1, :] = jnp.sum(branch_low.astype(f32), axis=0, keepdims=True)
    vec_out[6:8, :] = jnp.zeros((2, width), f32)
    vec_out[8 + fold :, :] = jnp.zeros((vec_out.shape[0] - 8 - fold, width), f32)
    for r in range(4):
        da_refs[r][...] = lax.dot_general(
            branch_low, wo[group_rows(r), :], CONTRACT_LAST, preferred_element_type=f32
        ).astype(bf16)
        go[group_rows(r), :] = lax.dot_general(
            att_refs[r][...], branch_low, CONTRACT_FIRST, preferred_element_type=f32
        ).astype(bf16)
    units = [g2.at[k] for k in range(fold)] + [g1.at[k] for k in range(fold)] + [go]
    if aligned:
        block = n_b * own_rows
        for i, part in enumerate(unit_parts(fold)):
            for dc in range(2):
                target, sem = targets[2 * i + dc], out_sem.at[2 * i + dc]
                for dx in range(2):
                    for jz in range(n_q):
                        m = ((zi ^ jz) * 2 + (xi ^ dx)) * 2 + (ci ^ dc)
                        at = pl.ds(pl.multiple_of(m * block, 16), block)
                        for place, unit in enumerate(part):
                            dst = target.at[dx, jz, :, lanes(place)]
                            pltpu.make_async_copy(units[unit].at[at], dst, sem).start()
    else:
        for i, unit in enumerate(units):
            pltpu.make_async_copy(unit, targets[0].at[:, lanes(i)], out_sem.at[0]).start()
    for i, dst in enumerate(targets):
        pltpu.make_async_copy(dst, dst, out_sem.at[i]).wait()


def unit_parts(fold):
    count = 1 + 2 * fold
    edges = [count * i // 3 for i in range(4)]
    return [range(edges[i], edges[i + 1]) for i in range(3)]


def ffn_block(layout, where, att, x, cot, vectors, ebias, packed):
    n_q, n_b, own_rows, fold, aligned = layout
    rows, width = x.shape
    ff = fold * width
    operands = [where, *att, x, cot, vectors, ebias, packed]
    in_specs = [pl.BlockSpec(memory_space=pltpu.SMEM)] + vmem_specs(8)
    in_specs += [pl.BlockSpec(memory_space=pl.ANY)]
    out_shape = [
        jax.ShapeDtypeStruct((rows, width), bf16),
        jax.ShapeDtypeStruct((rows, width), f32),
        *[jax.ShapeDtypeStruct((rows, OWN_WIDTH), bf16)] * 4,
        jax.ShapeDtypeStruct((16, width), f32),
    ]
    if aligned:
        lead = (2, n_q, n_b * own_rows)
        sizes = [len(part) * width for part in unit_parts(fold)]
        targets = [jax.ShapeDtypeStruct((*lead, size), bf16) for size in sizes for _ in range(2)]
    else:
        targets = [jax.ShapeDtypeStruct((width, width + 2 * ff), bf16)]
    weight_scratch = [
        pltpu.VMEM((width, width), bf16),
        pltpu.VMEM((fold, width, width), bf16),
        pltpu.VMEM((fold, width, width), bf16),
    ]
    return pl.pallas_call(
        partial(ffn_kernel, layout),
        out_shape=out_shape + targets,
        in_specs=in_specs,
        out_specs=vmem_specs(len(out_shape)) + [pl.BlockSpec(memory_space=pl.ANY)] * len(targets),
        scratch_shapes=weight_scratch
        + weight_scratch
        + [
            pltpu.VMEM((fold, rows, width), bf16),
            pltpu.VMEM((fold, rows, width), f32),
            pltpu.SemaphoreType.DMA((1 + 2 * fold,)),
            pltpu.SemaphoreType.DMA((6,)),
        ],
        compiler_params=pltpu.CompilerParams(vmem_limit_bytes=34 * MIB),
        cost_estimate=pl.CostEstimate(
            flops=int(2e10), transcendentals=2 * rows * ff, bytes_accessed=int(3e7)
        ),
        name="feed_forward",
    )(*operands)


def order_kernel(n_q, n_b, where_ref, blocks_ref, out_ref):
    group, zi, bi = [where_ref[i] for i in range(3)]
    rows = blocks_ref.shape[3]
    for m in range(4 * n_q):
        q, g = m // 4, m % 4
        far, r = lax.rem(q + n_q - zi, n_q), g ^ group
        both = [
            blocks_ref[lax.rem(b + n_b - bi, n_b), far, r].astype(f32) for b in range(n_b)
        ]
        at = slice(m * n_b * rows, (m + 1) * n_b * rows)
        out_ref[at, :] = jnp.concatenate(both, axis=0).astype(bf16)


def order_rows(n_q, n_b, where, blocks):
    rows, lanes = blocks.shape[3:]
    return pl.pallas_call(
        partial(order_kernel, n_q, n_b),
        out_shape=jax.ShapeDtypeStruct((4 * n_q * n_b * rows, lanes), bf16),
        in_specs=[pl.BlockSpec(memory_space=pltpu.SMEM)] + vmem_specs(1),
        out_specs=vmem_specs(1)[0],
        compiler_params=pltpu.CompilerParams(vmem_limit_bytes=12 * MIB),
        name="order_rows",
    )(where, blocks)


def from_shift(value, axis, count, step):
    return lax.ppermute(value, axis, [((i + step) % count, i) for i in range(count)])


def square_swap(value, r):
    if r == 0:
        return value
    if r == 1:
        return lax.ppermute(value, "c", [(0, 1), (1, 0)])
    if r == 2:
        return lax.ppermute(value, "x", [(0, 1), (1, 0)])
    return lax.ppermute(value, ("x", "c"), [(0, 3), (3, 0), (1, 2), (2, 1)])


def pick(stacked, index, dim=0):
    return lax.dynamic_index_in_dim(stacked, index, dim, keepdims=False)


class Chain:
    def __init__(self, state, *steps):
        self.state, self.steps = tuple(state), list(steps)


def launch(chain):
    chain.state = tuple(chain.steps.pop(0)(*chain.state))


def run_stage(chains, outs=(), settle=()):
    for chain in chains:
        launch(chain)
    joined = [*chains, *settle]
    outs, states = lax.optimization_barrier((tuple(outs), [c.state for c in joined]))
    for chain, state in zip(joined, states):
        chain.state = tuple(state)
    return outs


def away_sum(total, axis, count):
    parts = [total[j].astype(bf16) for j in range(1, count)]
    return [from_shift(part, axis, count, count - j - 1) for j, part in enumerate(parts)]


def weight_sum(keep, send, n_q, n_b, bi):
    def own_b(keep, got, j):
        shape = (2, n_q, n_b, -1, keep.shape[-1])
        both = [pick(v.reshape(shape), (bi + j) % n_b, 2).astype(f32) for v in (keep, got)]
        return both[0] + both[1]

    def over_core(keep, send):
        return keep, square_swap(send, 1)

    def over_b(keep, got):
        away = [own_b(keep, got, j).astype(bf16) for j in range(1, n_b)]
        return keep, got, *[from_shift(v, "b", n_b, n_b - 1 - j) for j, v in enumerate(away)]

    def over_x(keep, got, *more):
        total = own_b(keep, got, 0) + sum(v.astype(f32) for v in more)
        return total[0], *away_sum(total, "x", 2)

    def halve(half):
        def over_q(own, got):
            total = own + got.astype(f32)
            pairs = [(i, i ^ half) for i in range(n_q)]
            return total[:half], lax.ppermute(total[half:].astype(bf16), "q", pairs)

        return over_q

    halves = [n_q >> (k + 1) for k in range(n_q.bit_length() - 1)]
    return Chain((keep, send), over_core, over_b, over_x, *[halve(half) for half in halves])


def toward(j, n_q):
    return (j - 1, n_q - 1) if 2 * j <= n_q else ((j + 1) % n_q, 1)


def token_sum(keep, send, n_q, j, farther):
    def over_core(keep, send):
        return keep, square_swap(send, 1)

    def over_x(keep, got):
        total = keep.astype(f32) + got.astype(f32)
        return total[0], square_swap(total[1].astype(bf16), 2)

    def over_q(own, got):
        total = own + got.astype(f32) + sum(chain_sum(c) for c in farther)
        return (from_shift(total.astype(bf16), "q", n_q, toward(j, n_q)[1]),)

    return Chain((keep, send), over_core, over_x, *([over_q] if j else []))


def chain_sum(chain):
    return sum(v.astype(f32).reshape(chain.state[0].shape) for v in chain.state)


def deinterleave(fold):
    size = fold * LANES
    lane = jnp.arange(size)
    return (lane[:, None] // fold + (lane[:, None] % fold) * LANES == lane[None, :]).astype(bf16)


def per_device(
    n_q,
    n_b,
    inputs,
    lengths,
    cotangent,
    triple_weight,
    query_bias,
    value_bias,
    output_weight,
    output_bias,
    first_gain,
    first_shift,
    expand_weight,
    expand_bias,
    shrink_weight,
    shrink_bias,
    second_gain,
    second_shift,
):
    zi, xi, ci, bi = [lax.axis_index(a) for a in AXES]
    group = 2 * xi + ci
    _, seq_rows, width = inputs.shape
    own_rows = triple_weight.shape[0]
    ff = expand_weight.shape[1]
    fold = ff // width
    aligned = n_b * own_rows % 16 == 0 and n_q & (n_q - 1) == 0
    x_own = inputs[0]

    turn = deinterleave(fold)
    expand_own = expand_weight.astype(bf16).reshape(own_rows, -1, fold * LANES)
    expand_own = jnp.einsum("rbs,st->rbt", expand_own, turn, preferred_element_type=f32)
    expand_own = expand_own.astype(bf16).reshape(own_rows, -1, fold, LANES).transpose(0, 2, 1, 3)
    packed = jnp.concatenate(
        [
            output_weight.astype(bf16),
            expand_own.reshape(own_rows, ff),
            shrink_weight.astype(bf16).reshape(own_rows, ff),
        ],
        axis=1,
    )
    gathered_ffn = lax.all_gather(packed, AXES, axis=0, tiled=True)

    names = [query_bias, value_bias, output_bias, first_gain, first_shift]
    names += [shrink_bias, second_gain, second_shift]
    vectors = jnp.stack(names, axis=1)
    vectors = jnp.concatenate([vectors, expand_bias.reshape(own_rows, fold)], axis=1).astype(bf16)
    n_vec = vectors.shape[1]
    vectors = jnp.pad(vectors, ((0, 0), (0, WIDE - VECTORS - n_vec)))
    thirds = triple_weight.astype(bf16).reshape(own_rows, 3, GROUPS, OWN_WIDTH)

    def columns_of(g):
        mine = [pick(thirds[:, t], g, 1) for t in range(3)]
        return jnp.concatenate(mine + [vectors], axis=1)

    def rows_square(*blocks):
        return [square_swap(block, r) for r, block in enumerate(blocks)]

    def rows_q(*blocks):
        square = jnp.stack(blocks)
        return [square] + [from_shift(square, "q", n_q, j) for j in range(1, n_q)]

    def rows_b(*blocks):
        both = jnp.stack(blocks)
        return [both] + [from_shift(both, "b", n_b, j) for j in range(1, n_b)]

    weight_rows = Chain([columns_of(group ^ r) for r in range(4)], rows_square, rows_q, rows_b)

    def token_chunk(j):
        def over_q():
            source, step = toward(j, n_q)
            own = chunks[source].state[0] if source else x_own
            if j not in (0, 1):
                own = lax.optimization_barrier((own, weight_rows.state))[0]
            return (from_shift(own, "q", n_q, n_q - step),)

        def over_x(own):
            return own, square_swap(own, 2)

        def over_core(own, other):
            halves = square_swap(jnp.stack([own, other]), 1)
            return own, halves[0], other, halves[1]

        return Chain(() if j else (x_own,), *([over_q] if j else []), over_x, over_core)

    arrival = []
    for j in [k for pair in zip(range(1, n_q), range(n_q - 1, 0, -1)) for k in pair]:
        arrival += [] if j in arrival else [j]
    arrival = [0] + arrival
    chunks = {j: token_chunk(j) for j in arrival}
    line = [chunks[j] for j in arrival]

    for slot in range(3):
        run_stage([weight_rows] + [c for c in line[:2] if c.steps and (slot < 2 or c is line[1])])
    chunk_x = {}

    by_distance = jnp.stack(weight_rows.state)
    if aligned:
        spot = jnp.stack([group, zi, bi]).astype(jnp.int32)
        w_own = order_rows(n_q, n_b, spot, by_distance)
    else:
        ordered = jnp.stack([pick(by_distance, (i - bi) % n_b) for i in range(n_b)], axis=3)
        ordered = jnp.stack([pick(ordered, group ^ g, 1) for g in range(4)], axis=1)
        ordered = jnp.stack([pick(ordered, (i - zi) % n_q) for i in range(n_q)])
        w_own = ordered.transpose(0, 1, 3, 2, 4).reshape(width, WIDE)
    turned = w_own[:, VECTORS : VECTORS + n_vec].astype(f32)
    turned = turned.T
    ebias = turned[8:]
    turned = turned[:8]
    own_bias = lax.dynamic_slice_in_dim(turned, group * OWN_WIDTH, OWN_WIDTH, 1)
    zero = jnp.zeros((1, OWN_WIDTH), f32)
    bias_row = jnp.concatenate(
        [own_bias[:1], zero, own_bias[1:2], jnp.zeros((1, WIDE - VECTORS), f32)], axis=1
    )

    def where_of(j):
        zj = (zi + j) % n_q
        spots = [(zj * 4 + (group ^ r)) * seq_rows for r in range(4)]
        return jnp.stack(spots + [lengths[0]]).astype(jnp.int32)

    weights = (w_own, bias_row)
    kept = {}
    carry = None
    for step, j in enumerate(arrival):
        first, last = step == 0, step == n_q - 1
        if chunks[j].steps:
            run_stage([chunks[j]])
        assert not chunks[j].steps
        chunk_x[j] = chunks[j].state
        outs = attend_chunk(first, last, where_of(j), chunk_x[j], weights, carry)
        outs = run_stage([c for i in (step + 1, step + 2) if i > 1 for c in line[i : i + 1]], outs)
        kept[j] = (outs[0], outs[1])
        outs = outs[2:]
        if first:
            qx, qp = outs[:2]
            outs = outs[2:]
        carry = (qx, *outs)
    att, attx, qx2 = carry[1:5], carry[5], carry[6]

    att = [square_swap(att[r], r) for r in range(4)]
    start = (zi * 4 + group) * seq_rows
    where = jnp.stack([group, zi, xi, ci, bi, start, lengths[0]]).astype(jnp.int32)
    layout = (n_q, n_b, own_rows, fold, aligned)
    outs = ffn_block(layout, where, att, x_own, cotangent[0], turned, ebias, gathered_ffn)
    output, resid_first_grad = outs[:2]
    att_grads, vec_grads, summands = outs[2:6], outs[6], outs[7:]
    square = Chain(att_grads, lambda *parts: [square_swap(v, r) for r, v in enumerate(parts)])

    sums = []
    if aligned:
        for i in range(3):
            sums.append(weight_sum(summands[2 * i], summands[2 * i + 1], n_q, n_b, bi))
    else:
        summed = lax.psum_scatter(summands[0], AXES, scatter_dimension=0, tiled=True).astype(f32)
    run_stage([square] + sums[:2])
    for chain in sums[2:]:
        launch(chain)
    plan = [
        ([0], [2], [1], []),
        ([0], [1], [2], [2]),
        ([1, 0], [], [2], [2]),
        ([1, 2, 0], [], [], []),
    ]
    shared = (qx2, qp, w_own, square.state, attx)
    carry = None
    moving, moving_to = [], {}
    for step, j in enumerate(reversed(arrival)):
        first, last = step == 0, step == n_q - 1
        with_it, ending, going_on, after_it = [], [], [], []
        if sums and step < len(plan):
            with_it, ending, going_on, after_it = [[sums[i] for i in part] for part in plan[step]]
        outs = attend_back_chunk(first, last, kept[j], chunk_x[j], shared, carry)
        for chain in going_on:
            launch(chain)
        outs = run_stage(with_it + [c for c in moving if c.steps], outs, settle=ending)
        keep, send = outs[:2]
        farther = [c for k, c in moving_to.items() if k and toward(k, n_q)[0] == j and j]
        moving_to[j] = token_sum(keep, send, n_q, j, farther)
        moving.append(moving_to[j])
        outs = outs[2:]
        if first:
            dox = outs[0]
            outs = outs[1:]
        carry = (dox, *outs)
        if not last:
            carry = run_stage(moving[-1:], carry, settle=after_it)
    grad_joint, col = carry[1:]

    own_bias = jnp.stack([col[0, :OWN_WIDTH], col[0, 2 * OWN_WIDTH : 3 * OWN_WIDTH]])
    bias_grads = lax.dynamic_update_slice(
        jnp.zeros((2, width), f32), own_bias, (0, group * OWN_WIDTH)
    )
    tall = jnp.concatenate([bias_grads, vec_grads[:6], vec_grads[8 : 8 + fold]], axis=0).T
    tall_high = tall.astype(bf16)
    tall_low = (tall - tall_high.astype(f32)).astype(bf16)
    room = jnp.zeros((width, WIDE - VECTORS - 2 * n_vec), bf16)
    blocks = jnp.concatenate([grad_joint[:, :VECTORS], tall_high, tall_low, room], axis=1)
    total = blocks.reshape(n_q, 4, n_b, own_rows, WIDE)

    def rows_over_b(total):
        parts = [pick(total, (bi + j) % n_b, 2) for j in range(n_b)]
        return parts[0], *away_sum(parts, "b", n_b)

    def rows_over_q(*parts):
        total = sum(v.astype(f32) for v in parts)
        parts = [pick(total, (zi + j) % n_q) for j in range(n_q)]
        return parts[0], *away_sum(parts, "q", n_q)

    def rows_over_square(*parts):
        total = sum(v.astype(f32) for v in parts).astype(bf16)
        return [square_swap(pick(total, group ^ r), r) for r in range(4)]

    rows = Chain((total,), rows_over_b, rows_over_q, rows_over_square)
    run_stage([], settle=[rows, *sums, *moving])
    while any(c.steps for c in [rows, *sums, *moving]):
        run_stage([c for c in [rows, *sums, *moving] if c.steps])
    token_grad = resid_first_grad
    for j, chain in moving_to.items():
        if j == 0 or toward(j, n_q)[0] == 0:
            token_grad = token_grad + chain_sum(chain)
    input_grad = token_grad.astype(bf16)
    if aligned:
        summed = jnp.concatenate([chain_sum(c)[0] for c in sums], axis=1)
    parts = jnp.stack(rows.state)
    parts = jnp.stack([pick(parts, group ^ g) for g in range(4)])
    grad_triple = parts[:, :, :VECTORS].reshape(GROUPS, own_rows, 3, OWN_WIDTH)
    grad_triple = grad_triple.transpose(1, 2, 0, 3).reshape(own_rows, -1).astype(f32)
    small = jnp.sum(parts[:, :, VECTORS : VECTORS + 2 * n_vec].astype(f32), axis=0)
    small = small[:, :n_vec] + small[:, n_vec:]
    grad_expand = summed[:, ff : 2 * ff].reshape(own_rows, fold, -1, LANES).transpose(0, 2, 1, 3)
    grad_expand = jnp.einsum(
        "rbs,ts->rbt",
        grad_expand.reshape(own_rows, -1, fold * LANES),
        turn.astype(f32),
        precision=lax.Precision.HIGHEST,
        preferred_element_type=f32,
    ).reshape(own_rows, ff)
    return (
        output[None],
        input_grad[None],
        grad_triple,
        small[:, 0],
        small[:, 1],
        summed[:, 2 * ff :],
        small[:, 2],
        small[:, 3],
        small[:, 4],
        grad_expand,
        small[:, 8:].reshape(-1),
        summed[:, :ff].reshape(-1, width),
        small[:, 5],
        small[:, 6],
        small[:, 7],
    )


def solution(mesh):
    n_seq, n_b = mesh.shape["seq"], mesh.shape["batch"]
    n_q = n_seq // GROUPS
    fine = Mesh(mesh.devices.reshape(n_q, 2, 2, n_b), AXES)
    tokens = P("b", ("q", "x", "c"), None)
    matrix = P(AXES, None)
    vector = P(AXES)
    in_specs = (
        tokens,
        P("b"),
        tokens,
        matrix,
        vector,
        vector,
        matrix,
        vector,
        vector,
        vector,
        matrix,
        vector,
        matrix,
        vector,
        vector,
        vector,
    )
    out_specs = (
        tokens,
        tokens,
        matrix,
        vector,
        vector,
        matrix,
        vector,
        vector,
        vector,
        matrix,
        vector,
        matrix,
        vector,
        vector,
        vector,
    )
    return jax.shard_map(
        partial(per_device, n_q, n_b),
        mesh=fine,
        in_specs=in_specs,
        out_specs=out_specs,
        check_vma=False,
    )
```

```python
from functools import partial
import math

import jax
import jax.numpy as jnp
from jax import lax
from jax.experimental import pallas as pl
from jax.experimental.pallas import tpu as pltpu
from jax.sharding import Mesh, PartitionSpec as P

HEADS = 12
HEAD_DIM = 64
GROUPS = 4
OWN_HEADS = HEADS // GROUPS
OWN_WIDTH = OWN_HEADS * HEAD_DIM
LANES = 128
WIDE = 640
VECTORS = 3 * OWN_WIDTH

bf16 = jnp.bfloat16
f32 = jnp.float32
masked_score = -1e30
norm_eps = 1e-12
log2_e = 1.4426950408889634
CONTRACT_LAST = (((1,), (1,)), ((), ()))
MIB = 1024 * 1024
AXES = ("q", "x", "c", "b")


def split_three(value):
    high = value.astype(bf16).astype(f32)
    rest = value - high
    mid = rest.astype(bf16).astype(f32)
    low = (rest - mid).astype(bf16).astype(f32)
    return high, mid, low


def low_half(tile, lane, from_high):
    turned = pltpu.roll(tile, HEAD_DIM, 1)
    low = lane < HEAD_DIM
    return jnp.where(low, turned, tile) if from_high else jnp.where(low, tile, turned)


def place_of(kind, h):
    slot = kind * OWN_HEADS + h
    return slot // 2, slot % 2


def forward_kernel(first, last, block_q, block_k, *refs):
    refs = list(refs)
    where_ref = refs.pop(0)
    far = [refs.pop(0) for _ in range(5)]
    bias_ref = refs.pop(0)
    if not first:
        qx_ref, peak_in, sum_in = [refs.pop(0) for _ in range(3)]
    kept = [refs.pop(0) for _ in range(2)]
    if first:
        qx_ref, qp_ref = [refs.pop(0) for _ in range(2)]
    if last:
        att_refs = [refs.pop(0) for _ in range(4)]
        attx_ref, qx2_ref = [refs.pop(0) for _ in range(2)]
    else:
        peak_out, sum_out = [refs.pop(0) for _ in range(2)]
    vt_ref, kx_ref, vx_ref, sem, *near = refs
    loads = [pltpu.make_async_copy(f, n, sem.at[2 + i]) for i, (f, n) in enumerate(zip(far, near))]
    for i in (4, 0, 1, 2, 3):
        loads[i].start()
    *pieces, w_ref = near
    stores = [
        pltpu.make_async_copy(kx_ref, kept[0], sem.at[0]),
        pltpu.make_async_copy(vx_ref, kept[1], sem.at[1]),
    ]
    piece_rows = pieces[0].shape[0]
    rows_in = 4 * piece_rows
    lane = lax.broadcasted_iota(jnp.int32, (piece_rows, LANES), 1)
    row = lax.broadcasted_iota(jnp.int32, (piece_rows, LANES), 0)
    low = lane < HEAD_DIM
    length = where_ref[4]
    three = (lane >= HEAD_DIM) & (lane < HEAD_DIM + 3)
    skip = 0 if first else LANES
    for p in range(4):
        rows = slice(p * piece_rows, (p + 1) * piece_rows)
        if p == 0:
            loads[4].wait()
        loads[p].wait()
        joint = jnp.dot(pieces[p][...], w_ref[:, skip:], preferred_element_type=f32)
        joint = joint + bias_ref[:, skip:]
        bias = jnp.where(where_ref[p] + row < length, 0.0, masked_score)
        key_extra = jnp.where(three, 1.0, jnp.where(lane == HEAD_DIM + 3, bias, 0.0))

        def head_of(kind, h):
            tile, high = place_of(kind, h)
            return low_half(joint[:, tile * LANES - skip : (tile + 1) * LANES - skip], lane, high)

        for h in range(OWN_HEADS):
            k = head_of(1, h)
            kx_ref[h, rows, :LANES] = k.astype(bf16)
            kx_ref[h, rows, LANES:] = jnp.where(low, k, key_extra).astype(bf16)
            v = jnp.where(low, head_of(2, h), 0.0)
            vx_ref[h, rows, :] = jnp.where(three, -1.0, v).astype(bf16)
            vt = jnp.where(lane == HEAD_DIM, 1.0, v).T
            vt_ref[h, :, rows] = vt[:80].astype(bf16)
            if first:
                q = head_of(0, h).astype(bf16).astype(f32)
                qp_ref[h, rows, :] = jnp.where(low, q, 0.0).astype(bf16)
                high, mid, rest = split_three(q * (HEAD_DIM**-0.5 * log2_e))
                qx_ref[h, rows, :LANES] = jnp.where(low, high, mid).astype(bf16)
                one = jnp.where(lane == HEAD_DIM + 3, 1.0, 0.0)
                qx_ref[h, rows, LANES:] = jnp.where(low, rest, one).astype(bf16)
    for store in stores:
        store.start()
    for h in range(OWN_HEADS):
        for i in range(rows_in // block_q):
            cols = slice(i * block_q, (i + 1) * block_q)
            q = qx_ref[h, cols, :]
            if first:
                peak = jnp.full((1, block_q), masked_score, f32)
                total = jnp.zeros((80, block_q), f32)
            else:
                peak = peak_in[h, :1, cols]
                total = sum_in[h, :, cols]
            for j in range(rows_in // block_k):
                ks = slice(j * block_k, (j + 1) * block_k)
                s = lax.dot_general(kx_ref[h, ks, :], q, CONTRACT_LAST, preferred_element_type=f32)
                new_peak = jnp.maximum(peak, jnp.max(s, axis=0, keepdims=True))
                prob = jnp.exp2(s - new_peak).astype(bf16)
                total = total * jnp.exp2(peak - new_peak) + jnp.dot(
                    vt_ref[h, :, ks], prob, preferred_element_type=f32
                )
                peak = new_peak
            if last:
                denom = total[HEAD_DIM : HEAD_DIM + 1]
                n_high, n_mid, n_low = split_three(-(peak + jnp.log2(denom)))
                tall = jnp.concatenate(
                    [
                        total[:HEAD_DIM] / denom,
                        n_high,
                        n_mid,
                        n_low,
                        jnp.zeros((HEAD_DIM - 3, block_q), f32),
                    ],
                    axis=0,
                )
                attx_ref[h, cols, :] = tall.T
            else:
                peak_out[h, :, cols] = jnp.broadcast_to(peak, (8, block_q))
                sum_out[h, :, cols] = total
    if last:
        for p in range(4):
            rows = slice(p * piece_rows, (p + 1) * piece_rows)
            heads = [attx_ref[h, rows, :] for h in range(OWN_HEADS)]
            pair = jnp.where(low, heads[0], pltpu.roll(heads[1], HEAD_DIM, 1))
            att_refs[p][:, :LANES] = pair.astype(bf16)
            att_refs[p][:, LANES:] = heads[2][:, :HEAD_DIM].astype(bf16)
            for h in range(OWN_HEADS):
                qx2_ref[h, rows, :LANES] = qx_ref[h, rows, :LANES]
                old = qx_ref[h, rows, LANES:].astype(f32)
                qx2_ref[h, rows, LANES:] = jnp.where(three, heads[h], old).astype(bf16)
    for store in stores:
        store.wait()


def in_hbm(value):
    return pltpu.with_memory_space_constraint(value, pltpu.HBM)


def vmem_specs(n):
    return [pl.BlockSpec(memory_space=pltpu.VMEM) for _ in range(n)]


def attend_chunk(first, last, where, pieces, weights, carry):
    piece_rows = pieces[0].shape[0]
    rows = 4 * piece_rows
    w, bias_row = weights
    far = [in_hbm(v) for v in (*pieces, w)]
    operands = [where, *far, bias_row]
    operands += [] if first else list(carry)
    wide_keys = jax.ShapeDtypeStruct((OWN_HEADS, rows, 2 * LANES), bf16)
    out_shape = [pltpu.HBM(wide_keys.shape, bf16), pltpu.HBM((OWN_HEADS, rows, LANES), bf16)]
    if first:
        out_shape += [wide_keys, jax.ShapeDtypeStruct((OWN_HEADS, rows, LANES), bf16)]
    if last:
        out_shape += [jax.ShapeDtypeStruct((piece_rows, OWN_WIDTH), bf16)] * 4
        out_shape += [jax.ShapeDtypeStruct((OWN_HEADS, rows, LANES), f32), wide_keys]
    else:
        out_shape += [
            jax.ShapeDtypeStruct((OWN_HEADS, 8, rows), f32),
            jax.ShapeDtypeStruct((OWN_HEADS, 80, rows), f32),
        ]
    return pl.pallas_call(
        partial(forward_kernel, first, last, min(1024, rows), min(1024, rows)),
        out_shape=out_shape,
        in_specs=[pl.BlockSpec(memory_space=pltpu.SMEM)]
        + [pl.BlockSpec(memory_space=pltpu.HBM)] * len(far)
        + vmem_specs(len(operands) - 1 - len(far)),
        out_specs=[pl.BlockSpec(memory_space=pltpu.HBM)] * 2 + vmem_specs(len(out_shape) - 2),
        scratch_shapes=[
            pltpu.VMEM((OWN_HEADS, 80, rows), bf16),
            pltpu.VMEM((OWN_HEADS, rows, 2 * LANES), bf16),
            pltpu.VMEM((OWN_HEADS, rows, LANES), bf16),
            pltpu.SemaphoreType.DMA((7,)),
            *[pltpu.VMEM(v.shape, v.dtype) for v in (*pieces, w)],
        ],
        compiler_params=pltpu.CompilerParams(vmem_limit_bytes=20 * MIB),
        cost_estimate=pl.CostEstimate(
            flops=int(8e9), transcendentals=OWN_HEADS * rows * rows, bytes_accessed=int(1e7)
        ),
        name="attend_forward",
    )(*operands)


def backward_kernel(first, last, block_q, block_k, *refs):
    refs = list(refs)
    far = [refs.pop(0) for _ in range(7)]
    qx_ref, qp_ref = [refs.pop(0) for _ in range(2)]
    if first:
        grads = [refs.pop(0) for _ in range(4)]
        attx_ref = refs.pop(0)
    else:
        dox_ref, dqt_in, dw_in, col_in = [refs.pop(0) for _ in range(4)]
    keep_ref, send_ref = [refs.pop(0) for _ in range(2)]
    if first:
        dox_ref = refs.pop(0)
    if last:
        dw_out, col_out = [refs.pop(0) for _ in range(2)]
        dqt_ref = refs.pop()
    else:
        dqt_ref, dw_out, col_out = [refs.pop(0) for _ in range(3)]
    kt_ref, all_ref, sem = refs[:3]
    near = refs[3:]
    kx_ref, vx_ref, w_ref, *pieces = near
    loads = []
    for f, n in zip(far[:2], near[:2]):
        loads += [(f.at[h], n.at[h]) for h in range(OWN_HEADS)]
    loads += list(zip(far[2:], near[2:]))
    loads = [pltpu.make_async_copy(f, n, sem.at[i]) for i, (f, n) in enumerate(loads)]
    for i in (0, OWN_HEADS, *range(1, OWN_HEADS), *range(OWN_HEADS + 1, len(loads))):
        loads[i].start()
    rows_in = kx_ref.shape[1]
    piece_rows = rows_in // 4
    scale = HEAD_DIM**-0.5
    lane = lax.broadcasted_iota(jnp.int32, (piece_rows, LANES), 1)
    if first:
        for p in range(4):
            rows = slice(p * piece_rows, (p + 1) * piece_rows)
            left = grads[p][:, :LANES].astype(f32)
            right = grads[p][:, LANES:].astype(f32)
            right = jnp.concatenate([right, jnp.zeros_like(right)], axis=1)
            for h, wide in enumerate((left, pltpu.roll(left, HEAD_DIM, 1), right)):
                grad = jnp.where(lane < HEAD_DIM, wide, 0.0)
                delta = jnp.sum(grad * attx_ref[h, rows, :], axis=1, keepdims=True)
                d_high, d_mid, d_low = split_three(delta)
                grad = jnp.where(lane == HEAD_DIM, d_high, grad)
                grad = jnp.where(lane == HEAD_DIM + 1, d_mid, grad)
                grad = jnp.where(lane == HEAD_DIM + 2, d_low, grad)
                dox_ref[h, rows, :] = grad.astype(bf16)
        dqt_ref[...] = jnp.zeros_like(dqt_ref)
    else:
        dqt_ref[...] = dqt_in[...]
    lane_k = lax.broadcasted_iota(jnp.int32, (block_k, LANES), 1)
    low_k = lane_k < HEAD_DIM
    for j in range(rows_in // block_k):
        ks = slice(j * block_k, (j + 1) * block_k)
        parts = {}
        for h in range(OWN_HEADS):
            if j == 0:
                loads[h].wait()
                loads[OWN_HEADS + h].wait()
                kt_ref[h] = kx_ref[h, :, LANES:].astype(f32).T[:HEAD_DIM].astype(bf16)
            k = kx_ref[h, ks, :]
            v = vx_ref[h, ks, :]
            kt = kt_ref[h, :, ks]
            dk = jnp.zeros((block_k, LANES), f32)
            dv = jnp.zeros((block_k, LANES), f32)
            for i in range(rows_in // block_q):
                qs = slice(i * block_q, (i + 1) * block_q)
                s = lax.dot_general(k, qx_ref[h, qs, :], CONTRACT_LAST, preferred_element_type=f32)
                prob = jnp.exp2(s)
                do = dox_ref[h, qs, :]
                dp = lax.dot_general(v, do, CONTRACT_LAST, preferred_element_type=f32)
                ds = (prob * dp).astype(bf16)
                dv = dv + jnp.dot(prob.astype(bf16), do, preferred_element_type=f32)
                dk = dk + jnp.dot(ds, qp_ref[h, qs, :], preferred_element_type=f32)
                dqt_ref[h, :, qs] += jnp.dot(kt, ds, preferred_element_type=f32)
            parts[OWN_HEADS + h] = dk * scale
            parts[2 * OWN_HEADS + h] = dv
        for tile in range(1, WIDE // LANES):
            left, right = parts.get(2 * tile), parts.get(2 * tile + 1)
            left = jnp.zeros((block_k, LANES), f32) if left is None else left
            right = 0.0 if right is None else pltpu.roll(right, HEAD_DIM, 1)
            both = jnp.where(low_k, left, right).astype(bf16)
            all_ref[ks, tile * LANES : (tile + 1) * LANES] = both
    if last:
        tall = jnp.concatenate([dqt_ref[0], dqt_ref[1]], axis=0) * scale
        all_ref[:, :LANES] = tall.T.astype(bf16)
        tall = dqt_ref[2] * scale
        tall = jnp.concatenate([tall, jnp.zeros_like(tall)], axis=0).T
        lane_all = lax.broadcasted_iota(jnp.int32, (rows_in, LANES), 1)
        old = all_ref[:, LANES : 2 * LANES].astype(f32)
        all_ref[:, LANES : 2 * LANES] = jnp.where(lane_all < HEAD_DIM, tall, old).astype(bf16)
    skip = 0 if last else LANES
    for load in loads[2 * OWN_HEADS :]:
        load.wait()
    d_weight = [None, None]
    for p in range(4):
        rows = slice(p * piece_rows, (p + 1) * piece_rows)
        own = all_ref[rows, skip:]
        dx = lax.dot_general(own, w_ref[:, skip:], CONTRACT_LAST, preferred_element_type=f32)
        out_ref = keep_ref if p % 2 == 0 else send_ref
        out_ref[p // 2] = dx.astype(bf16)
        piece = lax.dot_general(
            pieces[p][...], own, (((0,), (0,)), ((), ())), preferred_element_type=f32
        )
        d_weight[0] = piece if p == 0 else d_weight[0] + piece
        col = jnp.sum(own.astype(f32), axis=0, keepdims=True)
        d_weight[1] = col if p == 0 else d_weight[1] + col
    grad, col = d_weight
    if last:
        dw_out[:, :LANES] = grad[:, :LANES].astype(bf16)
        dw_out[:, LANES:] = (grad[:, LANES:] + dw_in[...]).astype(bf16)
        col_out[:, :LANES] = jnp.broadcast_to(col[:, :LANES], (8, LANES))
        col_out[:, LANES:] = col[:, LANES:] + col_in[...]
    elif first:
        dw_out[...] = grad
        col_out[...] = jnp.broadcast_to(col, col_out.shape)
    else:
        dw_out[...] = grad + dw_in[...]
        col_out[...] = col + col_in[...]


def attend_back_chunk(first, last, chunk, pieces, shared, carry):
    kx, vx = chunk
    qx2, qp, w, grads, attx = shared
    rows, width = kx.shape[1], w.shape[0]
    far = [in_hbm(v) for v in (kx, vx, w, *pieces)]
    operands = [*far, qx2, qp]
    operands += [*grads, attx] if first else list(carry)
    half = jax.ShapeDtypeStruct((2, rows // 4, width), bf16)
    out_shape = [half, half]
    scratch = [
        pltpu.VMEM((OWN_HEADS, HEAD_DIM, rows), bf16),
        pltpu.VMEM((rows, WIDE), bf16),
        pltpu.SemaphoreType.DMA((2 * OWN_HEADS + 5,)),
        *[pltpu.VMEM(v.shape, v.dtype) for v in far],
    ]
    if first:
        out_shape.append(jax.ShapeDtypeStruct((OWN_HEADS, rows, LANES), bf16))
    if last:
        out_shape.append(jax.ShapeDtypeStruct((width, WIDE), bf16))
        out_shape.append(jax.ShapeDtypeStruct((8, WIDE), f32))
        scratch.append(pltpu.VMEM((OWN_HEADS, HEAD_DIM, rows), f32))
    else:
        out_shape.append(jax.ShapeDtypeStruct((OWN_HEADS, HEAD_DIM, rows), f32))
        out_shape.append(jax.ShapeDtypeStruct((width, WIDE - LANES), f32))
        out_shape.append(jax.ShapeDtypeStruct((8, WIDE - LANES), f32))
    return pl.pallas_call(
        partial(backward_kernel, first, last, min(256, rows), min(1024, rows)),
        out_shape=out_shape,
        in_specs=[pl.BlockSpec(memory_space=pltpu.HBM)] * len(far)
        + vmem_specs(len(operands) - len(far)),
        out_specs=vmem_specs(len(out_shape)),
        scratch_shapes=scratch,
        compiler_params=pltpu.CompilerParams(vmem_limit_bytes=26 * MIB),
        cost_estimate=pl.CostEstimate(
            flops=int(1.5e10), transcendentals=OWN_HEADS * rows * rows, bytes_accessed=int(1e7)
        ),
        name="attend_backward",
    )(*operands)


def norm_forward(value, gain, shift):
    center = value - jnp.mean(value, axis=-1, keepdims=True)
    spread = jnp.mean(center * center, axis=-1, keepdims=True)
    inverse = lax.rsqrt(spread + norm_eps)
    normal = center * inverse
    return normal * gain + shift, normal, inverse


def norm_backward(grad, gain, normal, inverse):
    inner = grad * gain
    mean = jnp.mean(inner, axis=-1, keepdims=True)
    along = jnp.mean(inner * normal, axis=-1, keepdims=True)
    return inverse * (inner - mean - normal * along)


CONTRACT_FIRST = (((0,), (0,)), ((), ()))


def ffn_kernel(layout, *refs):
    n_q, n_b, own_rows, fold, aligned = layout
    refs = list(refs)
    where_ref = refs.pop(0)
    att_refs = [refs.pop(0) for _ in range(4)]
    x_ref, cot_ref, vec_ref, eb_ref, packed = [refs.pop(0) for _ in range(5)]
    out_ref, resid_ref = [refs.pop(0) for _ in range(2)]
    da_refs = [refs.pop(0) for _ in range(4)]
    vec_out = refs.pop(0)
    targets = [refs.pop(0) for _ in range(6 if aligned else 1)]
    wo, w1, w2, go, g1, g2, act, slope, in_sem, out_sem = refs
    group, zi, xi, ci, bi, start, length = [where_ref[i] for i in range(7)]
    rows, width = x_ref.shape

    def lanes(i):
        return slice(i * width, (i + 1) * width)

    loads = [pltpu.make_async_copy(packed.at[:, lanes(0)], wo, in_sem.at[0])]
    for k in range(fold):
        loads.append(pltpu.make_async_copy(packed.at[:, lanes(1 + k)], w1.at[k], in_sem.at[1 + k]))
    for k in range(fold):
        sem = in_sem.at[1 + fold + k]
        loads.append(pltpu.make_async_copy(packed.at[:, lanes(1 + fold + k)], w2.at[k], sem))
    for load in loads:
        load.start()

    def group_rows(r):
        other = (2 * (xi ^ (r // 2))) + (ci ^ (r % 2))
        return pl.ds(pl.multiple_of(other * OWN_WIDTH, HEAD_DIM), OWN_WIDTH)

    obias, gain1, shift1, sbias, gain2, shift2 = [vec_ref[i : i + 1, :] for i in range(2, 8)]
    loads[0].wait()
    branch = obias + jnp.zeros((rows, width), f32)
    for r in range(4):
        branch += jnp.dot(att_refs[r][...], wo[group_rows(r), :], preferred_element_type=f32)
    hidden, normal1, inverse1 = norm_forward(x_ref[...].astype(f32) + branch, gain1, shift1)
    hidden_low = hidden.astype(bf16)
    shrunk = sbias + hidden
    for k in range(fold):
        loads[1 + k].wait()
        expanded = jnp.dot(hidden_low, w1[k], preferred_element_type=f32) + eb_ref[k : k + 1, :]
        cdf = 0.5 * (1.0 + lax.erf(expanded * (2.0**-0.5)))
        pdf = jnp.exp(-0.5 * expanded * expanded) * ((2.0 * math.pi) ** -0.5)
        act[k] = (expanded * cdf).astype(bf16)
        slope[k] = cdf + expanded * pdf
        loads[1 + fold + k].wait()
        shrunk += jnp.dot(act[k], w2[k], preferred_element_type=f32)
    result, normal2, inverse2 = norm_forward(shrunk, gain2, shift2)
    out_ref[...] = result.astype(bf16)
    row = lax.broadcasted_iota(jnp.int32, (rows, width), 0)
    seed = jnp.where(start + row < length, cot_ref[...].astype(f32), 0.0)
    vec_out[4:5, :] = jnp.sum(seed * normal2, axis=0, keepdims=True)
    vec_out[5:6, :] = jnp.sum(seed, axis=0, keepdims=True)
    resid2 = norm_backward(seed, gain2, normal2, inverse2)
    shrunk_low = resid2.astype(bf16)
    vec_out[3:4, :] = jnp.sum(shrunk_low.astype(f32), axis=0, keepdims=True)
    hidden_grad = resid2
    for k in range(fold):
        active_grad = lax.dot_general(
            shrunk_low, w2[k], CONTRACT_LAST, preferred_element_type=f32
        )
        expanded_low = (active_grad * slope[k]).astype(bf16)
        vec_out[8 + k : 9 + k, :] = jnp.sum(expanded_low.astype(f32), axis=0, keepdims=True)
        hidden_grad += lax.dot_general(
            expanded_low, w1[k], CONTRACT_LAST, preferred_element_type=f32
        )
        g2[k] = lax.dot_general(
            act[k], shrunk_low, CONTRACT_FIRST, preferred_element_type=f32
        ).astype(bf16)
        g1[k] = lax.dot_general(
            hidden_low, expanded_low, CONTRACT_FIRST, preferred_element_type=f32
        ).astype(bf16)
    vec_out[1:2, :] = jnp.sum(hidden_grad * normal1, axis=0, keepdims=True)
    vec_out[2:3, :] = jnp.sum(hidden_grad, axis=0, keepdims=True)
    resid1 = norm_backward(hidden_grad, gain1, normal1, inverse1)
    resid_ref[...] = resid1
    branch_low = resid1.astype(bf16)
    vec_out[0:1, :] = jnp.sum(branch_low.astype(f32), axis=0, keepdims=True)
    vec_out[6:8, :] = jnp.zeros((2, width), f32)
    vec_out[8 + fold :, :] = jnp.zeros((vec_out.shape[0] - 8 - fold, width), f32)
    for r in range(4):
        da_refs[r][...] = lax.dot_general(
            branch_low, wo[group_rows(r), :], CONTRACT_LAST, preferred_element_type=f32
        ).astype(bf16)
        go[group_rows(r), :] = lax.dot_general(
            att_refs[r][...], branch_low, CONTRACT_FIRST, preferred_element_type=f32
        ).astype(bf16)
    units = [g2.at[k] for k in range(fold)] + [g1.at[k] for k in range(fold)] + [go]
    if aligned:
        block = n_b * own_rows
        for i, part in enumerate(unit_parts(fold)):
            for dc in range(2):
                target, sem = targets[2 * i + dc], out_sem.at[2 * i + dc]
                for dx in range(2):
                    for jz in range(n_q):
                        m = ((zi ^ jz) * 2 + (xi ^ dx)) * 2 + (ci ^ dc)
                        at = pl.ds(pl.multiple_of(m * block, 16), block)
                        for place, unit in enumerate(part):
                            dst = target.at[dx, jz, :, lanes(place)]
                            pltpu.make_async_copy(units[unit].at[at], dst, sem).start()
    else:
        for i, unit in enumerate(units):
            pltpu.make_async_copy(unit, targets[0].at[:, lanes(i)], out_sem.at[0]).start()
    for i, dst in enumerate(targets):
        pltpu.make_async_copy(dst, dst, out_sem.at[i]).wait()


def unit_parts(fold):
    count = 1 + 2 * fold
    edges = [count * i // 3 for i in range(4)]
    return [range(edges[i], edges[i + 1]) for i in range(3)]


def ffn_block(layout, where, att, x, cot, vectors, ebias, packed):
    n_q, n_b, own_rows, fold, aligned = layout
    rows, width = x.shape
    ff = fold * width
    operands = [where, *att, x, cot, vectors, ebias, in_hbm(packed)]
    in_specs = [pl.BlockSpec(memory_space=pltpu.SMEM)] + vmem_specs(8)
    in_specs += [pl.BlockSpec(memory_space=pltpu.HBM)]
    out_shape = [
        jax.ShapeDtypeStruct((rows, width), bf16),
        jax.ShapeDtypeStruct((rows, width), f32),
        *[jax.ShapeDtypeStruct((rows, OWN_WIDTH), bf16)] * 4,
        jax.ShapeDtypeStruct((16, width), f32),
    ]
    if aligned:
        lead = (2, n_q, n_b * own_rows)
        sizes = [len(part) * width for part in unit_parts(fold)]
        targets = [pltpu.HBM((*lead, size), bf16) for size in sizes for _ in range(2)]
    else:
        targets = [pltpu.HBM((width, width + 2 * ff), bf16)]
    weight_scratch = [
        pltpu.VMEM((width, width), bf16),
        pltpu.VMEM((fold, width, width), bf16),
        pltpu.VMEM((fold, width, width), bf16),
    ]
    return pl.pallas_call(
        partial(ffn_kernel, layout),
        out_shape=out_shape + targets,
        in_specs=in_specs,
        out_specs=vmem_specs(len(out_shape)) + [pl.BlockSpec(memory_space=pltpu.HBM)] * len(targets),
        scratch_shapes=weight_scratch
        + weight_scratch
        + [
            pltpu.VMEM((fold, rows, width), bf16),
            pltpu.VMEM((fold, rows, width), f32),
            pltpu.SemaphoreType.DMA((1 + 2 * fold,)),
            pltpu.SemaphoreType.DMA((6,)),
        ],
        compiler_params=pltpu.CompilerParams(vmem_limit_bytes=32 * MIB),
        cost_estimate=pl.CostEstimate(
            flops=int(2e10), transcendentals=2 * rows * ff, bytes_accessed=int(3e7)
        ),
        name="feed_forward",
    )(*operands)


def order_kernel(n_q, n_b, where_ref, blocks_ref, out_ref):
    group, zi, bi = [where_ref[i] for i in range(3)]
    rows = blocks_ref.shape[3]
    for m in range(4 * n_q):
        q, g = m // 4, m % 4
        far, r = lax.rem(q + n_q - zi, n_q), g ^ group
        both = [
            blocks_ref[lax.rem(b + n_b - bi, n_b), far, r].astype(f32) for b in range(n_b)
        ]
        at = slice(m * n_b * rows, (m + 1) * n_b * rows)
        out_ref[at, :] = jnp.concatenate(both, axis=0).astype(bf16)


def order_rows(n_q, n_b, where, blocks):
    rows, lanes = blocks.shape[3:]
    return pl.pallas_call(
        partial(order_kernel, n_q, n_b),
        out_shape=jax.ShapeDtypeStruct((4 * n_q * n_b * rows, lanes), bf16),
        in_specs=[pl.BlockSpec(memory_space=pltpu.SMEM)] + vmem_specs(1),
        out_specs=vmem_specs(1)[0],
        compiler_params=pltpu.CompilerParams(vmem_limit_bytes=12 * MIB),
        name="order_rows",
    )(where, blocks)


def from_shift(value, axis, count, step):
    return lax.ppermute(value, axis, [((i + step) % count, i) for i in range(count)])


def square_swap(value, r):
    if r == 0:
        return value
    if r == 1:
        return lax.ppermute(value, "c", [(0, 1), (1, 0)])
    if r == 2:
        return lax.ppermute(value, "x", [(0, 1), (1, 0)])
    return lax.ppermute(value, ("x", "c"), [(0, 3), (3, 0), (1, 2), (2, 1)])


def pick(stacked, index, dim=0):
    return lax.dynamic_index_in_dim(stacked, index, dim, keepdims=False)


class Chain:
    def __init__(self, state, *steps):
        self.state, self.steps = tuple(state), list(steps)


def launch(chain):
    chain.state = tuple(chain.steps.pop(0)(*chain.state))


def run_stage(chains, outs=(), settle=()):
    for chain in chains:
        launch(chain)
    joined = [*chains, *settle]
    outs, states = lax.optimization_barrier((tuple(outs), [c.state for c in joined]))
    for chain, state in zip(joined, states):
        chain.state = tuple(state)
    return outs


def away_sum(total, axis, count):
    parts = [total[j].astype(bf16) for j in range(1, count)]
    return [from_shift(part, axis, count, count - j - 1) for j, part in enumerate(parts)]


def weight_sum(keep, send, n_q, n_b, bi):
    def own_b(keep, got, j):
        shape = (2, n_q, n_b, -1, keep.shape[-1])
        both = [pick(v.reshape(shape), (bi + j) % n_b, 2).astype(f32) for v in (keep, got)]
        return both[0] + both[1]

    def over_core(keep, send):
        return keep, square_swap(send, 1)

    def over_b(keep, got):
        away = [own_b(keep, got, j).astype(bf16) for j in range(1, n_b)]
        return keep, got, *[from_shift(v, "b", n_b, n_b - 1 - j) for j, v in enumerate(away)]

    def over_x(keep, got, *more):
        total = own_b(keep, got, 0) + sum(v.astype(f32) for v in more)
        return total[0], *away_sum(total, "x", 2)

    def halve(half):
        def over_q(own, got):
            total = own + got.astype(f32)
            pairs = [(i, i ^ half) for i in range(n_q)]
            return total[:half], lax.ppermute(total[half:].astype(bf16), "q", pairs)

        return over_q

    halves = [n_q >> (k + 1) for k in range(n_q.bit_length() - 1)]
    return Chain((keep, send), over_core, over_b, over_x, *[halve(half) for half in halves])


def toward(j, n_q):
    return (j - 1, n_q - 1) if 2 * j <= n_q else ((j + 1) % n_q, 1)


def token_sum(keep, send, n_q, j, farther):
    def over_core(keep, send):
        return keep, square_swap(send, 1)

    def over_x(keep, got):
        total = keep.astype(f32) + got.astype(f32)
        return total[0], square_swap(total[1].astype(bf16), 2)

    def over_q(own, got):
        total = own + got.astype(f32) + sum(chain_sum(c) for c in farther)
        return (from_shift(total.astype(bf16), "q", n_q, toward(j, n_q)[1]),)

    return Chain((keep, send), over_core, over_x, *([over_q] if j else []))


def chain_sum(chain):
    return sum(v.astype(f32).reshape(chain.state[0].shape) for v in chain.state)


def deinterleave(fold):
    size = fold * LANES
    lane = jnp.arange(size)
    return (lane[:, None] // fold + (lane[:, None] % fold) * LANES == lane[None, :]).astype(bf16)


def per_device(
    n_q,
    n_b,
    inputs,
    lengths,
    cotangent,
    triple_weight,
    query_bias,
    value_bias,
    output_weight,
    output_bias,
    first_gain,
    first_shift,
    expand_weight,
    expand_bias,
    shrink_weight,
    shrink_bias,
    second_gain,
    second_shift,
):
    zi, xi, ci, bi = [lax.axis_index(a) for a in AXES]
    group = 2 * xi + ci
    _, seq_rows, width = inputs.shape
    own_rows = triple_weight.shape[0]
    ff = expand_weight.shape[1]
    fold = ff // width
    aligned = n_b * own_rows % 16 == 0 and n_q & (n_q - 1) == 0
    x_own = inputs[0]

    turn = deinterleave(fold)
    expand_own = expand_weight.astype(bf16).reshape(own_rows, -1, fold * LANES)
    expand_own = jnp.einsum("rbs,st->rbt", expand_own, turn, preferred_element_type=f32)
    expand_own = expand_own.astype(bf16).reshape(own_rows, -1, fold, LANES).transpose(0, 2, 1, 3)
    packed = jnp.concatenate(
        [
            output_weight.astype(bf16),
            expand_own.reshape(own_rows, ff),
            shrink_weight.astype(bf16).reshape(own_rows, ff),
        ],
        axis=1,
    )
    gathered_ffn = lax.all_gather(packed, AXES, axis=0, tiled=True)

    names = [query_bias, value_bias, output_bias, first_gain, first_shift]
    names += [shrink_bias, second_gain, second_shift]
    vectors = jnp.stack(names, axis=1)
    vectors = jnp.concatenate([vectors, expand_bias.reshape(own_rows, fold)], axis=1).astype(bf16)
    n_vec = vectors.shape[1]
    vectors = jnp.pad(vectors, ((0, 0), (0, WIDE - VECTORS - n_vec)))
    thirds = triple_weight.astype(bf16).reshape(own_rows, 3, GROUPS, OWN_WIDTH)

    def columns_of(g):
        mine = [pick(thirds[:, t], g, 1) for t in range(3)]
        return jnp.concatenate(mine + [vectors], axis=1)

    def rows_square(*blocks):
        return [square_swap(block, r) for r, block in enumerate(blocks)]

    def rows_q(*blocks):
        square = jnp.stack(blocks)
        return [square] + [from_shift(square, "q", n_q, j) for j in range(1, n_q)]

    def rows_b(*blocks):
        both = jnp.stack(blocks)
        return [both] + [from_shift(both, "b", n_b, j) for j in range(1, n_b)]

    weight_rows = Chain([columns_of(group ^ r) for r in range(4)], rows_square, rows_q, rows_b)

    def token_chunk(j):
        def over_q():
            source, step = toward(j, n_q)
            own = chunks[source].state[0] if source else x_own
            return (from_shift(own, "q", n_q, n_q - step),)

        def over_x(own):
            return own, square_swap(own, 2)

        def over_core(own, other):
            halves = square_swap(jnp.stack([own, other]), 1)
            return own, halves[0], other, halves[1]

        return Chain(() if j else (x_own,), *([over_q] if j else []), over_x, over_core)

    arrival = []
    for j in [k for pair in zip(range(1, n_q), range(n_q - 1, 0, -1)) for k in pair]:
        arrival += [] if j in arrival else [j]
    arrival = [0] + arrival
    chunks = {j: token_chunk(j) for j in arrival}
    line = [chunks[j] for j in arrival]


    def stage(slot, outs=()):
        with_it = [weight_rows] if slot < 3 else []
        settle = []
        for i, c in enumerate(line):
            begin = max(0, i - 1) if i > 2 else 0
            if i < 3 and (slot - begin) in range(len(c.steps) and 3 if i else 2):
                with_it.append(c)
            elif i > 2 and slot in (begin, begin + 3):
                with_it.append(c)
            elif i > 2 and slot == begin + 1:
                launch(c)
            elif i > 2 and slot == begin + 2:
                settle.append(c)
        return run_stage(with_it, outs, settle)

    for slot in range(3):
        stage(slot)
    chunk_x = {}

    by_distance = jnp.stack(weight_rows.state)
    if aligned:
        spot = jnp.stack([group, zi, bi]).astype(jnp.int32)
        w_own = order_rows(n_q, n_b, spot, by_distance)
    else:
        ordered = jnp.stack([pick(by_distance, (i - bi) % n_b) for i in range(n_b)], axis=3)
        ordered = jnp.stack([pick(ordered, group ^ g, 1) for g in range(4)], axis=1)
        ordered = jnp.stack([pick(ordered, (i - zi) % n_q) for i in range(n_q)])
        w_own = ordered.transpose(0, 1, 3, 2, 4).reshape(width, WIDE)
    turned = w_own[:, VECTORS : VECTORS + n_vec].astype(f32)
    turned = turned.T
    ebias = turned[8:]
    turned = turned[:8]
    own_bias = lax.dynamic_slice_in_dim(turned, group * OWN_WIDTH, OWN_WIDTH, 1)
    zero = jnp.zeros((1, OWN_WIDTH), f32)
    bias_row = jnp.concatenate(
        [own_bias[:1], zero, own_bias[1:2], jnp.zeros((1, WIDE - VECTORS), f32)], axis=1
    )

    def where_of(j):
        zj = (zi + j) % n_q
        spots = [(zj * 4 + (group ^ r)) * seq_rows for r in range(4)]
        return jnp.stack(spots + [lengths[0]]).astype(jnp.int32)

    weights = (w_own, bias_row)
    kept = {}
    carry = None
    for step, j in enumerate(arrival):
        first, last = step == 0, step == n_q - 1
        assert not chunks[j].steps
        chunk_x[j] = chunks[j].state
        outs = attend_chunk(first, last, where_of(j), chunk_x[j], weights, carry)
        outs = stage(3 + step, outs)
        kept[j] = (outs[0], outs[1])
        outs = outs[2:]
        if first:
            qx, qp = outs[:2]
            outs = outs[2:]
        carry = (qx, *outs)
    att, attx, qx2 = carry[1:5], carry[5], carry[6]

    att = [square_swap(att[r], r) for r in range(4)]
    start = (zi * 4 + group) * seq_rows
    where = jnp.stack([group, zi, xi, ci, bi, start, lengths[0]]).astype(jnp.int32)
    layout = (n_q, n_b, own_rows, fold, aligned)
    outs = ffn_block(layout, where, att, x_own, cotangent[0], turned, ebias, gathered_ffn)
    output, resid_first_grad = outs[:2]
    att_grads, vec_grads, summands = outs[2:6], outs[6], outs[7:]
    square = Chain(att_grads, lambda *parts: [square_swap(v, r) for r, v in enumerate(parts)])

    sums = []
    if aligned:
        for i in range(3):
            sums.append(weight_sum(summands[2 * i], summands[2 * i + 1], n_q, n_b, bi))
    else:
        summed = lax.psum_scatter(summands[0], AXES, scatter_dimension=0, tiled=True).astype(f32)
    run_stage([square] + sums[:2])
    for chain in sums[2:]:
        launch(chain)
    plan = [
        ([0], [2], [1], []),
        ([0], [1], [2], [2]),
        ([1, 0], [], [2], [2]),
        ([1, 2, 0], [], [], []),
    ]
    shared = (qx2, qp, w_own, square.state, attx)
    carry = None
    moving, moving_to = [], {}
    for step, j in enumerate(reversed(arrival)):
        first, last = step == 0, step == n_q - 1
        with_it, ending, going_on, after_it = [], [], [], []
        if sums and step < len(plan):
            with_it, ending, going_on, after_it = [[sums[i] for i in part] for part in plan[step]]
        outs = attend_back_chunk(first, last, kept[j], chunk_x[j], shared, carry)
        for chain in going_on:
            launch(chain)
        outs = run_stage(with_it + [c for c in moving if c.steps], outs, settle=ending)
        keep, send = outs[:2]
        farther = [c for k, c in moving_to.items() if k and toward(k, n_q)[0] == j and j]
        moving_to[j] = token_sum(keep, send, n_q, j, farther)
        moving.append(moving_to[j])
        outs = outs[2:]
        if first:
            dox = outs[0]
            outs = outs[1:]
        carry = (dox, *outs)
        if not last:
            carry = run_stage(moving[-1:], carry, settle=after_it)
    grad_joint, col = carry[1:]

    own_bias = jnp.stack([col[0, :OWN_WIDTH], col[0, 2 * OWN_WIDTH : 3 * OWN_WIDTH]])
    bias_grads = lax.dynamic_update_slice(
        jnp.zeros((2, width), f32), own_bias, (0, group * OWN_WIDTH)
    )
    tall = jnp.concatenate([bias_grads, vec_grads[:6], vec_grads[8 : 8 + fold]], axis=0).T
    tall_high = tall.astype(bf16)
    tall_low = (tall - tall_high.astype(f32)).astype(bf16)
    room = jnp.zeros((width, WIDE - VECTORS - 2 * n_vec), bf16)
    blocks = jnp.concatenate([grad_joint[:, :VECTORS], tall_high, tall_low, room], axis=1)
    total = blocks.reshape(n_q, 4, n_b, own_rows, WIDE)

    def rows_over_b(total):
        parts = [pick(total, (bi + j) % n_b, 2) for j in range(n_b)]
        return parts[0], *away_sum(parts, "b", n_b)

    def rows_over_q(*parts):
        total = sum(v.astype(f32) for v in parts)
        parts = [pick(total, (zi + j) % n_q) for j in range(n_q)]
        return parts[0], *away_sum(parts, "q", n_q)

    def rows_over_square(*parts):
        total = sum(v.astype(f32) for v in parts).astype(bf16)
        return [square_swap(pick(total, group ^ r), r) for r in range(4)]

    rows = Chain((total,), rows_over_b, rows_over_q, rows_over_square)
    run_stage([], settle=[rows, *sums, *moving])
    while any(c.steps for c in [rows, *sums, *moving]):
        run_stage([c for c in [rows, *sums, *moving] if c.steps])
    token_grad = resid_first_grad
    for j, chain in moving_to.items():
        if j == 0 or toward(j, n_q)[0] == 0:
            token_grad = token_grad + chain_sum(chain)
    input_grad = token_grad.astype(bf16)
    if aligned:
        summed = jnp.concatenate([chain_sum(c)[0] for c in sums], axis=1)
    parts = jnp.stack(rows.state)
    parts = jnp.stack([pick(parts, group ^ g) for g in range(4)])
    grad_triple = parts[:, :, :VECTORS].reshape(GROUPS, own_rows, 3, OWN_WIDTH)
    grad_triple = grad_triple.transpose(1, 2, 0, 3).reshape(own_rows, -1).astype(f32)
    small = jnp.sum(parts[:, :, VECTORS : VECTORS + 2 * n_vec].astype(f32), axis=0)
    small = small[:, :n_vec] + small[:, n_vec:]
    grad_expand = summed[:, ff : 2 * ff].reshape(own_rows, fold, -1, LANES).transpose(0, 2, 1, 3)
    grad_expand = jnp.einsum(
        "rbs,ts->rbt",
        grad_expand.reshape(own_rows, -1, fold * LANES),
        turn.astype(f32),
        precision=lax.Precision.HIGHEST,
        preferred_element_type=f32,
    ).reshape(own_rows, ff)
    return (
        output[None],
        input_grad[None],
        grad_triple,
        small[:, 0],
        small[:, 1],
        summed[:, 2 * ff :],
        small[:, 2],
        small[:, 3],
        small[:, 4],
        grad_expand,
        small[:, 8:].reshape(-1),
        summed[:, :ff].reshape(-1, width),
        small[:, 5],
        small[:, 6],
        small[:, 7],
    )


def solution(mesh):
    n_seq, n_b = mesh.shape["seq"], mesh.shape["batch"]
    n_q = n_seq // GROUPS
    fine = Mesh(mesh.devices.reshape(n_q, 2, 2, n_b), AXES)
    tokens = P("b", ("q", "x", "c"), None)
    matrix = P(AXES, None)
    vector = P(AXES)
    in_specs = (
        tokens,
        P("b"),
        tokens,
        matrix,
        vector,
        vector,
        matrix,
        vector,
        vector,
        vector,
        matrix,
        vector,
        matrix,
        vector,
        vector,
        vector,
    )
    out_specs = (
        tokens,
        tokens,
        matrix,
        vector,
        vector,
        matrix,
        vector,
        vector,
        vector,
        matrix,
        vector,
        matrix,
        vector,
        vector,
        vector,
    )
    return jax.shard_map(
        partial(per_device, n_q, n_b),
        mesh=fine,
        in_specs=in_specs,
        out_specs=out_specs,
        check_vma=False,
    )
```

```python
from functools import partial
import math

import jax
import jax.numpy as jnp
from jax import lax
from jax.experimental import pallas as pl
from jax.experimental.pallas import tpu as pltpu
from jax.sharding import Mesh, PartitionSpec as P

HEADS = 12
HEAD_DIM = 64
GROUPS = 4
OWN_HEADS = HEADS // GROUPS
OWN_WIDTH = OWN_HEADS * HEAD_DIM
LANES = 128
WIDE = 640
VECTORS = 3 * OWN_WIDTH

bf16 = jnp.bfloat16
f32 = jnp.float32
masked_score = -1e30
norm_eps = 1e-12
log2_e = 1.4426950408889634
CONTRACT_LAST = (((1,), (1,)), ((), ()))
MIB = 1024 * 1024
AXES = ("q", "x", "c", "b")


def split_three(value):
    high = value.astype(bf16).astype(f32)
    rest = value - high
    mid = rest.astype(bf16).astype(f32)
    low = (rest - mid).astype(bf16).astype(f32)
    return high, mid, low


def low_half(tile, lane, from_high):
    turned = pltpu.roll(tile, HEAD_DIM, 1)
    low = lane < HEAD_DIM
    return jnp.where(low, turned, tile) if from_high else jnp.where(low, tile, turned)


def place_of(kind, h):
    slot = kind * OWN_HEADS + h
    return slot // 2, slot % 2


def forward_kernel(first, last, block_q, block_k, *refs):
    refs = list(refs)
    where_ref = refs.pop(0)
    far = [refs.pop(0) for _ in range(5)]
    bias_ref = refs.pop(0)
    if not first:
        qx_ref, peak_in, sum_in = [refs.pop(0) for _ in range(3)]
    kept = [refs.pop(0) for _ in range(2)]
    if first:
        qx_ref, qp_ref = [refs.pop(0) for _ in range(2)]
    if last:
        att_refs = [refs.pop(0) for _ in range(4)]
        attx_ref, qx2_ref = [refs.pop(0) for _ in range(2)]
    else:
        peak_out, sum_out = [refs.pop(0) for _ in range(2)]
    vt_ref, kx_ref, vx_ref, sem, *near = refs
    loads = [pltpu.make_async_copy(f, n, sem.at[2 + i]) for i, (f, n) in enumerate(zip(far, near))]
    for i in (4, 0, 1, 2, 3):
        loads[i].start()
    *pieces, w_ref = near
    stores = [
        pltpu.make_async_copy(kx_ref, kept[0], sem.at[0]),
        pltpu.make_async_copy(vx_ref, kept[1], sem.at[1]),
    ]
    piece_rows = pieces[0].shape[0]
    rows_in = 4 * piece_rows
    lane = lax.broadcasted_iota(jnp.int32, (piece_rows, LANES), 1)
    row = lax.broadcasted_iota(jnp.int32, (piece_rows, LANES), 0)
    low = lane < HEAD_DIM
    length = where_ref[4]
    three = (lane >= HEAD_DIM) & (lane < HEAD_DIM + 3)
    skip = 0 if first else LANES
    for p in range(4):
        rows = slice(p * piece_rows, (p + 1) * piece_rows)
        if p == 0:
            loads[4].wait()
        loads[p].wait()
        joint = jnp.dot(pieces[p][...], w_ref[:, skip:], preferred_element_type=f32)
        joint = joint + bias_ref[:, skip:]
        bias = jnp.where(where_ref[p] + row < length, 0.0, masked_score)
        key_extra = jnp.where(three, 1.0, jnp.where(lane == HEAD_DIM + 3, bias, 0.0))

        def head_of(kind, h):
            tile, high = place_of(kind, h)
            return low_half(joint[:, tile * LANES - skip : (tile + 1) * LANES - skip], lane, high)

        for h in range(OWN_HEADS):
            k = head_of(1, h)
            kx_ref[h, rows, :LANES] = k.astype(bf16)
            kx_ref[h, rows, LANES:] = jnp.where(low, k, key_extra).astype(bf16)
            v = jnp.where(low, head_of(2, h), 0.0)
            vx_ref[h, rows, :] = jnp.where(three, -1.0, v).astype(bf16)
            vt = jnp.where(lane == HEAD_DIM, 1.0, v).T
            vt_ref[h, :, rows] = vt[:80].astype(bf16)
            if first:
                q = head_of(0, h).astype(bf16).astype(f32)
                qp_ref[h, rows, :] = jnp.where(low, q, 0.0).astype(bf16)
                high, mid, rest = split_three(q * (HEAD_DIM**-0.5 * log2_e))
                qx_ref[h, rows, :LANES] = jnp.where(low, high, mid).astype(bf16)
                one = jnp.where(lane == HEAD_DIM + 3, 1.0, 0.0)
                qx_ref[h, rows, LANES:] = jnp.where(low, rest, one).astype(bf16)
    for store in stores:
        store.start()
    for h in range(OWN_HEADS):
        for i in range(rows_in // block_q):
            cols = slice(i * block_q, (i + 1) * block_q)
            q = qx_ref[h, cols, :]
            if first:
                peak = jnp.full((1, block_q), masked_score, f32)
                total = jnp.zeros((80, block_q), f32)
            else:
                peak = peak_in[h, :1, cols]
                total = sum_in[h, :, cols]
            for j in range(rows_in // block_k):
                ks = slice(j * block_k, (j + 1) * block_k)
                s = lax.dot_general(kx_ref[h, ks, :], q, CONTRACT_LAST, preferred_element_type=f32)
                new_peak = jnp.maximum(peak, jnp.max(s, axis=0, keepdims=True))
                prob = jnp.exp2(s - new_peak).astype(bf16)
                total = total * jnp.exp2(peak - new_peak) + jnp.dot(
                    vt_ref[h, :, ks], prob, preferred_element_type=f32
                )
                peak = new_peak
            if last:
                denom = total[HEAD_DIM : HEAD_DIM + 1]
                n_high, n_mid, n_low = split_three(-(peak + jnp.log2(denom)))
                tall = jnp.concatenate(
                    [
                        total[:HEAD_DIM] / denom,
                        n_high,
                        n_mid,
                        n_low,
                        jnp.zeros((HEAD_DIM - 3, block_q), f32),
                    ],
                    axis=0,
                )
                attx_ref[h, cols, :] = tall.T
            else:
                peak_out[h, :, cols] = jnp.broadcast_to(peak, (8, block_q))
                sum_out[h, :, cols] = total
    if last:
        for p in range(4):
            rows = slice(p * piece_rows, (p + 1) * piece_rows)
            heads = [attx_ref[h, rows, :] for h in range(OWN_HEADS)]
            pair = jnp.where(low, heads[0], pltpu.roll(heads[1], HEAD_DIM, 1))
            att_refs[p][:, :LANES] = pair.astype(bf16)
            att_refs[p][:, LANES:] = heads[2][:, :HEAD_DIM].astype(bf16)
            for h in range(OWN_HEADS):
                qx2_ref[h, rows, :LANES] = qx_ref[h, rows, :LANES]
                old = qx_ref[h, rows, LANES:].astype(f32)
                qx2_ref[h, rows, LANES:] = jnp.where(three, heads[h], old).astype(bf16)
    for store in stores:
        store.wait()


def in_hbm(value):
    return pltpu.with_memory_space_constraint(value, pltpu.HBM)


def vmem_specs(n):
    return [pl.BlockSpec(memory_space=pltpu.VMEM) for _ in range(n)]


def attend_chunk(first, last, where, pieces, weights, carry):
    piece_rows = pieces[0].shape[0]
    rows = 4 * piece_rows
    w, bias_row = weights
    far = [in_hbm(v) for v in (*pieces, w)]
    operands = [where, *far, bias_row]
    operands += [] if first else list(carry)
    wide_keys = jax.ShapeDtypeStruct((OWN_HEADS, rows, 2 * LANES), bf16)
    out_shape = [pltpu.HBM(wide_keys.shape, bf16), pltpu.HBM((OWN_HEADS, rows, LANES), bf16)]
    if first:
        out_shape += [wide_keys, jax.ShapeDtypeStruct((OWN_HEADS, rows, LANES), bf16)]
    if last:
        out_shape += [jax.ShapeDtypeStruct((piece_rows, OWN_WIDTH), bf16)] * 4
        out_shape += [jax.ShapeDtypeStruct((OWN_HEADS, rows, LANES), f32), wide_keys]
    else:
        out_shape += [
            jax.ShapeDtypeStruct((OWN_HEADS, 8, rows), f32),
            jax.ShapeDtypeStruct((OWN_HEADS, 80, rows), f32),
        ]
    return pl.pallas_call(
        partial(forward_kernel, first, last, min(1024, rows), min(1024, rows)),
        out_shape=out_shape,
        in_specs=[pl.BlockSpec(memory_space=pltpu.SMEM)]
        + [pl.BlockSpec(memory_space=pltpu.HBM)] * len(far)
        + vmem_specs(len(operands) - 1 - len(far)),
        out_specs=[pl.BlockSpec(memory_space=pltpu.HBM)] * 2 + vmem_specs(len(out_shape) - 2),
        scratch_shapes=[
            pltpu.VMEM((OWN_HEADS, 80, rows), bf16),
            pltpu.VMEM((OWN_HEADS, rows, 2 * LANES), bf16),
            pltpu.VMEM((OWN_HEADS, rows, LANES), bf16),
            pltpu.SemaphoreType.DMA((7,)),
            *[pltpu.VMEM(v.shape, v.dtype) for v in (*pieces, w)],
        ],
        compiler_params=pltpu.CompilerParams(vmem_limit_bytes=20 * MIB),
        cost_estimate=pl.CostEstimate(
            flops=int(8e9), transcendentals=OWN_HEADS * rows * rows, bytes_accessed=int(1e7)
        ),
        name="attend_forward",
    )(*operands)


def backward_kernel(first, last, block_q, block_k, *refs):
    refs = list(refs)
    far = [refs.pop(0) for _ in range(7)]
    qx_ref, qp_ref = [refs.pop(0) for _ in range(2)]
    if first:
        grads = [refs.pop(0) for _ in range(4)]
        attx_ref = refs.pop(0)
    else:
        dox_ref, dqt_in, dw_in, col_in = [refs.pop(0) for _ in range(4)]
    keep_ref, send_ref = [refs.pop(0) for _ in range(2)]
    if first:
        dox_ref = refs.pop(0)
    if last:
        dw_out, col_out = [refs.pop(0) for _ in range(2)]
        dqt_ref = refs.pop()
    else:
        dqt_ref, dw_out, col_out = [refs.pop(0) for _ in range(3)]
    kt_ref, all_ref, sem = refs[:3]
    near = refs[3:]
    kx_ref, vx_ref, w_ref, *pieces = near
    loads = []
    for f, n in zip(far[:2], near[:2]):
        loads += [(f.at[h], n.at[h]) for h in range(OWN_HEADS)]
    loads += list(zip(far[2:], near[2:]))
    loads = [pltpu.make_async_copy(f, n, sem.at[i]) for i, (f, n) in enumerate(loads)]
    for i in (0, OWN_HEADS, *range(1, OWN_HEADS), *range(OWN_HEADS + 1, len(loads))):
        loads[i].start()
    rows_in = kx_ref.shape[1]
    piece_rows = rows_in // 4
    scale = HEAD_DIM**-0.5
    lane = lax.broadcasted_iota(jnp.int32, (piece_rows, LANES), 1)
    if first:
        for p in range(4):
            rows = slice(p * piece_rows, (p + 1) * piece_rows)
            left = grads[p][:, :LANES].astype(f32)
            right = grads[p][:, LANES:].astype(f32)
            right = jnp.concatenate([right, jnp.zeros_like(right)], axis=1)
            for h, wide in enumerate((left, pltpu.roll(left, HEAD_DIM, 1), right)):
                grad = jnp.where(lane < HEAD_DIM, wide, 0.0)
                delta = jnp.sum(grad * attx_ref[h, rows, :], axis=1, keepdims=True)
                d_high, d_mid, d_low = split_three(delta)
                grad = jnp.where(lane == HEAD_DIM, d_high, grad)
                grad = jnp.where(lane == HEAD_DIM + 1, d_mid, grad)
                grad = jnp.where(lane == HEAD_DIM + 2, d_low, grad)
                dox_ref[h, rows, :] = grad.astype(bf16)
        dqt_ref[...] = jnp.zeros_like(dqt_ref)
    else:
        dqt_ref[...] = dqt_in[...]
    lane_k = lax.broadcasted_iota(jnp.int32, (block_k, LANES), 1)
    low_k = lane_k < HEAD_DIM
    for j in range(rows_in // block_k):
        ks = slice(j * block_k, (j + 1) * block_k)
        parts = {}
        for h in range(OWN_HEADS):
            if j == 0:
                loads[h].wait()
                loads[OWN_HEADS + h].wait()
                kt_ref[h] = kx_ref[h, :, LANES:].astype(f32).T[:HEAD_DIM].astype(bf16)
            k = kx_ref[h, ks, :]
            v = vx_ref[h, ks, :]
            kt = kt_ref[h, :, ks]
            dk = jnp.zeros((block_k, LANES), f32)
            dv = jnp.zeros((block_k, LANES), f32)
            for i in range(rows_in // block_q):
                qs = slice(i * block_q, (i + 1) * block_q)
                s = lax.dot_general(k, qx_ref[h, qs, :], CONTRACT_LAST, preferred_element_type=f32)
                prob = jnp.exp2(s)
                do = dox_ref[h, qs, :]
                dp = lax.dot_general(v, do, CONTRACT_LAST, preferred_element_type=f32)
                ds = (prob * dp).astype(bf16)
                dv = dv + jnp.dot(prob.astype(bf16), do, preferred_element_type=f32)
                dk = dk + jnp.dot(ds, qp_ref[h, qs, :], preferred_element_type=f32)
                dqt_ref[h, :, qs] += jnp.dot(kt, ds, preferred_element_type=f32)
            parts[OWN_HEADS + h] = dk * scale
            parts[2 * OWN_HEADS + h] = dv
        for tile in range(1, WIDE // LANES):
            left, right = parts.get(2 * tile), parts.get(2 * tile + 1)
            left = jnp.zeros((block_k, LANES), f32) if left is None else left
            right = 0.0 if right is None else pltpu.roll(right, HEAD_DIM, 1)
            both = jnp.where(low_k, left, right).astype(bf16)
            all_ref[ks, tile * LANES : (tile + 1) * LANES] = both
    if last:
        tall = jnp.concatenate([dqt_ref[0], dqt_ref[1]], axis=0) * scale
        all_ref[:, :LANES] = tall.T.astype(bf16)
        tall = dqt_ref[2] * scale
        tall = jnp.concatenate([tall, jnp.zeros_like(tall)], axis=0).T
        lane_all = lax.broadcasted_iota(jnp.int32, (rows_in, LANES), 1)
        old = all_ref[:, LANES : 2 * LANES].astype(f32)
        all_ref[:, LANES : 2 * LANES] = jnp.where(lane_all < HEAD_DIM, tall, old).astype(bf16)
    skip = 0 if last else LANES
    for load in loads[2 * OWN_HEADS :]:
        load.wait()
    d_weight = [None, None]
    for p in range(4):
        rows = slice(p * piece_rows, (p + 1) * piece_rows)
        own = all_ref[rows, skip:]
        dx = lax.dot_general(own, w_ref[:, skip:], CONTRACT_LAST, preferred_element_type=f32)
        out_ref = keep_ref if p % 2 == 0 else send_ref
        out_ref[p // 2] = dx.astype(bf16)
        piece = lax.dot_general(
            pieces[p][...], own, (((0,), (0,)), ((), ())), preferred_element_type=f32
        )
        d_weight[0] = piece if p == 0 else d_weight[0] + piece
        col = jnp.sum(own.astype(f32), axis=0, keepdims=True)
        d_weight[1] = col if p == 0 else d_weight[1] + col
    grad, col = d_weight
    if last:
        dw_out[:, :LANES] = grad[:, :LANES].astype(bf16)
        dw_out[:, LANES:] = (grad[:, LANES:] + dw_in[...]).astype(bf16)
        col_out[:, :LANES] = jnp.broadcast_to(col[:, :LANES], (8, LANES))
        col_out[:, LANES:] = col[:, LANES:] + col_in[...]
    elif first:
        dw_out[...] = grad
        col_out[...] = jnp.broadcast_to(col, col_out.shape)
    else:
        dw_out[...] = grad + dw_in[...]
        col_out[...] = col + col_in[...]


def attend_back_chunk(first, last, chunk, pieces, shared, carry):
    kx, vx = chunk
    qx2, qp, w, grads, attx = shared
    rows, width = kx.shape[1], w.shape[0]
    far = [in_hbm(v) for v in (kx, vx, w, *pieces)]
    operands = [*far, qx2, qp]
    operands += [*grads, attx] if first else list(carry)
    half = jax.ShapeDtypeStruct((2, rows // 4, width), bf16)
    out_shape = [half, half]
    scratch = [
        pltpu.VMEM((OWN_HEADS, HEAD_DIM, rows), bf16),
        pltpu.VMEM((rows, WIDE), bf16),
        pltpu.SemaphoreType.DMA((2 * OWN_HEADS + 5,)),
        *[pltpu.VMEM(v.shape, v.dtype) for v in far],
    ]
    if first:
        out_shape.append(jax.ShapeDtypeStruct((OWN_HEADS, rows, LANES), bf16))
    if last:
        out_shape.append(jax.ShapeDtypeStruct((width, WIDE), bf16))
        out_shape.append(jax.ShapeDtypeStruct((8, WIDE), f32))
        scratch.append(pltpu.VMEM((OWN_HEADS, HEAD_DIM, rows), f32))
    else:
        out_shape.append(jax.ShapeDtypeStruct((OWN_HEADS, HEAD_DIM, rows), f32))
        out_shape.append(jax.ShapeDtypeStruct((width, WIDE - LANES), f32))
        out_shape.append(jax.ShapeDtypeStruct((8, WIDE - LANES), f32))
    return pl.pallas_call(
        partial(backward_kernel, first, last, min(256, rows), min(1024, rows)),
        out_shape=out_shape,
        in_specs=[pl.BlockSpec(memory_space=pltpu.HBM)] * len(far)
        + vmem_specs(len(operands) - len(far)),
        out_specs=vmem_specs(len(out_shape)),
        scratch_shapes=scratch,
        compiler_params=pltpu.CompilerParams(vmem_limit_bytes=26 * MIB),
        cost_estimate=pl.CostEstimate(
            flops=int(1.5e10), transcendentals=OWN_HEADS * rows * rows, bytes_accessed=int(1e7)
        ),
        name="attend_backward",
    )(*operands)


def norm_forward(value, gain, shift):
    center = value - jnp.mean(value, axis=-1, keepdims=True)
    spread = jnp.mean(center * center, axis=-1, keepdims=True)
    inverse = lax.rsqrt(spread + norm_eps)
    normal = center * inverse
    return normal * gain + shift, normal, inverse


def norm_backward(grad, gain, normal, inverse):
    inner = grad * gain
    mean = jnp.mean(inner, axis=-1, keepdims=True)
    along = jnp.mean(inner * normal, axis=-1, keepdims=True)
    return inverse * (inner - mean - normal * along)


CONTRACT_FIRST = (((0,), (0,)), ((), ()))


def ffn_kernel(layout, *refs):
    n_q, n_b, own_rows, fold, aligned = layout
    refs = list(refs)
    where_ref = refs.pop(0)
    att_refs = [refs.pop(0) for _ in range(4)]
    x_ref, cot_ref, vec_ref, eb_ref = [refs.pop(0) for _ in range(4)]
    packed = [refs.pop(0) for _ in range(2 if aligned else 1)]
    out_ref, resid_ref = [refs.pop(0) for _ in range(2)]
    da_refs = [refs.pop(0) for _ in range(4)]
    vec_out = refs.pop(0)
    targets = [refs.pop(0) for _ in range(5 if aligned else 1)]
    wo, w1, w2, go, g1, g2, act, slope, in_sem, out_sem = refs
    group, zi, xi, ci, bi, start, length = [where_ref[i] for i in range(7)]
    rows, width = x_ref.shape

    def lanes(i):
        return slice(i * width, (i + 1) * width)

    weights = [wo, *[w1.at[k] for k in range(fold)], *[w2.at[k] for k in range(fold)]]
    block = n_b * own_rows
    for i, weight in enumerate(weights):
        if not aligned:
            pltpu.make_async_copy(packed[0].at[:, lanes(i)], weight, in_sem.at[i]).start()
            continue
        for half in range(2):
            for m in range(2 * n_q):
                src = packed[half].at[m * block : (m + 1) * block, lanes(i)]
                at = pl.ds(pl.multiple_of((2 * m + (ci ^ half)) * block, 16), block)
                pltpu.make_async_copy(src, weight.at[at], in_sem.at[i]).start()
    loads = [pltpu.make_async_copy(w, w, in_sem.at[i]) for i, w in enumerate(weights)]

    def group_rows(r):
        other = (2 * (xi ^ (r // 2))) + (ci ^ (r % 2))
        return pl.ds(pl.multiple_of(other * OWN_WIDTH, HEAD_DIM), OWN_WIDTH)

    obias, gain1, shift1, sbias, gain2, shift2 = [vec_ref[i : i + 1, :] for i in range(2, 8)]
    loads[0].wait()
    branch = obias + jnp.zeros((rows, width), f32)
    for r in range(4):
        branch += jnp.dot(att_refs[r][...], wo[group_rows(r), :], preferred_element_type=f32)
    hidden, normal1, inverse1 = norm_forward(x_ref[...].astype(f32) + branch, gain1, shift1)
    hidden_low = hidden.astype(bf16)
    shrunk = sbias + hidden
    for k in range(fold):
        loads[1 + k].wait()
        expanded = jnp.dot(hidden_low, w1[k], preferred_element_type=f32) + eb_ref[k : k + 1, :]
        cdf = 0.5 * (1.0 + lax.erf(expanded * (2.0**-0.5)))
        pdf = jnp.exp(-0.5 * expanded * expanded) * ((2.0 * math.pi) ** -0.5)
        act[k] = (expanded * cdf).astype(bf16)
        slope[k] = cdf + expanded * pdf
        loads[1 + fold + k].wait()
        shrunk += jnp.dot(act[k], w2[k], preferred_element_type=f32)
    result, normal2, inverse2 = norm_forward(shrunk, gain2, shift2)
    out_ref[...] = result.astype(bf16)
    row = lax.broadcasted_iota(jnp.int32, (rows, width), 0)
    seed = jnp.where(start + row < length, cot_ref[...].astype(f32), 0.0)
    vec_out[4:5, :] = jnp.sum(seed * normal2, axis=0, keepdims=True)
    vec_out[5:6, :] = jnp.sum(seed, axis=0, keepdims=True)
    resid2 = norm_backward(seed, gain2, normal2, inverse2)
    shrunk_low = resid2.astype(bf16)
    vec_out[3:4, :] = jnp.sum(shrunk_low.astype(f32), axis=0, keepdims=True)
    hidden_grad = resid2
    for k in range(fold):
        active_grad = lax.dot_general(
            shrunk_low, w2[k], CONTRACT_LAST, preferred_element_type=f32
        )
        expanded_low = (active_grad * slope[k]).astype(bf16)
        vec_out[8 + k : 9 + k, :] = jnp.sum(expanded_low.astype(f32), axis=0, keepdims=True)
        hidden_grad += lax.dot_general(
            expanded_low, w1[k], CONTRACT_LAST, preferred_element_type=f32
        )
        g2[k] = lax.dot_general(
            act[k], shrunk_low, CONTRACT_FIRST, preferred_element_type=f32
        ).astype(bf16)
        g1[k] = lax.dot_general(
            hidden_low, expanded_low, CONTRACT_FIRST, preferred_element_type=f32
        ).astype(bf16)
    vec_out[1:2, :] = jnp.sum(hidden_grad * normal1, axis=0, keepdims=True)
    vec_out[2:3, :] = jnp.sum(hidden_grad, axis=0, keepdims=True)
    resid1 = norm_backward(hidden_grad, gain1, normal1, inverse1)
    resid_ref[...] = resid1
    branch_low = resid1.astype(bf16)
    vec_out[0:1, :] = jnp.sum(branch_low.astype(f32), axis=0, keepdims=True)
    vec_out[6:8, :] = jnp.zeros((2, width), f32)
    vec_out[8 + fold :, :] = jnp.zeros((vec_out.shape[0] - 8 - fold, width), f32)
    for r in range(4):
        da_refs[r][...] = lax.dot_general(
            branch_low, wo[group_rows(r), :], CONTRACT_LAST, preferred_element_type=f32
        ).astype(bf16)
        go[group_rows(r), :] = lax.dot_general(
            att_refs[r][...], branch_low, CONTRACT_FIRST, preferred_element_type=f32
        ).astype(bf16)
    units = [g2.at[k] for k in range(fold)] + [g1.at[k] for k in range(fold)] + [go]
    if aligned:
        *parts, whole = unit_parts(fold)
        for i, part in enumerate(parts):
            for dc in range(2):
                target, sem = targets[2 * i + dc], out_sem.at[2 * i + dc]
                for dx in range(2):
                    for jz in range(n_q):
                        m = ((zi ^ jz) * 2 + (xi ^ dx)) * 2 + (ci ^ dc)
                        at = pl.ds(pl.multiple_of(m * block, 16), block)
                        for place, unit in enumerate(part):
                            dst = target.at[dx, jz, :, lanes(place)]
                            pltpu.make_async_copy(units[unit].at[at], dst, sem).start()
        for place, unit in enumerate(whole):
            dst = targets[-1].at[:, lanes(place)]
            pltpu.make_async_copy(units[unit], dst, out_sem.at[len(targets) - 1]).start()
    else:
        for i, unit in enumerate(units):
            pltpu.make_async_copy(unit, targets[0].at[:, lanes(i)], out_sem.at[0]).start()
    for i, dst in enumerate(targets):
        pltpu.make_async_copy(dst, dst, out_sem.at[i]).wait()


def unit_parts(fold):
    count = 1 + 2 * fold
    edges = [count * i // 3 for i in range(4)]
    return [range(edges[i], edges[i + 1]) for i in range(3)]


def ffn_block(layout, where, att, x, cot, vectors, ebias, packed):
    n_q, n_b, own_rows, fold, aligned = layout
    rows, width = x.shape
    ff = fold * width
    operands = [where, *att, x, cot, vectors, ebias, *[in_hbm(v) for v in packed]]
    in_specs = [pl.BlockSpec(memory_space=pltpu.SMEM)] + vmem_specs(8)
    in_specs += [pl.BlockSpec(memory_space=pltpu.HBM)] * len(packed)
    out_shape = [
        jax.ShapeDtypeStruct((rows, width), bf16),
        jax.ShapeDtypeStruct((rows, width), f32),
        *[jax.ShapeDtypeStruct((rows, OWN_WIDTH), bf16)] * 4,
        jax.ShapeDtypeStruct((16, width), f32),
    ]
    if aligned:
        lead = (2, n_q, n_b * own_rows)
        sizes = [len(part) * width for part in unit_parts(fold)]
        targets = [pltpu.HBM((*lead, size), bf16) for size in sizes[:-1] for _ in range(2)]
        targets.append(pltpu.HBM((width, sizes[-1]), bf16))
    else:
        targets = [pltpu.HBM((width, width + 2 * ff), bf16)]
    weight_scratch = [
        pltpu.VMEM((width, width), bf16),
        pltpu.VMEM((fold, width, width), bf16),
        pltpu.VMEM((fold, width, width), bf16),
    ]
    return pl.pallas_call(
        partial(ffn_kernel, layout),
        out_shape=out_shape + targets,
        in_specs=in_specs,
        out_specs=vmem_specs(len(out_shape)) + [pl.BlockSpec(memory_space=pltpu.HBM)] * len(targets),
        scratch_shapes=weight_scratch
        + weight_scratch
        + [
            pltpu.VMEM((fold, rows, width), bf16),
            pltpu.VMEM((fold, rows, width), f32),
            pltpu.SemaphoreType.DMA((1 + 2 * fold,)),
            pltpu.SemaphoreType.DMA((6,)),
        ],
        compiler_params=pltpu.CompilerParams(vmem_limit_bytes=32 * MIB),
        cost_estimate=pl.CostEstimate(
            flops=int(2e10), transcendentals=2 * rows * ff, bytes_accessed=int(3e7)
        ),
        name="feed_forward",
    )(*operands)


def order_kernel(n_q, n_b, where_ref, blocks_ref, out_ref):
    group, zi, bi = [where_ref[i] for i in range(3)]
    rows = blocks_ref.shape[3]
    for m in range(4 * n_q):
        q, g = m // 4, m % 4
        far, r = lax.rem(q + n_q - zi, n_q), g ^ group
        both = [
            blocks_ref[lax.rem(b + n_b - bi, n_b), far, r].astype(f32) for b in range(n_b)
        ]
        at = slice(m * n_b * rows, (m + 1) * n_b * rows)
        out_ref[at, :] = jnp.concatenate(both, axis=0).astype(bf16)


def order_rows(n_q, n_b, where, blocks):
    rows, lanes = blocks.shape[3:]
    return pl.pallas_call(
        partial(order_kernel, n_q, n_b),
        out_shape=jax.ShapeDtypeStruct((4 * n_q * n_b * rows, lanes), bf16),
        in_specs=[pl.BlockSpec(memory_space=pltpu.SMEM)] + vmem_specs(1),
        out_specs=vmem_specs(1)[0],
        compiler_params=pltpu.CompilerParams(vmem_limit_bytes=12 * MIB),
        name="order_rows",
    )(where, blocks)


def from_shift(value, axis, count, step):
    return lax.ppermute(value, axis, [((i + step) % count, i) for i in range(count)])


def square_swap(value, r):
    if r == 0:
        return value
    if r == 1:
        return lax.ppermute(value, "c", [(0, 1), (1, 0)])
    if r == 2:
        return lax.ppermute(value, "x", [(0, 1), (1, 0)])
    return lax.ppermute(value, ("x", "c"), [(0, 3), (3, 0), (1, 2), (2, 1)])


def pick(stacked, index, dim=0):
    return lax.dynamic_index_in_dim(stacked, index, dim, keepdims=False)


class Chain:
    def __init__(self, state, *steps):
        self.state, self.steps = tuple(state), list(steps)


def launch(chain):
    chain.state = tuple(chain.steps.pop(0)(*chain.state))


def run_stage(chains, outs=(), settle=()):
    for chain in chains:
        launch(chain)
    joined = [*chains, *settle]
    outs, states = lax.optimization_barrier((tuple(outs), [c.state for c in joined]))
    for chain, state in zip(joined, states):
        chain.state = tuple(state)
    return outs


def away_sum(total, axis, count):
    parts = [total[j].astype(bf16) for j in range(1, count)]
    return [from_shift(part, axis, count, count - j - 1) for j, part in enumerate(parts)]


def weight_sum(keep, send, n_q, n_b, bi, order):
    def own_b(keep, got, j):
        shape = (2, n_q, n_b, -1, keep.shape[-1])
        both = [pick(v.reshape(shape), (bi + j) % n_b, 2).astype(f32) for v in (keep, got)]
        return both[0] + both[1]

    def over_core(keep, send):
        return keep, square_swap(send, 1)

    def over_b(keep, got):
        if order:
            keep = lax.optimization_barrier((keep, order.pop()))[0]
        away = [own_b(keep, got, j).astype(bf16) for j in range(1, n_b)]
        order.append(away[0])
        return keep, got, *[from_shift(v, "b", n_b, n_b - 1 - j) for j, v in enumerate(away)]

    def over_x(keep, got, *more):
        total = own_b(keep, got, 0) + sum(v.astype(f32) for v in more)
        return total[0], *away_sum(total, "x", 2)

    def halve(half):
        def over_q(own, got):
            total = own + got.astype(f32)
            pairs = [(i, i ^ half) for i in range(n_q)]
            return total[:half], lax.ppermute(total[half:].astype(bf16), "q", pairs)

        return over_q

    halves = [n_q >> (k + 1) for k in range(n_q.bit_length() - 1)]
    return Chain((keep, send), over_core, over_b, over_x, *[halve(half) for half in halves])


def toward(j, n_q):
    return (j - 1, n_q - 1) if 2 * j <= n_q else ((j + 1) % n_q, 1)


def token_sum(keep, send, n_q, j, farther):
    def over_core(keep, send):
        return keep, square_swap(send, 1)

    def over_x(keep, got):
        total = keep.astype(f32) + got.astype(f32)
        return total[0], square_swap(total[1].astype(bf16), 2)

    def over_q(own, got):
        total = own + got.astype(f32) + sum(chain_sum(c) for c in farther)
        return (from_shift(total.astype(bf16), "q", n_q, toward(j, n_q)[1]),)

    return Chain((keep, send), over_core, over_x, *([over_q] if j else []))


def chain_sum(chain):
    return sum(v.astype(f32).reshape(chain.state[0].shape) for v in chain.state)


def deinterleave(fold):
    size = fold * LANES
    lane = jnp.arange(size)
    return (lane[:, None] // fold + (lane[:, None] % fold) * LANES == lane[None, :]).astype(bf16)


def per_device(
    n_q,
    n_b,
    inputs,
    lengths,
    cotangent,
    triple_weight,
    query_bias,
    value_bias,
    output_weight,
    output_bias,
    first_gain,
    first_shift,
    expand_weight,
    expand_bias,
    shrink_weight,
    shrink_bias,
    second_gain,
    second_shift,
):
    zi, xi, ci, bi = [lax.axis_index(a) for a in AXES]
    group = 2 * xi + ci
    _, seq_rows, width = inputs.shape
    own_rows = triple_weight.shape[0]
    ff = expand_weight.shape[1]
    fold = ff // width
    aligned = n_b * own_rows % 16 == 0 and n_q & (n_q - 1) == 0
    x_own = inputs[0]

    turn = deinterleave(fold)
    expand_own = expand_weight.astype(bf16).reshape(own_rows, -1, fold * LANES)
    expand_own = jnp.einsum("rbs,st->rbt", expand_own, turn, preferred_element_type=f32)
    expand_own = expand_own.astype(bf16).reshape(own_rows, -1, fold, LANES).transpose(0, 2, 1, 3)
    packed = jnp.concatenate(
        [
            output_weight.astype(bf16),
            expand_own.reshape(own_rows, ff),
            shrink_weight.astype(bf16).reshape(own_rows, ff),
        ],
        axis=1,
    )
    if aligned:
        own_half = lax.all_gather(packed, ("q", "x", "b"), axis=0, tiled=True)
    else:
        gathered_ffn = [lax.all_gather(packed, AXES, axis=0, tiled=True)]

    names = [query_bias, value_bias, output_bias, first_gain, first_shift]
    names += [shrink_bias, second_gain, second_shift]
    vectors = jnp.stack(names, axis=1)
    vectors = jnp.concatenate([vectors, expand_bias.reshape(own_rows, fold)], axis=1).astype(bf16)
    n_vec = vectors.shape[1]
    vectors = jnp.pad(vectors, ((0, 0), (0, WIDE - VECTORS - n_vec)))
    thirds = triple_weight.astype(bf16).reshape(own_rows, 3, GROUPS, OWN_WIDTH)

    def columns_of(g):
        mine = [pick(thirds[:, t], g, 1) for t in range(3)]
        return jnp.concatenate(mine + [vectors], axis=1)

    def rows_square(*blocks):
        return [square_swap(block, r) for r, block in enumerate(blocks)]

    def rows_q(*blocks):
        square = jnp.stack(blocks)
        return [square] + [from_shift(square, "q", n_q, j) for j in range(1, n_q)]

    def rows_b(*blocks):
        both = jnp.stack(blocks)
        return [both] + [from_shift(both, "b", n_b, j) for j in range(1, n_b)]

    weight_rows = Chain([columns_of(group ^ r) for r in range(4)], rows_square, rows_q, rows_b)

    def token_chunk(j):
        def over_q():
            source, step = toward(j, n_q)
            own = chunks[source].state[0] if source else x_own
            if j not in arrival[:2]:
                before = line[arrival.index(j) - 1].state[0] if j != arrival[2] else weight_rows.state
                own = lax.optimization_barrier((own, before))[0]
            return (from_shift(own, "q", n_q, n_q - step),)

        def over_x(own):
            return own, square_swap(own, 2)

        def over_core(own, other):
            halves = square_swap(jnp.stack([own, other]), 1)
            return own, halves[0], other, halves[1]

        return Chain(() if j else (x_own,), *([over_q] if j else []), over_x, over_core)

    arrival = []
    for j in [k for pair in zip(range(1, n_q), range(n_q - 1, 0, -1)) for k in pair]:
        arrival += [] if j in arrival else [j]
    arrival = [0] + arrival
    chunks = {j: token_chunk(j) for j in arrival}
    line = [chunks[j] for j in arrival]


    for slot in range(3):
        run_stage([weight_rows] + [c for c in line[:2] if c.steps and (slot < 2 or c is line[1])])
    chunk_x = {}

    by_distance = jnp.stack(weight_rows.state)
    if aligned:
        spot = jnp.stack([group, zi, bi]).astype(jnp.int32)
        w_own = order_rows(n_q, n_b, spot, by_distance)
    else:
        ordered = jnp.stack([pick(by_distance, (i - bi) % n_b) for i in range(n_b)], axis=3)
        ordered = jnp.stack([pick(ordered, group ^ g, 1) for g in range(4)], axis=1)
        ordered = jnp.stack([pick(ordered, (i - zi) % n_q) for i in range(n_q)])
        w_own = ordered.transpose(0, 1, 3, 2, 4).reshape(width, WIDE)
    turned = w_own[:, VECTORS : VECTORS + n_vec].astype(f32)
    turned = turned.T
    ebias = turned[8:]
    turned = turned[:8]
    own_bias = lax.dynamic_slice_in_dim(turned, group * OWN_WIDTH, OWN_WIDTH, 1)
    zero = jnp.zeros((1, OWN_WIDTH), f32)
    bias_row = jnp.concatenate(
        [own_bias[:1], zero, own_bias[1:2], jnp.zeros((1, WIDE - VECTORS), f32)], axis=1
    )

    def where_of(j):
        zj = (zi + j) % n_q
        spots = [(zj * 4 + (group ^ r)) * seq_rows for r in range(4)]
        return jnp.stack(spots + [lengths[0]]).astype(jnp.int32)

    weights = (w_own, bias_row)
    kept = {}
    carry = None
    for step, j in enumerate(arrival):
        first, last = step == 0, step == n_q - 1
        if chunks[j].steps:
            run_stage([chunks[j]])
        chunk_x[j] = chunks[j].state
        outs = attend_chunk(first, last, where_of(j), chunk_x[j], weights, carry)
        outs = run_stage([c for i in (step + 1, step + 2) if i > 1 for c in line[i : i + 1]], outs)
        kept[j] = (outs[0], outs[1])
        outs = outs[2:]
        if first:
            qx, qp = outs[:2]
            outs = outs[2:]
        carry = (qx, *outs)
    att, attx, qx2 = carry[1:5], carry[5], carry[6]

    if aligned:
        own_half, att = lax.optimization_barrier((own_half, att))
        gathered_ffn = [own_half, square_swap(own_half, 1)]
    att = [square_swap(att[r], r) for r in range(4)]
    start = (zi * 4 + group) * seq_rows
    where = jnp.stack([group, zi, xi, ci, bi, start, lengths[0]]).astype(jnp.int32)
    layout = (n_q, n_b, own_rows, fold, aligned)
    outs = ffn_block(layout, where, att, x_own, cotangent[0], turned, ebias, gathered_ffn)
    output, resid_first_grad = outs[:2]
    att_grads, vec_grads, summands = outs[2:6], outs[6], outs[7:]
    square = Chain(att_grads, lambda *parts: [square_swap(v, r) for r, v in enumerate(parts)])

    sums, order = [], []
    if aligned:
        for i in range(2):
            sums.append(weight_sum(summands[2 * i], summands[2 * i + 1], n_q, n_b, bi, order))
    summed = lax.psum_scatter(summands[-1], AXES, scatter_dimension=0, tiled=True).astype(f32)
    run_stage([square] + sums)
    plan = [
        ([0], [], [1], []),
        ([0], [1], [], []),
        ([1, 0], [], [], []),
        ([1, 0], [], [], []),
    ]
    shared = (qx2, qp, w_own, square.state, attx)
    carry = None
    moving, moving_to = [], {}
    for step, j in enumerate(reversed(arrival)):
        first, last = step == 0, step == n_q - 1
        with_it, ending, going_on, after_it = [], [], [], []
        if sums and step < len(plan):
            with_it, ending, going_on, after_it = [[sums[i] for i in part] for part in plan[step]]
        outs = attend_back_chunk(first, last, kept[j], chunk_x[j], shared, carry)
        run = with_it + [c for c in moving if c.steps]
        for chain in run + going_on:
            launch(chain)
        outs = run_stage([], outs, settle=run + ending)
        keep, send = outs[:2]
        farther = [c for k, c in moving_to.items() if k and toward(k, n_q)[0] == j and j]
        moving_to[j] = token_sum(keep, send, n_q, j, farther)
        moving.append(moving_to[j])
        outs = outs[2:]
        if first:
            dox = outs[0]
            outs = outs[1:]
        carry = (dox, *outs)
        if not last:
            carry = run_stage(moving[-1:], carry, settle=after_it)
    grad_joint, col = carry[1:]

    own_bias = jnp.stack([col[0, :OWN_WIDTH], col[0, 2 * OWN_WIDTH : 3 * OWN_WIDTH]])
    bias_grads = lax.dynamic_update_slice(
        jnp.zeros((2, width), f32), own_bias, (0, group * OWN_WIDTH)
    )
    tall = jnp.concatenate([bias_grads, vec_grads[:6], vec_grads[8 : 8 + fold]], axis=0).T
    tall_high = tall.astype(bf16)
    tall_low = (tall - tall_high.astype(f32)).astype(bf16)
    room = jnp.zeros((width, WIDE - VECTORS - 2 * n_vec), bf16)
    blocks = jnp.concatenate([grad_joint[:, :VECTORS], tall_high, tall_low, room], axis=1)
    total = blocks.reshape(n_q, 4, n_b, own_rows, WIDE)

    def rows_over_b(total):
        parts = [pick(total, (bi + j) % n_b, 2) for j in range(n_b)]
        return parts[0], *away_sum(parts, "b", n_b)

    def rows_over_q(*parts):
        total = sum(v.astype(f32) for v in parts)
        parts = [pick(total, (zi + j) % n_q) for j in range(n_q)]
        return parts[0], *away_sum(parts, "q", n_q)

    def rows_over_square(*parts):
        total = sum(v.astype(f32) for v in parts).astype(bf16)
        return [square_swap(pick(total, group ^ r), r) for r in range(4)]

    rows = Chain((total,), rows_over_b, rows_over_q, rows_over_square)
    run_stage([], settle=[rows, *sums, *moving])
    while any(c.steps for c in [rows, *sums, *moving]):
        run_stage([c for c in [rows, *sums, *moving] if c.steps])
    summed = lax.optimization_barrier((summed, rows.state))[0]
    token_grad = resid_first_grad
    for j, chain in moving_to.items():
        if j == 0 or toward(j, n_q)[0] == 0:
            token_grad = token_grad + chain_sum(chain)
    input_grad = token_grad.astype(bf16)
    if aligned:
        summed = jnp.concatenate([*[chain_sum(c)[0] for c in sums], summed], axis=1)
    parts = jnp.stack(rows.state)
    parts = jnp.stack([pick(parts, group ^ g) for g in range(4)])
    grad_triple = parts[:, :, :VECTORS].reshape(GROUPS, own_rows, 3, OWN_WIDTH)
    grad_triple = grad_triple.transpose(1, 2, 0, 3).reshape(own_rows, -1).astype(f32)
    small = jnp.sum(parts[:, :, VECTORS : VECTORS + 2 * n_vec].astype(f32), axis=0)
    small = small[:, :n_vec] + small[:, n_vec:]
    grad_expand = summed[:, ff : 2 * ff].reshape(own_rows, fold, -1, LANES).transpose(0, 2, 1, 3)
    grad_expand = jnp.einsum(
        "rbs,ts->rbt",
        grad_expand.reshape(own_rows, -1, fold * LANES),
        turn.astype(f32),
        precision=lax.Precision.HIGHEST,
        preferred_element_type=f32,
    ).reshape(own_rows, ff)
    return (
        output[None],
        input_grad[None],
        grad_triple,
        small[:, 0],
        small[:, 1],
        summed[:, 2 * ff :],
        small[:, 2],
        small[:, 3],
        small[:, 4],
        grad_expand,
        small[:, 8:].reshape(-1),
        summed[:, :ff].reshape(-1, width),
        small[:, 5],
        small[:, 6],
        small[:, 7],
    )


def solution(mesh):
    n_seq, n_b = mesh.shape["seq"], mesh.shape["batch"]
    n_q = n_seq // GROUPS
    fine = Mesh(mesh.devices.reshape(n_q, 2, 2, n_b), AXES)
    tokens = P("b", ("q", "x", "c"), None)
    matrix = P(AXES, None)
    vector = P(AXES)
    in_specs = (
        tokens,
        P("b"),
        tokens,
        matrix,
        vector,
        vector,
        matrix,
        vector,
        vector,
        vector,
        matrix,
        vector,
        matrix,
        vector,
        vector,
        vector,
    )
    out_specs = (
        tokens,
        tokens,
        matrix,
        vector,
        vector,
        matrix,
        vector,
        vector,
        vector,
        matrix,
        vector,
        matrix,
        vector,
        vector,
        vector,
    )
    return jax.shard_map(
        partial(per_device, n_q, n_b),
        mesh=fine,
        in_specs=in_specs,
        out_specs=out_specs,
        check_vma=False,
    )
```

```python
from functools import partial
import math

import jax
import jax.numpy as jnp
from jax import lax
from jax.experimental import pallas as pl
from jax.experimental.pallas import tpu as pltpu
from jax.sharding import Mesh, PartitionSpec as P

HEADS = 12
HEAD_DIM = 64
GROUPS = 4
OWN_HEADS = HEADS // GROUPS
OWN_WIDTH = OWN_HEADS * HEAD_DIM
LANES = 128
WIDE = 640
VECTORS = 3 * OWN_WIDTH

bf16 = jnp.bfloat16
f32 = jnp.float32
masked_score = -1e30
norm_eps = 1e-12
log2_e = 1.4426950408889634
CONTRACT_LAST = (((1,), (1,)), ((), ()))
MIB = 1024 * 1024
AXES = ("q", "x", "c", "b")


def split_three(value):
    high = value.astype(bf16).astype(f32)
    rest = value - high
    mid = rest.astype(bf16).astype(f32)
    low = (rest - mid).astype(bf16).astype(f32)
    return high, mid, low


def low_half(tile, lane, from_high):
    turned = pltpu.roll(tile, HEAD_DIM, 1)
    low = lane < HEAD_DIM
    return jnp.where(low, turned, tile) if from_high else jnp.where(low, tile, turned)


def place_of(kind, h):
    slot = kind * OWN_HEADS + h
    return slot // 2, slot % 2


def forward_kernel(first, last, block_q, block_k, *refs):
    refs = list(refs)
    where_ref = refs.pop(0)
    far = [refs.pop(0) for _ in range(5)]
    bias_ref = refs.pop(0)
    if not first:
        qx_ref, peak_in, sum_in = [refs.pop(0) for _ in range(3)]
    kept = [refs.pop(0) for _ in range(2)]
    if first:
        qx_ref, qp_ref = [refs.pop(0) for _ in range(2)]
    if last:
        att_refs = [refs.pop(0) for _ in range(4)]
        attx_ref, qx2_ref = [refs.pop(0) for _ in range(2)]
    else:
        peak_out, sum_out = [refs.pop(0) for _ in range(2)]
    vt_ref, kx_ref, vx_ref, sem, *near = refs
    loads = [pltpu.make_async_copy(f, n, sem.at[2 + i]) for i, (f, n) in enumerate(zip(far, near))]
    for i in (4, 0, 1, 2, 3):
        loads[i].start()
    *pieces, w_ref = near
    stores = [
        pltpu.make_async_copy(kx_ref, kept[0], sem.at[0]),
        pltpu.make_async_copy(vx_ref, kept[1], sem.at[1]),
    ]
    piece_rows = pieces[0].shape[0]
    rows_in = 4 * piece_rows
    lane = lax.broadcasted_iota(jnp.int32, (piece_rows, LANES), 1)
    row = lax.broadcasted_iota(jnp.int32, (piece_rows, LANES), 0)
    low = lane < HEAD_DIM
    length = where_ref[4]
    three = (lane >= HEAD_DIM) & (lane < HEAD_DIM + 3)
    skip = 0 if first else LANES
    for p in range(4):
        rows = slice(p * piece_rows, (p + 1) * piece_rows)
        if p == 0:
            loads[4].wait()
        loads[p].wait()
        joint = jnp.dot(pieces[p][...], w_ref[:, skip:], preferred_element_type=f32)
        joint = joint + bias_ref[:, skip:]
        bias = jnp.where(where_ref[p] + row < length, 0.0, masked_score)
        key_extra = jnp.where(three, 1.0, jnp.where(lane == HEAD_DIM + 3, bias, 0.0))

        def head_of(kind, h):
            tile, high = place_of(kind, h)
            return low_half(joint[:, tile * LANES - skip : (tile + 1) * LANES - skip], lane, high)

        for h in range(OWN_HEADS):
            k = head_of(1, h)
            kx_ref[h, rows, :LANES] = k.astype(bf16)
            kx_ref[h, rows, LANES:] = jnp.where(low, k, key_extra).astype(bf16)
            v = jnp.where(low, head_of(2, h), 0.0)
            vx_ref[h, rows, :] = jnp.where(three, -1.0, v).astype(bf16)
            vt = jnp.where(lane == HEAD_DIM, 1.0, v).T
            vt_ref[h, :, rows] = vt[:80].astype(bf16)
            if first:
                q = head_of(0, h).astype(bf16).astype(f32)
                qp_ref[h, rows, :] = jnp.where(low, q, 0.0).astype(bf16)
                high, mid, rest = split_three(q * (HEAD_DIM**-0.5 * log2_e))
                qx_ref[h, rows, :LANES] = jnp.where(low, high, mid).astype(bf16)
                one = jnp.where(lane == HEAD_DIM + 3, 1.0, 0.0)
                qx_ref[h, rows, LANES:] = jnp.where(low, rest, one).astype(bf16)
    for store in stores:
        store.start()
    for h in range(OWN_HEADS):
        for i in range(rows_in // block_q):
            cols = slice(i * block_q, (i + 1) * block_q)
            q = qx_ref[h, cols, :]
            if first:
                peak = jnp.full((1, block_q), masked_score, f32)
                total = jnp.zeros((80, block_q), f32)
            else:
                peak = peak_in[h, :1, cols]
                total = sum_in[h, :, cols]
            for j in range(rows_in // block_k):
                ks = slice(j * block_k, (j + 1) * block_k)
                s = lax.dot_general(kx_ref[h, ks, :], q, CONTRACT_LAST, preferred_element_type=f32)
                new_peak = jnp.maximum(peak, jnp.max(s, axis=0, keepdims=True))
                prob = jnp.exp2(s - new_peak).astype(bf16)
                total = total * jnp.exp2(peak - new_peak) + jnp.dot(
                    vt_ref[h, :, ks], prob, preferred_element_type=f32
                )
                peak = new_peak
            if last:
                denom = total[HEAD_DIM : HEAD_DIM + 1]
                n_high, n_mid, n_low = split_three(-(peak + jnp.log2(denom)))
                tall = jnp.concatenate(
                    [
                        total[:HEAD_DIM] / denom,
                        n_high,
                        n_mid,
                        n_low,
                        jnp.zeros((HEAD_DIM - 3, block_q), f32),
                    ],
                    axis=0,
                )
                attx_ref[h, cols, :] = tall.T
            else:
                peak_out[h, :, cols] = jnp.broadcast_to(peak, (8, block_q))
                sum_out[h, :, cols] = total
    if last:
        for p in range(4):
            rows = slice(p * piece_rows, (p + 1) * piece_rows)
            heads = [attx_ref[h, rows, :] for h in range(OWN_HEADS)]
            pair = jnp.where(low, heads[0], pltpu.roll(heads[1], HEAD_DIM, 1))
            att_refs[p][:, :LANES] = pair.astype(bf16)
            att_refs[p][:, LANES:] = heads[2][:, :HEAD_DIM].astype(bf16)
            for h in range(OWN_HEADS):
                qx2_ref[h, rows, :LANES] = qx_ref[h, rows, :LANES]
                old = qx_ref[h, rows, LANES:].astype(f32)
                qx2_ref[h, rows, LANES:] = jnp.where(three, heads[h], old).astype(bf16)
    for store in stores:
        store.wait()


def in_hbm(value):
    return pltpu.with_memory_space_constraint(value, pltpu.HBM)


def vmem_specs(n):
    return [pl.BlockSpec(memory_space=pltpu.VMEM) for _ in range(n)]


def attend_chunk(first, last, where, pieces, weights, carry):
    piece_rows = pieces[0].shape[0]
    rows = 4 * piece_rows
    w, bias_row = weights
    far = [in_hbm(v) for v in (*pieces, w)]
    operands = [where, *far, bias_row]
    operands += [] if first else list(carry)
    wide_keys = jax.ShapeDtypeStruct((OWN_HEADS, rows, 2 * LANES), bf16)
    out_shape = [pltpu.HBM(wide_keys.shape, bf16), pltpu.HBM((OWN_HEADS, rows, LANES), bf16)]
    if first:
        out_shape += [wide_keys, jax.ShapeDtypeStruct((OWN_HEADS, rows, LANES), bf16)]
    if last:
        out_shape += [jax.ShapeDtypeStruct((piece_rows, OWN_WIDTH), bf16)] * 4
        out_shape += [jax.ShapeDtypeStruct((OWN_HEADS, rows, LANES), f32), wide_keys]
    else:
        out_shape += [
            jax.ShapeDtypeStruct((OWN_HEADS, 8, rows), f32),
            jax.ShapeDtypeStruct((OWN_HEADS, 80, rows), f32),
        ]
    return pl.pallas_call(
        partial(forward_kernel, first, last, min(1024, rows), min(1024, rows)),
        out_shape=out_shape,
        in_specs=[pl.BlockSpec(memory_space=pltpu.SMEM)]
        + [pl.BlockSpec(memory_space=pltpu.HBM)] * len(far)
        + vmem_specs(len(operands) - 1 - len(far)),
        out_specs=[pl.BlockSpec(memory_space=pltpu.HBM)] * 2 + vmem_specs(len(out_shape) - 2),
        scratch_shapes=[
            pltpu.VMEM((OWN_HEADS, 80, rows), bf16),
            pltpu.VMEM((OWN_HEADS, rows, 2 * LANES), bf16),
            pltpu.VMEM((OWN_HEADS, rows, LANES), bf16),
            pltpu.SemaphoreType.DMA((7,)),
            *[pltpu.VMEM(v.shape, v.dtype) for v in (*pieces, w)],
        ],
        compiler_params=pltpu.CompilerParams(vmem_limit_bytes=20 * MIB),
        cost_estimate=pl.CostEstimate(
            flops=int(8e9), transcendentals=OWN_HEADS * rows * rows, bytes_accessed=int(1e7)
        ),
        name="attend_forward",
    )(*operands)


def backward_kernel(first, last, block_q, block_k, *refs):
    refs = list(refs)
    far = [refs.pop(0) for _ in range(7)]
    qx_ref, qp_ref = [refs.pop(0) for _ in range(2)]
    if first:
        grads = [refs.pop(0) for _ in range(4)]
        attx_ref = refs.pop(0)
    else:
        dox_ref, dqt_in, dw_in, col_in = [refs.pop(0) for _ in range(4)]
    keep_ref, send_ref = [refs.pop(0) for _ in range(2)]
    if first:
        dox_ref = refs.pop(0)
    if last:
        dw_out, col_out = [refs.pop(0) for _ in range(2)]
        dqt_ref = refs.pop()
    else:
        dqt_ref, dw_out, col_out = [refs.pop(0) for _ in range(3)]
    kt_ref, all_ref, sem = refs[:3]
    near = refs[3:]
    kx_ref, vx_ref, w_ref, *pieces = near
    loads = []
    for f, n in zip(far[:2], near[:2]):
        loads += [(f.at[h], n.at[h]) for h in range(OWN_HEADS)]
    loads += list(zip(far[2:], near[2:]))
    loads = [pltpu.make_async_copy(f, n, sem.at[i]) for i, (f, n) in enumerate(loads)]
    for i in (0, OWN_HEADS, *range(1, OWN_HEADS), *range(OWN_HEADS + 1, len(loads))):
        loads[i].start()
    rows_in = kx_ref.shape[1]
    piece_rows = rows_in // 4
    scale = HEAD_DIM**-0.5
    lane = lax.broadcasted_iota(jnp.int32, (piece_rows, LANES), 1)
    if first:
        for p in range(4):
            rows = slice(p * piece_rows, (p + 1) * piece_rows)
            left = grads[p][:, :LANES].astype(f32)
            right = grads[p][:, LANES:].astype(f32)
            right = jnp.concatenate([right, jnp.zeros_like(right)], axis=1)
            for h, wide in enumerate((left, pltpu.roll(left, HEAD_DIM, 1), right)):
                grad = jnp.where(lane < HEAD_DIM, wide, 0.0)
                delta = jnp.sum(grad * attx_ref[h, rows, :], axis=1, keepdims=True)
                d_high, d_mid, d_low = split_three(delta)
                grad = jnp.where(lane == HEAD_DIM, d_high, grad)
                grad = jnp.where(lane == HEAD_DIM + 1, d_mid, grad)
                grad = jnp.where(lane == HEAD_DIM + 2, d_low, grad)
                dox_ref[h, rows, :] = grad.astype(bf16)
        dqt_ref[...] = jnp.zeros_like(dqt_ref)
    else:
        dqt_ref[...] = dqt_in[...]
    lane_k = lax.broadcasted_iota(jnp.int32, (block_k, LANES), 1)
    low_k = lane_k < HEAD_DIM
    for j in range(rows_in // block_k):
        ks = slice(j * block_k, (j + 1) * block_k)
        parts = {}
        for h in range(OWN_HEADS):
            if j == 0:
                loads[h].wait()
                loads[OWN_HEADS + h].wait()
                kt_ref[h] = kx_ref[h, :, LANES:].astype(f32).T[:HEAD_DIM].astype(bf16)
            k = kx_ref[h, ks, :]
            v = vx_ref[h, ks, :]
            kt = kt_ref[h, :, ks]
            dk = jnp.zeros((block_k, LANES), f32)
            dv = jnp.zeros((block_k, LANES), f32)
            for i in range(rows_in // block_q):
                qs = slice(i * block_q, (i + 1) * block_q)
                s = lax.dot_general(k, qx_ref[h, qs, :], CONTRACT_LAST, preferred_element_type=f32)
                prob = jnp.exp2(s)
                do = dox_ref[h, qs, :]
                dp = lax.dot_general(v, do, CONTRACT_LAST, preferred_element_type=f32)
                ds = (prob * dp).astype(bf16)
                dv = dv + jnp.dot(prob.astype(bf16), do, preferred_element_type=f32)
                dk = dk + jnp.dot(ds, qp_ref[h, qs, :], preferred_element_type=f32)
                dqt_ref[h, :, qs] += jnp.dot(kt, ds, preferred_element_type=f32)
            parts[OWN_HEADS + h] = dk * scale
            parts[2 * OWN_HEADS + h] = dv
        for tile in range(1, WIDE // LANES):
            left, right = parts.get(2 * tile), parts.get(2 * tile + 1)
            left = jnp.zeros((block_k, LANES), f32) if left is None else left
            right = 0.0 if right is None else pltpu.roll(right, HEAD_DIM, 1)
            both = jnp.where(low_k, left, right).astype(bf16)
            all_ref[ks, tile * LANES : (tile + 1) * LANES] = both
    if last:
        tall = jnp.concatenate([dqt_ref[0], dqt_ref[1]], axis=0) * scale
        all_ref[:, :LANES] = tall.T.astype(bf16)
        tall = dqt_ref[2] * scale
        tall = jnp.concatenate([tall, jnp.zeros_like(tall)], axis=0).T
        lane_all = lax.broadcasted_iota(jnp.int32, (rows_in, LANES), 1)
        old = all_ref[:, LANES : 2 * LANES].astype(f32)
        all_ref[:, LANES : 2 * LANES] = jnp.where(lane_all < HEAD_DIM, tall, old).astype(bf16)
    skip = 0 if last else LANES
    for load in loads[2 * OWN_HEADS :]:
        load.wait()
    d_weight = [None, None]
    for p in range(4):
        rows = slice(p * piece_rows, (p + 1) * piece_rows)
        own = all_ref[rows, skip:]
        dx = lax.dot_general(own, w_ref[:, skip:], CONTRACT_LAST, preferred_element_type=f32)
        out_ref = keep_ref if p % 2 == 0 else send_ref
        out_ref[p // 2] = dx.astype(bf16)
        piece = lax.dot_general(
            pieces[p][...], own, (((0,), (0,)), ((), ())), preferred_element_type=f32
        )
        d_weight[0] = piece if p == 0 else d_weight[0] + piece
        col = jnp.sum(own.astype(f32), axis=0, keepdims=True)
        d_weight[1] = col if p == 0 else d_weight[1] + col
    grad, col = d_weight
    if last:
        dw_out[:, :LANES] = grad[:, :LANES].astype(bf16)
        dw_out[:, LANES:] = (grad[:, LANES:] + dw_in[...]).astype(bf16)
        col_out[:, :LANES] = jnp.broadcast_to(col[:, :LANES], (8, LANES))
        col_out[:, LANES:] = col[:, LANES:] + col_in[...]
    elif first:
        dw_out[...] = grad
        col_out[...] = jnp.broadcast_to(col, col_out.shape)
    else:
        dw_out[...] = grad + dw_in[...]
        col_out[...] = col + col_in[...]


def attend_back_chunk(first, last, chunk, pieces, shared, carry):
    kx, vx = chunk
    qx2, qp, w, grads, attx = shared
    rows, width = kx.shape[1], w.shape[0]
    far = [in_hbm(v) for v in (kx, vx, w, *pieces)]
    operands = [*far, qx2, qp]
    operands += [*grads, attx] if first else list(carry)
    half = jax.ShapeDtypeStruct((2, rows // 4, width), bf16)
    out_shape = [half, half]
    scratch = [
        pltpu.VMEM((OWN_HEADS, HEAD_DIM, rows), bf16),
        pltpu.VMEM((rows, WIDE), bf16),
        pltpu.SemaphoreType.DMA((2 * OWN_HEADS + 5,)),
        *[pltpu.VMEM(v.shape, v.dtype) for v in far],
    ]
    if first:
        out_shape.append(jax.ShapeDtypeStruct((OWN_HEADS, rows, LANES), bf16))
    if last:
        out_shape.append(jax.ShapeDtypeStruct((width, WIDE), bf16))
        out_shape.append(jax.ShapeDtypeStruct((8, WIDE), f32))
        scratch.append(pltpu.VMEM((OWN_HEADS, HEAD_DIM, rows), f32))
    else:
        out_shape.append(jax.ShapeDtypeStruct((OWN_HEADS, HEAD_DIM, rows), f32))
        out_shape.append(jax.ShapeDtypeStruct((width, WIDE - LANES), f32))
        out_shape.append(jax.ShapeDtypeStruct((8, WIDE - LANES), f32))
    return pl.pallas_call(
        partial(backward_kernel, first, last, min(256, rows), min(1024, rows)),
        out_shape=out_shape,
        in_specs=[pl.BlockSpec(memory_space=pltpu.HBM)] * len(far)
        + vmem_specs(len(operands) - len(far)),
        out_specs=vmem_specs(len(out_shape)),
        scratch_shapes=scratch,
        compiler_params=pltpu.CompilerParams(vmem_limit_bytes=26 * MIB),
        cost_estimate=pl.CostEstimate(
            flops=int(1.5e10), transcendentals=OWN_HEADS * rows * rows, bytes_accessed=int(1e7)
        ),
        name="attend_backward",
    )(*operands)


def norm_forward(value, gain, shift):
    center = value - jnp.mean(value, axis=-1, keepdims=True)
    spread = jnp.mean(center * center, axis=-1, keepdims=True)
    inverse = lax.rsqrt(spread + norm_eps)
    normal = center * inverse
    return normal * gain + shift, normal, inverse


def norm_backward(grad, gain, normal, inverse):
    inner = grad * gain
    mean = jnp.mean(inner, axis=-1, keepdims=True)
    along = jnp.mean(inner * normal, axis=-1, keepdims=True)
    return inverse * (inner - mean - normal * along)


CONTRACT_FIRST = (((0,), (0,)), ((), ()))


def ffn_kernel(layout, *refs):
    n_q, n_b, own_rows, fold, aligned = layout
    refs = list(refs)
    where_ref = refs.pop(0)
    att_refs = [refs.pop(0) for _ in range(4)]
    x_ref, cot_ref, vec_ref, eb_ref = [refs.pop(0) for _ in range(4)]
    packed = [refs.pop(0) for _ in range(2 if aligned else 1)]
    out_ref, resid_ref = [refs.pop(0) for _ in range(2)]
    da_refs = [refs.pop(0) for _ in range(4)]
    vec_out = refs.pop(0)
    targets = [refs.pop(0) for _ in range(5 if aligned else 1)]
    wo, w1, w2, go, g1, g2, act, slope, in_sem, out_sem = refs
    group, zi, xi, ci, bi, start, length = [where_ref[i] for i in range(7)]
    rows, width = x_ref.shape

    def lanes(i):
        return slice(i * width, (i + 1) * width)

    weights = [wo, *[w1.at[k] for k in range(fold)], *[w2.at[k] for k in range(fold)]]
    block = n_b * own_rows
    for i, weight in enumerate(weights):
        if not aligned:
            pltpu.make_async_copy(packed[0].at[:, lanes(i)], weight, in_sem.at[i]).start()
            continue
        for half in range(2):
            for m in range(2 * n_q):
                src = packed[half].at[m * block : (m + 1) * block, lanes(i)]
                at = pl.ds(pl.multiple_of((2 * m + (ci ^ half)) * block, 16), block)
                pltpu.make_async_copy(src, weight.at[at], in_sem.at[i]).start()
    loads = [pltpu.make_async_copy(w, w, in_sem.at[i]) for i, w in enumerate(weights)]

    def group_rows(r):
        other = (2 * (xi ^ (r // 2))) + (ci ^ (r % 2))
        return pl.ds(pl.multiple_of(other * OWN_WIDTH, HEAD_DIM), OWN_WIDTH)

    obias, gain1, shift1, sbias, gain2, shift2 = [vec_ref[i : i + 1, :] for i in range(2, 8)]
    loads[0].wait()
    branch = obias + jnp.zeros((rows, width), f32)
    for r in range(4):
        branch += jnp.dot(att_refs[r][...], wo[group_rows(r), :], preferred_element_type=f32)
    hidden, normal1, inverse1 = norm_forward(x_ref[...].astype(f32) + branch, gain1, shift1)
    hidden_low = hidden.astype(bf16)
    shrunk = sbias + hidden
    for k in range(fold):
        loads[1 + k].wait()
        expanded = jnp.dot(hidden_low, w1[k], preferred_element_type=f32) + eb_ref[k : k + 1, :]
        cdf = 0.5 * (1.0 + lax.erf(expanded * (2.0**-0.5)))
        pdf = jnp.exp(-0.5 * expanded * expanded) * ((2.0 * math.pi) ** -0.5)
        act[k] = (expanded * cdf).astype(bf16)
        slope[k] = cdf + expanded * pdf
        loads[1 + fold + k].wait()
        shrunk += jnp.dot(act[k], w2[k], preferred_element_type=f32)
    result, normal2, inverse2 = norm_forward(shrunk, gain2, shift2)
    out_ref[...] = result.astype(bf16)
    row = lax.broadcasted_iota(jnp.int32, (rows, width), 0)
    seed = jnp.where(start + row < length, cot_ref[...].astype(f32), 0.0)
    vec_out[4:5, :] = jnp.sum(seed * normal2, axis=0, keepdims=True)
    vec_out[5:6, :] = jnp.sum(seed, axis=0, keepdims=True)
    resid2 = norm_backward(seed, gain2, normal2, inverse2)
    shrunk_low = resid2.astype(bf16)
    vec_out[3:4, :] = jnp.sum(shrunk_low.astype(f32), axis=0, keepdims=True)
    hidden_grad = resid2
    for k in range(fold):
        active_grad = lax.dot_general(
            shrunk_low, w2[k], CONTRACT_LAST, preferred_element_type=f32
        )
        expanded_low = (active_grad * slope[k]).astype(bf16)
        vec_out[8 + k : 9 + k, :] = jnp.sum(expanded_low.astype(f32), axis=0, keepdims=True)
        hidden_grad += lax.dot_general(
            expanded_low, w1[k], CONTRACT_LAST, preferred_element_type=f32
        )
        g2[k] = lax.dot_general(
            act[k], shrunk_low, CONTRACT_FIRST, preferred_element_type=f32
        ).astype(bf16)
        g1[k] = lax.dot_general(
            hidden_low, expanded_low, CONTRACT_FIRST, preferred_element_type=f32
        ).astype(bf16)
    vec_out[1:2, :] = jnp.sum(hidden_grad * normal1, axis=0, keepdims=True)
    vec_out[2:3, :] = jnp.sum(hidden_grad, axis=0, keepdims=True)
    resid1 = norm_backward(hidden_grad, gain1, normal1, inverse1)
    resid_ref[...] = resid1
    branch_low = resid1.astype(bf16)
    vec_out[0:1, :] = jnp.sum(branch_low.astype(f32), axis=0, keepdims=True)
    vec_out[6:8, :] = jnp.zeros((2, width), f32)
    vec_out[8 + fold :, :] = jnp.zeros((vec_out.shape[0] - 8 - fold, width), f32)
    for r in range(4):
        da_refs[r][...] = lax.dot_general(
            branch_low, wo[group_rows(r), :], CONTRACT_LAST, preferred_element_type=f32
        ).astype(bf16)
        go[group_rows(r), :] = lax.dot_general(
            att_refs[r][...], branch_low, CONTRACT_FIRST, preferred_element_type=f32
        ).astype(bf16)
    units = [g2.at[k] for k in range(fold)] + [g1.at[k] for k in range(fold)] + [go]
    if aligned:
        *parts, whole = unit_parts(fold)
        for i, part in enumerate(parts):
            for dc in range(2):
                target, sem = targets[2 * i + dc], out_sem.at[2 * i + dc]
                for dx in range(2):
                    for jz in range(n_q):
                        m = ((zi ^ jz) * 2 + (xi ^ dx)) * 2 + (ci ^ dc)
                        at = pl.ds(pl.multiple_of(m * block, 16), block)
                        for place, unit in enumerate(part):
                            dst = target.at[dx, jz, :, lanes(place)]
                            pltpu.make_async_copy(units[unit].at[at], dst, sem).start()
        for place, unit in enumerate(whole):
            dst = targets[-1].at[:, lanes(place)]
            pltpu.make_async_copy(units[unit], dst, out_sem.at[len(targets) - 1]).start()
    else:
        for i, unit in enumerate(units):
            pltpu.make_async_copy(unit, targets[0].at[:, lanes(i)], out_sem.at[0]).start()
    for i, dst in enumerate(targets):
        pltpu.make_async_copy(dst, dst, out_sem.at[i]).wait()


def unit_parts(fold):
    count = 1 + 2 * fold
    edges = [0, count // 3, (count + 1) // 2, count]
    return [range(edges[i], edges[i + 1]) for i in range(3)]


def ffn_block(layout, where, att, x, cot, vectors, ebias, packed):
    n_q, n_b, own_rows, fold, aligned = layout
    rows, width = x.shape
    ff = fold * width
    operands = [where, *att, x, cot, vectors, ebias, *[in_hbm(v) for v in packed]]
    in_specs = [pl.BlockSpec(memory_space=pltpu.SMEM)] + vmem_specs(8)
    in_specs += [pl.BlockSpec(memory_space=pltpu.HBM)] * len(packed)
    out_shape = [
        jax.ShapeDtypeStruct((rows, width), bf16),
        jax.ShapeDtypeStruct((rows, width), f32),
        *[jax.ShapeDtypeStruct((rows, OWN_WIDTH), bf16)] * 4,
        jax.ShapeDtypeStruct((16, width), f32),
    ]
    if aligned:
        lead = (2, n_q, n_b * own_rows)
        sizes = [len(part) * width for part in unit_parts(fold)]
        targets = [pltpu.HBM((*lead, size), bf16) for size in sizes[:-1] for _ in range(2)]
        targets.append(pltpu.HBM((width, sizes[-1]), bf16))
    else:
        targets = [pltpu.HBM((width, width + 2 * ff), bf16)]
    weight_scratch = [
        pltpu.VMEM((width, width), bf16),
        pltpu.VMEM((fold, width, width), bf16),
        pltpu.VMEM((fold, width, width), bf16),
    ]
    return pl.pallas_call(
        partial(ffn_kernel, layout),
        out_shape=out_shape + targets,
        in_specs=in_specs,
        out_specs=vmem_specs(len(out_shape)) + [pl.BlockSpec(memory_space=pltpu.HBM)] * len(targets),
        scratch_shapes=weight_scratch
        + weight_scratch
        + [
            pltpu.VMEM((fold, rows, width), bf16),
            pltpu.VMEM((fold, rows, width), f32),
            pltpu.SemaphoreType.DMA((1 + 2 * fold,)),
            pltpu.SemaphoreType.DMA((6,)),
        ],
        compiler_params=pltpu.CompilerParams(vmem_limit_bytes=32 * MIB),
        cost_estimate=pl.CostEstimate(
            flops=int(2e10), transcendentals=2 * rows * ff, bytes_accessed=int(3e7)
        ),
        name="feed_forward",
    )(*operands)


def order_kernel(n_q, n_b, where_ref, blocks_ref, out_ref):
    group, zi, bi = [where_ref[i] for i in range(3)]
    rows = blocks_ref.shape[3]
    for m in range(4 * n_q):
        q, g = m // 4, m % 4
        far, r = lax.rem(q + n_q - zi, n_q), g ^ group
        both = [
            blocks_ref[lax.rem(b + n_b - bi, n_b), far, r].astype(f32) for b in range(n_b)
        ]
        at = slice(m * n_b * rows, (m + 1) * n_b * rows)
        out_ref[at, :] = jnp.concatenate(both, axis=0).astype(bf16)


def order_rows(n_q, n_b, where, blocks):
    rows, lanes = blocks.shape[3:]
    return pl.pallas_call(
        partial(order_kernel, n_q, n_b),
        out_shape=jax.ShapeDtypeStruct((4 * n_q * n_b * rows, lanes), bf16),
        in_specs=[pl.BlockSpec(memory_space=pltpu.SMEM)] + vmem_specs(1),
        out_specs=vmem_specs(1)[0],
        compiler_params=pltpu.CompilerParams(vmem_limit_bytes=12 * MIB),
        name="order_rows",
    )(where, blocks)


def from_shift(value, axis, count, step):
    return lax.ppermute(value, axis, [((i + step) % count, i) for i in range(count)])


def square_swap(value, r):
    if r == 0:
        return value
    if r == 1:
        return lax.ppermute(value, "c", [(0, 1), (1, 0)])
    if r == 2:
        return lax.ppermute(value, "x", [(0, 1), (1, 0)])
    return lax.ppermute(value, ("x", "c"), [(0, 3), (3, 0), (1, 2), (2, 1)])


def pick(stacked, index, dim=0):
    return lax.dynamic_index_in_dim(stacked, index, dim, keepdims=False)


class Chain:
    def __init__(self, state, *steps):
        self.state, self.steps = tuple(state), list(steps)


def launch(chain):
    chain.state = tuple(chain.steps.pop(0)(*chain.state))


def run_stage(chains, outs=(), settle=()):
    for chain in chains:
        launch(chain)
    joined = [*chains, *settle]
    outs, states = lax.optimization_barrier((tuple(outs), [c.state for c in joined]))
    for chain, state in zip(joined, states):
        chain.state = tuple(state)
    return outs


def away_sum(total, axis, count):
    parts = [total[j].astype(bf16) for j in range(1, count)]
    return [from_shift(part, axis, count, count - j - 1) for j, part in enumerate(parts)]


def weight_sum(keep, send, n_q, n_b, bi, order):
    def own_b(keep, got, j):
        shape = (2, n_q, n_b, -1, keep.shape[-1])
        both = [pick(v.reshape(shape), (bi + j) % n_b, 2).astype(f32) for v in (keep, got)]
        return both[0] + both[1]

    def over_core(keep, send):
        return keep, square_swap(send, 1)

    def over_b(keep, got):
        if order:
            keep = lax.optimization_barrier((keep, order.pop()))[0]
        away = [own_b(keep, got, j).astype(bf16) for j in range(1, n_b)]
        order.append(away[0])
        return keep, got, *[from_shift(v, "b", n_b, n_b - 1 - j) for j, v in enumerate(away)]

    def over_x(keep, got, *more):
        total = own_b(keep, got, 0) + sum(v.astype(f32) for v in more)
        return total[0], *away_sum(total, "x", 2)

    def halve(half):
        def over_q(own, got):
            total = own + got.astype(f32)
            pairs = [(i, i ^ half) for i in range(n_q)]
            return total[:half], lax.ppermute(total[half:].astype(bf16), "q", pairs)

        return over_q

    halves = [n_q >> (k + 1) for k in range(n_q.bit_length() - 1)]
    return Chain((keep, send), over_core, over_b, over_x, *[halve(half) for half in halves])


def toward(j, n_q):
    return (j - 1, n_q - 1) if 2 * j <= n_q else ((j + 1) % n_q, 1)


def token_sum(keep, send, n_q, j, farther):
    def over_core(keep, send):
        return keep, square_swap(send, 1)

    def over_x(keep, got):
        total = keep.astype(f32) + got.astype(f32)
        return total[0], square_swap(total[1].astype(bf16), 2)

    def over_q(own, got):
        total = own + got.astype(f32) + sum(chain_sum(c) for c in farther)
        return (from_shift(total.astype(bf16), "q", n_q, toward(j, n_q)[1]),)

    return Chain((keep, send), over_core, over_x, *([over_q] if j else []))


def chain_sum(chain):
    return sum(v.astype(f32).reshape(chain.state[0].shape) for v in chain.state)


def deinterleave(fold):
    size = fold * LANES
    lane = jnp.arange(size)
    return (lane[:, None] // fold + (lane[:, None] % fold) * LANES == lane[None, :]).astype(bf16)


def per_device(
    n_q,
    n_b,
    inputs,
    lengths,
    cotangent,
    triple_weight,
    query_bias,
    value_bias,
    output_weight,
    output_bias,
    first_gain,
    first_shift,
    expand_weight,
    expand_bias,
    shrink_weight,
    shrink_bias,
    second_gain,
    second_shift,
):
    zi, xi, ci, bi = [lax.axis_index(a) for a in AXES]
    group = 2 * xi + ci
    _, seq_rows, width = inputs.shape
    own_rows = triple_weight.shape[0]
    ff = expand_weight.shape[1]
    fold = ff // width
    aligned = n_b * own_rows % 16 == 0 and n_q & (n_q - 1) == 0
    x_own = inputs[0]

    turn = deinterleave(fold)
    expand_own = expand_weight.astype(bf16).reshape(own_rows, -1, fold * LANES)
    expand_own = jnp.einsum("rbs,st->rbt", expand_own, turn, preferred_element_type=f32)
    expand_own = expand_own.astype(bf16).reshape(own_rows, -1, fold, LANES).transpose(0, 2, 1, 3)
    packed = jnp.concatenate(
        [
            output_weight.astype(bf16),
            expand_own.reshape(own_rows, ff),
            shrink_weight.astype(bf16).reshape(own_rows, ff),
        ],
        axis=1,
    )
    if aligned:
        own_half = lax.all_gather(packed, ("q", "x", "b"), axis=0, tiled=True)
    else:
        gathered_ffn = [lax.all_gather(packed, AXES, axis=0, tiled=True)]

    names = [query_bias, value_bias, output_bias, first_gain, first_shift]
    names += [shrink_bias, second_gain, second_shift]
    vectors = jnp.stack(names, axis=1)
    vectors = jnp.concatenate([vectors, expand_bias.reshape(own_rows, fold)], axis=1).astype(bf16)
    n_vec = vectors.shape[1]
    vectors = jnp.pad(vectors, ((0, 0), (0, WIDE - VECTORS - n_vec)))
    thirds = triple_weight.astype(bf16).reshape(own_rows, 3, GROUPS, OWN_WIDTH)

    def columns_of(g):
        mine = [pick(thirds[:, t], g, 1) for t in range(3)]
        return jnp.concatenate(mine + [vectors], axis=1)

    def rows_square(*blocks):
        return [square_swap(block, r) for r, block in enumerate(blocks)]

    def rows_q(*blocks):
        square = jnp.stack(blocks)
        return [square] + [from_shift(square, "q", n_q, j) for j in range(1, n_q)]

    def rows_b(*blocks):
        both = jnp.stack(blocks)
        return [both] + [from_shift(both, "b", n_b, j) for j in range(1, n_b)]

    weight_rows = Chain([columns_of(group ^ r) for r in range(4)], rows_square, rows_q, rows_b)

    def token_chunk(j):
        def over_q():
            source, step = toward(j, n_q)
            own = chunks[source].state[0] if source else x_own
            if j not in arrival[:2]:
                at = arrival.index(j)
                before = line[at - 1].state[0] if at > 2 else weight_rows.state
                own = lax.optimization_barrier((own, before))[0]
            return (from_shift(own, "q", n_q, n_q - step),)

        def over_x(own):
            return own, square_swap(own, 2)

        def over_core(own, other):
            halves = square_swap(jnp.stack([own, other]), 1)
            return own, halves[0], other, halves[1]

        return Chain(() if j else (x_own,), *([over_q] if j else []), over_x, over_core)

    arrival = []
    for j in [k for pair in zip(range(1, n_q), range(n_q - 1, 0, -1)) for k in pair]:
        arrival += [] if j in arrival else [j]
    arrival = [0] + arrival
    chunks = {j: token_chunk(j) for j in arrival}
    line = [chunks[j] for j in arrival]


    for slot in range(3):
        ready = line[:2] if slot < 2 else line[1:3]
        run_stage([c for c in ready if c.steps] + [weight_rows])
    chunk_x = {}

    by_distance = jnp.stack(weight_rows.state)
    if aligned:
        spot = jnp.stack([group, zi, bi]).astype(jnp.int32)
        w_own = order_rows(n_q, n_b, spot, by_distance)
    else:
        ordered = jnp.stack([pick(by_distance, (i - bi) % n_b) for i in range(n_b)], axis=3)
        ordered = jnp.stack([pick(ordered, group ^ g, 1) for g in range(4)], axis=1)
        ordered = jnp.stack([pick(ordered, (i - zi) % n_q) for i in range(n_q)])
        w_own = ordered.transpose(0, 1, 3, 2, 4).reshape(width, WIDE)
    turned = w_own[:, VECTORS : VECTORS + n_vec].astype(f32)
    turned = turned.T
    ebias = turned[8:]
    turned = turned[:8]
    own_bias = lax.dynamic_slice_in_dim(turned, group * OWN_WIDTH, OWN_WIDTH, 1)
    zero = jnp.zeros((1, OWN_WIDTH), f32)
    bias_row = jnp.concatenate(
        [own_bias[:1], zero, own_bias[1:2], jnp.zeros((1, WIDE - VECTORS), f32)], axis=1
    )

    def where_of(j):
        zj = (zi + j) % n_q
        spots = [(zj * 4 + (group ^ r)) * seq_rows for r in range(4)]
        return jnp.stack(spots + [lengths[0]]).astype(jnp.int32)

    weights = (w_own, bias_row)
    kept = {}
    carry = None
    for step, j in enumerate(arrival):
        first, last = step == 0, step == n_q - 1
        if chunks[j].steps:
            run_stage([chunks[j]])
        chunk_x[j] = chunks[j].state
        outs = attend_chunk(first, last, where_of(j), chunk_x[j], weights, carry)
        ready = line[2:3] if step < 2 else line[step + 1 : step + 2]
        for chain in ready + line[step + 3 : step + 4]:
            launch(chain)
        settle = line[step + 2 : step + 3] if step else []
        outs = run_stage([], outs, settle=ready + [c for c in settle if c not in ready])
        kept[j] = (outs[0], outs[1])
        outs = outs[2:]
        if first:
            qx, qp = outs[:2]
            outs = outs[2:]
        carry = (qx, *outs)
    att, attx, qx2 = carry[1:5], carry[5], carry[6]

    if aligned:
        own_half, att = lax.optimization_barrier((own_half, att))
        gathered_ffn = [own_half, square_swap(own_half, 1)]
    att = [square_swap(att[r], r) for r in range(4)]
    start = (zi * 4 + group) * seq_rows
    where = jnp.stack([group, zi, xi, ci, bi, start, lengths[0]]).astype(jnp.int32)
    layout = (n_q, n_b, own_rows, fold, aligned)
    outs = ffn_block(layout, where, att, x_own, cotangent[0], turned, ebias, gathered_ffn)
    output, resid_first_grad = outs[:2]
    att_grads, vec_grads, summands = outs[2:6], outs[6], outs[7:]
    square = Chain(att_grads, lambda *parts: [square_swap(v, r) for r, v in enumerate(parts)])

    sums, order = [], []
    if aligned:
        for i in range(2):
            sums.append(weight_sum(summands[2 * i], summands[2 * i + 1], n_q, n_b, bi, order))
    reduced = lax.psum_scatter(summands[-1], AXES, scatter_dimension=0, tiled=True)
    run_stage([square] + sums)
    plan = [([0], [], [1]), ([0], [1], []), ([1, 0], [], []), ([1, 0], [], [])]
    shared = (qx2, qp, w_own, square.state, attx)
    carry = None
    moving, moving_to = [], {}
    for step, j in enumerate(reversed(arrival)):
        first, last = step == 0, step == n_q - 1
        with_it, ending, going_on = [], [], []
        if sums and step < len(plan):
            with_it, ending, going_on = [[sums[i] for i in part] for part in plan[step]]
        outs = attend_back_chunk(first, last, kept[j], chunk_x[j], shared, carry)
        run = with_it + [c for c in moving if c.steps]
        for chain in run + going_on:
            launch(chain)
        outs = run_stage([], outs, settle=run + ending)
        keep, send = outs[:2]
        farther = [c for k, c in moving_to.items() if k and toward(k, n_q)[0] == j and j]
        moving_to[j] = token_sum(keep, send, n_q, j, farther)
        moving.append(moving_to[j])
        outs = outs[2:]
        if first:
            dox = outs[0]
            outs = outs[1:]
        carry = (dox, *outs)
        if not last:
            carry = run_stage(moving[-1:], carry)
    grad_joint, col = carry[1:]

    own_bias = jnp.stack([col[0, :OWN_WIDTH], col[0, 2 * OWN_WIDTH : 3 * OWN_WIDTH]])
    bias_grads = lax.dynamic_update_slice(
        jnp.zeros((2, width), f32), own_bias, (0, group * OWN_WIDTH)
    )
    tall = jnp.concatenate([bias_grads, vec_grads[:6], vec_grads[8 : 8 + fold]], axis=0).T
    tall_high = tall.astype(bf16)
    tall_low = (tall - tall_high.astype(f32)).astype(bf16)
    room = jnp.zeros((width, WIDE - VECTORS - 2 * n_vec), bf16)
    blocks = jnp.concatenate([grad_joint[:, :VECTORS], tall_high, tall_low, room], axis=1)
    total = blocks.reshape(n_q, 4, n_b, own_rows, WIDE)

    def rows_over_b(total):
        parts = [pick(total, (bi + j) % n_b, 2) for j in range(n_b)]
        return parts[0], *away_sum(parts, "b", n_b)

    def rows_over_q(*parts):
        total = sum(v.astype(f32) for v in parts)
        parts = [pick(total, (zi + j) % n_q) for j in range(n_q)]
        return parts[0], *away_sum(parts, "q", n_q)

    def rows_over_square(*parts):
        total = sum(v.astype(f32) for v in parts).astype(bf16)
        return [square_swap(pick(total, group ^ r), r) for r in range(4)]

    rows = Chain((total,), rows_over_b, rows_over_q, rows_over_square)
    run_stage([], settle=[rows, *sums, *moving])
    while any(c.steps for c in [rows, *sums, *moving]):
        run_stage([c for c in [rows, *sums, *moving] if c.steps])
        if len(rows.steps) == 1:
            reduced, rows.state = lax.optimization_barrier((reduced, rows.state))
    summed = reduced.astype(f32)
    token_grad = resid_first_grad
    for j, chain in moving_to.items():
        if j == 0 or toward(j, n_q)[0] == 0:
            token_grad = token_grad + chain_sum(chain)
    input_grad = token_grad.astype(bf16)
    if aligned:
        summed = jnp.concatenate([*[chain_sum(c)[0] for c in sums], summed], axis=1)
    parts = jnp.stack(rows.state)
    parts = jnp.stack([pick(parts, group ^ g) for g in range(4)])
    grad_triple = parts[:, :, :VECTORS].reshape(GROUPS, own_rows, 3, OWN_WIDTH)
    grad_triple = grad_triple.transpose(1, 2, 0, 3).reshape(own_rows, -1).astype(f32)
    small = jnp.sum(parts[:, :, VECTORS : VECTORS + 2 * n_vec].astype(f32), axis=0)
    small = small[:, :n_vec] + small[:, n_vec:]
    grad_expand = summed[:, ff : 2 * ff].reshape(own_rows, fold, -1, LANES).transpose(0, 2, 1, 3)
    grad_expand = jnp.einsum(
        "rbs,ts->rbt",
        grad_expand.reshape(own_rows, -1, fold * LANES),
        turn.astype(f32),
        precision=lax.Precision.HIGHEST,
        preferred_element_type=f32,
    ).reshape(own_rows, ff)
    return (
        output[None],
        input_grad[None],
        grad_triple,
        small[:, 0],
        small[:, 1],
        summed[:, 2 * ff :],
        small[:, 2],
        small[:, 3],
        small[:, 4],
        grad_expand,
        small[:, 8:].reshape(-1),
        summed[:, :ff].reshape(-1, width),
        small[:, 5],
        small[:, 6],
        small[:, 7],
    )


def solution(mesh):
    n_seq, n_b = mesh.shape["seq"], mesh.shape["batch"]
    n_q = n_seq // GROUPS
    fine = Mesh(mesh.devices.reshape(n_q, 2, 2, n_b), AXES)
    tokens = P("b", ("q", "x", "c"), None)
    matrix = P(AXES, None)
    vector = P(AXES)
    in_specs = (
        tokens,
        P("b"),
        tokens,
        matrix,
        vector,
        vector,
        matrix,
        vector,
        vector,
        vector,
        matrix,
        vector,
        matrix,
        vector,
        vector,
        vector,
    )
    out_specs = (
        tokens,
        tokens,
        matrix,
        vector,
        vector,
        matrix,
        vector,
        vector,
        vector,
        matrix,
        vector,
        matrix,
        vector,
        vector,
        vector,
    )
    return jax.shard_map(
        partial(per_device, n_q, n_b),
        mesh=fine,
        in_specs=in_specs,
        out_specs=out_specs,
        check_vma=False,
    )
```

```python
from functools import partial
import math

import jax
import jax.numpy as jnp
from jax import lax
from jax.experimental import pallas as pl
from jax.experimental.pallas import tpu as pltpu
from jax.sharding import Mesh, PartitionSpec as P

HEADS = 12
HEAD_DIM = 64
GROUPS = 4
OWN_HEADS = HEADS // GROUPS
OWN_WIDTH = OWN_HEADS * HEAD_DIM
LANES = 128
WIDE = 640
VECTORS = 3 * OWN_WIDTH

bf16 = jnp.bfloat16
f32 = jnp.float32
masked_score = -1e30
norm_eps = 1e-12
log2_e = 1.4426950408889634
CONTRACT_LAST = (((1,), (1,)), ((), ()))
MIB = 1024 * 1024
AXES = ("q", "x", "c", "b")


def split_three(value):
    high = value.astype(bf16).astype(f32)
    rest = value - high
    mid = rest.astype(bf16).astype(f32)
    low = (rest - mid).astype(bf16).astype(f32)
    return high, mid, low


def low_half(tile, lane, from_high):
    turned = pltpu.roll(tile, HEAD_DIM, 1)
    low = lane < HEAD_DIM
    return jnp.where(low, turned, tile) if from_high else jnp.where(low, tile, turned)


def place_of(kind, h):
    slot = kind * OWN_HEADS + h
    return slot // 2, slot % 2


def forward_kernel(first, last, block_q, block_k, *refs):
    refs = list(refs)
    where_ref = refs.pop(0)
    far = [refs.pop(0) for _ in range(5)]
    bias_ref = refs.pop(0)
    if not first:
        qx_ref, peak_in, sum_in = [refs.pop(0) for _ in range(3)]
    kept = [refs.pop(0) for _ in range(2)]
    if first:
        qx_ref, qp_ref = [refs.pop(0) for _ in range(2)]
    if last:
        att_refs = [refs.pop(0) for _ in range(4)]
        attx_ref, qx2_ref = [refs.pop(0) for _ in range(2)]
    else:
        peak_out, sum_out = [refs.pop(0) for _ in range(2)]
    vt_ref, kx_ref, vx_ref, sem, *near = refs
    loads = [pltpu.make_async_copy(f, n, sem.at[2 + i]) for i, (f, n) in enumerate(zip(far, near))]
    for i in (4, 0, 1, 2, 3):
        loads[i].start()
    *pieces, w_ref = near
    stores = [
        pltpu.make_async_copy(kx_ref, kept[0], sem.at[0]),
        pltpu.make_async_copy(vx_ref, kept[1], sem.at[1]),
    ]
    piece_rows = pieces[0].shape[0]
    rows_in = 4 * piece_rows
    lane = lax.broadcasted_iota(jnp.int32, (piece_rows, LANES), 1)
    row = lax.broadcasted_iota(jnp.int32, (piece_rows, LANES), 0)
    low = lane < HEAD_DIM
    length = where_ref[4]
    three = (lane >= HEAD_DIM) & (lane < HEAD_DIM + 3)
    skip = 0 if first else LANES
    for p in range(4):
        rows = slice(p * piece_rows, (p + 1) * piece_rows)
        if p == 0:
            loads[4].wait()
        loads[p].wait()
        joint = jnp.dot(pieces[p][...], w_ref[:, skip:], preferred_element_type=f32)
        joint = joint + bias_ref[:, skip:]
        bias = jnp.where(where_ref[p] + row < length, 0.0, masked_score)
        key_extra = jnp.where(three, 1.0, jnp.where(lane == HEAD_DIM + 3, bias, 0.0))

        def head_of(kind, h):
            tile, high = place_of(kind, h)
            return low_half(joint[:, tile * LANES - skip : (tile + 1) * LANES - skip], lane, high)

        for h in range(OWN_HEADS):
            k = head_of(1, h)
            kx_ref[h, rows, :LANES] = k.astype(bf16)
            kx_ref[h, rows, LANES:] = jnp.where(low, k, key_extra).astype(bf16)
            v = jnp.where(low, head_of(2, h), 0.0)
            vx_ref[h, rows, :] = jnp.where(three, -1.0, v).astype(bf16)
            vt = jnp.where(lane == HEAD_DIM, 1.0, v).T
            vt_ref[h, :, rows] = vt[:80].astype(bf16)
            if first:
                q = head_of(0, h).astype(bf16).astype(f32)
                qp_ref[h, rows, :] = jnp.where(low, q, 0.0).astype(bf16)
                high, mid, rest = split_three(q * (HEAD_DIM**-0.5 * log2_e))
                qx_ref[h, rows, :LANES] = jnp.where(low, high, mid).astype(bf16)
                one = jnp.where(lane == HEAD_DIM + 3, 1.0, 0.0)
                qx_ref[h, rows, LANES:] = jnp.where(low, rest, one).astype(bf16)
    for store in stores:
        store.start()
    for h in range(OWN_HEADS):
        for i in range(rows_in // block_q):
            cols = slice(i * block_q, (i + 1) * block_q)
            q = qx_ref[h, cols, :]
            if first:
                peak = jnp.full((1, block_q), masked_score, f32)
                total = jnp.zeros((80, block_q), f32)
            else:
                peak = peak_in[h, :1, cols]
                total = sum_in[h, :, cols]
            for j in range(rows_in // block_k):
                ks = slice(j * block_k, (j + 1) * block_k)
                s = lax.dot_general(kx_ref[h, ks, :], q, CONTRACT_LAST, preferred_element_type=f32)
                new_peak = jnp.maximum(peak, jnp.max(s, axis=0, keepdims=True))
                prob = jnp.exp2(s - new_peak).astype(bf16)
                total = total * jnp.exp2(peak - new_peak) + jnp.dot(
                    vt_ref[h, :, ks], prob, preferred_element_type=f32
                )
                peak = new_peak
            if last:
                denom = total[HEAD_DIM : HEAD_DIM + 1]
                n_high, n_mid, n_low = split_three(-(peak + jnp.log2(denom)))
                tall = jnp.concatenate(
                    [
                        total[:HEAD_DIM] / denom,
                        n_high,
                        n_mid,
                        n_low,
                        jnp.zeros((HEAD_DIM - 3, block_q), f32),
                    ],
                    axis=0,
                )
                attx_ref[h, cols, :] = tall.T
            else:
                peak_out[h, :, cols] = jnp.broadcast_to(peak, (8, block_q))
                sum_out[h, :, cols] = total
    if last:
        for p in range(4):
            rows = slice(p * piece_rows, (p + 1) * piece_rows)
            heads = [attx_ref[h, rows, :] for h in range(OWN_HEADS)]
            pair = jnp.where(low, heads[0], pltpu.roll(heads[1], HEAD_DIM, 1))
            att_refs[p][:, :LANES] = pair.astype(bf16)
            att_refs[p][:, LANES:] = heads[2][:, :HEAD_DIM].astype(bf16)
            for h in range(OWN_HEADS):
                qx2_ref[h, rows, :LANES] = qx_ref[h, rows, :LANES]
                old = qx_ref[h, rows, LANES:].astype(f32)
                qx2_ref[h, rows, LANES:] = jnp.where(three, heads[h], old).astype(bf16)
    for store in stores:
        store.wait()


def in_hbm(value):
    return pltpu.with_memory_space_constraint(value, pltpu.HBM)


def vmem_specs(n):
    return [pl.BlockSpec(memory_space=pltpu.VMEM) for _ in range(n)]


def attend_chunk(first, last, where, pieces, weights, carry):
    piece_rows = pieces[0].shape[0]
    rows = 4 * piece_rows
    w, bias_row = weights
    far = [in_hbm(v) for v in (*pieces, w)]
    operands = [where, *far, bias_row]
    operands += [] if first else list(carry)
    wide_keys = jax.ShapeDtypeStruct((OWN_HEADS, rows, 2 * LANES), bf16)
    out_shape = [pltpu.HBM(wide_keys.shape, bf16), pltpu.HBM((OWN_HEADS, rows, LANES), bf16)]
    if first:
        out_shape += [wide_keys, jax.ShapeDtypeStruct((OWN_HEADS, rows, LANES), bf16)]
    if last:
        out_shape += [jax.ShapeDtypeStruct((piece_rows, OWN_WIDTH), bf16)] * 4
        out_shape += [jax.ShapeDtypeStruct((OWN_HEADS, rows, LANES), f32), wide_keys]
    else:
        out_shape += [
            jax.ShapeDtypeStruct((OWN_HEADS, 8, rows), f32),
            jax.ShapeDtypeStruct((OWN_HEADS, 80, rows), f32),
        ]
    return pl.pallas_call(
        partial(forward_kernel, first, last, min(1024, rows), min(1024, rows)),
        out_shape=out_shape,
        in_specs=[pl.BlockSpec(memory_space=pltpu.SMEM)]
        + [pl.BlockSpec(memory_space=pltpu.HBM)] * len(far)
        + vmem_specs(len(operands) - 1 - len(far)),
        out_specs=[pl.BlockSpec(memory_space=pltpu.HBM)] * 2 + vmem_specs(len(out_shape) - 2),
        scratch_shapes=[
            pltpu.VMEM((OWN_HEADS, 80, rows), bf16),
            pltpu.VMEM((OWN_HEADS, rows, 2 * LANES), bf16),
            pltpu.VMEM((OWN_HEADS, rows, LANES), bf16),
            pltpu.SemaphoreType.DMA((7,)),
            *[pltpu.VMEM(v.shape, v.dtype) for v in (*pieces, w)],
        ],
        compiler_params=pltpu.CompilerParams(vmem_limit_bytes=20 * MIB),
        cost_estimate=pl.CostEstimate(
            flops=int(8e9), transcendentals=OWN_HEADS * rows * rows, bytes_accessed=int(1e7)
        ),
        name="attend_forward",
    )(*operands)


def backward_kernel(first, last, block_q, block_k, *refs):
    refs = list(refs)
    far = [refs.pop(0) for _ in range(7)]
    qx_ref, qp_ref = [refs.pop(0) for _ in range(2)]
    if first:
        grads = [refs.pop(0) for _ in range(4)]
        attx_ref = refs.pop(0)
    else:
        dox_ref, dqt_in, dw_in, col_in = [refs.pop(0) for _ in range(4)]
    keep_ref, send_ref = [refs.pop(0) for _ in range(2)]
    if first:
        dox_ref = refs.pop(0)
    if last:
        dw_out, col_out = [refs.pop(0) for _ in range(2)]
        dqt_ref = refs.pop()
    else:
        dqt_ref, dw_out, col_out = [refs.pop(0) for _ in range(3)]
    kt_ref, all_ref, sem = refs[:3]
    near = refs[3:]
    kx_ref, vx_ref, w_ref, *pieces = near
    loads = []
    for f, n in zip(far[:2], near[:2]):
        loads += [(f.at[h], n.at[h]) for h in range(OWN_HEADS)]
    loads += list(zip(far[2:], near[2:]))
    loads = [pltpu.make_async_copy(f, n, sem.at[i]) for i, (f, n) in enumerate(loads)]
    for i in (0, OWN_HEADS, *range(1, OWN_HEADS), *range(OWN_HEADS + 1, len(loads))):
        loads[i].start()
    rows_in = kx_ref.shape[1]
    piece_rows = rows_in // 4
    scale = HEAD_DIM**-0.5
    lane = lax.broadcasted_iota(jnp.int32, (piece_rows, LANES), 1)
    if first:
        for p in range(4):
            rows = slice(p * piece_rows, (p + 1) * piece_rows)
            left = grads[p][:, :LANES].astype(f32)
            right = grads[p][:, LANES:].astype(f32)
            right = jnp.concatenate([right, jnp.zeros_like(right)], axis=1)
            for h, wide in enumerate((left, pltpu.roll(left, HEAD_DIM, 1), right)):
                grad = jnp.where(lane < HEAD_DIM, wide, 0.0)
                delta = jnp.sum(grad * attx_ref[h, rows, :], axis=1, keepdims=True)
                d_high, d_mid, d_low = split_three(delta)
                grad = jnp.where(lane == HEAD_DIM, d_high, grad)
                grad = jnp.where(lane == HEAD_DIM + 1, d_mid, grad)
                grad = jnp.where(lane == HEAD_DIM + 2, d_low, grad)
                dox_ref[h, rows, :] = grad.astype(bf16)
        dqt_ref[...] = jnp.zeros_like(dqt_ref)
    else:
        dqt_ref[...] = dqt_in[...]
    lane_k = lax.broadcasted_iota(jnp.int32, (block_k, LANES), 1)
    low_k = lane_k < HEAD_DIM
    for j in range(rows_in // block_k):
        ks = slice(j * block_k, (j + 1) * block_k)
        parts = {}
        for h in range(OWN_HEADS):
            if j == 0:
                loads[h].wait()
                loads[OWN_HEADS + h].wait()
                kt_ref[h] = kx_ref[h, :, LANES:].astype(f32).T[:HEAD_DIM].astype(bf16)
            k = kx_ref[h, ks, :]
            v = vx_ref[h, ks, :]
            kt = kt_ref[h, :, ks]
            dk = jnp.zeros((block_k, LANES), f32)
            dv = jnp.zeros((block_k, LANES), f32)
            for i in range(rows_in // block_q):
                qs = slice(i * block_q, (i + 1) * block_q)
                s = lax.dot_general(k, qx_ref[h, qs, :], CONTRACT_LAST, preferred_element_type=f32)
                prob = jnp.exp2(s)
                do = dox_ref[h, qs, :]
                dp = lax.dot_general(v, do, CONTRACT_LAST, preferred_element_type=f32)
                ds = (prob * dp).astype(bf16)
                dv = dv + jnp.dot(prob.astype(bf16), do, preferred_element_type=f32)
                dk = dk + jnp.dot(ds, qp_ref[h, qs, :], preferred_element_type=f32)
                dqt_ref[h, :, qs] += jnp.dot(kt, ds, preferred_element_type=f32)
            parts[OWN_HEADS + h] = dk * scale
            parts[2 * OWN_HEADS + h] = dv
        for tile in range(1, WIDE // LANES):
            left, right = parts.get(2 * tile), parts.get(2 * tile + 1)
            left = jnp.zeros((block_k, LANES), f32) if left is None else left
            right = 0.0 if right is None else pltpu.roll(right, HEAD_DIM, 1)
            both = jnp.where(low_k, left, right).astype(bf16)
            all_ref[ks, tile * LANES : (tile + 1) * LANES] = both
    if last:
        tall = jnp.concatenate([dqt_ref[0], dqt_ref[1]], axis=0) * scale
        all_ref[:, :LANES] = tall.T.astype(bf16)
        tall = dqt_ref[2] * scale
        tall = jnp.concatenate([tall, jnp.zeros_like(tall)], axis=0).T
        lane_all = lax.broadcasted_iota(jnp.int32, (rows_in, LANES), 1)
        old = all_ref[:, LANES : 2 * LANES].astype(f32)
        all_ref[:, LANES : 2 * LANES] = jnp.where(lane_all < HEAD_DIM, tall, old).astype(bf16)
    skip = 0 if last else LANES
    for load in loads[2 * OWN_HEADS :]:
        load.wait()
    d_weight = [None, None]
    for p in range(4):
        rows = slice(p * piece_rows, (p + 1) * piece_rows)
        own = all_ref[rows, skip:]
        dx = lax.dot_general(own, w_ref[:, skip:], CONTRACT_LAST, preferred_element_type=f32)
        out_ref = keep_ref if p % 2 == 0 else send_ref
        out_ref[p // 2] = dx.astype(bf16)
        piece = lax.dot_general(
            pieces[p][...], own, (((0,), (0,)), ((), ())), preferred_element_type=f32
        )
        d_weight[0] = piece if p == 0 else d_weight[0] + piece
        col = jnp.sum(own.astype(f32), axis=0, keepdims=True)
        d_weight[1] = col if p == 0 else d_weight[1] + col
    grad, col = d_weight
    if last:
        dw_out[:, :LANES] = grad[:, :LANES].astype(bf16)
        dw_out[:, LANES:] = (grad[:, LANES:] + dw_in[...]).astype(bf16)
        col_out[:, :LANES] = jnp.broadcast_to(col[:, :LANES], (8, LANES))
        col_out[:, LANES:] = col[:, LANES:] + col_in[...]
    elif first:
        dw_out[...] = grad
        col_out[...] = jnp.broadcast_to(col, col_out.shape)
    else:
        dw_out[...] = grad + dw_in[...]
        col_out[...] = col + col_in[...]


def attend_back_chunk(first, last, chunk, pieces, shared, carry):
    kx, vx = chunk
    qx2, qp, w, grads, attx = shared
    rows, width = kx.shape[1], w.shape[0]
    far = [in_hbm(v) for v in (kx, vx, w, *pieces)]
    operands = [*far, qx2, qp]
    operands += [*grads, attx] if first else list(carry)
    half = jax.ShapeDtypeStruct((2, rows // 4, width), bf16)
    out_shape = [half, half]
    scratch = [
        pltpu.VMEM((OWN_HEADS, HEAD_DIM, rows), bf16),
        pltpu.VMEM((rows, WIDE), bf16),
        pltpu.SemaphoreType.DMA((2 * OWN_HEADS + 5,)),
        *[pltpu.VMEM(v.shape, v.dtype) for v in far],
    ]
    if first:
        out_shape.append(jax.ShapeDtypeStruct((OWN_HEADS, rows, LANES), bf16))
    if last:
        out_shape.append(jax.ShapeDtypeStruct((width, WIDE), bf16))
        out_shape.append(jax.ShapeDtypeStruct((8, WIDE), f32))
        scratch.append(pltpu.VMEM((OWN_HEADS, HEAD_DIM, rows), f32))
    else:
        out_shape.append(jax.ShapeDtypeStruct((OWN_HEADS, HEAD_DIM, rows), f32))
        out_shape.append(jax.ShapeDtypeStruct((width, WIDE - LANES), f32))
        out_shape.append(jax.ShapeDtypeStruct((8, WIDE - LANES), f32))
    return pl.pallas_call(
        partial(backward_kernel, first, last, min(256, rows), min(1024, rows)),
        out_shape=out_shape,
        in_specs=[pl.BlockSpec(memory_space=pltpu.HBM)] * len(far)
        + vmem_specs(len(operands) - len(far)),
        out_specs=vmem_specs(len(out_shape)),
        scratch_shapes=scratch,
        compiler_params=pltpu.CompilerParams(vmem_limit_bytes=26 * MIB),
        cost_estimate=pl.CostEstimate(
            flops=int(1.5e10), transcendentals=OWN_HEADS * rows * rows, bytes_accessed=int(1e7)
        ),
        name="attend_backward",
    )(*operands)


def norm_forward(value, gain, shift):
    center = value - jnp.mean(value, axis=-1, keepdims=True)
    spread = jnp.mean(center * center, axis=-1, keepdims=True)
    inverse = lax.rsqrt(spread + norm_eps)
    normal = center * inverse
    return normal * gain + shift, normal, inverse


def norm_backward(grad, gain, normal, inverse):
    inner = grad * gain
    mean = jnp.mean(inner, axis=-1, keepdims=True)
    along = jnp.mean(inner * normal, axis=-1, keepdims=True)
    return inverse * (inner - mean - normal * along)


CONTRACT_FIRST = (((0,), (0,)), ((), ()))


def ffn_kernel(layout, *refs):
    n_q, n_b, own_rows, fold, aligned = layout
    refs = list(refs)
    where_ref = refs.pop(0)
    att_refs = [refs.pop(0) for _ in range(4)]
    x_ref, cot_ref, vec_ref, eb_ref = [refs.pop(0) for _ in range(4)]
    packed = [refs.pop(0) for _ in range(2 if aligned else 1)]
    out_ref, resid_ref = [refs.pop(0) for _ in range(2)]
    da_refs = [refs.pop(0) for _ in range(4)]
    vec_out = refs.pop(0)
    targets = [refs.pop(0) for _ in range(5 if aligned else 1)]
    wo, w1, w2, go, g1, g2, act, slope, in_sem, out_sem = refs
    group, zi, xi, ci, bi, start, length = [where_ref[i] for i in range(7)]
    rows, width = x_ref.shape

    def lanes(i):
        return slice(i * width, (i + 1) * width)

    weights = [wo, *[w1.at[k] for k in range(fold)], *[w2.at[k] for k in range(fold)]]
    block = n_b * own_rows
    for i, weight in enumerate(weights):
        if not aligned:
            pltpu.make_async_copy(packed[0].at[:, lanes(i)], weight, in_sem.at[i]).start()
            continue
        for half in range(2):
            for m in range(2 * n_q):
                src = packed[half].at[m * block : (m + 1) * block, lanes(i)]
                at = pl.ds(pl.multiple_of((2 * m + (ci ^ half)) * block, 16), block)
                pltpu.make_async_copy(src, weight.at[at], in_sem.at[i]).start()
    loads = [pltpu.make_async_copy(w, w, in_sem.at[i]) for i, w in enumerate(weights)]

    def group_rows(r):
        other = (2 * (xi ^ (r // 2))) + (ci ^ (r % 2))
        return pl.ds(pl.multiple_of(other * OWN_WIDTH, HEAD_DIM), OWN_WIDTH)

    obias, gain1, shift1, sbias, gain2, shift2 = [vec_ref[i : i + 1, :] for i in range(2, 8)]
    loads[0].wait()
    branch = obias + jnp.zeros((rows, width), f32)
    for r in range(4):
        branch += jnp.dot(att_refs[r][...], wo[group_rows(r), :], preferred_element_type=f32)
    hidden, normal1, inverse1 = norm_forward(x_ref[...].astype(f32) + branch, gain1, shift1)
    hidden_low = hidden.astype(bf16)
    shrunk = sbias + hidden
    for k in range(fold):
        loads[1 + k].wait()
        expanded = jnp.dot(hidden_low, w1[k], preferred_element_type=f32) + eb_ref[k : k + 1, :]
        cdf = 0.5 * (1.0 + lax.erf(expanded * (2.0**-0.5)))
        pdf = jnp.exp(-0.5 * expanded * expanded) * ((2.0 * math.pi) ** -0.5)
        act[k] = (expanded * cdf).astype(bf16)
        slope[k] = cdf + expanded * pdf
        loads[1 + fold + k].wait()
        shrunk += jnp.dot(act[k], w2[k], preferred_element_type=f32)
    result, normal2, inverse2 = norm_forward(shrunk, gain2, shift2)
    out_ref[...] = result.astype(bf16)
    row = lax.broadcasted_iota(jnp.int32, (rows, width), 0)
    seed = jnp.where(start + row < length, cot_ref[...].astype(f32), 0.0)
    vec_out[4:5, :] = jnp.sum(seed * normal2, axis=0, keepdims=True)
    vec_out[5:6, :] = jnp.sum(seed, axis=0, keepdims=True)
    resid2 = norm_backward(seed, gain2, normal2, inverse2)
    shrunk_low = resid2.astype(bf16)
    vec_out[3:4, :] = jnp.sum(shrunk_low.astype(f32), axis=0, keepdims=True)
    hidden_grad = resid2
    for k in range(fold):
        active_grad = lax.dot_general(
            shrunk_low, w2[k], CONTRACT_LAST, preferred_element_type=f32
        )
        expanded_low = (active_grad * slope[k]).astype(bf16)
        vec_out[8 + k : 9 + k, :] = jnp.sum(expanded_low.astype(f32), axis=0, keepdims=True)
        hidden_grad += lax.dot_general(
            expanded_low, w1[k], CONTRACT_LAST, preferred_element_type=f32
        )
        g2[k] = lax.dot_general(
            act[k], shrunk_low, CONTRACT_FIRST, preferred_element_type=f32
        ).astype(bf16)
        g1[k] = lax.dot_general(
            hidden_low, expanded_low, CONTRACT_FIRST, preferred_element_type=f32
        ).astype(bf16)
    vec_out[1:2, :] = jnp.sum(hidden_grad * normal1, axis=0, keepdims=True)
    vec_out[2:3, :] = jnp.sum(hidden_grad, axis=0, keepdims=True)
    resid1 = norm_backward(hidden_grad, gain1, normal1, inverse1)
    resid_ref[...] = resid1
    branch_low = resid1.astype(bf16)
    vec_out[0:1, :] = jnp.sum(branch_low.astype(f32), axis=0, keepdims=True)
    vec_out[6:8, :] = jnp.zeros((2, width), f32)
    vec_out[8 + fold :, :] = jnp.zeros((vec_out.shape[0] - 8 - fold, width), f32)
    for r in range(4):
        da_refs[r][...] = lax.dot_general(
            branch_low, wo[group_rows(r), :], CONTRACT_LAST, preferred_element_type=f32
        ).astype(bf16)
        go[group_rows(r), :] = lax.dot_general(
            att_refs[r][...], branch_low, CONTRACT_FIRST, preferred_element_type=f32
        ).astype(bf16)
    units = [g2.at[k] for k in range(fold)] + [g1.at[k] for k in range(fold)] + [go]
    if aligned:
        *parts, whole = unit_parts(fold)
        for i, part in enumerate(parts):
            for dc in range(2):
                target, sem = targets[2 * i + dc], out_sem.at[2 * i + dc]
                for dx in range(2):
                    for jz in range(n_q):
                        m = ((zi ^ jz) * 2 + (xi ^ dx)) * 2 + (ci ^ dc)
                        at = pl.ds(pl.multiple_of(m * block, 16), block)
                        for place, unit in enumerate(part):
                            dst = target.at[dx, jz, :, lanes(place)]
                            pltpu.make_async_copy(units[unit].at[at], dst, sem).start()
        for place, unit in enumerate(whole):
            dst = targets[-1].at[:, lanes(place)]
            pltpu.make_async_copy(units[unit], dst, out_sem.at[len(targets) - 1]).start()
    else:
        for i, unit in enumerate(units):
            pltpu.make_async_copy(unit, targets[0].at[:, lanes(i)], out_sem.at[0]).start()
    for i, dst in enumerate(targets):
        pltpu.make_async_copy(dst, dst, out_sem.at[i]).wait()


def unit_parts(fold):
    count = 1 + 2 * fold
    edges = [0, count // 3, (count + 1) // 2, count]
    return [range(edges[i], edges[i + 1]) for i in range(3)]


def ffn_block(layout, where, att, x, cot, vectors, ebias, packed):
    n_q, n_b, own_rows, fold, aligned = layout
    rows, width = x.shape
    ff = fold * width
    operands = [where, *att, x, cot, vectors, ebias, *[in_hbm(v) for v in packed]]
    in_specs = [pl.BlockSpec(memory_space=pltpu.SMEM)] + vmem_specs(8)
    in_specs += [pl.BlockSpec(memory_space=pltpu.HBM)] * len(packed)
    out_shape = [
        jax.ShapeDtypeStruct((rows, width), bf16),
        jax.ShapeDtypeStruct((rows, width), f32),
        *[jax.ShapeDtypeStruct((rows, OWN_WIDTH), bf16)] * 4,
        jax.ShapeDtypeStruct((16, width), f32),
    ]
    if aligned:
        lead = (2, n_q, n_b * own_rows)
        sizes = [len(part) * width for part in unit_parts(fold)]
        targets = [pltpu.HBM((*lead, size), bf16) for size in sizes[:-1] for _ in range(2)]
        targets.append(pltpu.HBM((width, sizes[-1]), bf16))
    else:
        targets = [pltpu.HBM((width, width + 2 * ff), bf16)]
    weight_scratch = [
        pltpu.VMEM((width, width), bf16),
        pltpu.VMEM((fold, width, width), bf16),
        pltpu.VMEM((fold, width, width), bf16),
    ]
    return pl.pallas_call(
        partial(ffn_kernel, layout),
        out_shape=out_shape + targets,
        in_specs=in_specs,
        out_specs=vmem_specs(len(out_shape)) + [pl.BlockSpec(memory_space=pltpu.HBM)] * len(targets),
        scratch_shapes=weight_scratch
        + weight_scratch
        + [
            pltpu.VMEM((fold, rows, width), bf16),
            pltpu.VMEM((fold, rows, width), f32),
            pltpu.SemaphoreType.DMA((1 + 2 * fold,)),
            pltpu.SemaphoreType.DMA((6,)),
        ],
        compiler_params=pltpu.CompilerParams(vmem_limit_bytes=32 * MIB),
        cost_estimate=pl.CostEstimate(
            flops=int(2e10), transcendentals=2 * rows * ff, bytes_accessed=int(3e7)
        ),
        name="feed_forward",
    )(*operands)


def order_kernel(n_q, n_b, where_ref, blocks_ref, out_ref):
    group, zi, bi = [where_ref[i] for i in range(3)]
    rows = blocks_ref.shape[3]
    for m in range(4 * n_q):
        q, g = m // 4, m % 4
        far, r = lax.rem(q + n_q - zi, n_q), g ^ group
        both = [
            blocks_ref[lax.rem(b + n_b - bi, n_b), far, r].astype(f32) for b in range(n_b)
        ]
        at = slice(m * n_b * rows, (m + 1) * n_b * rows)
        out_ref[at, :] = jnp.concatenate(both, axis=0).astype(bf16)


def order_rows(n_q, n_b, where, blocks):
    rows, lanes = blocks.shape[3:]
    return pl.pallas_call(
        partial(order_kernel, n_q, n_b),
        out_shape=jax.ShapeDtypeStruct((4 * n_q * n_b * rows, lanes), bf16),
        in_specs=[pl.BlockSpec(memory_space=pltpu.SMEM)] + vmem_specs(1),
        out_specs=vmem_specs(1)[0],
        compiler_params=pltpu.CompilerParams(vmem_limit_bytes=12 * MIB),
        name="order_rows",
    )(where, blocks)


def from_shift(value, axis, count, step):
    return lax.ppermute(value, axis, [((i + step) % count, i) for i in range(count)])


def square_swap(value, r):
    if r == 0:
        return value
    if r == 1:
        return lax.ppermute(value, "c", [(0, 1), (1, 0)])
    if r == 2:
        return lax.ppermute(value, "x", [(0, 1), (1, 0)])
    return lax.ppermute(value, ("x", "c"), [(0, 3), (3, 0), (1, 2), (2, 1)])


def pick(stacked, index, dim=0):
    return lax.dynamic_index_in_dim(stacked, index, dim, keepdims=False)


class Chain:
    def __init__(self, state, *steps):
        self.state, self.steps = tuple(state), list(steps)


def launch(chain):
    chain.state = tuple(chain.steps.pop(0)(*chain.state))


def run_stage(chains, outs=(), settle=()):
    for chain in chains:
        launch(chain)
    joined = [*chains, *settle]
    outs, states = lax.optimization_barrier((tuple(outs), [c.state for c in joined]))
    for chain, state in zip(joined, states):
        chain.state = tuple(state)
    return outs


def away_sum(total, axis, count):
    parts = [total[j].astype(bf16) for j in range(1, count)]
    return [from_shift(part, axis, count, count - j - 1) for j, part in enumerate(parts)]


def weight_sum(keep, send, n_q, n_b, bi, order):
    def own_b(keep, got, j):
        shape = (2, n_q, n_b, -1, keep.shape[-1])
        both = [pick(v.reshape(shape), (bi + j) % n_b, 2).astype(f32) for v in (keep, got)]
        return both[0] + both[1]

    def over_core(keep, send):
        return keep, square_swap(send, 1)

    def over_b(keep, got):
        if order:
            keep = lax.optimization_barrier((keep, order.pop()))[0]
        away = [own_b(keep, got, j).astype(bf16) for j in range(1, n_b)]
        order.append(away[0])
        return keep, got, *[from_shift(v, "b", n_b, n_b - 1 - j) for j, v in enumerate(away)]

    def over_x(keep, got, *more):
        total = own_b(keep, got, 0) + sum(v.astype(f32) for v in more)
        return total[0], *away_sum(total, "x", 2)

    def halve(half):
        def over_q(own, got):
            total = own + got.astype(f32)
            pairs = [(i, i ^ half) for i in range(n_q)]
            return total[:half], lax.ppermute(total[half:].astype(bf16), "q", pairs)

        return over_q

    halves = [n_q >> (k + 1) for k in range(n_q.bit_length() - 1)]
    return Chain((keep, send), over_core, over_b, over_x, *[halve(half) for half in halves])


def toward(j, n_q):
    return (j - 1, n_q - 1) if 2 * j <= n_q else ((j + 1) % n_q, 1)


def token_sum(keep, send, n_q, j, farther):
    def over_core(keep, send):
        return keep, square_swap(send, 1)

    def over_x(keep, got):
        total = keep.astype(f32) + got.astype(f32)
        return total[0], square_swap(total[1].astype(bf16), 2)

    def over_q(own, got):
        total = own + got.astype(f32) + sum(chain_sum(c) for c in farther)
        return (from_shift(total.astype(bf16), "q", n_q, toward(j, n_q)[1]),)

    return Chain((keep, send), over_core, over_x, *([over_q] if j else []))


def chain_sum(chain):
    return sum(v.astype(f32).reshape(chain.state[0].shape) for v in chain.state)


def deinterleave(fold):
    size = fold * LANES
    lane = jnp.arange(size)
    return (lane[:, None] // fold + (lane[:, None] % fold) * LANES == lane[None, :]).astype(bf16)


def per_device(
    n_q,
    n_b,
    inputs,
    lengths,
    cotangent,
    triple_weight,
    query_bias,
    value_bias,
    output_weight,
    output_bias,
    first_gain,
    first_shift,
    expand_weight,
    expand_bias,
    shrink_weight,
    shrink_bias,
    second_gain,
    second_shift,
):
    zi, xi, ci, bi = [lax.axis_index(a) for a in AXES]
    group = 2 * xi + ci
    _, seq_rows, width = inputs.shape
    own_rows = triple_weight.shape[0]
    ff = expand_weight.shape[1]
    fold = ff // width
    aligned = n_b * own_rows % 16 == 0 and n_q & (n_q - 1) == 0
    x_own = inputs[0]

    turn = deinterleave(fold)
    expand_own = expand_weight.astype(bf16).reshape(own_rows, -1, fold * LANES)
    expand_own = jnp.einsum("rbs,st->rbt", expand_own, turn, preferred_element_type=f32)
    expand_own = expand_own.astype(bf16).reshape(own_rows, -1, fold, LANES).transpose(0, 2, 1, 3)
    packed = jnp.concatenate(
        [
            output_weight.astype(bf16),
            expand_own.reshape(own_rows, ff),
            shrink_weight.astype(bf16).reshape(own_rows, ff),
        ],
        axis=1,
    )
    if aligned:
        own_half = lax.all_gather(packed, ("q", "x", "b"), axis=0, tiled=True)
    else:
        gathered_ffn = [lax.all_gather(packed, AXES, axis=0, tiled=True)]

    names = [query_bias, value_bias, output_bias, first_gain, first_shift]
    names += [shrink_bias, second_gain, second_shift]
    vectors = jnp.stack(names, axis=1)
    vectors = jnp.concatenate([vectors, expand_bias.reshape(own_rows, fold)], axis=1).astype(bf16)
    n_vec = vectors.shape[1]
    vectors = jnp.pad(vectors, ((0, 0), (0, WIDE - VECTORS - n_vec)))
    thirds = triple_weight.astype(bf16).reshape(own_rows, 3, GROUPS, OWN_WIDTH)

    def columns_of(g):
        mine = [pick(thirds[:, t], g, 1) for t in range(3)]
        return jnp.concatenate(mine + [vectors], axis=1)

    def rows_square(*blocks):
        return [square_swap(block, r) for r, block in enumerate(blocks)]

    def rows_q(*blocks):
        square = jnp.stack(blocks)
        return [square] + [from_shift(square, "q", n_q, j) for j in range(1, n_q)]

    def rows_b(*blocks):
        both = jnp.stack(blocks)
        return [both] + [from_shift(both, "b", n_b, j) for j in range(1, n_b)]

    weight_rows = Chain([columns_of(group ^ r) for r in range(4)], rows_square, rows_q, rows_b)

    def token_chunk(j):
        def over_q():
            source, step = toward(j, n_q)
            own = chunks[source].state[0] if source else x_own
            if j not in arrival[:2]:
                at = arrival.index(j)
                before = line[at - 1].state[0] if at > 2 else weight_rows.state
                own = lax.optimization_barrier((own, before))[0]
            return (from_shift(own, "q", n_q, n_q - step),)

        def over_x(own):
            return own, square_swap(own, 2)

        def over_core(own, other):
            halves = square_swap(jnp.stack([own, other]), 1)
            return own, halves[0], other, halves[1]

        return Chain(() if j else (x_own,), *([over_q] if j else []), over_x, over_core)

    arrival = []
    for j in [k for pair in zip(range(1, n_q), range(n_q - 1, 0, -1)) for k in pair]:
        arrival += [] if j in arrival else [j]
    arrival = [0] + arrival
    chunks = {j: token_chunk(j) for j in arrival}
    line = [chunks[j] for j in arrival]


    for slot in range(3):
        ready = line[:2] if slot < 2 else line[1:3]
        run_stage([c for c in ready if c.steps] + [weight_rows])
    chunk_x = {}

    by_distance = jnp.stack(weight_rows.state)
    if aligned:
        spot = jnp.stack([group, zi, bi]).astype(jnp.int32)
        w_own = order_rows(n_q, n_b, spot, by_distance)
    else:
        ordered = jnp.stack([pick(by_distance, (i - bi) % n_b) for i in range(n_b)], axis=3)
        ordered = jnp.stack([pick(ordered, group ^ g, 1) for g in range(4)], axis=1)
        ordered = jnp.stack([pick(ordered, (i - zi) % n_q) for i in range(n_q)])
        w_own = ordered.transpose(0, 1, 3, 2, 4).reshape(width, WIDE)
    turned = w_own[:, VECTORS : VECTORS + n_vec].astype(f32)
    turned = turned.T
    ebias = turned[8:]
    turned = turned[:8]
    own_bias = lax.dynamic_slice_in_dim(turned, group * OWN_WIDTH, OWN_WIDTH, 1)
    zero = jnp.zeros((1, OWN_WIDTH), f32)
    bias_row = jnp.concatenate(
        [own_bias[:1], zero, own_bias[1:2], jnp.zeros((1, WIDE - VECTORS), f32)], axis=1
    )

    def where_of(j):
        zj = (zi + j) % n_q
        spots = [(zj * 4 + (group ^ r)) * seq_rows for r in range(4)]
        return jnp.stack(spots + [lengths[0]]).astype(jnp.int32)

    weights = (w_own, bias_row)
    kept = {}
    carry = None
    for step, j in enumerate(arrival):
        first, last = step == 0, step == n_q - 1
        if chunks[j].steps:
            run_stage([chunks[j]])
        chunk_x[j] = chunks[j].state
        outs = attend_chunk(first, last, where_of(j), chunk_x[j], weights, carry)
        ready = line[max(2, step + 1) : step + 4]
        outs = run_stage([c for c in ready if c.steps], outs)
        kept[j] = (outs[0], outs[1])
        outs = outs[2:]
        if first:
            qx, qp = outs[:2]
            outs = outs[2:]
        carry = (qx, *outs)
    att, attx, qx2 = carry[1:5], carry[5], carry[6]

    if aligned:
        own_half, att = lax.optimization_barrier((own_half, att))
        gathered_ffn = [own_half, square_swap(own_half, 1)]
    att = [square_swap(att[r], r) for r in range(4)]
    start = (zi * 4 + group) * seq_rows
    where = jnp.stack([group, zi, xi, ci, bi, start, lengths[0]]).astype(jnp.int32)
    layout = (n_q, n_b, own_rows, fold, aligned)
    outs = ffn_block(layout, where, att, x_own, cotangent[0], turned, ebias, gathered_ffn)
    output, resid_first_grad = outs[:2]
    att_grads, vec_grads, summands = outs[2:6], outs[6], outs[7:]
    square = Chain(att_grads, lambda *parts: [square_swap(v, r) for r, v in enumerate(parts)])

    sums, order = [], []
    if aligned:
        for i in range(2):
            sums.append(weight_sum(summands[2 * i], summands[2 * i + 1], n_q, n_b, bi, order))
    reduced = lax.psum_scatter(summands[-1], AXES, scatter_dimension=0, tiled=True)
    run_stage([square] + sums)
    plan = [([0], [], [1]), ([0], [1], []), ([1, 0], [], []), ([1, 0], [], [])]
    shared = (qx2, qp, w_own, square.state, attx)
    carry = None
    moving, moving_to = [], {}
    for step, j in enumerate(reversed(arrival)):
        first, last = step == 0, step == n_q - 1
        with_it, ending, going_on = [], [], []
        if sums and step < len(plan):
            with_it, ending, going_on = [[sums[i] for i in part] for part in plan[step]]
        outs = attend_back_chunk(first, last, kept[j], chunk_x[j], shared, carry)
        run = with_it + [c for c in moving if c.steps]
        for chain in run + going_on:
            launch(chain)
        free = outs[2:] if last else []
        outs = run_stage([], outs[:2] if last else outs, settle=run + ending)
        outs = (*outs, *free)
        keep, send = outs[:2]
        farther = [c for k, c in moving_to.items() if k and toward(k, n_q)[0] == j and j]
        moving_to[j] = token_sum(keep, send, n_q, j, farther)
        moving.append(moving_to[j])
        outs = outs[2:]
        if first:
            dox = outs[0]
            outs = outs[1:]
        carry = (dox, *outs)
        if not last:
            carry = run_stage(moving[-1:], carry)
    grad_joint, col = carry[1:]

    own_bias = jnp.stack([col[0, :OWN_WIDTH], col[0, 2 * OWN_WIDTH : 3 * OWN_WIDTH]])
    bias_grads = lax.dynamic_update_slice(
        jnp.zeros((2, width), f32), own_bias, (0, group * OWN_WIDTH)
    )
    tall = jnp.concatenate([bias_grads, vec_grads[:6], vec_grads[8 : 8 + fold]], axis=0).T
    tall_high = tall.astype(bf16)
    tall_low = (tall - tall_high.astype(f32)).astype(bf16)
    room = jnp.zeros((width, WIDE - VECTORS - 2 * n_vec), bf16)
    blocks = jnp.concatenate([grad_joint[:, :VECTORS], tall_high, tall_low, room], axis=1)
    total = blocks.reshape(n_q, 4, n_b, own_rows, WIDE)

    def rows_over_b(total):
        parts = [pick(total, (bi + j) % n_b, 2) for j in range(n_b)]
        return parts[0], *away_sum(parts, "b", n_b)

    def rows_over_q(*parts):
        total = sum(v.astype(f32) for v in parts)
        parts = [pick(total, (zi + j) % n_q) for j in range(n_q)]
        return parts[0], *away_sum(parts, "q", n_q)

    def rows_over_square(*parts):
        total = sum(v.astype(f32) for v in parts).astype(bf16)
        return [square_swap(pick(total, group ^ r), r) for r in range(4)]

    rows = Chain((total,), rows_over_b, rows_over_q, rows_over_square)
    while any(c.steps for c in [rows, *sums, *moving]):
        run_stage([c for c in [rows, *sums, *moving] if c.steps])
        if len(rows.steps) == 1:
            reduced, rows.state = lax.optimization_barrier((reduced, rows.state))
    summed = reduced.astype(f32)
    token_grad = resid_first_grad
    for j, chain in moving_to.items():
        if j == 0 or toward(j, n_q)[0] == 0:
            token_grad = token_grad + chain_sum(chain)
    input_grad = token_grad.astype(bf16)
    if aligned:
        summed = jnp.concatenate([*[chain_sum(c)[0] for c in sums], summed], axis=1)
    parts = jnp.stack(rows.state)
    parts = jnp.stack([pick(parts, group ^ g) for g in range(4)])
    grad_triple = parts[:, :, :VECTORS].reshape(GROUPS, own_rows, 3, OWN_WIDTH)
    grad_triple = grad_triple.transpose(1, 2, 0, 3).reshape(own_rows, -1).astype(f32)
    small = jnp.sum(parts[:, :, VECTORS : VECTORS + 2 * n_vec].astype(f32), axis=0)
    small = small[:, :n_vec] + small[:, n_vec:]
    grad_expand = summed[:, ff : 2 * ff].reshape(own_rows, fold, -1, LANES).transpose(0, 2, 1, 3)
    grad_expand = jnp.einsum(
        "rbs,ts->rbt",
        grad_expand.reshape(own_rows, -1, fold * LANES),
        turn.astype(f32),
        precision=lax.Precision.HIGHEST,
        preferred_element_type=f32,
    ).reshape(own_rows, ff)
    return (
        output[None],
        input_grad[None],
        grad_triple,
        small[:, 0],
        small[:, 1],
        summed[:, 2 * ff :],
        small[:, 2],
        small[:, 3],
        small[:, 4],
        grad_expand,
        small[:, 8:].reshape(-1),
        summed[:, :ff].reshape(-1, width),
        small[:, 5],
        small[:, 6],
        small[:, 7],
    )


def solution(mesh):
    n_seq, n_b = mesh.shape["seq"], mesh.shape["batch"]
    n_q = n_seq // GROUPS
    fine = Mesh(mesh.devices.reshape(n_q, 2, 2, n_b), AXES)
    tokens = P("b", ("q", "x", "c"), None)
    matrix = P(AXES, None)
    vector = P(AXES)
    in_specs = (
        tokens,
        P("b"),
        tokens,
        matrix,
        vector,
        vector,
        matrix,
        vector,
        vector,
        vector,
        matrix,
        vector,
        matrix,
        vector,
        vector,
        vector,
    )
    out_specs = (
        tokens,
        tokens,
        matrix,
        vector,
        vector,
        matrix,
        vector,
        vector,
        vector,
        matrix,
        vector,
        matrix,
        vector,
        vector,
        vector,
    )
    return jax.shard_map(
        partial(per_device, n_q, n_b),
        mesh=fine,
        in_specs=in_specs,
        out_specs=out_specs,
        check_vma=False,
    )
```

```python
from functools import partial
import math

import jax
import jax.numpy as jnp
from jax import lax
from jax.experimental import pallas as pl
from jax.experimental.pallas import tpu as pltpu
from jax.sharding import Mesh, PartitionSpec as P

HEADS = 12
HEAD_DIM = 64
GROUPS = 4
OWN_HEADS = HEADS // GROUPS
OWN_WIDTH = OWN_HEADS * HEAD_DIM
LANES = 128
WIDE = 640
VECTORS = 3 * OWN_WIDTH

bf16 = jnp.bfloat16
f32 = jnp.float32
masked_score = -1e30
norm_eps = 1e-12
log2_e = 1.4426950408889634
CONTRACT_LAST = (((1,), (1,)), ((), ()))
MIB = 1024 * 1024
AXES = ("q", "x", "c", "b")


def split_three(value):
    high = value.astype(bf16).astype(f32)
    rest = value - high
    mid = rest.astype(bf16).astype(f32)
    low = (rest - mid).astype(bf16).astype(f32)
    return high, mid, low


def low_half(tile, lane, from_high):
    turned = pltpu.roll(tile, HEAD_DIM, 1)
    low = lane < HEAD_DIM
    return jnp.where(low, turned, tile) if from_high else jnp.where(low, tile, turned)


def place_of(kind, h):
    slot = kind * OWN_HEADS + h
    return slot // 2, slot % 2


def forward_kernel(first, last, block_q, block_k, *refs):
    refs = list(refs)
    where_ref = refs.pop(0)
    far = [refs.pop(0) for _ in range(5)]
    bias_ref = refs.pop(0)
    if not first:
        qx_ref, peak_in, sum_in = [refs.pop(0) for _ in range(3)]
    kept = [refs.pop(0) for _ in range(2)]
    if first:
        qx_ref, qp_ref = [refs.pop(0) for _ in range(2)]
    if last:
        att_refs = [refs.pop(0) for _ in range(4)]
        attx_ref, qx2_ref = [refs.pop(0) for _ in range(2)]
    else:
        peak_out, sum_out = [refs.pop(0) for _ in range(2)]
    vt_ref, kx_ref, vx_ref, sem, *near = refs
    loads = [pltpu.make_async_copy(f, n, sem.at[2 + i]) for i, (f, n) in enumerate(zip(far, near))]
    for i in (4, 0, 1, 2, 3):
        loads[i].start()
    *pieces, w_ref = near
    stores = [
        pltpu.make_async_copy(kx_ref, kept[0], sem.at[0]),
        pltpu.make_async_copy(vx_ref, kept[1], sem.at[1]),
    ]
    piece_rows = pieces[0].shape[0]
    rows_in = 4 * piece_rows
    lane = lax.broadcasted_iota(jnp.int32, (piece_rows, LANES), 1)
    row = lax.broadcasted_iota(jnp.int32, (piece_rows, LANES), 0)
    low = lane < HEAD_DIM
    length = where_ref[4]
    three = (lane >= HEAD_DIM) & (lane < HEAD_DIM + 3)
    skip = 0 if first else LANES
    for p in range(4):
        rows = slice(p * piece_rows, (p + 1) * piece_rows)
        if p == 0:
            loads[4].wait()
        loads[p].wait()
        joint = jnp.dot(pieces[p][...], w_ref[:, skip:], preferred_element_type=f32)
        joint = joint + bias_ref[:, skip:]
        bias = jnp.where(where_ref[p] + row < length, 0.0, masked_score)
        key_extra = jnp.where(three, 1.0, jnp.where(lane == HEAD_DIM + 3, bias, 0.0))

        def head_of(kind, h):
            tile, high = place_of(kind, h)
            return low_half(joint[:, tile * LANES - skip : (tile + 1) * LANES - skip], lane, high)

        for h in range(OWN_HEADS):
            k = head_of(1, h)
            kx_ref[h, rows, :LANES] = k.astype(bf16)
            kx_ref[h, rows, LANES:] = jnp.where(low, k, key_extra).astype(bf16)
            v = jnp.where(low, head_of(2, h), 0.0)
            vx_ref[h, rows, :] = jnp.where(three, -1.0, v).astype(bf16)
            vt = jnp.where(lane == HEAD_DIM, 1.0, v).T
            vt_ref[h, :, rows] = vt[:80].astype(bf16)
            if first:
                q = head_of(0, h).astype(bf16).astype(f32)
                qp_ref[h, rows, :] = jnp.where(low, q, 0.0).astype(bf16)
                high, mid, rest = split_three(q * (HEAD_DIM**-0.5 * log2_e))
                qx_ref[h, rows, :LANES] = jnp.where(low, high, mid).astype(bf16)
                one = jnp.where(lane == HEAD_DIM + 3, 1.0, 0.0)
                qx_ref[h, rows, LANES:] = jnp.where(low, rest, one).astype(bf16)
    for store in stores:
        store.start()
    for h in range(OWN_HEADS):
        for i in range(rows_in // block_q):
            cols = slice(i * block_q, (i + 1) * block_q)
            q = qx_ref[h, cols, :]
            if first:
                peak = jnp.full((1, block_q), masked_score, f32)
                total = jnp.zeros((80, block_q), f32)
            else:
                peak = peak_in[h, :1, cols]
                total = sum_in[h, :, cols]
            for j in range(rows_in // block_k):
                ks = slice(j * block_k, (j + 1) * block_k)
                s = lax.dot_general(kx_ref[h, ks, :], q, CONTRACT_LAST, preferred_element_type=f32)
                new_peak = jnp.maximum(peak, jnp.max(s, axis=0, keepdims=True))
                prob = jnp.exp2(s - new_peak).astype(bf16)
                total = total * jnp.exp2(peak - new_peak) + jnp.dot(
                    vt_ref[h, :, ks], prob, preferred_element_type=f32
                )
                peak = new_peak
            if last:
                denom = total[HEAD_DIM : HEAD_DIM + 1]
                n_high, n_mid, n_low = split_three(-(peak + jnp.log2(denom)))
                tall = jnp.concatenate(
                    [
                        total[:HEAD_DIM] / denom,
                        n_high,
                        n_mid,
                        n_low,
                        jnp.zeros((HEAD_DIM - 3, block_q), f32),
                    ],
                    axis=0,
                )
                attx_ref[h, cols, :] = tall.T
            else:
                peak_out[h, :, cols] = jnp.broadcast_to(peak, (8, block_q))
                sum_out[h, :, cols] = total
    if last:
        for p in range(4):
            rows = slice(p * piece_rows, (p + 1) * piece_rows)
            heads = [attx_ref[h, rows, :] for h in range(OWN_HEADS)]
            pair = jnp.where(low, heads[0], pltpu.roll(heads[1], HEAD_DIM, 1))
            att_refs[p][:, :LANES] = pair.astype(bf16)
            att_refs[p][:, LANES:] = heads[2][:, :HEAD_DIM].astype(bf16)
            for h in range(OWN_HEADS):
                qx2_ref[h, rows, :LANES] = qx_ref[h, rows, :LANES]
                old = qx_ref[h, rows, LANES:].astype(f32)
                qx2_ref[h, rows, LANES:] = jnp.where(three, heads[h], old).astype(bf16)
    for store in stores:
        store.wait()


def in_hbm(value):
    return pltpu.with_memory_space_constraint(value, pltpu.HBM)


def vmem_specs(n):
    return [pl.BlockSpec(memory_space=pltpu.VMEM) for _ in range(n)]


def attend_chunk(first, last, where, pieces, weights, carry):
    piece_rows = pieces[0].shape[0]
    rows = 4 * piece_rows
    w, bias_row = weights
    far = [in_hbm(v) for v in (*pieces, w)]
    operands = [where, *far, bias_row]
    operands += [] if first else list(carry)
    wide_keys = jax.ShapeDtypeStruct((OWN_HEADS, rows, 2 * LANES), bf16)
    out_shape = [pltpu.HBM(wide_keys.shape, bf16), pltpu.HBM((OWN_HEADS, rows, LANES), bf16)]
    if first:
        out_shape += [wide_keys, jax.ShapeDtypeStruct((OWN_HEADS, rows, LANES), bf16)]
    if last:
        out_shape += [jax.ShapeDtypeStruct((piece_rows, OWN_WIDTH), bf16)] * 4
        out_shape += [jax.ShapeDtypeStruct((OWN_HEADS, rows, LANES), f32), wide_keys]
    else:
        out_shape += [
            jax.ShapeDtypeStruct((OWN_HEADS, 8, rows), f32),
            jax.ShapeDtypeStruct((OWN_HEADS, 80, rows), f32),
        ]
    return pl.pallas_call(
        partial(forward_kernel, first, last, min(1024, rows), min(1024, rows)),
        out_shape=out_shape,
        in_specs=[pl.BlockSpec(memory_space=pltpu.SMEM)]
        + [pl.BlockSpec(memory_space=pltpu.HBM)] * len(far)
        + vmem_specs(len(operands) - 1 - len(far)),
        out_specs=[pl.BlockSpec(memory_space=pltpu.HBM)] * 2 + vmem_specs(len(out_shape) - 2),
        scratch_shapes=[
            pltpu.VMEM((OWN_HEADS, 80, rows), bf16),
            pltpu.VMEM((OWN_HEADS, rows, 2 * LANES), bf16),
            pltpu.VMEM((OWN_HEADS, rows, LANES), bf16),
            pltpu.SemaphoreType.DMA((7,)),
            *[pltpu.VMEM(v.shape, v.dtype) for v in (*pieces, w)],
        ],
        compiler_params=pltpu.CompilerParams(vmem_limit_bytes=20 * MIB),
        cost_estimate=pl.CostEstimate(
            flops=int(8e9), transcendentals=OWN_HEADS * rows * rows, bytes_accessed=int(1e7)
        ),
        name="attend_forward",
    )(*operands)


def backward_kernel(first, last, block_q, block_k, *refs):
    refs = list(refs)
    far = [refs.pop(0) for _ in range(7)]
    qx_ref, qp_ref = [refs.pop(0) for _ in range(2)]
    if first:
        grads = [refs.pop(0) for _ in range(4)]
        attx_ref = refs.pop(0)
    else:
        dox_ref, dqt_in, dw_in, col_in = [refs.pop(0) for _ in range(4)]
    keep_ref, send_ref = [refs.pop(0) for _ in range(2)]
    if first:
        dox_ref = refs.pop(0)
    if last:
        dw_out, col_out = [refs.pop(0) for _ in range(2)]
        dqt_ref = refs.pop()
    else:
        dqt_ref, dw_out, col_out = [refs.pop(0) for _ in range(3)]
    kt_ref, all_ref, sem = refs[:3]
    near = refs[3:]
    kx_ref, vx_ref, w_ref, *pieces = near
    loads = []
    for f, n in zip(far[:2], near[:2]):
        loads += [(f.at[h], n.at[h]) for h in range(OWN_HEADS)]
    loads += list(zip(far[2:], near[2:]))
    loads = [pltpu.make_async_copy(f, n, sem.at[i]) for i, (f, n) in enumerate(loads)]
    for i in (0, OWN_HEADS, *range(1, OWN_HEADS), *range(OWN_HEADS + 1, len(loads))):
        loads[i].start()
    rows_in = kx_ref.shape[1]
    piece_rows = rows_in // 4
    scale = HEAD_DIM**-0.5
    lane = lax.broadcasted_iota(jnp.int32, (piece_rows, LANES), 1)
    if first:
        for p in range(4):
            rows = slice(p * piece_rows, (p + 1) * piece_rows)
            left = grads[p][:, :LANES].astype(f32)
            right = grads[p][:, LANES:].astype(f32)
            right = jnp.concatenate([right, jnp.zeros_like(right)], axis=1)
            for h, wide in enumerate((left, pltpu.roll(left, HEAD_DIM, 1), right)):
                grad = jnp.where(lane < HEAD_DIM, wide, 0.0)
                delta = jnp.sum(grad * attx_ref[h, rows, :], axis=1, keepdims=True)
                d_high, d_mid, d_low = split_three(delta)
                grad = jnp.where(lane == HEAD_DIM, d_high, grad)
                grad = jnp.where(lane == HEAD_DIM + 1, d_mid, grad)
                grad = jnp.where(lane == HEAD_DIM + 2, d_low, grad)
                dox_ref[h, rows, :] = grad.astype(bf16)
        dqt_ref[...] = jnp.zeros_like(dqt_ref)
    else:
        dqt_ref[...] = dqt_in[...]
    lane_k = lax.broadcasted_iota(jnp.int32, (block_k, LANES), 1)
    low_k = lane_k < HEAD_DIM
    for j in range(rows_in // block_k):
        ks = slice(j * block_k, (j + 1) * block_k)
        parts = {}
        for h in range(OWN_HEADS):
            if j == 0:
                loads[h].wait()
                loads[OWN_HEADS + h].wait()
                kt_ref[h] = kx_ref[h, :, LANES:].astype(f32).T[:HEAD_DIM].astype(bf16)
            k = kx_ref[h, ks, :]
            v = vx_ref[h, ks, :]
            kt = kt_ref[h, :, ks]
            dk = jnp.zeros((block_k, LANES), f32)
            dv = jnp.zeros((block_k, LANES), f32)
            for i in range(rows_in // block_q):
                qs = slice(i * block_q, (i + 1) * block_q)
                s = lax.dot_general(k, qx_ref[h, qs, :], CONTRACT_LAST, preferred_element_type=f32)
                prob = jnp.exp2(s)
                do = dox_ref[h, qs, :]
                dp = lax.dot_general(v, do, CONTRACT_LAST, preferred_element_type=f32)
                ds = (prob * dp).astype(bf16)
                dv = dv + jnp.dot(prob.astype(bf16), do, preferred_element_type=f32)
                dk = dk + jnp.dot(ds, qp_ref[h, qs, :], preferred_element_type=f32)
                dqt_ref[h, :, qs] += jnp.dot(kt, ds, preferred_element_type=f32)
            parts[OWN_HEADS + h] = dk * scale
            parts[2 * OWN_HEADS + h] = dv
        for tile in range(1, WIDE // LANES):
            left, right = parts.get(2 * tile), parts.get(2 * tile + 1)
            left = jnp.zeros((block_k, LANES), f32) if left is None else left
            right = 0.0 if right is None else pltpu.roll(right, HEAD_DIM, 1)
            both = jnp.where(low_k, left, right).astype(bf16)
            all_ref[ks, tile * LANES : (tile + 1) * LANES] = both
    if last:
        tall = jnp.concatenate([dqt_ref[0], dqt_ref[1]], axis=0) * scale
        all_ref[:, :LANES] = tall.T.astype(bf16)
        tall = dqt_ref[2] * scale
        tall = jnp.concatenate([tall, jnp.zeros_like(tall)], axis=0).T
        lane_all = lax.broadcasted_iota(jnp.int32, (rows_in, LANES), 1)
        old = all_ref[:, LANES : 2 * LANES].astype(f32)
        all_ref[:, LANES : 2 * LANES] = jnp.where(lane_all < HEAD_DIM, tall, old).astype(bf16)
    skip = 0 if last else LANES
    for load in loads[2 * OWN_HEADS :]:
        load.wait()
    d_weight = [None, None]
    for p in range(4):
        rows = slice(p * piece_rows, (p + 1) * piece_rows)
        own = all_ref[rows, skip:]
        dx = lax.dot_general(own, w_ref[:, skip:], CONTRACT_LAST, preferred_element_type=f32)
        out_ref = keep_ref if p % 2 == 0 else send_ref
        out_ref[p // 2] = dx.astype(bf16)
        piece = lax.dot_general(
            pieces[p][...], own, (((0,), (0,)), ((), ())), preferred_element_type=f32
        )
        d_weight[0] = piece if p == 0 else d_weight[0] + piece
        col = jnp.sum(own.astype(f32), axis=0, keepdims=True)
        d_weight[1] = col if p == 0 else d_weight[1] + col
    grad, col = d_weight
    if last:
        dw_out[:, :LANES] = grad[:, :LANES].astype(bf16)
        dw_out[:, LANES:] = (grad[:, LANES:] + dw_in[...]).astype(bf16)
        col_out[:, :LANES] = jnp.broadcast_to(col[:, :LANES], (8, LANES))
        col_out[:, LANES:] = col[:, LANES:] + col_in[...]
    elif first:
        dw_out[...] = grad
        col_out[...] = jnp.broadcast_to(col, col_out.shape)
    else:
        dw_out[...] = grad + dw_in[...]
        col_out[...] = col + col_in[...]


def attend_back_chunk(first, last, chunk, pieces, shared, carry):
    kx, vx = chunk
    qx2, qp, w, grads, attx = shared
    rows, width = kx.shape[1], w.shape[0]
    far = [in_hbm(v) for v in (kx, vx, w, *pieces)]
    operands = [*far, qx2, qp]
    operands += [*grads, attx] if first else list(carry)
    half = jax.ShapeDtypeStruct((2, rows // 4, width), bf16)
    out_shape = [half, half]
    scratch = [
        pltpu.VMEM((OWN_HEADS, HEAD_DIM, rows), bf16),
        pltpu.VMEM((rows, WIDE), bf16),
        pltpu.SemaphoreType.DMA((2 * OWN_HEADS + 5,)),
        *[pltpu.VMEM(v.shape, v.dtype) for v in far],
    ]
    if first:
        out_shape.append(jax.ShapeDtypeStruct((OWN_HEADS, rows, LANES), bf16))
    if last:
        out_shape.append(jax.ShapeDtypeStruct((width, WIDE), bf16))
        out_shape.append(jax.ShapeDtypeStruct((8, WIDE), f32))
        scratch.append(pltpu.VMEM((OWN_HEADS, HEAD_DIM, rows), f32))
    else:
        out_shape.append(jax.ShapeDtypeStruct((OWN_HEADS, HEAD_DIM, rows), f32))
        out_shape.append(jax.ShapeDtypeStruct((width, WIDE - LANES), f32))
        out_shape.append(jax.ShapeDtypeStruct((8, WIDE - LANES), f32))
    return pl.pallas_call(
        partial(backward_kernel, first, last, min(256, rows), min(1024, rows)),
        out_shape=out_shape,
        in_specs=[pl.BlockSpec(memory_space=pltpu.HBM)] * len(far)
        + vmem_specs(len(operands) - len(far)),
        out_specs=vmem_specs(len(out_shape)),
        scratch_shapes=scratch,
        compiler_params=pltpu.CompilerParams(vmem_limit_bytes=26 * MIB),
        cost_estimate=pl.CostEstimate(
            flops=int(1.5e10), transcendentals=OWN_HEADS * rows * rows, bytes_accessed=int(1e7)
        ),
        name="attend_backward",
    )(*operands)


def norm_forward(value, gain, shift):
    center = value - jnp.mean(value, axis=-1, keepdims=True)
    spread = jnp.mean(center * center, axis=-1, keepdims=True)
    inverse = lax.rsqrt(spread + norm_eps)
    normal = center * inverse
    return normal * gain + shift, normal, inverse


def norm_backward(grad, gain, normal, inverse):
    inner = grad * gain
    mean = jnp.mean(inner, axis=-1, keepdims=True)
    along = jnp.mean(inner * normal, axis=-1, keepdims=True)
    return inverse * (inner - mean - normal * along)


CONTRACT_FIRST = (((0,), (0,)), ((), ()))


def ffn_kernel(layout, *refs):
    n_q, n_b, own_rows, fold, aligned = layout
    refs = list(refs)
    where_ref = refs.pop(0)
    att_refs = [refs.pop(0) for _ in range(4)]
    x_ref, cot_ref, vec_ref, eb_ref = [refs.pop(0) for _ in range(4)]
    packed = [refs.pop(0) for _ in range(2 if aligned else 1)]
    out_ref, resid_ref = [refs.pop(0) for _ in range(2)]
    da_refs = [refs.pop(0) for _ in range(4)]
    vec_out = refs.pop(0)
    targets = [refs.pop(0) for _ in range(3 if aligned else 1)]
    wo, w1, w2, go, g1, g2, act, slope, in_sem, out_sem = refs
    group, zi, xi, ci, bi, start, length = [where_ref[i] for i in range(7)]
    rows, width = x_ref.shape

    def lanes(i):
        return slice(i * width, (i + 1) * width)

    weights = [wo, *[w1.at[k] for k in range(fold)], *[w2.at[k] for k in range(fold)]]
    block = n_b * own_rows
    for i, weight in enumerate(weights):
        if not aligned:
            pltpu.make_async_copy(packed[0].at[:, lanes(i)], weight, in_sem.at[i]).start()
            continue
        for half in range(2):
            for m in range(2 * n_q):
                src = packed[half].at[m * block : (m + 1) * block, lanes(i)]
                at = pl.ds(pl.multiple_of((2 * m + (ci ^ half)) * block, 16), block)
                pltpu.make_async_copy(src, weight.at[at], in_sem.at[i]).start()
    loads = [pltpu.make_async_copy(w, w, in_sem.at[i]) for i, w in enumerate(weights)]

    def group_rows(r):
        other = (2 * (xi ^ (r // 2))) + (ci ^ (r % 2))
        return pl.ds(pl.multiple_of(other * OWN_WIDTH, HEAD_DIM), OWN_WIDTH)

    obias, gain1, shift1, sbias, gain2, shift2 = [vec_ref[i : i + 1, :] for i in range(2, 8)]
    loads[0].wait()
    branch = obias + jnp.zeros((rows, width), f32)
    for r in range(4):
        branch += jnp.dot(att_refs[r][...], wo[group_rows(r), :], preferred_element_type=f32)
    hidden, normal1, inverse1 = norm_forward(x_ref[...].astype(f32) + branch, gain1, shift1)
    hidden_low = hidden.astype(bf16)
    shrunk = sbias + hidden
    for k in range(fold):
        loads[1 + k].wait()
        expanded = jnp.dot(hidden_low, w1[k], preferred_element_type=f32) + eb_ref[k : k + 1, :]
        cdf = 0.5 * (1.0 + lax.erf(expanded * (2.0**-0.5)))
        pdf = jnp.exp(-0.5 * expanded * expanded) * ((2.0 * math.pi) ** -0.5)
        act[k] = (expanded * cdf).astype(bf16)
        slope[k] = cdf + expanded * pdf
        loads[1 + fold + k].wait()
        shrunk += jnp.dot(act[k], w2[k], preferred_element_type=f32)
    result, normal2, inverse2 = norm_forward(shrunk, gain2, shift2)
    out_ref[...] = result.astype(bf16)
    row = lax.broadcasted_iota(jnp.int32, (rows, width), 0)
    seed = jnp.where(start + row < length, cot_ref[...].astype(f32), 0.0)
    vec_out[4:5, :] = jnp.sum(seed * normal2, axis=0, keepdims=True)
    vec_out[5:6, :] = jnp.sum(seed, axis=0, keepdims=True)
    resid2 = norm_backward(seed, gain2, normal2, inverse2)
    shrunk_low = resid2.astype(bf16)
    vec_out[3:4, :] = jnp.sum(shrunk_low.astype(f32), axis=0, keepdims=True)
    hidden_grad = resid2
    for k in range(fold):
        active_grad = lax.dot_general(
            shrunk_low, w2[k], CONTRACT_LAST, preferred_element_type=f32
        )
        expanded_low = (active_grad * slope[k]).astype(bf16)
        vec_out[8 + k : 9 + k, :] = jnp.sum(expanded_low.astype(f32), axis=0, keepdims=True)
        hidden_grad += lax.dot_general(
            expanded_low, w1[k], CONTRACT_LAST, preferred_element_type=f32
        )
        g2[k] = lax.dot_general(
            act[k], shrunk_low, CONTRACT_FIRST, preferred_element_type=f32
        ).astype(bf16)
        g1[k] = lax.dot_general(
            hidden_low, expanded_low, CONTRACT_FIRST, preferred_element_type=f32
        ).astype(bf16)
    vec_out[1:2, :] = jnp.sum(hidden_grad * normal1, axis=0, keepdims=True)
    vec_out[2:3, :] = jnp.sum(hidden_grad, axis=0, keepdims=True)
    resid1 = norm_backward(hidden_grad, gain1, normal1, inverse1)
    resid_ref[...] = resid1
    branch_low = resid1.astype(bf16)
    vec_out[0:1, :] = jnp.sum(branch_low.astype(f32), axis=0, keepdims=True)
    vec_out[6:8, :] = jnp.zeros((2, width), f32)
    vec_out[8 + fold :, :] = jnp.zeros((vec_out.shape[0] - 8 - fold, width), f32)
    for r in range(4):
        da_refs[r][...] = lax.dot_general(
            branch_low, wo[group_rows(r), :], CONTRACT_LAST, preferred_element_type=f32
        ).astype(bf16)
        go[group_rows(r), :] = lax.dot_general(
            att_refs[r][...], branch_low, CONTRACT_FIRST, preferred_element_type=f32
        ).astype(bf16)
    units = [g2.at[k] for k in range(fold)] + [g1.at[k] for k in range(fold)] + [go]
    if aligned:
        *parts, whole = unit_parts(fold)
        for i, part in enumerate(parts):
            for dc in range(2):
                target, sem = targets[2 * i + dc], out_sem.at[2 * i + dc]
                for dx in range(2):
                    for jz in range(n_q):
                        m = ((zi ^ jz) * 2 + (xi ^ dx)) * 2 + (ci ^ dc)
                        at = pl.ds(pl.multiple_of(m * block, 16), block)
                        for place, unit in enumerate(part):
                            dst = target.at[dx, jz, :, lanes(place)]
                            pltpu.make_async_copy(units[unit].at[at], dst, sem).start()
        for place, unit in enumerate(whole):
            dst = targets[-1].at[:, lanes(place)]
            pltpu.make_async_copy(units[unit], dst, out_sem.at[len(targets) - 1]).start()
    else:
        for i, unit in enumerate(units):
            pltpu.make_async_copy(unit, targets[0].at[:, lanes(i)], out_sem.at[0]).start()
    for i, dst in enumerate(targets):
        pltpu.make_async_copy(dst, dst, out_sem.at[i]).wait()


def unit_parts(fold):
    count = 1 + 2 * fold
    return [range(count // 3), range(count // 3, count)]


def ffn_block(layout, where, att, x, cot, vectors, ebias, packed):
    n_q, n_b, own_rows, fold, aligned = layout
    rows, width = x.shape
    ff = fold * width
    operands = [where, *att, x, cot, vectors, ebias, *[in_hbm(v) for v in packed]]
    in_specs = [pl.BlockSpec(memory_space=pltpu.SMEM)] + vmem_specs(8)
    in_specs += [pl.BlockSpec(memory_space=pltpu.HBM)] * len(packed)
    out_shape = [
        jax.ShapeDtypeStruct((rows, width), bf16),
        jax.ShapeDtypeStruct((rows, width), f32),
        *[jax.ShapeDtypeStruct((rows, OWN_WIDTH), bf16)] * 4,
        jax.ShapeDtypeStruct((16, width), f32),
    ]
    if aligned:
        lead = (2, n_q, n_b * own_rows)
        sizes = [len(part) * width for part in unit_parts(fold)]
        targets = [pltpu.HBM((*lead, size), bf16) for size in sizes[:-1] for _ in range(2)]
        targets.append(pltpu.HBM((width, sizes[-1]), bf16))
    else:
        targets = [pltpu.HBM((width, width + 2 * ff), bf16)]
    weight_scratch = [
        pltpu.VMEM((width, width), bf16),
        pltpu.VMEM((fold, width, width), bf16),
        pltpu.VMEM((fold, width, width), bf16),
    ]
    return pl.pallas_call(
        partial(ffn_kernel, layout),
        out_shape=out_shape + targets,
        in_specs=in_specs,
        out_specs=vmem_specs(len(out_shape)) + [pl.BlockSpec(memory_space=pltpu.HBM)] * len(targets),
        scratch_shapes=weight_scratch
        + weight_scratch
        + [
            pltpu.VMEM((fold, rows, width), bf16),
            pltpu.VMEM((fold, rows, width), f32),
            pltpu.SemaphoreType.DMA((1 + 2 * fold,)),
            pltpu.SemaphoreType.DMA((6,)),
        ],
        compiler_params=pltpu.CompilerParams(vmem_limit_bytes=32 * MIB),
        cost_estimate=pl.CostEstimate(
            flops=int(2e10), transcendentals=2 * rows * ff, bytes_accessed=int(3e7)
        ),
        name="feed_forward",
    )(*operands)


def order_kernel(n_q, n_b, where_ref, blocks_ref, out_ref):
    group, zi, bi = [where_ref[i] for i in range(3)]
    rows = blocks_ref.shape[3]
    for m in range(4 * n_q):
        q, g = m // 4, m % 4
        far, r = lax.rem(q + n_q - zi, n_q), g ^ group
        both = [
            blocks_ref[lax.rem(b + n_b - bi, n_b), far, r].astype(f32) for b in range(n_b)
        ]
        at = slice(m * n_b * rows, (m + 1) * n_b * rows)
        out_ref[at, :] = jnp.concatenate(both, axis=0).astype(bf16)


def order_rows(n_q, n_b, where, blocks):
    rows, lanes = blocks.shape[3:]
    return pl.pallas_call(
        partial(order_kernel, n_q, n_b),
        out_shape=jax.ShapeDtypeStruct((4 * n_q * n_b * rows, lanes), bf16),
        in_specs=[pl.BlockSpec(memory_space=pltpu.SMEM)] + vmem_specs(1),
        out_specs=vmem_specs(1)[0],
        compiler_params=pltpu.CompilerParams(vmem_limit_bytes=12 * MIB),
        name="order_rows",
    )(where, blocks)


def from_shift(value, axis, count, step):
    return lax.ppermute(value, axis, [((i + step) % count, i) for i in range(count)])


def square_swap(value, r):
    if r == 0:
        return value
    if r == 1:
        return lax.ppermute(value, "c", [(0, 1), (1, 0)])
    if r == 2:
        return lax.ppermute(value, "x", [(0, 1), (1, 0)])
    return lax.ppermute(value, ("x", "c"), [(0, 3), (3, 0), (1, 2), (2, 1)])


def pick(stacked, index, dim=0):
    return lax.dynamic_index_in_dim(stacked, index, dim, keepdims=False)


class Chain:
    def __init__(self, state, *steps):
        self.state, self.steps = tuple(state), list(steps)


def launch(chain):
    chain.state = tuple(chain.steps.pop(0)(*chain.state))


def run_stage(chains, outs=(), settle=()):
    for chain in chains:
        launch(chain)
    joined = [*chains, *settle]
    outs, states = lax.optimization_barrier((tuple(outs), [c.state for c in joined]))
    for chain, state in zip(joined, states):
        chain.state = tuple(state)
    return outs


def away_sum(total, axis, count):
    parts = [total[j].astype(bf16) for j in range(1, count)]
    return [from_shift(part, axis, count, count - j - 1) for j, part in enumerate(parts)]


def weight_sum(keep, send, n_q, n_b, bi):
    def own_b(keep, got, j):
        shape = (2, n_q, n_b, -1, keep.shape[-1])
        both = [pick(v.reshape(shape), (bi + j) % n_b, 2).astype(f32) for v in (keep, got)]
        return both[0] + both[1]

    def over_core(keep, send):
        return keep, square_swap(send, 1)

    def over_b(keep, got):
        away = [own_b(keep, got, j).astype(bf16) for j in range(1, n_b)]
        return keep, got, *[from_shift(v, "b", n_b, n_b - 1 - j) for j, v in enumerate(away)]

    def over_x(keep, got, *more):
        total = own_b(keep, got, 0) + sum(v.astype(f32) for v in more)
        return total[0], *away_sum(total, "x", 2)

    def halve(half):
        def over_q(own, got):
            total = own + got.astype(f32)
            pairs = [(i, i ^ half) for i in range(n_q)]
            return total[:half], lax.ppermute(total[half:].astype(bf16), "q", pairs)

        return over_q

    halves = [n_q >> (k + 1) for k in range(n_q.bit_length() - 1)]
    return Chain((keep, send), over_core, over_b, over_x, *[halve(half) for half in halves])


def toward(j, n_q):
    return (j - 1, n_q - 1) if 2 * j <= n_q else ((j + 1) % n_q, 1)


def token_sum(keep, send, n_q, j, farther):
    def over_core(keep, send):
        return keep, square_swap(send, 1)

    def over_x(keep, got):
        total = keep.astype(f32) + got.astype(f32)
        return total[0], square_swap(total[1].astype(bf16), 2)

    def over_q(own, got):
        total = own + got.astype(f32) + sum(chain_sum(c) for c in farther)
        return (from_shift(total.astype(bf16), "q", n_q, toward(j, n_q)[1]),)

    return Chain((keep, send), over_core, over_x, *([over_q] if j else []))


def chain_sum(chain):
    return sum(v.astype(f32).reshape(chain.state[0].shape) for v in chain.state)


def deinterleave(fold):
    size = fold * LANES
    lane = jnp.arange(size)
    return (lane[:, None] // fold + (lane[:, None] % fold) * LANES == lane[None, :]).astype(bf16)


def per_device(
    n_q,
    n_b,
    inputs,
    lengths,
    cotangent,
    triple_weight,
    query_bias,
    value_bias,
    output_weight,
    output_bias,
    first_gain,
    first_shift,
    expand_weight,
    expand_bias,
    shrink_weight,
    shrink_bias,
    second_gain,
    second_shift,
):
    zi, xi, ci, bi = [lax.axis_index(a) for a in AXES]
    group = 2 * xi + ci
    _, seq_rows, width = inputs.shape
    own_rows = triple_weight.shape[0]
    ff = expand_weight.shape[1]
    fold = ff // width
    aligned = n_b * own_rows % 16 == 0 and n_q & (n_q - 1) == 0
    x_own = inputs[0]

    turn = deinterleave(fold)
    expand_own = expand_weight.astype(bf16).reshape(own_rows, -1, fold * LANES)
    expand_own = jnp.einsum("rbs,st->rbt", expand_own, turn, preferred_element_type=f32)
    expand_own = expand_own.astype(bf16).reshape(own_rows, -1, fold, LANES).transpose(0, 2, 1, 3)
    packed = jnp.concatenate(
        [
            output_weight.astype(bf16),
            expand_own.reshape(own_rows, ff),
            shrink_weight.astype(bf16).reshape(own_rows, ff),
        ],
        axis=1,
    )
    if aligned:
        own_half = lax.all_gather(packed, ("q", "x", "b"), axis=0, tiled=True)
    else:
        gathered_ffn = [lax.all_gather(packed, AXES, axis=0, tiled=True)]

    names = [query_bias, value_bias, output_bias, first_gain, first_shift]
    names += [shrink_bias, second_gain, second_shift]
    vectors = jnp.stack(names, axis=1)
    vectors = jnp.concatenate([vectors, expand_bias.reshape(own_rows, fold)], axis=1).astype(bf16)
    n_vec = vectors.shape[1]
    vectors = jnp.pad(vectors, ((0, 0), (0, WIDE - VECTORS - n_vec)))
    thirds = triple_weight.astype(bf16).reshape(own_rows, 3, GROUPS, OWN_WIDTH)

    def columns_of(g):
        mine = [pick(thirds[:, t], g, 1) for t in range(3)]
        return jnp.concatenate(mine + [vectors], axis=1)

    def rows_square(*blocks):
        return [square_swap(block, r) for r, block in enumerate(blocks)]

    def rows_q(*blocks):
        square = jnp.stack(blocks)
        return [square] + [from_shift(square, "q", n_q, j) for j in range(1, n_q)]

    def rows_b(*blocks):
        both = jnp.stack(blocks)
        return [both] + [from_shift(both, "b", n_b, j) for j in range(1, n_b)]

    weight_rows = Chain([columns_of(group ^ r) for r in range(4)], rows_square, rows_q, rows_b)

    def token_chunk(j):
        def over_q():
            source, step = toward(j, n_q)
            own = chunks[source].state[0] if source else x_own
            if j not in arrival[:2]:
                at = arrival.index(j)
                before = line[at - 1].state[0] if at > 2 else weight_rows.state
                own = lax.optimization_barrier((own, before))[0]
            return (from_shift(own, "q", n_q, n_q - step),)

        def over_x(own):
            return own, square_swap(own, 2)

        def over_core(own, other):
            halves = square_swap(jnp.stack([own, other]), 1)
            return own, halves[0], other, halves[1]

        return Chain(() if j else (x_own,), *([over_q] if j else []), over_x, over_core)

    arrival = []
    for j in [k for pair in zip(range(1, n_q), range(n_q - 1, 0, -1)) for k in pair]:
        arrival += [] if j in arrival else [j]
    arrival = [0] + arrival
    chunks = {j: token_chunk(j) for j in arrival}
    line = [chunks[j] for j in arrival]


    for slot in range(3):
        ready = line[:2] if slot < 2 else line[1:3]
        run_stage([c for c in ready if c.steps] + [weight_rows])
    chunk_x = {}

    by_distance = jnp.stack(weight_rows.state)
    if aligned:
        spot = jnp.stack([group, zi, bi]).astype(jnp.int32)
        w_own = order_rows(n_q, n_b, spot, by_distance)
    else:
        ordered = jnp.stack([pick(by_distance, (i - bi) % n_b) for i in range(n_b)], axis=3)
        ordered = jnp.stack([pick(ordered, group ^ g, 1) for g in range(4)], axis=1)
        ordered = jnp.stack([pick(ordered, (i - zi) % n_q) for i in range(n_q)])
        w_own = ordered.transpose(0, 1, 3, 2, 4).reshape(width, WIDE)
    turned = w_own[:, VECTORS : VECTORS + n_vec].astype(f32)
    turned = turned.T
    ebias = turned[8:]
    turned = turned[:8]
    own_bias = lax.dynamic_slice_in_dim(turned, group * OWN_WIDTH, OWN_WIDTH, 1)
    zero = jnp.zeros((1, OWN_WIDTH), f32)
    bias_row = jnp.concatenate(
        [own_bias[:1], zero, own_bias[1:2], jnp.zeros((1, WIDE - VECTORS), f32)], axis=1
    )

    def where_of(j):
        zj = (zi + j) % n_q
        spots = [(zj * 4 + (group ^ r)) * seq_rows for r in range(4)]
        return jnp.stack(spots + [lengths[0]]).astype(jnp.int32)

    weights = (w_own, bias_row)
    kept = {}
    carry = None
    for step, j in enumerate(arrival):
        first, last = step == 0, step == n_q - 1
        if chunks[j].steps:
            run_stage([chunks[j]])
        chunk_x[j] = chunks[j].state
        outs = attend_chunk(first, last, where_of(j), chunk_x[j], weights, carry)
        ready = line[max(2, step + 1) : step + 4]
        outs = run_stage([c for c in ready if c.steps], outs)
        kept[j] = (outs[0], outs[1])
        outs = outs[2:]
        if first:
            qx, qp = outs[:2]
            outs = outs[2:]
        carry = (qx, *outs)
    att, attx, qx2 = carry[1:5], carry[5], carry[6]

    if aligned:
        own_half, att = lax.optimization_barrier((own_half, att))
        gathered_ffn = [own_half, square_swap(own_half, 1)]
    att = [square_swap(att[r], r) for r in range(4)]
    start = (zi * 4 + group) * seq_rows
    where = jnp.stack([group, zi, xi, ci, bi, start, lengths[0]]).astype(jnp.int32)
    layout = (n_q, n_b, own_rows, fold, aligned)
    outs = ffn_block(layout, where, att, x_own, cotangent[0], turned, ebias, gathered_ffn)
    output, resid_first_grad = outs[:2]
    att_grads, vec_grads, summands = outs[2:6], outs[6], outs[7:]
    square = Chain(att_grads, lambda *parts: [square_swap(v, r) for r, v in enumerate(parts)])

    sums = []
    if aligned:
        sums.append(weight_sum(summands[0], summands[1], n_q, n_b, bi))
    reduced = lax.psum_scatter(summands[-1], AXES, scatter_dimension=0, tiled=True)
    run_stage([square] + sums)
    plan = [([0], [], [])] * 4
    shared = (qx2, qp, w_own, square.state, attx)
    carry = None
    moving, moving_to = [], {}
    for step, j in enumerate(reversed(arrival)):
        first, last = step == 0, step == n_q - 1
        with_it, ending, going_on = [], [], []
        if sums and step < len(plan):
            with_it, ending, going_on = [[sums[i] for i in part] for part in plan[step]]
        outs = attend_back_chunk(first, last, kept[j], chunk_x[j], shared, carry)
        run = with_it + [c for c in moving if c.steps]
        for chain in run + going_on:
            launch(chain)
        free = outs[2:] if last else []
        outs = run_stage([], outs[:2] if last else outs, settle=run + ending)
        outs = (*outs, *free)
        keep, send = outs[:2]
        farther = [c for k, c in moving_to.items() if k and toward(k, n_q)[0] == j and j]
        moving_to[j] = token_sum(keep, send, n_q, j, farther)
        moving.append(moving_to[j])
        outs = outs[2:]
        if first:
            dox = outs[0]
            outs = outs[1:]
        carry = (dox, *outs)
        if not last:
            carry = run_stage(moving[-1:], carry)
    grad_joint, col = carry[1:]

    own_bias = jnp.stack([col[0, :OWN_WIDTH], col[0, 2 * OWN_WIDTH : 3 * OWN_WIDTH]])
    bias_grads = lax.dynamic_update_slice(
        jnp.zeros((2, width), f32), own_bias, (0, group * OWN_WIDTH)
    )
    tall = jnp.concatenate([bias_grads, vec_grads[:6], vec_grads[8 : 8 + fold]], axis=0).T
    tall_high = tall.astype(bf16)
    tall_low = (tall - tall_high.astype(f32)).astype(bf16)
    room = jnp.zeros((width, WIDE - VECTORS - 2 * n_vec), bf16)
    blocks = jnp.concatenate([grad_joint[:, :VECTORS], tall_high, tall_low, room], axis=1)
    total = blocks.reshape(n_q, 4, n_b, own_rows, WIDE)

    def rows_over_b(total):
        parts = [pick(total, (bi + j) % n_b, 2) for j in range(n_b)]
        return parts[0], *away_sum(parts, "b", n_b)

    def rows_over_q(*parts):
        total = sum(v.astype(f32) for v in parts)
        parts = [pick(total, (zi + j) % n_q) for j in range(n_q)]
        return parts[0], *away_sum(parts, "q", n_q)

    def rows_over_square(*parts):
        total = sum(v.astype(f32) for v in parts).astype(bf16)
        return [square_swap(pick(total, group ^ r), r) for r in range(4)]

    rows = Chain((total,), rows_over_b, rows_over_q, rows_over_square)
    while any(c.steps for c in [rows, *sums, *moving]):
        run_stage([c for c in [rows, *sums, *moving] if c.steps])
        if not rows.steps:
            reduced, rows.state = lax.optimization_barrier((reduced, rows.state))
    summed = reduced.astype(f32)
    token_grad = resid_first_grad
    for j, chain in moving_to.items():
        if j == 0 or toward(j, n_q)[0] == 0:
            token_grad = token_grad + chain_sum(chain)
    input_grad = token_grad.astype(bf16)
    if aligned:
        summed = jnp.concatenate([*[chain_sum(c)[0] for c in sums], summed], axis=1)
    parts = jnp.stack(rows.state)
    parts = jnp.stack([pick(parts, group ^ g) for g in range(4)])
    grad_triple = parts[:, :, :VECTORS].reshape(GROUPS, own_rows, 3, OWN_WIDTH)
    grad_triple = grad_triple.transpose(1, 2, 0, 3).reshape(own_rows, -1).astype(f32)
    small = jnp.sum(parts[:, :, VECTORS : VECTORS + 2 * n_vec].astype(f32), axis=0)
    small = small[:, :n_vec] + small[:, n_vec:]
    grad_expand = summed[:, ff : 2 * ff].reshape(own_rows, fold, -1, LANES).transpose(0, 2, 1, 3)
    grad_expand = jnp.einsum(
        "rbs,ts->rbt",
        grad_expand.reshape(own_rows, -1, fold * LANES),
        turn.astype(f32),
        precision=lax.Precision.HIGHEST,
        preferred_element_type=f32,
    ).reshape(own_rows, ff)
    return (
        output[None],
        input_grad[None],
        grad_triple,
        small[:, 0],
        small[:, 1],
        summed[:, 2 * ff :],
        small[:, 2],
        small[:, 3],
        small[:, 4],
        grad_expand,
        small[:, 8:].reshape(-1),
        summed[:, :ff].reshape(-1, width),
        small[:, 5],
        small[:, 6],
        small[:, 7],
    )


def solution(mesh):
    n_seq, n_b = mesh.shape["seq"], mesh.shape["batch"]
    n_q = n_seq // GROUPS
    fine = Mesh(mesh.devices.reshape(n_q, 2, 2, n_b), AXES)
    tokens = P("b", ("q", "x", "c"), None)
    matrix = P(AXES, None)
    vector = P(AXES)
    in_specs = (
        tokens,
        P("b"),
        tokens,
        matrix,
        vector,
        vector,
        matrix,
        vector,
        vector,
        vector,
        matrix,
        vector,
        matrix,
        vector,
        vector,
        vector,
    )
    out_specs = (
        tokens,
        tokens,
        matrix,
        vector,
        vector,
        matrix,
        vector,
        vector,
        vector,
        matrix,
        vector,
        matrix,
        vector,
        vector,
        vector,
    )
    return jax.shard_map(
        partial(per_device, n_q, n_b),
        mesh=fine,
        in_specs=in_specs,
        out_specs=out_specs,
        check_vma=False,
    )
```

```python
from functools import partial
import math

import jax
import jax.numpy as jnp
from jax import lax
from jax.experimental import pallas as pl
from jax.experimental.pallas import tpu as pltpu
from jax.sharding import Mesh, PartitionSpec as P

HEADS = 12
HEAD_DIM = 64
GROUPS = 4
OWN_HEADS = HEADS // GROUPS
OWN_WIDTH = OWN_HEADS * HEAD_DIM
LANES = 128
WIDE = 640
VECTORS = 3 * OWN_WIDTH

bf16 = jnp.bfloat16
f32 = jnp.float32
masked_score = -1e30
norm_eps = 1e-12
log2_e = 1.4426950408889634
CONTRACT_LAST = (((1,), (1,)), ((), ()))
MIB = 1024 * 1024
AXES = ("q", "x", "c", "b")


def split_three(value):
    high = value.astype(bf16).astype(f32)
    rest = value - high
    mid = rest.astype(bf16).astype(f32)
    low = (rest - mid).astype(bf16).astype(f32)
    return high, mid, low


def low_half(tile, lane, from_high):
    turned = pltpu.roll(tile, HEAD_DIM, 1)
    low = lane < HEAD_DIM
    return jnp.where(low, turned, tile) if from_high else jnp.where(low, tile, turned)


def place_of(kind, h):
    slot = kind * OWN_HEADS + h
    return slot // 2, slot % 2


def forward_kernel(first, last, block_q, block_k, *refs):
    refs = list(refs)
    where_ref = refs.pop(0)
    far = [refs.pop(0) for _ in range(5)]
    bias_ref = refs.pop(0)
    if not first:
        qx_ref, peak_in, sum_in = [refs.pop(0) for _ in range(3)]
    kept = [refs.pop(0) for _ in range(2)]
    if first:
        qx_ref, qp_ref = [refs.pop(0) for _ in range(2)]
    if last:
        att_refs = [refs.pop(0) for _ in range(4)]
        attx_ref, qx2_ref = [refs.pop(0) for _ in range(2)]
    else:
        peak_out, sum_out = [refs.pop(0) for _ in range(2)]
    vt_ref, kx_ref, vx_ref, sem, *near = refs
    loads = [pltpu.make_async_copy(f, n, sem.at[2 + i]) for i, (f, n) in enumerate(zip(far, near))]
    for i in (4, 0, 1, 2, 3):
        loads[i].start()
    *pieces, w_ref = near
    stores = [
        pltpu.make_async_copy(kx_ref, kept[0], sem.at[0]),
        pltpu.make_async_copy(vx_ref, kept[1], sem.at[1]),
    ]
    piece_rows = pieces[0].shape[0]
    rows_in = 4 * piece_rows
    lane = lax.broadcasted_iota(jnp.int32, (piece_rows, LANES), 1)
    row = lax.broadcasted_iota(jnp.int32, (piece_rows, LANES), 0)
    low = lane < HEAD_DIM
    length = where_ref[4]
    three = (lane >= HEAD_DIM) & (lane < HEAD_DIM + 3)
    skip = 0 if first else LANES
    for p in range(4):
        rows = slice(p * piece_rows, (p + 1) * piece_rows)
        if p == 0:
            loads[4].wait()
        loads[p].wait()
        joint = jnp.dot(pieces[p][...], w_ref[:, skip:], preferred_element_type=f32)
        joint = joint + bias_ref[:, skip:]
        bias = jnp.where(where_ref[p] + row < length, 0.0, masked_score)
        key_extra = jnp.where(three, 1.0, jnp.where(lane == HEAD_DIM + 3, bias, 0.0))

        def head_of(kind, h):
            tile, high = place_of(kind, h)
            return low_half(joint[:, tile * LANES - skip : (tile + 1) * LANES - skip], lane, high)

        for h in range(OWN_HEADS):
            k = head_of(1, h)
            kx_ref[h, rows, :LANES] = k.astype(bf16)
            kx_ref[h, rows, LANES:] = jnp.where(low, k, key_extra).astype(bf16)
            v = jnp.where(low, head_of(2, h), 0.0)
            vx_ref[h, rows, :] = jnp.where(three, -1.0, v).astype(bf16)
            vt = jnp.where(lane == HEAD_DIM, 1.0, v).T
            vt_ref[h, :, rows] = vt[:80].astype(bf16)
            if first:
                q = head_of(0, h).astype(bf16).astype(f32)
                qp_ref[h, rows, :] = jnp.where(low, q, 0.0).astype(bf16)
                high, mid, rest = split_three(q * (HEAD_DIM**-0.5 * log2_e))
                qx_ref[h, rows, :LANES] = jnp.where(low, high, mid).astype(bf16)
                one = jnp.where(lane == HEAD_DIM + 3, 1.0, 0.0)
                qx_ref[h, rows, LANES:] = jnp.where(low, rest, one).astype(bf16)
    for store in stores:
        store.start()
    for h in range(OWN_HEADS):
        for i in range(rows_in // block_q):
            cols = slice(i * block_q, (i + 1) * block_q)
            q = qx_ref[h, cols, :]
            if first:
                peak = jnp.full((1, block_q), masked_score, f32)
                total = jnp.zeros((80, block_q), f32)
            else:
                peak = peak_in[h, :1, cols]
                total = sum_in[h, :, cols]
            for j in range(rows_in // block_k):
                ks = slice(j * block_k, (j + 1) * block_k)
                s = lax.dot_general(kx_ref[h, ks, :], q, CONTRACT_LAST, preferred_element_type=f32)
                new_peak = jnp.maximum(peak, jnp.max(s, axis=0, keepdims=True))
                prob = jnp.exp2(s - new_peak).astype(bf16)
                total = total * jnp.exp2(peak - new_peak) + jnp.dot(
                    vt_ref[h, :, ks], prob, preferred_element_type=f32
                )
                peak = new_peak
            if last:
                denom = total[HEAD_DIM : HEAD_DIM + 1]
                n_high, n_mid, n_low = split_three(-(peak + jnp.log2(denom)))
                tall = jnp.concatenate(
                    [
                        total[:HEAD_DIM] / denom,
                        n_high,
                        n_mid,
                        n_low,
                        jnp.zeros((HEAD_DIM - 3, block_q), f32),
                    ],
                    axis=0,
                )
                attx_ref[h, cols, :] = tall.T
            else:
                peak_out[h, :, cols] = jnp.broadcast_to(peak, (8, block_q))
                sum_out[h, :, cols] = total
    if last:
        for p in range(4):
            rows = slice(p * piece_rows, (p + 1) * piece_rows)
            heads = [attx_ref[h, rows, :] for h in range(OWN_HEADS)]
            pair = jnp.where(low, heads[0], pltpu.roll(heads[1], HEAD_DIM, 1))
            att_refs[p][:, :LANES] = pair.astype(bf16)
            att_refs[p][:, LANES:] = heads[2][:, :HEAD_DIM].astype(bf16)
            for h in range(OWN_HEADS):
                qx2_ref[h, rows, :LANES] = qx_ref[h, rows, :LANES]
                old = qx_ref[h, rows, LANES:].astype(f32)
                qx2_ref[h, rows, LANES:] = jnp.where(three, heads[h], old).astype(bf16)
    for store in stores:
        store.wait()


def in_hbm(value):
    return pltpu.with_memory_space_constraint(value, pltpu.HBM)


def vmem_specs(n):
    return [pl.BlockSpec(memory_space=pltpu.VMEM) for _ in range(n)]


def attend_chunk(first, last, where, pieces, weights, carry):
    piece_rows = pieces[0].shape[0]
    rows = 4 * piece_rows
    w, bias_row = weights
    far = [in_hbm(v) for v in (*pieces, w)]
    operands = [where, *far, bias_row]
    operands += [] if first else list(carry)
    wide_keys = jax.ShapeDtypeStruct((OWN_HEADS, rows, 2 * LANES), bf16)
    out_shape = [pltpu.HBM(wide_keys.shape, bf16), pltpu.HBM((OWN_HEADS, rows, LANES), bf16)]
    if first:
        out_shape += [wide_keys, jax.ShapeDtypeStruct((OWN_HEADS, rows, LANES), bf16)]
    if last:
        out_shape += [jax.ShapeDtypeStruct((piece_rows, OWN_WIDTH), bf16)] * 4
        out_shape += [jax.ShapeDtypeStruct((OWN_HEADS, rows, LANES), f32), wide_keys]
    else:
        out_shape += [
            jax.ShapeDtypeStruct((OWN_HEADS, 8, rows), f32),
            jax.ShapeDtypeStruct((OWN_HEADS, 80, rows), f32),
        ]
    return pl.pallas_call(
        partial(forward_kernel, first, last, min(1024, rows), min(1024, rows)),
        out_shape=out_shape,
        in_specs=[pl.BlockSpec(memory_space=pltpu.SMEM)]
        + [pl.BlockSpec(memory_space=pltpu.HBM)] * len(far)
        + vmem_specs(len(operands) - 1 - len(far)),
        out_specs=[pl.BlockSpec(memory_space=pltpu.HBM)] * 2 + vmem_specs(len(out_shape) - 2),
        scratch_shapes=[
            pltpu.VMEM((OWN_HEADS, 80, rows), bf16),
            pltpu.VMEM((OWN_HEADS, rows, 2 * LANES), bf16),
            pltpu.VMEM((OWN_HEADS, rows, LANES), bf16),
            pltpu.SemaphoreType.DMA((7,)),
            *[pltpu.VMEM(v.shape, v.dtype) for v in (*pieces, w)],
        ],
        compiler_params=pltpu.CompilerParams(vmem_limit_bytes=20 * MIB),
        cost_estimate=pl.CostEstimate(
            flops=int(8e9), transcendentals=OWN_HEADS * rows * rows, bytes_accessed=int(1e7)
        ),
        name="attend_forward",
    )(*operands)


def backward_kernel(first, last, block_q, block_k, *refs):
    refs = list(refs)
    far = [refs.pop(0) for _ in range(7)]
    qx_ref, qp_ref = [refs.pop(0) for _ in range(2)]
    if first:
        grads = [refs.pop(0) for _ in range(4)]
        attx_ref = refs.pop(0)
    else:
        dox_ref, dqt_in, dw_in, col_in = [refs.pop(0) for _ in range(4)]
    keep_ref, send_ref = [refs.pop(0) for _ in range(2)]
    if first:
        dox_ref = refs.pop(0)
    if last:
        dw_out, col_out = [refs.pop(0) for _ in range(2)]
        dqt_ref = refs.pop()
    else:
        dqt_ref, dw_out, col_out = [refs.pop(0) for _ in range(3)]
    kt_ref, all_ref, sem = refs[:3]
    near = refs[3:]
    kx_ref, vx_ref, w_ref, *pieces = near
    loads = []
    for f, n in zip(far[:2], near[:2]):
        loads += [(f.at[h], n.at[h]) for h in range(OWN_HEADS)]
    loads += list(zip(far[2:], near[2:]))
    loads = [pltpu.make_async_copy(f, n, sem.at[i]) for i, (f, n) in enumerate(loads)]
    for i in (0, OWN_HEADS, *range(1, OWN_HEADS), *range(OWN_HEADS + 1, len(loads))):
        loads[i].start()
    rows_in = kx_ref.shape[1]
    piece_rows = rows_in // 4
    scale = HEAD_DIM**-0.5
    lane = lax.broadcasted_iota(jnp.int32, (piece_rows, LANES), 1)
    if first:
        for p in range(4):
            rows = slice(p * piece_rows, (p + 1) * piece_rows)
            left = grads[p][:, :LANES].astype(f32)
            right = grads[p][:, LANES:].astype(f32)
            right = jnp.concatenate([right, jnp.zeros_like(right)], axis=1)
            for h, wide in enumerate((left, pltpu.roll(left, HEAD_DIM, 1), right)):
                grad = jnp.where(lane < HEAD_DIM, wide, 0.0)
                delta = jnp.sum(grad * attx_ref[h, rows, :], axis=1, keepdims=True)
                d_high, d_mid, d_low = split_three(delta)
                grad = jnp.where(lane == HEAD_DIM, d_high, grad)
                grad = jnp.where(lane == HEAD_DIM + 1, d_mid, grad)
                grad = jnp.where(lane == HEAD_DIM + 2, d_low, grad)
                dox_ref[h, rows, :] = grad.astype(bf16)
        dqt_ref[...] = jnp.zeros_like(dqt_ref)
    else:
        dqt_ref[...] = dqt_in[...]
    lane_k = lax.broadcasted_iota(jnp.int32, (block_k, LANES), 1)
    low_k = lane_k < HEAD_DIM
    for j in range(rows_in // block_k):
        ks = slice(j * block_k, (j + 1) * block_k)
        parts = {}
        for h in range(OWN_HEADS):
            if j == 0:
                loads[h].wait()
                loads[OWN_HEADS + h].wait()
                kt_ref[h] = kx_ref[h, :, LANES:].astype(f32).T[:HEAD_DIM].astype(bf16)
            k = kx_ref[h, ks, :]
            v = vx_ref[h, ks, :]
            kt = kt_ref[h, :, ks]
            dk = jnp.zeros((block_k, LANES), f32)
            dv = jnp.zeros((block_k, LANES), f32)
            for i in range(rows_in // block_q):
                qs = slice(i * block_q, (i + 1) * block_q)
                s = lax.dot_general(k, qx_ref[h, qs, :], CONTRACT_LAST, preferred_element_type=f32)
                prob = jnp.exp2(s)
                do = dox_ref[h, qs, :]
                dp = lax.dot_general(v, do, CONTRACT_LAST, preferred_element_type=f32)
                ds = (prob * dp).astype(bf16)
                dv = dv + jnp.dot(prob.astype(bf16), do, preferred_element_type=f32)
                dk = dk + jnp.dot(ds, qp_ref[h, qs, :], preferred_element_type=f32)
                dqt_ref[h, :, qs] += jnp.dot(kt, ds, preferred_element_type=f32)
            parts[OWN_HEADS + h] = dk * scale
            parts[2 * OWN_HEADS + h] = dv
        for tile in range(1, WIDE // LANES):
            left, right = parts.get(2 * tile), parts.get(2 * tile + 1)
            left = jnp.zeros((block_k, LANES), f32) if left is None else left
            right = 0.0 if right is None else pltpu.roll(right, HEAD_DIM, 1)
            both = jnp.where(low_k, left, right).astype(bf16)
            all_ref[ks, tile * LANES : (tile + 1) * LANES] = both
    if last:
        tall = jnp.concatenate([dqt_ref[0], dqt_ref[1]], axis=0) * scale
        all_ref[:, :LANES] = tall.T.astype(bf16)
        tall = dqt_ref[2] * scale
        tall = jnp.concatenate([tall, jnp.zeros_like(tall)], axis=0).T
        lane_all = lax.broadcasted_iota(jnp.int32, (rows_in, LANES), 1)
        old = all_ref[:, LANES : 2 * LANES].astype(f32)
        all_ref[:, LANES : 2 * LANES] = jnp.where(lane_all < HEAD_DIM, tall, old).astype(bf16)
    skip = 0 if last else LANES
    for load in loads[2 * OWN_HEADS :]:
        load.wait()
    d_weight = [None, None]
    for p in range(4):
        rows = slice(p * piece_rows, (p + 1) * piece_rows)
        own = all_ref[rows, skip:]
        dx = lax.dot_general(own, w_ref[:, skip:], CONTRACT_LAST, preferred_element_type=f32)
        out_ref = keep_ref if p % 2 == 0 else send_ref
        out_ref[p // 2] = dx.astype(bf16)
        piece = lax.dot_general(
            pieces[p][...], own, (((0,), (0,)), ((), ())), preferred_element_type=f32
        )
        d_weight[0] = piece if p == 0 else d_weight[0] + piece
        col = jnp.sum(own.astype(f32), axis=0, keepdims=True)
        d_weight[1] = col if p == 0 else d_weight[1] + col
    grad, col = d_weight
    if last:
        dw_out[:, :LANES] = grad[:, :LANES].astype(bf16)
        dw_out[:, LANES:] = (grad[:, LANES:] + dw_in[...]).astype(bf16)
        col_out[:, :LANES] = jnp.broadcast_to(col[:, :LANES], (8, LANES))
        col_out[:, LANES:] = col[:, LANES:] + col_in[...]
    elif first:
        dw_out[...] = grad
        col_out[...] = jnp.broadcast_to(col, col_out.shape)
    else:
        dw_out[...] = grad + dw_in[...]
        col_out[...] = col + col_in[...]


def attend_back_chunk(first, last, chunk, pieces, shared, carry):
    kx, vx = chunk
    qx2, qp, w, grads, attx = shared
    rows, width = kx.shape[1], w.shape[0]
    far = [in_hbm(v) for v in (kx, vx, w, *pieces)]
    operands = [*far, qx2, qp]
    operands += [*grads, attx] if first else list(carry)
    half = jax.ShapeDtypeStruct((2, rows // 4, width), bf16)
    out_shape = [half, half]
    scratch = [
        pltpu.VMEM((OWN_HEADS, HEAD_DIM, rows), bf16),
        pltpu.VMEM((rows, WIDE), bf16),
        pltpu.SemaphoreType.DMA((2 * OWN_HEADS + 5,)),
        *[pltpu.VMEM(v.shape, v.dtype) for v in far],
    ]
    if first:
        out_shape.append(jax.ShapeDtypeStruct((OWN_HEADS, rows, LANES), bf16))
    if last:
        out_shape.append(jax.ShapeDtypeStruct((width, WIDE), bf16))
        out_shape.append(jax.ShapeDtypeStruct((8, WIDE), f32))
        scratch.append(pltpu.VMEM((OWN_HEADS, HEAD_DIM, rows), f32))
    else:
        out_shape.append(jax.ShapeDtypeStruct((OWN_HEADS, HEAD_DIM, rows), f32))
        out_shape.append(jax.ShapeDtypeStruct((width, WIDE - LANES), f32))
        out_shape.append(jax.ShapeDtypeStruct((8, WIDE - LANES), f32))
    return pl.pallas_call(
        partial(backward_kernel, first, last, min(256, rows), min(1024, rows)),
        out_shape=out_shape,
        in_specs=[pl.BlockSpec(memory_space=pltpu.HBM)] * len(far)
        + vmem_specs(len(operands) - len(far)),
        out_specs=vmem_specs(len(out_shape)),
        scratch_shapes=scratch,
        compiler_params=pltpu.CompilerParams(vmem_limit_bytes=26 * MIB),
        cost_estimate=pl.CostEstimate(
            flops=int(1.5e10), transcendentals=OWN_HEADS * rows * rows, bytes_accessed=int(1e7)
        ),
        name="attend_backward",
    )(*operands)


def norm_forward(value, gain, shift):
    center = value - jnp.mean(value, axis=-1, keepdims=True)
    spread = jnp.mean(center * center, axis=-1, keepdims=True)
    inverse = lax.rsqrt(spread + norm_eps)
    normal = center * inverse
    return normal * gain + shift, normal, inverse


def norm_backward(grad, gain, normal, inverse):
    inner = grad * gain
    mean = jnp.mean(inner, axis=-1, keepdims=True)
    along = jnp.mean(inner * normal, axis=-1, keepdims=True)
    return inverse * (inner - mean - normal * along)


CONTRACT_FIRST = (((0,), (0,)), ((), ()))


def ffn_kernel(layout, *refs):
    n_q, n_b, own_rows, fold, aligned = layout
    refs = list(refs)
    where_ref = refs.pop(0)
    att_refs = [refs.pop(0) for _ in range(4)]
    x_ref, cot_ref, vec_ref, eb_ref = [refs.pop(0) for _ in range(4)]
    packed = [refs.pop(0) for _ in range(2 if aligned else 1)]
    out_ref, resid_ref = [refs.pop(0) for _ in range(2)]
    da_refs = [refs.pop(0) for _ in range(4)]
    vec_out = refs.pop(0)
    targets = [refs.pop(0) for _ in range(3 if aligned else 1)]
    wo, w1, w2, go, g1, g2, act, slope, in_sem, out_sem = refs
    group, zi, xi, ci, bi, start, length = [where_ref[i] for i in range(7)]
    rows, width = x_ref.shape

    def lanes(i):
        return slice(i * width, (i + 1) * width)

    weights = [wo, *[w1.at[k] for k in range(fold)], *[w2.at[k] for k in range(fold)]]
    block = n_b * own_rows
    for i, weight in enumerate(weights):
        if not aligned:
            pltpu.make_async_copy(packed[0].at[:, lanes(i)], weight, in_sem.at[i]).start()
            continue
        for half in range(2):
            for m in range(2 * n_q):
                src = packed[half].at[m * block : (m + 1) * block, lanes(i)]
                at = pl.ds(pl.multiple_of((2 * m + (ci ^ half)) * block, 16), block)
                pltpu.make_async_copy(src, weight.at[at], in_sem.at[i]).start()
    loads = [pltpu.make_async_copy(w, w, in_sem.at[i]) for i, w in enumerate(weights)]

    def group_rows(r):
        other = (2 * (xi ^ (r // 2))) + (ci ^ (r % 2))
        return pl.ds(pl.multiple_of(other * OWN_WIDTH, HEAD_DIM), OWN_WIDTH)

    obias, gain1, shift1, sbias, gain2, shift2 = [vec_ref[i : i + 1, :] for i in range(2, 8)]
    loads[0].wait()
    branch = obias + jnp.zeros((rows, width), f32)
    for r in range(4):
        branch += jnp.dot(att_refs[r][...], wo[group_rows(r), :], preferred_element_type=f32)
    hidden, normal1, inverse1 = norm_forward(x_ref[...].astype(f32) + branch, gain1, shift1)
    hidden_low = hidden.astype(bf16)
    shrunk = sbias + hidden
    for k in range(fold):
        loads[1 + k].wait()
        expanded = jnp.dot(hidden_low, w1[k], preferred_element_type=f32) + eb_ref[k : k + 1, :]
        cdf = 0.5 * (1.0 + lax.erf(expanded * (2.0**-0.5)))
        pdf = jnp.exp(-0.5 * expanded * expanded) * ((2.0 * math.pi) ** -0.5)
        act[k] = (expanded * cdf).astype(bf16)
        slope[k] = cdf + expanded * pdf
        loads[1 + fold + k].wait()
        shrunk += jnp.dot(act[k], w2[k], preferred_element_type=f32)
    result, normal2, inverse2 = norm_forward(shrunk, gain2, shift2)
    out_ref[...] = result.astype(bf16)
    row = lax.broadcasted_iota(jnp.int32, (rows, width), 0)
    seed = jnp.where(start + row < length, cot_ref[...].astype(f32), 0.0)
    vec_out[4:5, :] = jnp.sum(seed * normal2, axis=0, keepdims=True)
    vec_out[5:6, :] = jnp.sum(seed, axis=0, keepdims=True)
    resid2 = norm_backward(seed, gain2, normal2, inverse2)
    shrunk_low = resid2.astype(bf16)
    vec_out[3:4, :] = jnp.sum(shrunk_low.astype(f32), axis=0, keepdims=True)
    hidden_grad = resid2
    for k in range(fold):
        active_grad = lax.dot_general(
            shrunk_low, w2[k], CONTRACT_LAST, preferred_element_type=f32
        )
        expanded_low = (active_grad * slope[k]).astype(bf16)
        vec_out[8 + k : 9 + k, :] = jnp.sum(expanded_low.astype(f32), axis=0, keepdims=True)
        hidden_grad += lax.dot_general(
            expanded_low, w1[k], CONTRACT_LAST, preferred_element_type=f32
        )
        g2[k] = lax.dot_general(
            act[k], shrunk_low, CONTRACT_FIRST, preferred_element_type=f32
        ).astype(bf16)
        g1[k] = lax.dot_general(
            hidden_low, expanded_low, CONTRACT_FIRST, preferred_element_type=f32
        ).astype(bf16)
    vec_out[1:2, :] = jnp.sum(hidden_grad * normal1, axis=0, keepdims=True)
    vec_out[2:3, :] = jnp.sum(hidden_grad, axis=0, keepdims=True)
    resid1 = norm_backward(hidden_grad, gain1, normal1, inverse1)
    resid_ref[...] = resid1
    branch_low = resid1.astype(bf16)
    vec_out[0:1, :] = jnp.sum(branch_low.astype(f32), axis=0, keepdims=True)
    vec_out[6:8, :] = jnp.zeros((2, width), f32)
    vec_out[8 + fold :, :] = jnp.zeros((vec_out.shape[0] - 8 - fold, width), f32)
    for r in range(4):
        da_refs[r][...] = lax.dot_general(
            branch_low, wo[group_rows(r), :], CONTRACT_LAST, preferred_element_type=f32
        ).astype(bf16)
        go[group_rows(r), :] = lax.dot_general(
            att_refs[r][...], branch_low, CONTRACT_FIRST, preferred_element_type=f32
        ).astype(bf16)
    units = [g2.at[k] for k in range(fold)] + [g1.at[k] for k in range(fold)] + [go]
    if aligned:
        *parts, whole = unit_parts(fold)
        for i, part in enumerate(parts):
            for dc in range(2):
                target, sem = targets[2 * i + dc], out_sem.at[2 * i + dc]
                for dx in range(2):
                    for jz in range(n_q):
                        m = ((zi ^ jz) * 2 + (xi ^ dx)) * 2 + (ci ^ dc)
                        at = pl.ds(pl.multiple_of(m * block, 16), block)
                        for place, unit in enumerate(part):
                            dst = target.at[dx, jz, :, lanes(place)]
                            pltpu.make_async_copy(units[unit].at[at], dst, sem).start()
        for place, unit in enumerate(whole):
            dst = targets[-1].at[:, lanes(place)]
            pltpu.make_async_copy(units[unit], dst, out_sem.at[len(targets) - 1]).start()
    else:
        for i, unit in enumerate(units):
            pltpu.make_async_copy(unit, targets[0].at[:, lanes(i)], out_sem.at[0]).start()
    for i, dst in enumerate(targets):
        pltpu.make_async_copy(dst, dst, out_sem.at[i]).wait()


def unit_parts(fold):
    count = 1 + 2 * fold
    return [range(count // 3), range(count // 3, count)]


def ffn_block(layout, where, att, x, cot, vectors, ebias, packed):
    n_q, n_b, own_rows, fold, aligned = layout
    rows, width = x.shape
    ff = fold * width
    operands = [where, *att, x, cot, vectors, ebias, *[in_hbm(v) for v in packed]]
    in_specs = [pl.BlockSpec(memory_space=pltpu.SMEM)] + vmem_specs(8)
    in_specs += [pl.BlockSpec(memory_space=pltpu.HBM)] * len(packed)
    out_shape = [
        jax.ShapeDtypeStruct((rows, width), bf16),
        jax.ShapeDtypeStruct((rows, width), f32),
        *[jax.ShapeDtypeStruct((rows, OWN_WIDTH), bf16)] * 4,
        jax.ShapeDtypeStruct((16, width), f32),
    ]
    if aligned:
        lead = (2, n_q, n_b * own_rows)
        sizes = [len(part) * width for part in unit_parts(fold)]
        targets = [pltpu.HBM((*lead, size), bf16) for size in sizes[:-1] for _ in range(2)]
        targets.append(pltpu.HBM((width, sizes[-1]), bf16))
    else:
        targets = [pltpu.HBM((width, width + 2 * ff), bf16)]
    weight_scratch = [
        pltpu.VMEM((width, width), bf16),
        pltpu.VMEM((fold, width, width), bf16),
        pltpu.VMEM((fold, width, width), bf16),
    ]
    return pl.pallas_call(
        partial(ffn_kernel, layout),
        out_shape=out_shape + targets,
        in_specs=in_specs,
        out_specs=vmem_specs(len(out_shape)) + [pl.BlockSpec(memory_space=pltpu.HBM)] * len(targets),
        scratch_shapes=weight_scratch
        + weight_scratch
        + [
            pltpu.VMEM((fold, rows, width), bf16),
            pltpu.VMEM((fold, rows, width), f32),
            pltpu.SemaphoreType.DMA((1 + 2 * fold,)),
            pltpu.SemaphoreType.DMA((6,)),
        ],
        compiler_params=pltpu.CompilerParams(vmem_limit_bytes=32 * MIB),
        cost_estimate=pl.CostEstimate(
            flops=int(2e10), transcendentals=2 * rows * ff, bytes_accessed=int(3e7)
        ),
        name="feed_forward",
    )(*operands)


def order_kernel(n_q, n_b, where_ref, blocks_ref, out_ref):
    group, zi, bi = [where_ref[i] for i in range(3)]
    rows = blocks_ref.shape[3]
    for m in range(4 * n_q):
        q, g = m // 4, m % 4
        far, r = lax.rem(q + n_q - zi, n_q), g ^ group
        both = [
            blocks_ref[lax.rem(b + n_b - bi, n_b), far, r].astype(f32) for b in range(n_b)
        ]
        at = slice(m * n_b * rows, (m + 1) * n_b * rows)
        out_ref[at, :] = jnp.concatenate(both, axis=0).astype(bf16)


def order_rows(n_q, n_b, where, blocks):
    rows, lanes = blocks.shape[3:]
    return pl.pallas_call(
        partial(order_kernel, n_q, n_b),
        out_shape=jax.ShapeDtypeStruct((4 * n_q * n_b * rows, lanes), bf16),
        in_specs=[pl.BlockSpec(memory_space=pltpu.SMEM)] + vmem_specs(1),
        out_specs=vmem_specs(1)[0],
        compiler_params=pltpu.CompilerParams(vmem_limit_bytes=12 * MIB),
        name="order_rows",
    )(where, blocks)


def from_shift(value, axis, count, step):
    return lax.ppermute(value, axis, [((i + step) % count, i) for i in range(count)])


def square_swap(value, r):
    if r == 0:
        return value
    if r == 1:
        return lax.ppermute(value, "c", [(0, 1), (1, 0)])
    if r == 2:
        return lax.ppermute(value, "x", [(0, 1), (1, 0)])
    return lax.ppermute(value, ("x", "c"), [(0, 3), (3, 0), (1, 2), (2, 1)])


def pick(stacked, index, dim=0):
    return lax.dynamic_index_in_dim(stacked, index, dim, keepdims=False)


class Chain:
    def __init__(self, state, *steps):
        self.state, self.steps = tuple(state), list(steps)


def launch(chain):
    chain.state = tuple(chain.steps.pop(0)(*chain.state))


def run_stage(chains, outs=(), settle=()):
    for chain in chains:
        launch(chain)
    joined = [*chains, *settle]
    outs, states = lax.optimization_barrier((tuple(outs), [c.state for c in joined]))
    for chain, state in zip(joined, states):
        chain.state = tuple(state)
    return outs


def away_sum(total, axis, count):
    parts = [total[j].astype(bf16) for j in range(1, count)]
    return [from_shift(part, axis, count, count - j - 1) for j, part in enumerate(parts)]


def weight_sum(keep, send, n_q, n_b, bi):
    def own_b(keep, got, j):
        shape = (2, n_q, n_b, -1, keep.shape[-1])
        both = [pick(v.reshape(shape), (bi + j) % n_b, 2).astype(f32) for v in (keep, got)]
        return both[0] + both[1]

    def over_core(keep, send):
        return keep, square_swap(send, 1)

    def over_b(keep, got):
        away = [own_b(keep, got, j).astype(bf16) for j in range(1, n_b)]
        return keep, got, *[from_shift(v, "b", n_b, n_b - 1 - j) for j, v in enumerate(away)]

    def over_x(keep, got, *more):
        total = own_b(keep, got, 0) + sum(v.astype(f32) for v in more)
        return total[0], *away_sum(total, "x", 2)

    def halve(step):
        def over_q(own, got):
            total = own + got.astype(f32)
            pairs = [(i, i ^ step) for i in range(n_q)]
            return total[0::2], lax.ppermute(total[1::2].astype(bf16), "q", pairs)

        return over_q

    halves = [1 << k for k in range(n_q.bit_length() - 1)]
    return Chain((keep, send), over_core, over_b, over_x, *[halve(half) for half in halves])


def toward(j, n_q):
    return (j - 1, n_q - 1) if 2 * j <= n_q else ((j + 1) % n_q, 1)


def token_sum(keep, send, n_q, j, farther):
    def over_core(keep, send):
        return keep, square_swap(send, 1)

    def over_x(keep, got):
        total = keep.astype(f32) + got.astype(f32)
        return total[0], square_swap(total[1].astype(bf16), 2)

    def over_q(own, got):
        total = own + got.astype(f32) + sum(chain_sum(c) for c in farther)
        return (from_shift(total.astype(bf16), "q", n_q, toward(j, n_q)[1]),)

    return Chain((keep, send), over_core, over_x, *([over_q] if j else []))


def chain_sum(chain):
    return sum(v.astype(f32).reshape(chain.state[0].shape) for v in chain.state)


def deinterleave(fold):
    size = fold * LANES
    lane = jnp.arange(size)
    return (lane[:, None] // fold + (lane[:, None] % fold) * LANES == lane[None, :]).astype(bf16)


def per_device(
    n_q,
    n_b,
    inputs,
    lengths,
    cotangent,
    triple_weight,
    query_bias,
    value_bias,
    output_weight,
    output_bias,
    first_gain,
    first_shift,
    expand_weight,
    expand_bias,
    shrink_weight,
    shrink_bias,
    second_gain,
    second_shift,
):
    zi, xi, ci, bi = [lax.axis_index(a) for a in AXES]
    group = 2 * xi + ci
    _, seq_rows, width = inputs.shape
    own_rows = triple_weight.shape[0]
    ff = expand_weight.shape[1]
    fold = ff // width
    aligned = n_b * own_rows % 16 == 0 and n_q & (n_q - 1) == 0
    x_own = inputs[0]

    turn = deinterleave(fold)
    expand_own = expand_weight.astype(bf16).reshape(own_rows, -1, fold * LANES)
    expand_own = jnp.einsum("rbs,st->rbt", expand_own, turn, preferred_element_type=f32)
    expand_own = expand_own.astype(bf16).reshape(own_rows, -1, fold, LANES).transpose(0, 2, 1, 3)
    packed = jnp.concatenate(
        [
            output_weight.astype(bf16),
            expand_own.reshape(own_rows, ff),
            shrink_weight.astype(bf16).reshape(own_rows, ff),
        ],
        axis=1,
    )
    if aligned:
        own_half = lax.all_gather(packed, ("q", "x", "b"), axis=0, tiled=True)
    else:
        gathered_ffn = [lax.all_gather(packed, AXES, axis=0, tiled=True)]

    names = [query_bias, value_bias, output_bias, first_gain, first_shift]
    names += [shrink_bias, second_gain, second_shift]
    vectors = jnp.stack(names, axis=1)
    vectors = jnp.concatenate([vectors, expand_bias.reshape(own_rows, fold)], axis=1).astype(bf16)
    n_vec = vectors.shape[1]
    vectors = jnp.pad(vectors, ((0, 0), (0, WIDE - VECTORS - n_vec)))
    thirds = triple_weight.astype(bf16).reshape(own_rows, 3, GROUPS, OWN_WIDTH)

    def columns_of(g):
        mine = [pick(thirds[:, t], g, 1) for t in range(3)]
        return jnp.concatenate(mine + [vectors], axis=1)

    def rows_square(*blocks):
        return [square_swap(block, r) for r, block in enumerate(blocks)]

    def rows_q(*blocks):
        square = jnp.stack(blocks)
        return [square] + [from_shift(square, "q", n_q, j) for j in range(1, n_q)]

    def rows_b(*blocks):
        both = jnp.stack(blocks)
        return [both] + [from_shift(both, "b", n_b, j) for j in range(1, n_b)]

    weight_rows = Chain([columns_of(group ^ r) for r in range(4)], rows_square, rows_q, rows_b)

    def token_chunk(j):
        def over_q():
            source, step = toward(j, n_q)
            own = chunks[source].state[0] if source else x_own
            if j not in arrival[:2]:
                at = arrival.index(j)
                before = line[at - 1].state[0] if at > 2 else weight_rows.state
                own = lax.optimization_barrier((own, before))[0]
            return (from_shift(own, "q", n_q, n_q - step),)

        def over_x(own):
            return own, square_swap(own, 2)

        def over_core(own, other):
            halves = square_swap(jnp.stack([own, other]), 1)
            return own, halves[0], other, halves[1]

        return Chain(() if j else (x_own,), *([over_q] if j else []), over_x, over_core)

    arrival = []
    for j in [k for pair in zip(range(1, n_q), range(n_q - 1, 0, -1)) for k in pair]:
        arrival += [] if j in arrival else [j]
    arrival = [0] + arrival
    chunks = {j: token_chunk(j) for j in arrival}
    line = [chunks[j] for j in arrival]


    for slot in range(3):
        ready = line[:2] if slot < 2 else line[1:3]
        run_stage([c for c in ready if c.steps] + [weight_rows])
    chunk_x = {}

    by_distance = jnp.stack(weight_rows.state)
    if aligned:
        spot = jnp.stack([group, zi, bi]).astype(jnp.int32)
        w_own = order_rows(n_q, n_b, spot, by_distance)
    else:
        ordered = jnp.stack([pick(by_distance, (i - bi) % n_b) for i in range(n_b)], axis=3)
        ordered = jnp.stack([pick(ordered, group ^ g, 1) for g in range(4)], axis=1)
        ordered = jnp.stack([pick(ordered, (i - zi) % n_q) for i in range(n_q)])
        w_own = ordered.transpose(0, 1, 3, 2, 4).reshape(width, WIDE)
    turned = w_own[:, VECTORS : VECTORS + n_vec].astype(f32)
    turned = turned.T
    ebias = turned[8:]
    turned = turned[:8]
    own_bias = lax.dynamic_slice_in_dim(turned, group * OWN_WIDTH, OWN_WIDTH, 1)
    zero = jnp.zeros((1, OWN_WIDTH), f32)
    bias_row = jnp.concatenate(
        [own_bias[:1], zero, own_bias[1:2], jnp.zeros((1, WIDE - VECTORS), f32)], axis=1
    )

    def where_of(j):
        zj = (zi + j) % n_q
        spots = [(zj * 4 + (group ^ r)) * seq_rows for r in range(4)]
        return jnp.stack(spots + [lengths[0]]).astype(jnp.int32)

    weights = (w_own, bias_row)
    kept = {}
    carry = None
    for step, j in enumerate(arrival):
        first, last = step == 0, step == n_q - 1
        if chunks[j].steps:
            run_stage([chunks[j]])
        chunk_x[j] = chunks[j].state
        outs = attend_chunk(first, last, where_of(j), chunk_x[j], weights, carry)
        ready = line[max(2, step + 1) : step + 4]
        outs = run_stage([c for c in ready if c.steps], outs)
        kept[j] = (outs[0], outs[1])
        outs = outs[2:]
        if first:
            qx, qp = outs[:2]
            outs = outs[2:]
        carry = (qx, *outs)
    att, attx, qx2 = carry[1:5], carry[5], carry[6]

    if aligned:
        own_half, att = lax.optimization_barrier((own_half, att))
        gathered_ffn = [own_half, square_swap(own_half, 1)]
    att = [square_swap(att[r], r) for r in range(4)]
    start = (zi * 4 + group) * seq_rows
    where = jnp.stack([group, zi, xi, ci, bi, start, lengths[0]]).astype(jnp.int32)
    layout = (n_q, n_b, own_rows, fold, aligned)
    outs = ffn_block(layout, where, att, x_own, cotangent[0], turned, ebias, gathered_ffn)
    output, resid_first_grad = outs[:2]
    att_grads, vec_grads, summands = outs[2:6], outs[6], outs[7:]
    square = Chain(att_grads, lambda *parts: [square_swap(v, r) for r, v in enumerate(parts)])

    sums = []
    if aligned:
        sums.append(weight_sum(summands[0], summands[1], n_q, n_b, bi))
    reduced = lax.psum_scatter(summands[-1], AXES, scatter_dimension=0, tiled=True)
    run_stage([square] + sums)
    plan = [([0], [], [])] * 4
    shared = (qx2, qp, w_own, square.state, attx)
    carry = None
    moving, moving_to = [], {}
    for step, j in enumerate(reversed(arrival)):
        first, last = step == 0, step == n_q - 1
        with_it, ending, going_on = [], [], []
        if sums and step < len(plan):
            with_it, ending, going_on = [[sums[i] for i in part] for part in plan[step]]
        outs = attend_back_chunk(first, last, kept[j], chunk_x[j], shared, carry)
        run = with_it + [c for c in moving if c.steps]
        for chain in run + going_on:
            launch(chain)
        free = outs[2:] if last else []
        outs = run_stage([], outs[:2] if last else outs, settle=run + ending)
        outs = (*outs, *free)
        keep, send = outs[:2]
        farther = [c for k, c in moving_to.items() if k and toward(k, n_q)[0] == j and j]
        moving_to[j] = token_sum(keep, send, n_q, j, farther)
        moving.append(moving_to[j])
        outs = outs[2:]
        if first:
            dox = outs[0]
            outs = outs[1:]
        carry = (dox, *outs)
        if not last:
            carry = run_stage(moving[-1:], carry)
    grad_joint, col = carry[1:]

    own_bias = jnp.stack([col[0, :OWN_WIDTH], col[0, 2 * OWN_WIDTH : 3 * OWN_WIDTH]])
    bias_grads = lax.dynamic_update_slice(
        jnp.zeros((2, width), f32), own_bias, (0, group * OWN_WIDTH)
    )
    tall = jnp.concatenate([bias_grads, vec_grads[:6], vec_grads[8 : 8 + fold]], axis=0).T
    tall_high = tall.astype(bf16)
    tall_low = (tall - tall_high.astype(f32)).astype(bf16)
    room = jnp.zeros((width, WIDE - VECTORS - 2 * n_vec), bf16)
    blocks = jnp.concatenate([grad_joint[:, :VECTORS], tall_high, tall_low, room], axis=1)
    total = blocks.reshape(n_q, 4, n_b, own_rows, WIDE)

    def rows_over_b(total):
        parts = [pick(total, (bi + j) % n_b, 2) for j in range(n_b)]
        return parts[0], *away_sum(parts, "b", n_b)

    def rows_over_q(*parts):
        total = sum(v.astype(f32) for v in parts)
        parts = [pick(total, (zi + j) % n_q) for j in range(n_q)]
        return parts[0], *away_sum(parts, "q", n_q)

    def rows_over_square(*parts):
        total = sum(v.astype(f32) for v in parts).astype(bf16)
        return [square_swap(pick(total, group ^ r), r) for r in range(4)]

    rows = Chain((total,), rows_over_b, rows_over_q, rows_over_square)
    while any(c.steps for c in [rows, *sums, *moving]):
        run_stage([c for c in [rows, *sums, *moving] if c.steps])
        if not rows.steps:
            reduced, rows.state = lax.optimization_barrier((reduced, rows.state))
    summed = reduced.astype(f32)
    token_grad = resid_first_grad
    for j, chain in moving_to.items():
        if j == 0 or toward(j, n_q)[0] == 0:
            token_grad = token_grad + chain_sum(chain)
    input_grad = token_grad.astype(bf16)
    if aligned:
        summed = jnp.concatenate([*[chain_sum(c)[0] for c in sums], summed], axis=1)
    parts = jnp.stack(rows.state)
    parts = jnp.stack([pick(parts, group ^ g) for g in range(4)])
    grad_triple = parts[:, :, :VECTORS].reshape(GROUPS, own_rows, 3, OWN_WIDTH)
    grad_triple = grad_triple.transpose(1, 2, 0, 3).reshape(own_rows, -1).astype(f32)
    small = jnp.sum(parts[:, :, VECTORS : VECTORS + 2 * n_vec].astype(f32), axis=0)
    small = small[:, :n_vec] + small[:, n_vec:]
    grad_expand = summed[:, ff : 2 * ff].reshape(own_rows, fold, -1, LANES).transpose(0, 2, 1, 3)
    grad_expand = jnp.einsum(
        "rbs,ts->rbt",
        grad_expand.reshape(own_rows, -1, fold * LANES),
        turn.astype(f32),
        precision=lax.Precision.HIGHEST,
        preferred_element_type=f32,
    ).reshape(own_rows, ff)
    return (
        output[None],
        input_grad[None],
        grad_triple,
        small[:, 0],
        small[:, 1],
        summed[:, 2 * ff :],
        small[:, 2],
        small[:, 3],
        small[:, 4],
        grad_expand,
        small[:, 8:].reshape(-1),
        summed[:, :ff].reshape(-1, width),
        small[:, 5],
        small[:, 6],
        small[:, 7],
    )


def solution(mesh):
    n_seq, n_b = mesh.shape["seq"], mesh.shape["batch"]
    n_q = n_seq // GROUPS
    fine = Mesh(mesh.devices.reshape(n_q, 2, 2, n_b), AXES)
    tokens = P("b", ("q", "x", "c"), None)
    matrix = P(AXES, None)
    vector = P(AXES)
    in_specs = (
        tokens,
        P("b"),
        tokens,
        matrix,
        vector,
        vector,
        matrix,
        vector,
        vector,
        vector,
        matrix,
        vector,
        matrix,
        vector,
        vector,
        vector,
    )
    out_specs = (
        tokens,
        tokens,
        matrix,
        vector,
        vector,
        matrix,
        vector,
        vector,
        vector,
        matrix,
        vector,
        matrix,
        vector,
        vector,
        vector,
    )
    return jax.shard_map(
        partial(per_device, n_q, n_b),
        mesh=fine,
        in_specs=in_specs,
        out_specs=out_specs,
        check_vma=False,
    )
```
